32 devices in a mesh: ctx: 8 (over z, y), wsh: 4 (over x, core).
Axes of the slice: x: 2, y: 2, z: 4, core: 2. Of those that a mesh axis runs over, the one named last changes fastest.
Arguments:
- tokens: bfloat16 [4, 1024, 768], P('wsh', 'ctx'), may hold values from -6 to 6
- teacher: bfloat16 [4, 1024, 768], P('wsh', 'ctx'), may hold values from -6 to 6
- doc_lengths: int32 [4, 8], P('wsh'), may hold values from 1 to 512, 1024 in all within a row
- valid_len: int32 [4], P('wsh'), may hold values from 512 to 1024
- q_weight: bfloat16 [768, 768], P('wsh'), may hold values from -0.21875 to 0.21875
- q_bias: bfloat16 [768], P('wsh'), may hold values from -3 to 3
- k_weight: bfloat16 [768, 768], P('wsh'), may hold values from -0.21875 to 0.21875
- v_weight: bfloat16 [768, 768], P('wsh'), may hold values from -0.21875 to 0.21875
- v_bias: bfloat16 [768], P('wsh'), may hold values from -0.29882812 to 0.29882812
- o_weight: bfloat16 [768, 768], P('wsh'), may hold values from -1.25 to 1.25
- o_bias: bfloat16 [768], P('wsh'), may hold values from -3 to 3
- ln1_gain: bfloat16 [768], P('wsh'), may hold values from 0.25 to 1.75
- ln1_bias: bfloat16 [768], P('wsh'), may hold values from -3 to 3
- in_weight: bfloat16 [768, 3072], P('wsh'), may hold values from -0.21875 to 0.21875
- in_bias: bfloat16 [3072], P('wsh'), may hold values from -3 to 3
- out_weight: bfloat16 [3072, 768], P('wsh'), may hold values from -0.109375 to 0.109375
- out_bias: bfloat16 [768], P('wsh'), may hold values from -3 to 3
- ln2_gain: bfloat16 [768], P('wsh'), may hold values from 0.25 to 1.75
- ln2_bias: bfloat16 [768], P('wsh'), may hold values from -3 to 3
Outputs:
- output: bfloat16 [4, 1024, 768], P('wsh', 'ctx')
- loss: float32 [], replicated
- input_grad: float32 [4, 1024, 768], P('wsh', 'ctx')
- q_weight_grad: float32 [768, 768], P('wsh')
- q_bias_grad: float32 [768], P('wsh')
- k_weight_grad: float32 [768, 768], P('wsh')
- v_weight_grad: float32 [768, 768], P('wsh')
- v_bias_grad: float32 [768], P('wsh')
- o_weight_grad: float32 [768, 768], P('wsh')
- o_bias_grad: float32 [768], P('wsh')
- ln1_gain_grad: float32 [768], P('wsh')
- ln1_bias_grad: float32 [768], P('wsh')
- in_weight_grad: float32 [768, 3072], P('wsh')
- in_bias_grad: float32 [3072], P('wsh')
- out_weight_grad: float32 [3072, 768], P('wsh')
- out_bias_grad: float32 [768], P('wsh')
- ln2_gain_grad: float32 [768], P('wsh')
- ln2_bias_grad: float32 [768], P('wsh')
The draws below stay inside these ranges and needn't reach their ends.
Inputs may be any that keep to these rules, and one draw needn't show every extreme that they name: `doc_lengths`: row s lists, in order, the lengths of the documents that fill stream s; they sum to 1024 and the longest is exactly 512.
All inputs are finite; a program needn't handle non-finite values.
Results may differ from the reference program's by a relative error of at most 0.017.
Values may be sent and summed in bfloat16 or wider, within the bound.
A program may use at most 128 MiB of HBM per device.

```python
import math
import jax
import jax.numpy as jnp
import numpy as np
from jax import lax

D = 768
H = 12
HD = 64
FF = 3072
SEQ = 1024
STREAMS = 4
DOC_LEN = 512
DOCS = 8


def place_ends(values, key, smallest, largest):
    shape = values.shape
    place = [jax.random.randint(jax.random.fold_in(key, axis), (), 0, shape[axis]) for axis in range(len(shape))]
    values = values.at[tuple(place)].set(smallest)
    longest = shape.index(max(shape))
    place[longest] = (place[longest] + 1) % shape[longest]
    return values.at[tuple(place)].set(largest)


def level_of(rng, shape, cuts, least, high):
    level, own = 1.0, jax.random.fold_in(rng, 6)
    for axis_at, shards_of in cuts:
        draws = jnp.exp(jax.random.uniform(jax.random.fold_in(own, axis_at), (shards_of,), jnp.float32, least / len(cuts), high / len(cuts)))
        level = level * jnp.repeat(draws, shape[axis_at] // shards_of).reshape([-1 if axis == axis_at else 1 for axis in range(len(shape))])
    return level


def profile(number_of, total, reach, slope):
    portions = [(1 << 20) // math.isqrt(grade ** slope) + 1 for grade in range(2, number_of + 1)]
    surplus, given = total - reach - (number_of - 1), [1] * (number_of - 1)
    while surplus > 0:
        candidates = [i for i in range(number_of - 1) if given[i] < reach]
        whole, budget = sum([portions[i] for i in candidates]), surplus
        for i in candidates:
            extra = min(reach - given[i], max(1, budget * portions[i] // whole), surplus)
            given[i] = given[i] + extra
            surplus = surplus - extra
    return np.array([reach] + given)


def ragged_sizes(key, number_of, total, bound, lean):
    if number_of == 2:
        one = jax.random.randint(key, (), max(1, total - bound), min(bound, total - 1) + 1)
        return jnp.stack([one, total - one])
    sizes = jnp.asarray(profile(number_of, total, bound, lean), jnp.int32)
    pairs = (number_of - 1) // 2
    donor, receiver = sizes[1:1 + 2 * pairs:2], sizes[2:2 + 2 * pairs:2]
    room = jnp.minimum(donor - 1, bound - receiver)
    shifted = jax.random.randint(jax.random.fold_in(key, 1), (pairs,), 0, 1 << 20) % (room + 1)
    sizes = sizes.at[1:1 + 2 * pairs:2].set(donor - shifted).at[2:2 + 2 * pairs:2].set(receiver + shifted)
    return sizes[jax.random.permutation(jax.random.fold_in(key, 2), number_of)]


def normal_values(rng, shape, scale, reach, split=(), held_as=jnp.bfloat16):
    values = jax.random.normal(rng, shape, jnp.float32) * scale
    if len(split) > 0:
        values = level_of(rng, shape, split, -0.22, 0.18) * values
    return jnp.clip(values, min=-reach, max=reach).astype(held_as)


def setup_inputs(seed: int = 0) -> dict:
    streams_of = jax.random.split(jax.random.key(seed), 20)
    return {
        "tokens": normal_values(streams_of[0], (STREAMS, SEQ, D), 1.0, 6.0, ((0, 4), (1, 8))),
        "teacher": normal_values(streams_of[1], (STREAMS, SEQ, D), 1.0, 6.0, ((0, 4), (1, 8))),
        "doc_lengths": jax.vmap(lambda own: ragged_sizes(own, DOCS, SEQ, DOC_LEN, 1))(jax.random.split(streams_of[2], STREAMS)).reshape((STREAMS, DOCS)).astype(jnp.int32),
        "valid_len": place_ends(jax.random.randint(streams_of[3], (STREAMS,), SEQ // 2, SEQ + 1), jax.random.fold_in(streams_of[3], 1), SEQ // 2, SEQ).astype(jnp.int32),
        "q_weight": normal_values(streams_of[4], (D, D), D ** -0.5, 0.21875, ((0, 4),)),
        "q_bias": normal_values(streams_of[5], (D,), 0.5, 3.0, ((0, 4),)),
        "k_weight": normal_values(streams_of[6], (D, D), D ** -0.5, 0.21875, ((0, 4),)),
        "v_weight": normal_values(streams_of[7], (D, D), D ** -0.5, 0.21875, ((0, 4),)),
        "v_bias": normal_values(streams_of[8], (D,), 0.05, 0.29882812, ((0, 4),)),
        "o_weight": normal_values(streams_of[9], (D, D), (D // 32) ** -0.5, 1.25, ((0, 4),)),
        "o_bias": normal_values(streams_of[10], (D,), 0.5, 3.0, ((0, 4),)),
        "ln1_gain": jnp.clip(1.0 + 0.15 * jax.random.normal(streams_of[11], (D,), jnp.float32), 0.25, 1.75).astype(jnp.bfloat16),
        "ln1_bias": normal_values(streams_of[12], (D,), 0.5, 3.0, ((0, 4),)),
        "in_weight": normal_values(streams_of[13], (D, FF), D ** -0.5, 0.21875, ((0, 4),)),
        "in_bias": normal_values(streams_of[14], (FF,), 0.5, 3.0, ((0, 4),)),
        "out_weight": normal_values(streams_of[15], (FF, D), FF ** -0.5, 0.109375, ((0, 4),)),
        "out_bias": normal_values(streams_of[16], (D,), 0.5, 3.0, ((0, 4),)),
        "ln2_gain": jnp.clip(1.0 + 0.15 * jax.random.normal(streams_of[17], (D,), jnp.float32), 0.25, 1.75).astype(jnp.bfloat16),
        "ln2_bias": normal_values(streams_of[18], (D,), 0.5, 3.0, ((0, 4),)),
    }


EPSILON = 1e-06
HIGHEST = lax.Precision.HIGHEST

@jax.custom_vjp
def low(v):
    return lax.optimization_barrier(v.astype(jnp.bfloat16)).astype(jnp.float32)

@jax.custom_vjp
def low_back(v):
    return v

def low_keep(v):
    return (low(v), None)

def low_pass(kept, grad):
    return (grad,)

def back_keep(v):
    return (v, None)

def back_low(kept, grad):
    return (low(grad),)
low.defvjp(low_keep, low_pass)
low_back.defvjp(back_keep, back_low)

def matmul(left, right):
    return jnp.dot(left, right, precision=HIGHEST)

def layer_norm(value, gain, shift):
    mean = lax.optimization_barrier(jnp.mean(value, axis=-1, keepdims=True))
    centered = value - mean
    spread = lax.optimization_barrier(jnp.mean(centered * centered, axis=-1, keepdims=True))
    return centered * lax.rsqrt(spread + EPSILON) * gain + shift

def activate(value):
    return jax.nn.gelu(value, approximate=True)

def attend(queries, keys_all, values_all, documents, living):
    seq_len = queries.shape[0]
    query_heads = queries.reshape(seq_len, H, HD)
    key_heads = keys_all.reshape(seq_len, H, HD)
    value_heads = values_all.reshape(seq_len, H, HD)
    block_rows = math.gcd(seq_len, 512)
    score_scale = 1.0 / math.sqrt(HD)

    def one_block(start):
        query_block = lax.dynamic_slice_in_dim(query_heads, start, block_rows, 0)
        doc_block = lax.dynamic_slice_in_dim(documents, start, block_rows, 0)
        live_block = lax.dynamic_slice_in_dim(living, start, block_rows, 0)
        allowed = (doc_block[:, None] == documents[None, :]) & (live_block[:, None] == living[None, :])
        scores = low_back(jnp.einsum('qhd,khd->hqk', query_block, key_heads, precision=HIGHEST) * score_scale)
        weights = jnp.exp(jnp.where(allowed[None], scores, -1e+30))
        row_total = lax.optimization_barrier(jnp.sum(weights, axis=-1))
        weighted = low_back(jnp.einsum('hqk,khd->qhd', low(weights), value_heads, precision=HIGHEST))
        normed = weighted / jnp.transpose(row_total)[:, :, None]
        return low_back(low(normed)).reshape(block_rows, D)
    block_starts = jnp.arange(seq_len // block_rows, dtype=jnp.int32) * block_rows
    blocks = lax.map(jax.checkpoint(one_block), block_starts)
    return blocks.reshape(seq_len, D)

def one_stream(params, inputs, documents, living):
    w_query, b_query, w_key, w_value, b_value, w_out, b_out, gain_one, shift_one, w_inner, b_inner, w_back, b_back, gain_two, shift_two = params
    queries = low_back(low(matmul(inputs, w_query) + b_query))
    keys_all = low_back(low(matmul(inputs, w_key)))
    values_all = low_back(low(matmul(inputs, w_value) + b_value))
    context = attend(queries, keys_all, values_all, documents, living)
    attn = low_back(matmul(context, w_out) + b_out)
    settled = layer_norm(inputs + attn, gain_one, shift_one)
    inner = low_back(matmul(low(settled), w_inner) + b_inner)
    activated = low(activate(inner))
    branch = low_back(matmul(activated, w_back) + b_back)
    return layer_norm(settled + branch, gain_two, shift_two)

def reference(tokens, teacher, doc_lengths, valid_len, q_weight, q_bias, k_weight, v_weight, v_bias, o_weight, o_bias, ln1_gain, ln1_bias, in_weight, in_bias, out_weight, out_bias, ln2_gain, ln2_bias):
    params = tuple((item.astype(jnp.float32) for item in (q_weight, q_bias, k_weight, v_weight, v_bias, o_weight, o_bias, ln1_gain, ln1_bias, in_weight, in_bias, out_weight, out_bias, ln2_gain, ln2_bias)))
    inputs = tokens.astype(jnp.float32)
    positions = jnp.arange(SEQ, dtype=jnp.int32)
    lengths = doc_lengths.astype(jnp.int32)
    starts = (jnp.cumsum(lengths, axis=-1) - lengths).astype(jnp.int32)
    documents = (lax.optimization_barrier(jnp.sum((starts[:, None, :] <= positions[None, :, None]).astype(jnp.int32), axis=-1)) - 1).astype(jnp.int32)
    living = positions[None, :] < valid_len[:, None]

    def forward(weights_all, stream_inputs):

        def run(item):
            return one_stream(weights_all, item[0], item[1], item[2])
        return lax.map(run, (stream_inputs, documents, living))
    result, pullback = jax.vjp(forward, params, inputs)
    count = jnp.sum(valid_len).astype(jnp.float32)
    diff = jnp.where(living[:, :, None], result - teacher.astype(jnp.float32), 0.0)
    loss = jnp.sum(diff * diff) / (count * D)
    upstream = diff * (STREAMS * SEQ / count)
    param_grads, input_grad = pullback(upstream)
    g_query, g_qbias, g_key, g_value, g_vbias, g_out, g_obias, g_gain_one, g_shift_one, g_inner, g_ibias, g_back, g_bbias, g_gain_two, g_shift_two = param_grads
    return (result.astype(jnp.bfloat16), loss, input_grad, g_query, g_qbias, g_key, g_value, g_vbias, g_out, g_obias, g_gain_one, g_shift_one, g_inner, g_ibias, g_back, g_bbias, g_gain_two, g_shift_two)
```

```python
import math
import types

import jax
import jax.numpy as jnp
from jax import lax
from jax.experimental import pallas as pl
from jax.experimental.pallas import tpu as pltpu
from jax.sharding import PartitionSpec as P

D = 768
H = 12
HD = 64


EPSILON = 1e-06
MASKED = -1e30


def shifted(block, axis, distance):
    devices = range(lax.axis_size(axis))
    route = [((i - distance) % len(devices), i) for i in devices]
    return lax.ppermute(block, axis, route)


def layer_norm(value, gain, shift):
    mean = jnp.mean(value, axis=-1, keepdims=True)
    centered = value - mean
    spread = jnp.mean(centered * centered, axis=-1, keepdims=True)
    return centered * lax.rsqrt(spread + EPSILON) * gain + shift


def activate(value):
    return jax.nn.gelu(value, approximate=True)


def matmul(left, right):
    return jnp.dot(left, right, preferred_element_type=jnp.float32)


def left_product(left, right):
    return lax.dot_general(
        left, right, (((0,), (0,)), ((), ())), preferred_element_type=jnp.float32
    )


def right_product(left, right):
    return lax.dot_general(
        left, right, (((1,), (1,)), ((), ())), preferred_element_type=jnp.float32
    )


def document_of(positions, starts):
    return jnp.sum((starts[None, :] <= positions[:, None]).astype(jnp.int32), axis=1) - 1


def permitted(own_doc, own_live, other_doc, other_live):
    return (own_doc[:, None] == other_doc[None, :]) & (own_live[:, None] == other_live[None, :])


def block_weights(queries, key_block, allowed, score_scale):
    scores = (
        jnp.einsum("qhd,khd->hqk", queries, key_block, preferred_element_type=jnp.float32)
        * score_scale
    )
    return jnp.exp(jnp.where(allowed[None], scores, MASKED))


def forward_visit(sums_state, queries, key_block, value_block, allowed, score_scale):
    row_total, weighted = sums_state
    weights = block_weights(queries, key_block, allowed, score_scale)
    row_total = row_total + jnp.sum(weights, axis=-1)
    weighted = weighted + jnp.einsum(
        "hqk,khd->qhd",
        weights.astype(jnp.bfloat16),
        value_block,
        preferred_element_type=jnp.float32,
    )
    return (row_total, weighted)


def backward_visit(
    queries, key_block, value_block, allowed, score_scale, weighted_grad, total_grad
):
    weights = block_weights(queries, key_block, allowed, score_scale)
    value_part = jnp.einsum(
        "hqk,qhd->khd",
        weights.astype(jnp.bfloat16),
        weighted_grad,
        preferred_element_type=jnp.float32,
    )
    weight_grad = (
        jnp.einsum("qhd,khd->hqk", weighted_grad, value_block, preferred_element_type=jnp.float32)
        + total_grad[:, :, None]
    )
    score_grad = (weights * weight_grad).astype(jnp.bfloat16)
    query_part = (
        jnp.einsum("hqk,khd->qhd", score_grad, key_block, preferred_element_type=jnp.float32)
        * score_scale
    )
    key_part = (
        jnp.einsum("hqk,qhd->khd", score_grad, queries, preferred_element_type=jnp.float32)
        * score_scale
    )
    return (query_part, key_part, value_part)


def body(
    tokens,
    teacher,
    doc_lengths,
    valid_len,
    q_weight,
    q_bias,
    k_weight,
    v_weight,
    v_bias,
    o_weight,
    o_bias,
    ln1_gain,
    ln1_bias,
    in_weight,
    in_bias,
    out_weight,
    out_bias,
    ln2_gain,
    ln2_bias,
):
    gathered = (
        lax.all_gather(q_weight, "wsh", axis=0, tiled=True),
        lax.all_gather(q_bias, "wsh", axis=0, tiled=True),
        lax.all_gather(k_weight, "wsh", axis=0, tiled=True),
        lax.all_gather(v_weight, "wsh", axis=0, tiled=True),
        lax.all_gather(v_bias, "wsh", axis=0, tiled=True),
        lax.all_gather(o_weight, "wsh", axis=0, tiled=True),
        lax.all_gather(o_bias, "wsh", axis=0, tiled=True),
        lax.all_gather(ln1_gain, "wsh", axis=0, tiled=True),
        lax.all_gather(ln1_bias, "wsh", axis=0, tiled=True),
        lax.all_gather(in_weight, "wsh", axis=0, tiled=True),
        lax.all_gather(in_bias, "wsh", axis=0, tiled=True),
        lax.all_gather(out_weight, "wsh", axis=0, tiled=True),
        lax.all_gather(out_bias, "wsh", axis=0, tiled=True),
        lax.all_gather(ln2_gain, "wsh", axis=0, tiled=True),
        lax.all_gather(ln2_bias, "wsh", axis=0, tiled=True),
    )
    (
        w_query,
        b_query,
        w_key,
        w_value,
        b_value,
        w_out,
        b_out,
        gain_one,
        shift_one,
        w_inner,
        b_inner,
        w_back,
        b_back,
        gain_two,
        shift_two,
    ) = gathered
    gain_first = gain_one.astype(jnp.float32)
    shift_first = shift_one.astype(jnp.float32)
    gain_second = gain_two.astype(jnp.float32)
    shift_second = shift_two.astype(jnp.float32)
    inputs = tokens[0]
    row_count = inputs.shape[0]
    cycle_size = lax.axis_size("ctx")
    stream_count = lax.axis_size("wsh")
    position = lax.axis_index("ctx")
    score_scale = 1.0 / math.sqrt(HD)
    offsets = jnp.arange(row_count, dtype=jnp.int32)
    lengths = doc_lengths[0]
    starts = jnp.cumsum(lengths) - lengths
    limit = valid_len[0]

    def key_mask(block_index):
        where_rows = jnp.mod(block_index, cycle_size) * row_count + offsets
        return (document_of(where_rows, starts), where_rows < limit)

    own_doc, own_live = key_mask(position)
    input_float = inputs.astype(jnp.float32)
    queries = (
        (matmul(inputs, w_query) + b_query.astype(jnp.float32))
        .astype(jnp.bfloat16)
        .reshape(row_count, H, HD)
    )
    key_rows = matmul(inputs, w_key).astype(jnp.bfloat16).reshape(row_count, H, HD)
    value_rows = (
        (matmul(inputs, w_value) + b_value.astype(jnp.float32))
        .astype(jnp.bfloat16)
        .reshape(row_count, H, HD)
    )

    def visit_forward(sums_state, key_block, value_block, block_index):
        other_doc, other_live = key_mask(block_index)
        allowed = permitted(own_doc, own_live, other_doc, other_live)
        return forward_visit(sums_state, queries, key_block, value_block, allowed, score_scale)

    empty_state = (
        jnp.zeros((H, row_count), jnp.float32),
        jnp.zeros((row_count, H, HD), jnp.float32),
    )
    first_state = visit_forward(empty_state, key_rows, value_rows, position)

    def advance(step_index, loop_state):
        key_block, value_block, running = loop_state
        key_block, value_block = shifted((key_block, value_block), "ctx", 1)
        running = visit_forward(running, key_block, value_block, position - step_index)
        return (key_block, value_block, running)

    row_total, weighted = lax.fori_loop(
        1, cycle_size, advance, (key_rows, value_rows, first_state)
    )[2]
    normed = weighted / jnp.transpose(row_total)[:, :, None]
    context = normed.astype(jnp.bfloat16).reshape(row_count, D)
    attn = matmul(context, w_out) + b_out.astype(jnp.float32)
    first_sum = input_float + attn
    settled = layer_norm(first_sum, gain_first, shift_first)
    settled_low = settled.astype(jnp.bfloat16)
    inner = matmul(settled_low, w_inner) + b_inner.astype(jnp.float32)
    activated = activate(inner).astype(jnp.bfloat16)
    branch = matmul(activated, w_back) + b_back.astype(jnp.float32)
    second_sum = settled + branch
    result = layer_norm(second_sum, gain_second, shift_second)
    target = teacher[0].astype(jnp.float32)
    diff = jnp.where(own_live[:, None], result - target, 0.0)
    error_sum, live_count = lax.psum(
        (jnp.sum(diff * diff), jnp.sum(own_live.astype(jnp.float32))), ("ctx", "wsh")
    )
    loss = error_sum / (live_count * D)
    upstream = diff * (row_count * cycle_size * stream_count / live_count)
    unused_second, second_back = jax.vjp(layer_norm, second_sum, gain_second, shift_second)
    d_second, gain_two_grad, shift_two_grad = second_back(upstream)
    branch_grad = d_second.astype(jnp.bfloat16)
    back_weight_grad = left_product(activated, branch_grad)
    back_bias_grad = jnp.sum(branch_grad, axis=0, dtype=jnp.float32)
    d_activated = right_product(branch_grad, w_back)
    unused_inner, gelu_back = jax.vjp(activate, inner)
    inner_grad = gelu_back(d_activated)[0].astype(jnp.bfloat16)
    inner_weight_grad = left_product(settled_low, inner_grad)
    inner_bias_grad = jnp.sum(inner_grad, axis=0, dtype=jnp.float32)
    d_settled = d_second + right_product(inner_grad, w_inner)
    unused_first, first_back = jax.vjp(layer_norm, first_sum, gain_first, shift_first)
    d_first, gain_one_grad, shift_one_grad = first_back(d_settled)
    attn_grad = d_first.astype(jnp.bfloat16)
    out_weight_grad_local = left_product(context, attn_grad)
    out_bias_grad_local = jnp.sum(attn_grad, axis=0, dtype=jnp.float32)
    context_low = lax.optimization_barrier(right_product(attn_grad, w_out).astype(jnp.bfloat16))
    context_grad = context_low.astype(jnp.float32).reshape(row_count, H, HD)
    weighted_grad = (context_grad / jnp.transpose(row_total)[:, :, None]).astype(jnp.bfloat16)
    total_grad = -jnp.transpose(jnp.sum(context_grad * weighted, axis=-1)) / (row_total * row_total)

    def visit_backward(key_block, value_block, block_index):
        other_doc, other_live = key_mask(block_index)
        allowed = permitted(own_doc, own_live, other_doc, other_live)
        return backward_visit(
            queries, key_block, value_block, allowed, score_scale, weighted_grad, total_grad
        )

    query_sum, key_sum, value_sum = visit_backward(key_rows, value_rows, position)

    def advance_back(step_index, loop_state):
        key_block, value_block, query_acc, key_acc, value_acc = loop_state
        key_block, value_block = shifted((key_block, value_block), "ctx", 1)
        key_acc, value_acc = (
            shifted(key_acc.astype(jnp.bfloat16), "ctx", 1).astype(key_acc.dtype),
            shifted(value_acc.astype(jnp.bfloat16), "ctx", 1).astype(value_acc.dtype),
        )
        query_part, key_part, value_part = visit_backward(
            key_block, value_block, position - step_index
        )
        return (
            key_block,
            value_block,
            query_acc + query_part,
            key_acc + key_part,
            value_acc + value_part,
        )

    loop_state = lax.fori_loop(
        1, cycle_size, advance_back, (key_rows, value_rows, query_sum, key_sum, value_sum)
    )
    query_total = loop_state[2]
    key_total, value_total = (
        shifted(loop_state[3].astype(jnp.bfloat16), "ctx", 1).astype(jnp.float32),
        shifted(loop_state[4].astype(jnp.bfloat16), "ctx", 1).astype(jnp.float32),
    )
    query_grad = query_total.astype(jnp.bfloat16).reshape(row_count, D)
    key_grad = key_total.astype(jnp.bfloat16).reshape(row_count, D)
    value_grad = value_total.astype(jnp.bfloat16).reshape(row_count, D)
    query_weight_grad = left_product(inputs, query_grad)
    query_bias_grad = jnp.sum(query_grad, axis=0, dtype=jnp.float32)
    key_weight_grad = left_product(inputs, key_grad)
    value_weight_grad = left_product(inputs, value_grad)
    value_bias_grad = jnp.sum(value_grad, axis=0, dtype=jnp.float32)
    input_grad = (
        d_first
        + right_product(query_grad, w_query)
        + right_product(key_grad, w_key)
        + right_product(value_grad, w_value)
    )
    reduced = (
        lax.psum_scatter(
            query_weight_grad.astype(jnp.bfloat16), "wsh", scatter_dimension=0, tiled=True
        ).astype(jnp.float32),
        lax.psum_scatter(
            query_bias_grad.astype(jnp.bfloat16), "wsh", scatter_dimension=0, tiled=True
        ).astype(jnp.float32),
        lax.psum_scatter(
            key_weight_grad.astype(jnp.bfloat16), "wsh", scatter_dimension=0, tiled=True
        ).astype(jnp.float32),
        lax.psum_scatter(
            value_weight_grad.astype(jnp.bfloat16), "wsh", scatter_dimension=0, tiled=True
        ).astype(jnp.float32),
        lax.psum_scatter(
            value_bias_grad.astype(jnp.bfloat16), "wsh", scatter_dimension=0, tiled=True
        ).astype(jnp.float32),
        lax.psum_scatter(
            out_weight_grad_local.astype(jnp.bfloat16), "wsh", scatter_dimension=0, tiled=True
        ).astype(jnp.float32),
        lax.psum_scatter(
            out_bias_grad_local.astype(jnp.bfloat16), "wsh", scatter_dimension=0, tiled=True
        ).astype(jnp.float32),
        lax.psum_scatter(
            gain_one_grad.astype(jnp.bfloat16), "wsh", scatter_dimension=0, tiled=True
        ).astype(jnp.float32),
        lax.psum_scatter(
            shift_one_grad.astype(jnp.bfloat16), "wsh", scatter_dimension=0, tiled=True
        ).astype(jnp.float32),
        lax.psum_scatter(
            inner_weight_grad.astype(jnp.bfloat16), "wsh", scatter_dimension=0, tiled=True
        ).astype(jnp.float32),
        lax.psum_scatter(
            inner_bias_grad.astype(jnp.bfloat16), "wsh", scatter_dimension=0, tiled=True
        ).astype(jnp.float32),
        lax.psum_scatter(
            back_weight_grad.astype(jnp.bfloat16), "wsh", scatter_dimension=0, tiled=True
        ).astype(jnp.float32),
        lax.psum_scatter(
            back_bias_grad.astype(jnp.bfloat16), "wsh", scatter_dimension=0, tiled=True
        ).astype(jnp.float32),
        lax.psum_scatter(
            gain_two_grad.astype(jnp.bfloat16), "wsh", scatter_dimension=0, tiled=True
        ).astype(jnp.float32),
        lax.psum_scatter(
            shift_two_grad.astype(jnp.bfloat16), "wsh", scatter_dimension=0, tiled=True
        ).astype(jnp.float32),
    )
    summed = lax.psum(
        (
            reduced[0],
            reduced[1],
            reduced[2],
            reduced[3],
            reduced[4],
            reduced[5],
            reduced[6],
            reduced[7],
            reduced[8],
            reduced[9],
            reduced[10],
            reduced[11],
            reduced[12],
            reduced[13],
            reduced[14],
        ),
        "ctx",
    )
    return (
        result.astype(jnp.bfloat16)[None],
        loss,
        input_grad[None],
        summed[0],
        summed[1],
        summed[2],
        summed[3],
        summed[4],
        summed[5],
        summed[6],
        summed[7],
        summed[8],
        summed[9],
        summed[10],
        summed[11],
        summed[12],
        summed[13],
        summed[14],
    )


BF = jnp.bfloat16
F32 = jnp.float32
FF = 3072
ROWS = 128
HEADS = 3
HW = HEADS * HD
GROUP = 4
CTX = 8
MESH = pl.DeviceIdType.MESH

Q, K, V, O, IN, OUT = range(6)
WEIGHT_SHAPES = [(192, 768), (192, 768), (192, 768), (192, 768), (192, 3072), (768, 768)]
PART_SHAPES = [(384, 384), (384, 384), (384, 384), (384, 384), (384, 1536), (768, 768)]

(
    SMALL,
    WEIGHT_X,
    WEIGHT_Y,
    WEIGHT_CORE,
    WEIGHT_CORE_X,
    WEIGHT_CORE_Y,
    KEY_VALUE,
    QUERY,
    CONTEXT,
    CONTEXT_GRAD,
    KEY_VALUE_GRAD,
    QUERY_GRAD,
    X_ALL,
    SETTLED_ALL,
    CONTEXT_ALL,
    ATTN_GRAD_ALL,
    INNER_GRAD_ALL,
    ACTIVATED_ALL,
    BRANCH_GRAD_ALL,
    PROJECTED_GRAD_ALL,
    PAIR,
    LINE,
    BACK,
    GIVE,
    OWN,
    VECTORS_W,
    VECTORS_Z,
    VECTORS_Y,
    TOKENS,
    TEACHER,
    OUTPUT,
    INPUT_GRAD,
    LOAD,
) = range(33)


def fused_fits(mesh):
    return mesh.shape["ctx"] == CTX and mesh.shape["wsh"] == GROUP


def tn(left, right):
    return lax.dot_general(
        left, right, (((0,), (0,)), ((), ())), preferred_element_type=jnp.float32
    )


def norm_parts(value):
    mean = jnp.mean(value, axis=-1, keepdims=True)
    centered = value - mean
    spread = jnp.mean(centered * centered, axis=-1, keepdims=True)
    inverse = lax.rsqrt(spread + EPSILON)
    return centered * inverse, inverse


def norm_back(upstream_gained, normal, inverse):
    return (
        upstream_gained
        - jnp.mean(upstream_gained, axis=-1, keepdims=True)
        - normal * jnp.mean(upstream_gained * normal, axis=-1, keepdims=True)
    ) * inverse


GELU_C = math.sqrt(2.0 / math.pi)


class Numbers:
    def __init__(self):
        self.count = 0
        self.table = {}

    def take(self, key, size=1):
        if key not in self.table:
            self.table[key] = self.count
            self.count += size
        return self.table[key]


def scratch_table():
    s = types.SimpleNamespace()
    s.full = [pltpu.VMEM((GROUP, rows, cols), BF) for rows, cols in WEIGHT_SHAPES]
    s.x = pltpu.VMEM((ROWS, D), BF)
    s.teacher = pltpu.VMEM((ROWS, D), BF)
    s.small = pltpu.VMEM((GROUP, 16, D), F32)
    s.kv_send = pltpu.VMEM((4, 2 * HW, ROWS), BF)
    s.kv = pltpu.VMEM((CTX, 2 * HW, ROWS), BF)
    s.q_send = pltpu.VMEM((4, HW, ROWS), BF)
    s.q = pltpu.VMEM((4, HW, ROWS), BF)
    s.weights = pltpu.VMEM((CTX, HEADS, ROWS, 4 * ROWS), F32)
    s.mix = pltpu.VMEM((HEADS, HD, 4 * ROWS), F32)
    s.total = pltpu.VMEM((HEADS, 8, 4 * ROWS), F32)
    s.ctx_send = pltpu.VMEM((4, HW, ROWS), BF)
    s.ctx = pltpu.VMEM((4, HW, ROWS), BF)
    s.inner = pltpu.VMEM((4, ROWS, D), F32)
    s.act = pltpu.VMEM((4, ROWS, D), BF)
    s.first = pltpu.VMEM((ROWS, D), F32)
    s.keep = pltpu.VMEM((ROWS, D), F32)
    s.x_half = pltpu.VMEM((2, ROWS, 384), BF)
    s.set_half = pltpu.VMEM((2, ROWS, 384), BF)
    s.ag_half = pltpu.VMEM((2, ROWS, 384), BF)
    s.ig_half = pltpu.VMEM((2, ROWS, 1536), BF)
    s.bg = pltpu.VMEM((ROWS, D), BF)
    s.x_all = pltpu.VMEM((GROUP, ROWS, 384), BF)
    s.set_all = pltpu.VMEM((GROUP, ROWS, 384), BF)
    s.ctx_all = pltpu.VMEM((GROUP, 2, HW, ROWS), BF)
    s.ag_all = pltpu.VMEM((GROUP, ROWS, 384), BF)
    s.ig_all = pltpu.VMEM((GROUP, ROWS, 1536), BF)
    s.act_all = pltpu.VMEM((GROUP, ROWS, D), BF)
    s.bg_all = pltpu.VMEM((GROUP, ROWS, D), BF)
    s.projected_half = [pltpu.VMEM((2, ROWS, 384), BF) for name in (Q, K, V)]
    s.projected_all = [pltpu.VMEM((GROUP, ROWS, 384), BF) for name in (Q, K, V)]
    s.cg_send = pltpu.VMEM((4, HW, ROWS), BF)
    s.cg = pltpu.VMEM((4, HW, ROWS), BF)
    s.dkv_send = pltpu.VMEM((CTX, 2 * HW, ROWS), BF)
    s.dkv = pltpu.VMEM((CTX, 2 * HW, ROWS), BF)
    s.dq_send = pltpu.VMEM((4, HW, ROWS), BF)
    s.dq = pltpu.VMEM((4, HW, ROWS), BF)
    s.part = [pltpu.VMEM((rows, cols), BF) for rows, cols in PART_SHAPES]
    s.pair = [pltpu.VMEM((rows // 2, cols), BF) for rows, cols in PART_SHAPES]
    s.sum = [pltpu.VMEM((4, rows // 8, cols), BF) for rows, cols in PART_SHAPES]
    s.line = [pltpu.VMEM((3, rows // 8, cols), BF) for rows, cols in PART_SHAPES]
    s.done = [pltpu.VMEM((4, rows // 8, cols), BF) for rows, cols in PART_SHAPES]
    s.wg = pltpu.VMEM((HEADS, HD, 4 * ROWS), BF)
    s.smalls = pltpu.VMEM((GROUP, 16, HW), F32)
    s.sg = pltpu.VMEM((16, D), F32)
    s.sg_w = pltpu.VMEM((GROUP, 16, D), F32)
    s.sg_z = pltpu.VMEM((4, 16, D), F32)
    s.sg_y = pltpu.VMEM((2, 16, D), F32)
    s.out_low = pltpu.VMEM((ROWS, D), BF)
    return vars(s)


LOCAL_SEMS = 32
REMOTE_SEMS = 160


def is_memory(item):
    return not isinstance(item, (dict, list))


def scratch_shapes():
    return jax.tree.flatten(scratch_table(), is_leaf=is_memory)


def fused_kernel(*refs):
    (tokens, teacher), own_shards = refs[:2], refs[2:8]
    small_in, lengths, valid = refs[8:11]
    output, input_grad_out = refs[11:13]
    grad_out, smalls_out = refs[13:19], refs[19]
    flat, shape = scratch_shapes()
    S = types.SimpleNamespace(**jax.tree.unflatten(shape, refs[20 : 20 + len(flat)]))
    send_sems, recv_sems, local_sems = refs[20 + len(flat) :]

    c = lax.axis_index("ctx")
    w = lax.axis_index("wsh")
    a, b = c // 2, c % 2
    x, core = w // 2, w % 2

    numbers = Numbers()
    locals_ = Numbers()
    started = []

    def bit_xor(value, j):
        out = value
        bit = 1
        while bit <= j:
            if j & bit:
                has = (value // bit) % 2
                out = out + bit * (1 - 2 * has)
            bit *= 2
        return out

    def remote(key, src, dst, c_to, w_to, offset=0, size=1):
        number = numbers.take(key, size) + offset
        copy = pltpu.make_async_remote_copy(
            src_ref=src,
            dst_ref=dst,
            send_sem=send_sems.at[number],
            recv_sem=recv_sems.at[number],
            device_id={"ctx": c_to, "wsh": w_to},
            device_id_type=MESH,
        )
        copy.start()
        started.append(copy)
        return copy

    def arrived(key, landing, offset=0):
        number = numbers.take(key) + offset
        pltpu.make_async_copy(landing, landing, recv_sems.at[number]).wait()

    def local(key, src, dst):
        copy = pltpu.make_async_copy(src, dst, local_sems.at[locals_.take(key)])
        copy.start()
        return copy

    peers = [(c, bit_xor(w, j)) for j in (1, 2, 3)]
    peers += [(bit_xor(c, j), w) for j in range(1, CTX)]
    peers += [(bit_xor(c, 1), bit_xor(w, 1))]

    loads = {
        TOKENS: local(TOKENS, tokens.at[0], S.x),
        TEACHER: local(TEACHER, teacher.at[0], S.teacher),
        SMALL: local(SMALL, small_in, S.small.at[w]),
    }
    for name in range(6):
        loads[(LOAD, name)] = local((LOAD, name), own_shards[name], S.full[name].at[w])

    barrier = pltpu.get_barrier_semaphore()
    for c_to, w_to in peers:
        pl.semaphore_signal(
            barrier, inc=1, device_id={"ctx": c_to, "wsh": w_to}, device_id_type=MESH
        )
    pl.semaphore_wait(barrier, len(peers))

    for j in (1, 2, 3):
        remote((SMALL, j), small_in, S.small.at[w], c, bit_xor(w, j))

    def half_of(name, which):
        rows = WEIGHT_SHAPES[name][0] // 2
        return pl.ds(pl.multiple_of(which * rows, rows), rows)

    order = (K, V, Q, O, IN, OUT)
    for name in order:
        full = S.full[name]
        own = half_of(name, b)
        remote((WEIGHT_X, name), own_shards[name].at[own], full.at[w, own], c, bit_xor(w, 2))
        remote((WEIGHT_CORE, name), own_shards[name], full.at[w], c, bit_xor(w, 1))

    def pump_x(name):
        slot = S.full[name].at[bit_xor(w, 2), half_of(name, b)]
        arrived((WEIGHT_X, name), slot)
        remote((WEIGHT_Y, name), slot, slot, bit_xor(c, 1), w)
        remote((WEIGHT_CORE_X, name), slot, slot, c, bit_xor(w, 1))

    def pump_y(name):
        slot = S.full[name].at[bit_xor(w, 2), half_of(name, 1 - b)]
        arrived((WEIGHT_Y, name), slot)
        remote((WEIGHT_CORE_Y, name), slot, slot, c, bit_xor(w, 1))

    def weight_ready(name):
        full = S.full[name]
        loads[(LOAD, name)].wait()
        arrived((WEIGHT_CORE, name), full.at[bit_xor(w, 1)])
        arrived((WEIGHT_CORE_X, name), full.at[bit_xor(w, 3), half_of(name, b)])
        arrived((WEIGHT_CORE_Y, name), full.at[bit_xor(w, 3), half_of(name, 1 - b)])

    def square(name):
        return S.full[name][...].reshape(D, D)

    starts, running = [], 0
    for i in range(lengths.shape[1]):
        starts.append(running)
        running = running + lengths[0, i]
    limit = valid[0]

    def code_of(position):
        code = jnp.zeros(position.shape, jnp.int32)
        for start in starts:
            code = code + (start <= position).astype(jnp.int32)
        return 2 * code + (position < limit).astype(jnp.int32)

    lane = lax.broadcasted_iota(jnp.int32, (1, 4 * ROWS), 1)
    query_code = code_of((2 * (lane // ROWS) + b) * ROWS + lane % ROWS)

    def key_code(block):
        return code_of(block * ROWS + lax.broadcasted_iota(jnp.int32, (ROWS, 1), 0))

    own_live = c * ROWS + lax.broadcasted_iota(jnp.int32, (ROWS, 1), 0) < limit

    loads[TOKENS].wait()
    x_low = S.x[...]
    for i in range(2):
        S.x_half[i] = x_low[:, 384 * i : 384 * (i + 1)]

    loads[SMALL].wait()
    for j in (1, 2, 3):
        arrived((SMALL, j), S.small.at[bit_xor(w, j)])
    small = (S.small[0] + S.small[1]) + (S.small[2] + S.small[3])

    def vector(row):
        return small[row : row + 1, :]

    def project(name, bias):
        value = matmul(x_low, square(name))
        if bias is not None:
            value = value + vector(bias)
        return value.T.astype(BF)

    pump_x(K)
    pump_x(V)
    pump_y(K)
    weight_ready(K)
    turned = project(K, None)
    for i in range(4):
        S.kv_send[i, 0:HW, :] = turned[HW * i : HW * (i + 1), :]
    pump_x(Q)
    pump_y(V)
    weight_ready(V)
    turned = project(V, 1)
    for i in range(4):
        S.kv_send[i, HW : 2 * HW, :] = turned[HW * i : HW * (i + 1), :]
    for j in range(1, CTX):
        to = bit_xor(c, j)
        remote((KEY_VALUE, j), S.kv_send.at[to // 2], S.kv.at[c], to, w)
    S.kv[c] = S.kv_send[a]
    pump_x(O)
    pump_y(Q)
    weight_ready(Q)
    turned = project(Q, 0)
    for i in range(4):
        S.q_send[i] = turned[HW * i : HW * (i + 1), :]
    for j in (1, 2, 3):
        remote((QUERY, j), S.q_send.at[bit_xor(a, j)], S.q.at[a], bit_xor(c, 2 * j), w)
    S.q[a] = S.q_send[a]

    def to_group(key, source_of, everywhere):
        for j in (1, 2, 3):
            to = bit_xor(w, j)
            remote((*key, j), source_of(to), everywhere.at[w], c, to)

    def from_group(key, everywhere):
        for j in (1, 2, 3):
            arrived((*key, j), everywhere.at[bit_xor(w, j)])

    to_group((X_ALL,), lambda to: S.x_half.at[to // 2], S.x_all)
    S.x_all[w] = S.x_half[x]

    pump_x(IN)
    pump_y(O)

    for j in (1, 2, 3):
        arrived((QUERY, j), S.q.at[bit_xor(a, j)])
    for j in range(1, CTX):
        arrived((KEY_VALUE, j), S.kv.at[bit_xor(c, j)])

    score_scale = 1.0 / math.sqrt(HD)

    def wide(ref, h):
        return jnp.concatenate(
            [ref[i, HD * h : HD * (h + 1), :] for i in range(4)], axis=1
        )

    S.mix[...] = jnp.zeros(S.mix.shape, F32)
    S.total[...] = jnp.zeros(S.total.shape, F32)

    @pl.loop(0, CTX)
    def attend_block(block):
        allowed = key_code(block) == query_code
        for h in range(HEADS):
            key_t = S.kv[block, HD * h : HD * (h + 1), :]
            value_t = S.kv[block, HW + HD * h : HW + HD * (h + 1), :]
            scores = tn(key_t, wide(S.q, h)) * score_scale
            weights = jnp.exp(jnp.where(allowed, scores, MASKED))
            S.weights[block, h] = weights
            S.total[h, 0:1, :] += jnp.sum(weights, axis=0, keepdims=True)
            S.mix[h] += matmul(value_t, weights.astype(BF))

    for h in range(HEADS):
        context_t = (S.mix[h] / S.total[h, 0:1, :]).astype(BF)
        for i in range(4):
            S.ctx_send[i, HD * h : HD * (h + 1), :] = context_t[:, ROWS * i : ROWS * (i + 1)]
    for j in (1, 2, 3):
        to = bit_xor(a, j)
        remote((CONTEXT, j), S.ctx_send.at[to], S.ctx.at[a], bit_xor(c, 2 * j), w)
    S.ctx[a] = S.ctx_send[a]
    pump_x(OUT)
    pump_y(IN)
    weight_ready(O)
    for j in (1, 2, 3):
        arrived((CONTEXT, j), S.ctx.at[bit_xor(a, j)])

    to_group((CONTEXT_ALL,), lambda to: S.ctx.at[pl.ds(2 * (to // 2), 2)], S.ctx_all)
    S.ctx_all[w] = S.ctx[pl.ds(2 * x, 2)]
    attn = tn(S.ctx[...].reshape(D, ROWS), square(O)) + vector(2)
    first_sum = x_low.astype(F32) + attn
    normal_one, inverse_one = norm_parts(first_sum)
    settled = normal_one * vector(3) + vector(4)
    settled_low = settled.astype(BF)
    S.first[...] = normal_one
    S.keep[...] = settled
    for i in range(2):
        S.set_half[i] = settled_low[:, 384 * i : 384 * (i + 1)]
    to_group((SETTLED_ALL,), lambda to: S.set_half.at[to // 2], S.set_all)
    S.set_all[w] = S.set_half[x]
    pump_y(OUT)
    weight_ready(IN)
    for t in range(4):
        w_part = S.full[IN][:, :, D * t : D * (t + 1)].reshape(D, D)
        inner = matmul(settled_low, w_part) + vector(8 + t)
        S.inner[t] = inner
        S.act[t] = (
            0.5 * inner * (1.0 + jnp.tanh(GELU_C * (inner + 0.044715 * inner * inner * inner)))
        ).astype(BF)
    to_group((ACTIVATED_ALL,), lambda to: S.act.at[to], S.act_all)
    S.act_all[w] = S.act[w]
    weight_ready(OUT)
    branch = vector(5)
    for t in range(4):
        branch = branch + matmul(S.act[t], S.full[OUT][t])
    normal_two, inverse_two = norm_parts(S.keep[...] + branch)
    result = normal_two * vector(6) + vector(7)
    S.out_low[...] = result.astype(BF)
    finishing = [local(OUTPUT, S.out_low, output)]
    loads[TEACHER].wait()
    diff = jnp.where(own_live, result - S.teacher[...].astype(F32), 0.0)
    count = vector(12)
    upstream = diff * ((ROWS * CTX * GROUP) / count)
    S.sg[...] = jnp.zeros((16, D), F32)

    def note(row, value):
        S.sg[row : row + 1, :] = jnp.sum(value.astype(F32), axis=0, keepdims=True)

    note(12, diff * diff)
    S.sg[13:14, :] = count * (1.0 / (CTX * GROUP))
    note(6, upstream * normal_two)
    note(7, upstream)

    d_second = norm_back(upstream * vector(6), normal_two, inverse_two)
    branch_grad = d_second.astype(BF)
    S.bg[...] = branch_grad
    to_group((BRANCH_GRAD_ALL,), lambda to: S.bg, S.bg_all)
    S.bg_all[w] = branch_grad
    note(5, branch_grad)
    d_settled = d_second
    for t in range(4):
        d_act = right_product(branch_grad, S.full[OUT][t])
        inner = S.inner[t]
        squared = inner * inner
        bend = jnp.tanh(GELU_C * (inner + 0.044715 * squared * inner))
        slope = 0.5 * (1.0 + bend) + 0.5 * inner * (1.0 - bend * bend) * (
            GELU_C * (1.0 + 3 * 0.044715 * squared)
        )
        inner_grad = (d_act * slope).astype(BF)
        S.ig_half[t // 2, :, D * (t % 2) : D * (t % 2 + 1)] = inner_grad
        note(8 + t, inner_grad)
        w_part = S.full[IN][:, :, D * t : D * (t + 1)].reshape(D, D)
        d_settled = d_settled + right_product(inner_grad, w_part)
    to_group((INNER_GRAD_ALL,), lambda to: S.ig_half.at[to % 2], S.ig_all)
    S.ig_all[w] = S.ig_half[core]
    normal_one = S.first[...]
    note(3, d_settled * normal_one)
    note(4, d_settled)
    d_first = norm_back(d_settled * vector(3), normal_one, inverse_one)
    S.keep[...] = d_first
    attn_grad = d_first.astype(BF)
    note(2, attn_grad)
    context_grad = right_product(attn_grad, square(O)).T.astype(BF)
    for i in range(4):
        S.cg_send[i] = context_grad[HW * i : HW * (i + 1), :]
    for j in (1, 2, 3):
        to = bit_xor(a, j)
        remote((CONTEXT_GRAD, j), S.cg_send.at[to], S.cg.at[a], bit_xor(c, 2 * j), w)
    S.cg[a] = S.cg_send[a]
    for i in range(2):
        S.ag_half[i] = attn_grad[:, 384 * i : 384 * (i + 1)]
    to_group((ATTN_GRAD_ALL,), lambda to: S.ag_half.at[to % 2], S.ag_all)
    S.ag_all[w] = S.ag_half[core]

    def reduce_pair(name):
        half = PART_SHAPES[name][0] // 2
        there = pl.ds(pl.multiple_of((1 - b) * half, half), half)
        remote((PAIR, name), S.part[name].at[there], S.pair[name], bit_xor(c, 1), w)

    def reduce_line(name):
        rows, cols = PART_SHAPES[name]
        half = rows // 2
        arrived((PAIR, name), S.pair[name])
        here = pl.ds(pl.multiple_of(b * half, half), half)
        both = S.part[name][here, :].astype(F32) + S.pair[name][...].astype(F32)
        S.sum[name][...] = both.astype(BF).reshape(4, rows // 8, cols)
        for j in (1, 2, 3):
            remote(
                (LINE, name, j),
                S.sum[name].at[bit_xor(a, j)],
                S.line[name].at[j - 1],
                bit_xor(c, 2 * j),
                w,
            )

    def spread_line(name):
        for j in (1, 2, 3):
            arrived((LINE, name, j), S.line[name].at[j - 1])
        total = S.sum[name][a].astype(F32)
        for j in range(3):
            total = total + S.line[name][j].astype(F32)
        done = S.done[name]
        done[a] = total.astype(BF)
        for j in (1, 2, 3):
            remote((BACK, name, j), done.at[a], done.at[a], bit_xor(c, 2 * j), w)

    def spread_pair(name):
        done, out = S.done[name], grad_out[name]
        for j in (1, 2, 3):
            arrived((BACK, name, j), done.at[bit_xor(a, j)])
        if name == OUT:
            remote((GIVE, name), done, out.at[b], bit_xor(c, 1), w)
            finishing.append(local((GIVE, name), done, out.at[b]))
            return
        remote((GIVE, name), done, out.at[core], bit_xor(c, 1), 2 * x + b, core, 2)

        @pl.when(core == b)
        def keep_own():
            local((OWN, name), done, out.at[core])

        @pl.when(core != b)
        def give_core():
            remote((OWN, name), done, out.at[core], c, bit_xor(w, 1))
            started.pop()

    def settle(name):
        done, out = S.done[name], grad_out[name]
        if name == OUT:
            arrived((GIVE, name), out.at[1 - b])
            return

        @pl.when(core == b)
        def from_chip():
            pltpu.make_async_copy(
                done, out.at[core], local_sems.at[locals_.take((OWN, name))]
            ).wait()
            arrived((OWN, name), out.at[1 - core])

        @pl.when(core != b)
        def from_partner():
            arrived((GIVE, name), out.at[0], 0)
            arrived((GIVE, name), out.at[1], 1)
            sent = numbers.take((OWN, name))
            pltpu.make_async_copy(done, done, send_sems.at[sent]).wait()

    from_group((ACTIVATED_ALL,), S.act_all)
    from_group((BRANCH_GRAD_ALL,), S.bg_all)
    S.part[OUT][...] = tn(
        S.act_all[...].reshape(GROUP * ROWS, D), S.bg_all[...].reshape(GROUP * ROWS, D)
    ).astype(BF)
    reduce_pair(OUT)

    for j in (1, 2, 3):
        arrived((CONTEXT_GRAD, j), S.cg.at[bit_xor(a, j)])
    for h in range(HEADS):
        grad = wide(S.cg, h).astype(F32)
        row_total = S.total[h, 0:1, :]
        S.wg[h] = (grad / row_total).astype(BF)
        S.total[h, 1:2, :] = -jnp.sum(grad * S.mix[h], axis=0, keepdims=True) / (
            row_total * row_total
        )
    S.mix[...] = jnp.zeros(S.mix.shape, F32)

    @pl.loop(0, CTX)
    def attend_back(block):
        for h in range(HEADS):
            key_rows = slice(HD * h, HD * (h + 1))
            value_rows = slice(HW + HD * h, HW + HD * (h + 1))
            key_t = S.kv[block, key_rows, :]
            value_t = S.kv[block, value_rows, :]
            weights = S.weights[block, h]
            grad = S.wg[h]
            weight_grad = tn(value_t, grad) + S.total[h, 1:2, :]
            score_grad = (weights * weight_grad).astype(BF)
            S.mix[h] += matmul(key_t, score_grad)
            S.dkv_send[block, key_rows, :] = (
                right_product(wide(S.q, h), score_grad) * score_scale
            ).astype(BF)
            S.dkv_send[block, value_rows, :] = right_product(grad, weights.astype(BF)).astype(BF)

    for j in range(1, CTX):
        to = bit_xor(c, j)
        remote((KEY_VALUE_GRAD, j), S.dkv_send.at[to], S.dkv.at[c], to, w)
    S.dkv[c] = S.dkv_send[c]
    for h in range(HEADS):
        query_t = (S.mix[h] * score_scale).astype(BF)
        for i in range(4):
            S.dq_send[i, HD * h : HD * (h + 1), :] = query_t[:, ROWS * i : ROWS * (i + 1)]
    for j in (1, 2, 3):
        to = bit_xor(a, j)
        remote((QUERY_GRAD, j), S.dq_send.at[to], S.dq.at[a], bit_xor(c, 2 * j), w)
    S.dq[a] = S.dq_send[a]

    from_group((SETTLED_ALL,), S.set_all)
    from_group((INNER_GRAD_ALL,), S.ig_all)
    S.part[IN][...] = tn(
        S.set_all[...].reshape(GROUP * ROWS, 384), S.ig_all[...].reshape(GROUP * ROWS, 1536)
    ).astype(BF)
    reduce_pair(IN)
    reduce_line(OUT)
    from_group((CONTEXT_ALL,), S.ctx_all)
    from_group((ATTN_GRAD_ALL,), S.ag_all)
    context_all = jnp.concatenate(
        [S.ctx_all[i].reshape(384, ROWS) for i in range(GROUP)], axis=1
    )
    S.part[O][...] = matmul(context_all, S.ag_all[...].reshape(GROUP * ROWS, 384)).astype(BF)
    reduce_pair(O)
    reduce_line(IN)
    from_group((X_ALL,), S.x_all)

    for j in range(1, CTX):
        arrived((KEY_VALUE_GRAD, j), S.dkv.at[bit_xor(c, j)])
    for j in (1, 2, 3):
        arrived((QUERY_GRAD, j), S.dq.at[bit_xor(a, j)])

    def summed(first_row):
        parts = []
        for i in range(4):
            rows = slice(first_row, first_row + HW)
            both = S.dkv[2 * i, rows, :].astype(F32) + S.dkv[2 * i + 1, rows, :].astype(F32)
            parts.append(both)
        return jnp.concatenate(parts, axis=0).T.astype(BF)

    grads = {
        V: summed(HW),
        K: summed(0),
        Q: S.dq[...].reshape(D, ROWS).T,
    }
    note(1, grads[V])
    note(0, grads[Q])
    for name in (V, K, Q):
        for i in range(2):
            S.projected_half[name][i] = grads[name][:, 384 * i : 384 * (i + 1)]
        half = S.projected_half[name]
        to_group((PROJECTED_GRAD_ALL, name), lambda to: half.at[to % 2], S.projected_all[name])
        S.projected_all[name][w] = half[core]
    for j in (1, 2, 3):
        remote((VECTORS_W, j), S.sg, S.sg_w.at[w], c, bit_xor(w, j))
    S.sg_w[w] = S.sg[...]

    input_grad = S.keep[...]
    for name in (Q, K, V):
        input_grad = input_grad + right_product(grads[name], square(name))
    S.first[...] = input_grad
    finishing.append(local(INPUT_GRAD, S.first, input_grad_out))

    x_all = S.x_all[...].reshape(GROUP * ROWS, 384)
    spread_line(OUT)
    for name in (V, K, Q):
        from_group((PROJECTED_GRAD_ALL, name), S.projected_all[name])
        S.part[name][...] = tn(
            x_all, S.projected_all[name][...].reshape(GROUP * ROWS, 384)
        ).astype(BF)
        reduce_pair(name)
    reduce_line(O)
    spread_line(IN)
    for j in (1, 2, 3):
        arrived((VECTORS_W, j), S.sg_w.at[bit_xor(w, j)])
    S.sg_z[a] = (S.sg_w[0] + S.sg_w[1]) + (S.sg_w[2] + S.sg_w[3])
    for j in (1, 2, 3):
        remote((VECTORS_Z, j), S.sg_z.at[a], S.sg_z.at[a], bit_xor(c, 2 * j), w)
    spread_pair(OUT)
    reduce_line(V)
    spread_line(O)
    reduce_line(K)
    spread_pair(IN)
    reduce_line(Q)
    for j in (1, 2, 3):
        arrived((VECTORS_Z, j), S.sg_z.at[bit_xor(a, j)])
    S.sg_y[b] = (S.sg_z[0] + S.sg_z[1]) + (S.sg_z[2] + S.sg_z[3])
    remote(VECTORS_Y, S.sg_y.at[b], S.sg_y.at[b], bit_xor(c, 1), w)
    spread_line(V)
    spread_pair(O)
    spread_line(K)
    spread_line(Q)
    spread_pair(V)
    spread_pair(K)
    arrived(VECTORS_Y, S.sg_y.at[1 - b])
    everything = S.sg_y[0] + S.sg_y[1]
    for i in range(4):
        S.smalls[i] = everything[:, HW * i : HW * (i + 1)]
    finishing.append(local(VECTORS_Y, S.smalls, smalls_out))
    spread_pair(Q)

    for name in range(6):
        settle(name)
    for copy in finishing:
        copy.wait()
    for copy in started:
        copy.wait_send()


def finish_kernel(*refs):
    (g_q, g_k, g_v, g_o, g_in, g_out, smalls, output, input_grad) = refs[:9]
    (r_q, r_k, r_v, r_o, r_in, r_out, vectors, inner_bias, loss, r_output, r_input) = refs[9:]
    step = pl.program_id(0)
    for source, result in ((g_q, r_q), (g_k, r_k), (g_v, r_v), (g_o, r_o), (g_in, r_in)):
        width = source.shape[3]
        for i in range(2):
            result[:, width * i : width * (i + 1)] = source[i, 0].astype(F32)
    r_out[...] = g_out[0].reshape(HW, D).astype(F32)
    r_output[0] = output[...]
    r_input[0] = input_grad[...]

    @pl.when(step == 0)
    def once():
        w = lax.axis_index("wsh")
        vectors[...] = smalls[w, 0:8, :]
        for i in range(4):
            inner_bias[0:1, HW * i : HW * (i + 1)] = smalls[i, pl.ds(8 + w, 1), :]
        error = jnp.sum(smalls[:, 12:13, :])
        count = jnp.max(smalls[0, 13:14, :])
        loss[0, 0] = error / (count * D)


def fused_body(tokens, teacher, doc_lengths, valid_len, *weights):
    (
        q_weight,
        q_bias,
        k_weight,
        v_weight,
        v_bias,
        o_weight,
        o_bias,
        ln1_gain,
        ln1_bias,
        in_weight,
        in_bias,
        out_weight,
        out_bias,
        ln2_gain,
        ln2_bias,
    ) = weights
    w = lax.axis_index("wsh")
    own = (jnp.arange(GROUP) == w).astype(F32)
    rows = jnp.stack(
        [q_bias, v_bias, o_bias, ln1_gain, ln1_bias, out_bias, ln2_gain, ln2_bias]
    ).astype(F32)
    rows = (rows[:, None, :] * own[None, :, None]).reshape(8, D)
    inner_rows = in_bias.astype(F32)[None, :] * own[:, None]
    valid_row = jnp.broadcast_to(valid_len.astype(F32)[:, None], (1, D))
    small = jnp.concatenate([rows, inner_rows, valid_row, jnp.zeros((3, D), F32)], axis=0)

    hbm = pl.BlockSpec(memory_space=pl.ANY)
    smem = pl.BlockSpec(memory_space=pltpu.SMEM)
    low = lambda *shape: jax.ShapeDtypeStruct(shape, BF)
    full = lambda *shape: jax.ShapeDtypeStruct(shape, F32)
    output, input_grad, g_q, g_k, g_v, g_o, g_in, g_out, smalls = pl.pallas_call(
        fused_kernel,
        out_shape=(
            low(ROWS, D),
            full(ROWS, D),
            low(2, 4, 48, 384),
            low(2, 4, 48, 384),
            low(2, 4, 48, 384),
            low(2, 4, 48, 384),
            low(2, 4, 48, 1536),
            low(2, 4, 96, D),
            full(GROUP, 16, HW),
        ),
        in_specs=[hbm] * 9 + [smem] * 2,
        out_specs=[hbm] * 9,
        scratch_shapes=scratch_shapes()[0]
        + [
            pltpu.SemaphoreType.DMA((REMOTE_SEMS,)),
            pltpu.SemaphoreType.DMA((REMOTE_SEMS,)),
            pltpu.SemaphoreType.DMA((LOCAL_SEMS,)),
        ],
        compiler_params=pltpu.CompilerParams(
            collective_id=0, has_side_effects=True, vmem_limit_bytes=67043328
        ),
        name="layer",
    )(
        tokens,
        teacher,
        q_weight,
        k_weight,
        v_weight,
        o_weight,
        in_weight,
        out_weight,
        small,
        doc_lengths,
        valid_len,
    )

    steps = 4
    square_in = pl.BlockSpec((2, 1, HW // steps, 384), lambda i: (0, i, 0, 0))
    square_out = pl.BlockSpec((HW // steps, D), lambda i: (i, 0))
    whole = lambda *shape: pl.BlockSpec(shape, lambda i: (0,) * len(shape))
    results = pl.pallas_call(
        finish_kernel,
        grid=(steps,),
        out_shape=(
            full(HW, D),
            full(HW, D),
            full(HW, D),
            full(HW, D),
            full(HW, FF),
            full(D, D),
            full(8, HW),
            full(1, D),
            full(1, 1),
            low(1, ROWS, D),
            full(1, ROWS, D),
        ),
        in_specs=[square_in] * 4
        + [
            pl.BlockSpec((2, 1, HW // steps, 1536), lambda i: (0, i, 0, 0)),
            pl.BlockSpec((1, 2, 96, D), lambda i: (i // 2, i % 2, 0, 0)),
            whole(GROUP, 16, HW),
            pl.BlockSpec((ROWS // steps, D), lambda i: (i, 0)),
            pl.BlockSpec((ROWS // steps, D), lambda i: (i, 0)),
        ],
        out_specs=[square_out] * 4
        + [
            pl.BlockSpec((HW // steps, FF), lambda i: (i, 0)),
            pl.BlockSpec((D // steps, D), lambda i: (i, 0)),
            whole(8, HW),
            whole(1, D),
            pl.BlockSpec(memory_space=pltpu.SMEM),
            pl.BlockSpec((1, ROWS // steps, D), lambda i: (0, i, 0)),
            pl.BlockSpec((1, ROWS // steps, D), lambda i: (0, i, 0)),
        ],
        compiler_params=pltpu.CompilerParams(dimension_semantics=("arbitrary",)),
        name="finish",
    )(g_q, g_k, g_v, g_o, g_in, g_out, smalls, output, input_grad)
    r_q, r_k, r_v, r_o, r_in, r_out, vectors, inner_bias, loss, r_output, r_input = results
    return (
        r_output,
        loss[0, 0],
        r_input,
        r_q,
        vectors[0],
        r_k,
        r_v,
        vectors[1],
        r_o,
        vectors[2],
        vectors[3],
        vectors[4],
        r_in,
        inner_bias[0],
        r_out,
        vectors[5],
        vectors[6],
        vectors[7],
    )


def solution(mesh):
    in_specs = (
        P("wsh", "ctx", None),
        P("wsh", "ctx", None),
        P("wsh", None),
        P("wsh"),
        P("wsh", None),
        P("wsh"),
        P("wsh", None),
        P("wsh", None),
        P("wsh"),
        P("wsh", None),
        P("wsh"),
        P("wsh"),
        P("wsh"),
        P("wsh", None),
        P("wsh"),
        P("wsh", None),
        P("wsh"),
        P("wsh"),
        P("wsh"),
    )
    out_specs = (
        P("wsh", "ctx", None),
        P(),
        P("wsh", "ctx", None),
        P("wsh", None),
        P("wsh"),
        P("wsh", None),
        P("wsh", None),
        P("wsh"),
        P("wsh", None),
        P("wsh"),
        P("wsh"),
        P("wsh"),
        P("wsh", None),
        P("wsh"),
        P("wsh", None),
        P("wsh"),
        P("wsh"),
        P("wsh"),
    )
    program = fused_body if fused_fits(mesh) else body
    return jax.shard_map(program, mesh=mesh, in_specs=in_specs, out_specs=out_specs, check_vma=False)
```

```python
import math
import types

import jax
import jax.numpy as jnp
from jax import lax
from jax.experimental import pallas as pl
from jax.experimental.pallas import tpu as pltpu
from jax.sharding import PartitionSpec as P

D = 768
H = 12
HD = 64


EPSILON = 1e-06
MASKED = -1e30


def shifted(block, axis, distance):
    devices = range(lax.axis_size(axis))
    route = [((i - distance) % len(devices), i) for i in devices]
    return lax.ppermute(block, axis, route)


def layer_norm(value, gain, shift):
    mean = jnp.mean(value, axis=-1, keepdims=True)
    centered = value - mean
    spread = jnp.mean(centered * centered, axis=-1, keepdims=True)
    return centered * lax.rsqrt(spread + EPSILON) * gain + shift


def activate(value):
    return jax.nn.gelu(value, approximate=True)


def matmul(left, right):
    return jnp.dot(left, right, preferred_element_type=jnp.float32)


def left_product(left, right):
    return lax.dot_general(
        left, right, (((0,), (0,)), ((), ())), preferred_element_type=jnp.float32
    )


def right_product(left, right):
    return lax.dot_general(
        left, right, (((1,), (1,)), ((), ())), preferred_element_type=jnp.float32
    )


def document_of(positions, starts):
    return jnp.sum((starts[None, :] <= positions[:, None]).astype(jnp.int32), axis=1) - 1


def permitted(own_doc, own_live, other_doc, other_live):
    return (own_doc[:, None] == other_doc[None, :]) & (own_live[:, None] == other_live[None, :])


def block_weights(queries, key_block, allowed, score_scale):
    scores = (
        jnp.einsum("qhd,khd->hqk", queries, key_block, preferred_element_type=jnp.float32)
        * score_scale
    )
    return jnp.exp(jnp.where(allowed[None], scores, MASKED))


def forward_visit(sums_state, queries, key_block, value_block, allowed, score_scale):
    row_total, weighted = sums_state
    weights = block_weights(queries, key_block, allowed, score_scale)
    row_total = row_total + jnp.sum(weights, axis=-1)
    weighted = weighted + jnp.einsum(
        "hqk,khd->qhd",
        weights.astype(jnp.bfloat16),
        value_block,
        preferred_element_type=jnp.float32,
    )
    return (row_total, weighted)


def backward_visit(
    queries, key_block, value_block, allowed, score_scale, weighted_grad, total_grad
):
    weights = block_weights(queries, key_block, allowed, score_scale)
    value_part = jnp.einsum(
        "hqk,qhd->khd",
        weights.astype(jnp.bfloat16),
        weighted_grad,
        preferred_element_type=jnp.float32,
    )
    weight_grad = (
        jnp.einsum("qhd,khd->hqk", weighted_grad, value_block, preferred_element_type=jnp.float32)
        + total_grad[:, :, None]
    )
    score_grad = (weights * weight_grad).astype(jnp.bfloat16)
    query_part = (
        jnp.einsum("hqk,khd->qhd", score_grad, key_block, preferred_element_type=jnp.float32)
        * score_scale
    )
    key_part = (
        jnp.einsum("hqk,qhd->khd", score_grad, queries, preferred_element_type=jnp.float32)
        * score_scale
    )
    return (query_part, key_part, value_part)


def body(
    tokens,
    teacher,
    doc_lengths,
    valid_len,
    q_weight,
    q_bias,
    k_weight,
    v_weight,
    v_bias,
    o_weight,
    o_bias,
    ln1_gain,
    ln1_bias,
    in_weight,
    in_bias,
    out_weight,
    out_bias,
    ln2_gain,
    ln2_bias,
):
    gathered = (
        lax.all_gather(q_weight, "wsh", axis=0, tiled=True),
        lax.all_gather(q_bias, "wsh", axis=0, tiled=True),
        lax.all_gather(k_weight, "wsh", axis=0, tiled=True),
        lax.all_gather(v_weight, "wsh", axis=0, tiled=True),
        lax.all_gather(v_bias, "wsh", axis=0, tiled=True),
        lax.all_gather(o_weight, "wsh", axis=0, tiled=True),
        lax.all_gather(o_bias, "wsh", axis=0, tiled=True),
        lax.all_gather(ln1_gain, "wsh", axis=0, tiled=True),
        lax.all_gather(ln1_bias, "wsh", axis=0, tiled=True),
        lax.all_gather(in_weight, "wsh", axis=0, tiled=True),
        lax.all_gather(in_bias, "wsh", axis=0, tiled=True),
        lax.all_gather(out_weight, "wsh", axis=0, tiled=True),
        lax.all_gather(out_bias, "wsh", axis=0, tiled=True),
        lax.all_gather(ln2_gain, "wsh", axis=0, tiled=True),
        lax.all_gather(ln2_bias, "wsh", axis=0, tiled=True),
    )
    (
        w_query,
        b_query,
        w_key,
        w_value,
        b_value,
        w_out,
        b_out,
        gain_one,
        shift_one,
        w_inner,
        b_inner,
        w_back,
        b_back,
        gain_two,
        shift_two,
    ) = gathered
    gain_first = gain_one.astype(jnp.float32)
    shift_first = shift_one.astype(jnp.float32)
    gain_second = gain_two.astype(jnp.float32)
    shift_second = shift_two.astype(jnp.float32)
    inputs = tokens[0]
    row_count = inputs.shape[0]
    cycle_size = lax.axis_size("ctx")
    stream_count = lax.axis_size("wsh")
    position = lax.axis_index("ctx")
    score_scale = 1.0 / math.sqrt(HD)
    offsets = jnp.arange(row_count, dtype=jnp.int32)
    lengths = doc_lengths[0]
    starts = jnp.cumsum(lengths) - lengths
    limit = valid_len[0]

    def key_mask(block_index):
        where_rows = jnp.mod(block_index, cycle_size) * row_count + offsets
        return (document_of(where_rows, starts), where_rows < limit)

    own_doc, own_live = key_mask(position)
    input_float = inputs.astype(jnp.float32)
    queries = (
        (matmul(inputs, w_query) + b_query.astype(jnp.float32))
        .astype(jnp.bfloat16)
        .reshape(row_count, H, HD)
    )
    key_rows = matmul(inputs, w_key).astype(jnp.bfloat16).reshape(row_count, H, HD)
    value_rows = (
        (matmul(inputs, w_value) + b_value.astype(jnp.float32))
        .astype(jnp.bfloat16)
        .reshape(row_count, H, HD)
    )

    def visit_forward(sums_state, key_block, value_block, block_index):
        other_doc, other_live = key_mask(block_index)
        allowed = permitted(own_doc, own_live, other_doc, other_live)
        return forward_visit(sums_state, queries, key_block, value_block, allowed, score_scale)

    empty_state = (
        jnp.zeros((H, row_count), jnp.float32),
        jnp.zeros((row_count, H, HD), jnp.float32),
    )
    first_state = visit_forward(empty_state, key_rows, value_rows, position)

    def advance(step_index, loop_state):
        key_block, value_block, running = loop_state
        key_block, value_block = shifted((key_block, value_block), "ctx", 1)
        running = visit_forward(running, key_block, value_block, position - step_index)
        return (key_block, value_block, running)

    row_total, weighted = lax.fori_loop(
        1, cycle_size, advance, (key_rows, value_rows, first_state)
    )[2]
    normed = weighted / jnp.transpose(row_total)[:, :, None]
    context = normed.astype(jnp.bfloat16).reshape(row_count, D)
    attn = matmul(context, w_out) + b_out.astype(jnp.float32)
    first_sum = input_float + attn
    settled = layer_norm(first_sum, gain_first, shift_first)
    settled_low = settled.astype(jnp.bfloat16)
    inner = matmul(settled_low, w_inner) + b_inner.astype(jnp.float32)
    activated = activate(inner).astype(jnp.bfloat16)
    branch = matmul(activated, w_back) + b_back.astype(jnp.float32)
    second_sum = settled + branch
    result = layer_norm(second_sum, gain_second, shift_second)
    target = teacher[0].astype(jnp.float32)
    diff = jnp.where(own_live[:, None], result - target, 0.0)
    error_sum, live_count = lax.psum(
        (jnp.sum(diff * diff), jnp.sum(own_live.astype(jnp.float32))), ("ctx", "wsh")
    )
    loss = error_sum / (live_count * D)
    upstream = diff * (row_count * cycle_size * stream_count / live_count)
    unused_second, second_back = jax.vjp(layer_norm, second_sum, gain_second, shift_second)
    d_second, gain_two_grad, shift_two_grad = second_back(upstream)
    branch_grad = d_second.astype(jnp.bfloat16)
    back_weight_grad = left_product(activated, branch_grad)
    back_bias_grad = jnp.sum(branch_grad, axis=0, dtype=jnp.float32)
    d_activated = right_product(branch_grad, w_back)
    unused_inner, gelu_back = jax.vjp(activate, inner)
    inner_grad = gelu_back(d_activated)[0].astype(jnp.bfloat16)
    inner_weight_grad = left_product(settled_low, inner_grad)
    inner_bias_grad = jnp.sum(inner_grad, axis=0, dtype=jnp.float32)
    d_settled = d_second + right_product(inner_grad, w_inner)
    unused_first, first_back = jax.vjp(layer_norm, first_sum, gain_first, shift_first)
    d_first, gain_one_grad, shift_one_grad = first_back(d_settled)
    attn_grad = d_first.astype(jnp.bfloat16)
    out_weight_grad_local = left_product(context, attn_grad)
    out_bias_grad_local = jnp.sum(attn_grad, axis=0, dtype=jnp.float32)
    context_low = lax.optimization_barrier(right_product(attn_grad, w_out).astype(jnp.bfloat16))
    context_grad = context_low.astype(jnp.float32).reshape(row_count, H, HD)
    weighted_grad = (context_grad / jnp.transpose(row_total)[:, :, None]).astype(jnp.bfloat16)
    total_grad = -jnp.transpose(jnp.sum(context_grad * weighted, axis=-1)) / (row_total * row_total)

    def visit_backward(key_block, value_block, block_index):
        other_doc, other_live = key_mask(block_index)
        allowed = permitted(own_doc, own_live, other_doc, other_live)
        return backward_visit(
            queries, key_block, value_block, allowed, score_scale, weighted_grad, total_grad
        )

    query_sum, key_sum, value_sum = visit_backward(key_rows, value_rows, position)

    def advance_back(step_index, loop_state):
        key_block, value_block, query_acc, key_acc, value_acc = loop_state
        key_block, value_block = shifted((key_block, value_block), "ctx", 1)
        key_acc, value_acc = (
            shifted(key_acc.astype(jnp.bfloat16), "ctx", 1).astype(key_acc.dtype),
            shifted(value_acc.astype(jnp.bfloat16), "ctx", 1).astype(value_acc.dtype),
        )
        query_part, key_part, value_part = visit_backward(
            key_block, value_block, position - step_index
        )
        return (
            key_block,
            value_block,
            query_acc + query_part,
            key_acc + key_part,
            value_acc + value_part,
        )

    loop_state = lax.fori_loop(
        1, cycle_size, advance_back, (key_rows, value_rows, query_sum, key_sum, value_sum)
    )
    query_total = loop_state[2]
    key_total, value_total = (
        shifted(loop_state[3].astype(jnp.bfloat16), "ctx", 1).astype(jnp.float32),
        shifted(loop_state[4].astype(jnp.bfloat16), "ctx", 1).astype(jnp.float32),
    )
    query_grad = query_total.astype(jnp.bfloat16).reshape(row_count, D)
    key_grad = key_total.astype(jnp.bfloat16).reshape(row_count, D)
    value_grad = value_total.astype(jnp.bfloat16).reshape(row_count, D)
    query_weight_grad = left_product(inputs, query_grad)
    query_bias_grad = jnp.sum(query_grad, axis=0, dtype=jnp.float32)
    key_weight_grad = left_product(inputs, key_grad)
    value_weight_grad = left_product(inputs, value_grad)
    value_bias_grad = jnp.sum(value_grad, axis=0, dtype=jnp.float32)
    input_grad = (
        d_first
        + right_product(query_grad, w_query)
        + right_product(key_grad, w_key)
        + right_product(value_grad, w_value)
    )
    reduced = (
        lax.psum_scatter(
            query_weight_grad.astype(jnp.bfloat16), "wsh", scatter_dimension=0, tiled=True
        ).astype(jnp.float32),
        lax.psum_scatter(
            query_bias_grad.astype(jnp.bfloat16), "wsh", scatter_dimension=0, tiled=True
        ).astype(jnp.float32),
        lax.psum_scatter(
            key_weight_grad.astype(jnp.bfloat16), "wsh", scatter_dimension=0, tiled=True
        ).astype(jnp.float32),
        lax.psum_scatter(
            value_weight_grad.astype(jnp.bfloat16), "wsh", scatter_dimension=0, tiled=True
        ).astype(jnp.float32),
        lax.psum_scatter(
            value_bias_grad.astype(jnp.bfloat16), "wsh", scatter_dimension=0, tiled=True
        ).astype(jnp.float32),
        lax.psum_scatter(
            out_weight_grad_local.astype(jnp.bfloat16), "wsh", scatter_dimension=0, tiled=True
        ).astype(jnp.float32),
        lax.psum_scatter(
            out_bias_grad_local.astype(jnp.bfloat16), "wsh", scatter_dimension=0, tiled=True
        ).astype(jnp.float32),
        lax.psum_scatter(
            gain_one_grad.astype(jnp.bfloat16), "wsh", scatter_dimension=0, tiled=True
        ).astype(jnp.float32),
        lax.psum_scatter(
            shift_one_grad.astype(jnp.bfloat16), "wsh", scatter_dimension=0, tiled=True
        ).astype(jnp.float32),
        lax.psum_scatter(
            inner_weight_grad.astype(jnp.bfloat16), "wsh", scatter_dimension=0, tiled=True
        ).astype(jnp.float32),
        lax.psum_scatter(
            inner_bias_grad.astype(jnp.bfloat16), "wsh", scatter_dimension=0, tiled=True
        ).astype(jnp.float32),
        lax.psum_scatter(
            back_weight_grad.astype(jnp.bfloat16), "wsh", scatter_dimension=0, tiled=True
        ).astype(jnp.float32),
        lax.psum_scatter(
            back_bias_grad.astype(jnp.bfloat16), "wsh", scatter_dimension=0, tiled=True
        ).astype(jnp.float32),
        lax.psum_scatter(
            gain_two_grad.astype(jnp.bfloat16), "wsh", scatter_dimension=0, tiled=True
        ).astype(jnp.float32),
        lax.psum_scatter(
            shift_two_grad.astype(jnp.bfloat16), "wsh", scatter_dimension=0, tiled=True
        ).astype(jnp.float32),
    )
    summed = lax.psum(
        (
            reduced[0],
            reduced[1],
            reduced[2],
            reduced[3],
            reduced[4],
            reduced[5],
            reduced[6],
            reduced[7],
            reduced[8],
            reduced[9],
            reduced[10],
            reduced[11],
            reduced[12],
            reduced[13],
            reduced[14],
        ),
        "ctx",
    )
    return (
        result.astype(jnp.bfloat16)[None],
        loss,
        input_grad[None],
        summed[0],
        summed[1],
        summed[2],
        summed[3],
        summed[4],
        summed[5],
        summed[6],
        summed[7],
        summed[8],
        summed[9],
        summed[10],
        summed[11],
        summed[12],
        summed[13],
        summed[14],
    )


BF = jnp.bfloat16
F32 = jnp.float32
FF = 3072
ROWS = 128
HEADS = 3
HW = HEADS * HD
GROUP = 4
CTX = 8
MESH = pl.DeviceIdType.MESH

Q, K, V, O, IN, OUT, PART_Q, PART_K, PART_V = range(9)
SLICE = 256
WEIGHT_SHAPES = [(192, 768)] * 4 + [(192, 3072), (768, 768)] + [(192, SLICE)] * 3
SECOND_WAY = {Q: 2, K: 2, V: 2, O: 1, IN: 1, OUT: 2, PART_Q: 1, PART_K: 1, PART_V: 1}
PART_SHAPES = {O: (384, 384), IN: (384, 1536), OUT: (768, 768)}
HALVING = {O: (1, 2, 4), IN: (1, 2, 4), OUT: (1, 2, 4)}
HEAD_COLS = 640

(
    SMALL,
    WEIGHT_X,
    WEIGHT_SECOND,
    WEIGHT_CORE,
    WEIGHT_CORE_X,
    WEIGHT_CORE_SECOND,
    X_LINE,
    X_PAIR,
    CONTEXT,
    CONTEXT_GRAD,
    KEY_VALUE_GRAD,
    QUERY_GRAD,
    SETTLED_ALL,
    CONTEXT_ALL,
    ATTN_GRAD_ALL,
    INNER_GRAD_ALL,
    ACTIVATED_ALL,
    BRANCH_GRAD_ALL,
    REDUCE,
    SPREAD,
    GIVE,
    OWN,
    HEADS_CORE,
    HEADS_X,
    HEADS_Y,
    HEADS_LINE,
    HEADS_PAIR,
    VECTORS_W,
    VECTORS_Z,
    VECTORS_Y,
    TOKENS,
    TEACHER,
    OUTPUT,
    INPUT_GRAD,
    LOAD,
) = range(35)


def fused_fits(mesh):
    return mesh.shape["ctx"] == CTX and mesh.shape["wsh"] == GROUP


def tn(left, right):
    return lax.dot_general(
        left, right, (((0,), (0,)), ((), ())), preferred_element_type=jnp.float32
    )


def norm_parts(value):
    mean = jnp.mean(value, axis=-1, keepdims=True)
    centered = value - mean
    spread = jnp.mean(centered * centered, axis=-1, keepdims=True)
    inverse = lax.rsqrt(spread + EPSILON)
    return centered * inverse, inverse


def norm_back(upstream_gained, normal, inverse):
    return (
        upstream_gained
        - jnp.mean(upstream_gained, axis=-1, keepdims=True)
        - normal * jnp.mean(upstream_gained * normal, axis=-1, keepdims=True)
    ) * inverse


GELU_C = math.sqrt(2.0 / math.pi)


class Numbers:
    def __init__(self):
        self.count = 0
        self.table = {}

    def take(self, key, size=1):
        if key not in self.table:
            self.table[key] = self.count
            self.count += size
        return self.table[key]


def scratch_table():
    s = types.SimpleNamespace()
    s.full = [pltpu.VMEM((GROUP, rows, cols), BF) for rows, cols in WEIGHT_SHAPES]
    s.turned_weight = pltpu.VMEM((3 * SLICE, D), BF)
    s.x = pltpu.VMEM((ROWS, D), BF)
    s.xt = pltpu.VMEM((CTX, D, ROWS), BF)
    s.teacher = pltpu.VMEM((ROWS, D), BF)
    s.small = pltpu.VMEM((GROUP, 16, D), BF)
    s.vectors = pltpu.VMEM((16, D), F32)
    s.kt = pltpu.VMEM((CTX, SLICE, ROWS), BF)
    s.vt = pltpu.VMEM((CTX, SLICE, ROWS), BF)
    s.qt = pltpu.VMEM((4, SLICE, ROWS), BF)
    s.weights = pltpu.VMEM((CTX, HEADS, ROWS, 4 * ROWS), F32)
    s.mix = pltpu.VMEM((HEADS, HD, 4 * ROWS), F32)
    s.total = pltpu.VMEM((HEADS, 8, 4 * ROWS), F32)
    s.ctx_send = pltpu.VMEM((4, HW, ROWS), BF)
    s.ctx = pltpu.VMEM((4, HW, ROWS), BF)
    s.inner = pltpu.VMEM((4, ROWS, D), F32)
    s.act = pltpu.VMEM((4, ROWS, D), BF)
    s.first = pltpu.VMEM((ROWS, D), F32)
    s.keep = pltpu.VMEM((ROWS, D), F32)
    s.set_half = pltpu.VMEM((2, ROWS, 384), BF)
    s.ag_half = pltpu.VMEM((2, ROWS, 384), BF)
    s.ig_half = pltpu.VMEM((2, ROWS, 1536), BF)
    s.bg = pltpu.VMEM((ROWS, D), BF)
    s.set_all = pltpu.VMEM((GROUP, ROWS, 384), BF)
    s.ctx_all = pltpu.VMEM((GROUP, 2, HW, ROWS), BF)
    s.ag_all = pltpu.VMEM((GROUP, ROWS, 384), BF)
    s.ig_all = pltpu.VMEM((GROUP, ROWS, 1536), BF)
    s.act_all = pltpu.VMEM((GROUP, ROWS, D), BF)
    s.bg_all = pltpu.VMEM((GROUP, ROWS, D), BF)
    s.cg_send = pltpu.VMEM((4, HW, ROWS), BF)
    s.cg = pltpu.VMEM((4, HW, ROWS), BF)
    s.wg = pltpu.VMEM((HEADS, HD, 4 * ROWS), BF)
    s.dkv_send = pltpu.VMEM((CTX, 2 * HW, ROWS), BF)
    s.dkv = pltpu.VMEM((CTX, 2 * HW, ROWS), BF)
    s.dq_send = pltpu.VMEM((4, HW, ROWS), BF)
    s.dq = pltpu.VMEM((4, HW, ROWS), BF)
    s.heads = pltpu.VMEM((2, 2, HW, HEAD_COLS), BF)
    s.heads_core = pltpu.VMEM((2, HW, HEAD_COLS), BF)
    s.heads_sum = pltpu.VMEM((2, HW, HEAD_COLS), BF)
    s.heads_x = pltpu.VMEM((HW, HEAD_COLS), BF)
    s.heads_row = pltpu.VMEM((2, HW // 2, HEAD_COLS), BF)
    s.heads_y = pltpu.VMEM((HW // 2, HEAD_COLS), BF)
    s.heads_done = pltpu.VMEM((4, HW // 2, HEAD_COLS), BF)
    s.part = {k: pltpu.VMEM((2, r // 2, n), BF) for k, (r, n) in PART_SHAPES.items()}
    s.got = {
        k: [pltpu.VMEM((r >> i, n), BF) for i in (1, 2, 3)] for k, (r, n) in PART_SHAPES.items()
    }
    s.sum = {
        k: [pltpu.VMEM((2, r >> i, n), BF) for i in (2, 3)] for k, (r, n) in PART_SHAPES.items()
    }
    s.done = {k: pltpu.VMEM((2, 2, 2, r // 8, n), BF) for k, (r, n) in PART_SHAPES.items()}
    s.smalls = pltpu.VMEM((GROUP, 16, HW), F32)
    s.sg = pltpu.VMEM((16, D), F32)
    s.sg_rows = pltpu.VMEM((16, D), F32)
    s.sg_w = pltpu.VMEM((GROUP, 16, D), F32)
    s.sg_z = pltpu.VMEM((4, 16, D), F32)
    s.sg_y = pltpu.VMEM((2, 16, D), F32)
    s.out_low = pltpu.VMEM((ROWS, D), BF)
    return vars(s)


LOCAL_SEMS = 32
REMOTE_SEMS = 192


def is_memory(item):
    return not isinstance(item, (dict, list))


def scratch_shapes():
    return jax.tree.flatten(scratch_table(), is_leaf=is_memory)


def fused_kernel(*refs):
    (tokens, teacher), shards = refs[:2], refs[2:8]
    lengths, valid = refs[8:10]
    biases = refs[10:19]
    output, input_grad_out = refs[19:21]
    grad_out, heads_out, smalls_out, rows_out = refs[21:24], refs[24], refs[25], refs[26]
    grad_out = dict(zip((O, IN, OUT), grad_out))
    flat, shape = scratch_shapes()
    S = types.SimpleNamespace(**jax.tree.unflatten(shape, refs[27 : 27 + len(flat)]))
    send_sems, recv_sems, local_sems = refs[27 + len(flat) :]

    c = lax.axis_index("ctx")
    w = lax.axis_index("wsh")
    a, b = c // 2, c % 2
    x, core = w // 2, w % 2

    numbers = Numbers()
    locals_ = Numbers()
    started = []

    def bit_xor(value, j):
        out = value
        bit = 1
        while bit <= j:
            if j & bit:
                has = (value // bit) % 2
                out = out + bit * (1 - 2 * has)
            bit *= 2
        return out

    def remote(key, src, dst, c_to, w_to, offset=0, size=1):
        number = numbers.take(key, size) + offset
        copy = pltpu.make_async_remote_copy(
            src_ref=src,
            dst_ref=dst,
            send_sem=send_sems.at[number],
            recv_sem=recv_sems.at[number],
            device_id={"ctx": c_to, "wsh": w_to},
            device_id_type=MESH,
        )
        copy.start()
        started.append(copy)
        return copy

    def arrived(key, landing, offset=0):
        number = numbers.take(key) + offset
        pltpu.make_async_copy(landing, landing, recv_sems.at[number]).wait()

    def local(key, src, dst):
        copy = pltpu.make_async_copy(src, dst, local_sems.at[locals_.take(key)])
        copy.start()
        return copy

    peers = [(c, bit_xor(w, j)) for j in (1, 2, 3)]
    peers += [(bit_xor(c, j), w) for j in range(1, CTX)]
    peers += [(bit_xor(c, 1), bit_xor(w, 1))]

    def bit(value, mask):
        return (value // mask) % 2

    first_col = pl.multiple_of((3 * a) // 2 * 128, 128)
    first_row = pl.multiple_of(a % 2 * 64, 64)

    def shard(name):
        if name < PART_Q:
            return shards[name]
        return shards[name - PART_Q].at[:, pl.ds(first_col, SLICE)]

    loads = {TOKENS: local(TOKENS, tokens.at[0], S.x)}
    for name in (PART_K, PART_V, PART_Q, O, IN, OUT, K, V, Q):
        loads[name] = local((LOAD, name), shard(name), S.full[name].at[w])
    loads[TEACHER] = local(TEACHER, teacher.at[0], S.teacher)

    barrier = pltpu.get_barrier_semaphore()
    for c_to, w_to in peers:
        pl.semaphore_signal(
            barrier, inc=1, device_id={"ctx": c_to, "wsh": w_to}, device_id_type=MESH
        )
    loads[TOKENS].wait()
    x_low = S.x[...]
    S.xt[c] = x_low.T
    bias_rows = [row[...].astype(F32).reshape(1, HW) for row in biases[:8]]
    tall = jnp.concatenate(bias_rows, axis=0)
    valid_high = (valid[0] // 64).astype(F32)
    valid_low = (valid[0] % 64).astype(F32)
    wide_rows = [biases[8][...].astype(F32).reshape(1, D)]
    wide_rows += [jnp.full((1, D), 64.0, F32) * valid_high, jnp.full((1, D), 1.0, F32) * valid_low]
    wide_rows += [jnp.zeros((5, D), F32)]
    S.small[w, :, 0:HW] = jnp.concatenate(
        [tall, jnp.concatenate(wide_rows, axis=0)[:, 0:HW]], axis=0
    ).astype(BF)
    S.small[w, 8:16, HW:D] = jnp.concatenate(wide_rows, axis=0)[:, HW:D].astype(BF)

    pl.semaphore_wait(barrier, len(peers))

    def half_of(name, which):
        rows = WEIGHT_SHAPES[name][0] // 2
        return pl.ds(pl.multiple_of(which * rows, rows), rows)

    def mine(name):
        return bit(c, SECOND_WAY[name])

    def send_weight(name):
        full, own = S.full[name], half_of(name, mine(name))
        if name < PART_Q:
            half = shard(name).at[own]
        else:
            half = shards[name - PART_Q].at[own, pl.ds(first_col, SLICE)]
        remote((WEIGHT_X, name), half, full.at[w, own], c, bit_xor(w, 2))
        remote((WEIGHT_CORE, name), shard(name), full.at[w], c, bit_xor(w, 1))

    for name in (PART_K, PART_V, PART_Q):
        send_weight(name)
    for j in (1, 2, 3):
        remote((SMALL, j), S.small.at[w], S.small.at[w], c, bit_xor(w, j))
    remote((X_PAIR,), S.xt.at[c], S.xt.at[c], bit_xor(c, 1), w, 0, 4)
    for j in (1, 2, 3):
        remote((X_LINE, j), S.xt.at[c], S.xt.at[c], bit_xor(c, 2 * j), w)
    for name in (O, IN, OUT, K, V, Q):
        send_weight(name)

    def pump_x(name):
        slot = S.full[name].at[bit_xor(w, 2), half_of(name, mine(name))]
        arrived((WEIGHT_X, name), slot)
        remote((WEIGHT_SECOND, name), slot, slot, bit_xor(c, SECOND_WAY[name]), w)
        remote((WEIGHT_CORE_X, name), slot, slot, c, bit_xor(w, 1))

    def pump_second(name):
        slot = S.full[name].at[bit_xor(w, 2), half_of(name, 1 - mine(name))]
        arrived((WEIGHT_SECOND, name), slot)
        remote((WEIGHT_CORE_SECOND, name), slot, slot, c, bit_xor(w, 1))

    def weight_ready(name):
        full = S.full[name]
        loads[name].wait()
        arrived((WEIGHT_CORE, name), full.at[bit_xor(w, 1)])
        arrived((WEIGHT_CORE_X, name), full.at[bit_xor(w, 3), half_of(name, mine(name))])
        arrived((WEIGHT_CORE_SECOND, name), full.at[bit_xor(w, 3), half_of(name, 1 - mine(name))])

    def square(name):
        return S.full[name][...].reshape(D, D)

    starts, running = [], 0
    for i in range(lengths.shape[1]):
        starts.append(running)
        running = running + lengths[0, i]
    limit = valid[0]

    def code_of(position):
        code = jnp.zeros(position.shape, jnp.int32)
        for start in starts:
            code = code + (start <= position).astype(jnp.int32)
        return 2 * code + (position < limit).astype(jnp.int32)

    lane = lax.broadcasted_iota(jnp.int32, (1, 4 * ROWS), 1)
    query_code = code_of((2 * (lane // ROWS) + b) * ROWS + lane % ROWS)

    def key_code(block):
        return code_of(block * ROWS + lax.broadcasted_iota(jnp.int32, (ROWS, 1), 0))

    own_live = c * ROWS + lax.broadcasted_iota(jnp.int32, (ROWS, 1), 0) < limit

    def block_on(j, pair):
        if isinstance(j, int):
            return 2 * bit_xor(a, j) + pair
        low = (a % 2 + j % 2) % 2
        high = (a // 2 + j // 2) % 2
        return 2 * (2 * high + low) + pair

    def pass_on(j):
        block = S.xt.at[block_on(j, b)]
        arrived((X_LINE, j), block)
        remote((X_PAIR,), block, block, bit_xor(c, 1), w, j, 4)

    pump_x(PART_K)
    pump_x(PART_V)
    pump_x(PART_Q)
    for j in (1, 2, 3):
        arrived((SMALL, j), S.small.at[bit_xor(w, j)])
    S.vectors[0:8, :] = jnp.concatenate(
        [S.small[i, 0:8, 0:HW].astype(F32) for i in range(GROUP)], axis=1
    )
    small = [S.small[i, 8:16, :].astype(F32) for i in range(GROUP)]
    S.vectors[8:16, :] = jnp.concatenate(
        [part[0:1] for part in small]
        + [sum(part[1:2] + part[2:3] for part in small), jnp.zeros((3, D), F32)],
        axis=0,
    )

    def vector(row):
        return S.vectors[row : row + 1, :]

    def tall_bias(row):
        return jnp.broadcast_to(S.vectors[row : row + 1, pl.ds(first_col, SLICE)], (8, SLICE)).T[
            :, 0:1
        ]

    pass_on(1)
    pump_second(PART_K)
    pump_second(PART_V)
    pump_second(PART_Q)
    pass_on(2)
    for i, name in enumerate((PART_Q, PART_K, PART_V)):
        weight_ready(name)
        S.turned_weight[SLICE * i : SLICE * (i + 1), :] = S.full[name][...].reshape(D, SLICE).T
    query_bias, value_bias = tall_bias(0), tall_bias(1)

    def project(block):
        both = matmul(S.turned_weight[SLICE : 3 * SLICE, :], S.xt[block])
        S.kt[block] = both[0:SLICE].astype(BF)
        S.vt[block] = (both[SLICE : 2 * SLICE] + value_bias).astype(BF)

    def project_queries(j):
        block = block_on(j, b)
        queries = matmul(S.turned_weight[0:SLICE, :], S.xt[block]) + query_bias
        S.qt[block // 2] = queries.astype(BF)

    for j in (0, 1, 2):
        project_queries(j)
    pump_x(O)
    pass_on(3)
    project_queries(3)

    def to_group(key, source_of, everywhere):
        for j in (1, 2, 3):
            to = bit_xor(w, j)
            remote((*key, j), source_of(to), everywhere.at[w], c, to)

    def from_group(key, everywhere):
        for j in (1, 2, 3):
            arrived((*key, j), everywhere.at[bit_xor(w, j)])

    score_scale = 1.0 / math.sqrt(HD)

    def head(ref, block, h):
        return ref[block, pl.ds(first_row + HD * h, HD), :]

    def wide_queries(h):
        return jnp.concatenate([head(S.qt, i, h) for i in range(4)], axis=1)

    def wide(ref, h):
        return jnp.concatenate([ref[i, HD * h : HD * (h + 1), :] for i in range(4)], axis=1)

    S.mix[...] = jnp.zeros(S.mix.shape, F32)
    S.total[...] = jnp.zeros(S.total.shape, F32)

    def attend_block(block):
        project(block)
        allowed = key_code(block) == query_code
        for h in range(HEADS):
            scores = tn(head(S.kt, block, h), wide_queries(h)) * score_scale
            weights = jnp.exp(jnp.where(allowed, scores, MASKED))
            S.weights[block, h] = weights
            S.total[h, 0:1, :] += jnp.sum(weights, axis=0, keepdims=True)
            S.mix[h] += matmul(head(S.vt, block, h), weights.astype(BF))

    @pl.loop(0, 4)
    def attend_line(j):
        attend_block(block_on(j, b))

    pump_second(O)
    pump_x(IN)
    pair_base = numbers.take((X_PAIR,), 4)

    @pl.loop(0, 4)
    def attend_pair(j):
        block = block_on(j, 1 - b)
        landing = S.xt.at[block]
        pltpu.make_async_copy(landing, landing, recv_sems.at[pair_base + j]).wait()
        attend_block(block)

    for h in range(HEADS):
        context_t = (S.mix[h] / S.total[h, 0:1, :]).astype(BF)
        for i in range(4):
            S.ctx_send[i, HD * h : HD * (h + 1), :] = context_t[:, ROWS * i : ROWS * (i + 1)]
    for j in (1, 2, 3):
        to = bit_xor(a, j)
        remote((CONTEXT, j), S.ctx_send.at[to], S.ctx.at[a], bit_xor(c, 2 * j), w)
    S.ctx[a] = S.ctx_send[a]
    pump_second(IN)
    pump_x(OUT)
    weight_ready(O)
    for j in (1, 2, 3):
        arrived((CONTEXT, j), S.ctx.at[bit_xor(a, j)])

    to_group((CONTEXT_ALL,), lambda to: S.ctx.at[pl.ds(2 * (to // 2), 2)], S.ctx_all)
    S.ctx_all[w] = S.ctx[pl.ds(2 * x, 2)]
    attn = tn(S.ctx[...].reshape(D, ROWS), square(O)) + vector(2)
    first_sum = x_low.astype(F32) + attn
    normal_one, inverse_one = norm_parts(first_sum)
    settled = normal_one * vector(3) + vector(4)
    settled_low = settled.astype(BF)
    S.first[...] = normal_one
    S.keep[...] = settled
    for i in range(2):
        S.set_half[i] = settled_low[:, 384 * i : 384 * (i + 1)]
    to_group((SETTLED_ALL,), lambda to: S.set_half.at[to // 2], S.set_all)
    S.set_all[w] = S.set_half[x]
    weight_ready(IN)
    pump_second(OUT)
    for t in range(4):
        w_part = S.full[IN][:, :, D * t : D * (t + 1)].reshape(D, D)
        inner = matmul(settled_low, w_part) + vector(8 + t)
        S.inner[t] = inner
        S.act[t] = (
            0.5 * inner * (1.0 + jnp.tanh(GELU_C * (inner + 0.044715 * inner * inner * inner)))
        ).astype(BF)
    to_group((ACTIVATED_ALL,), lambda to: S.act.at[to], S.act_all)
    S.act_all[w] = S.act[w]
    weight_ready(OUT)
    branch = vector(5)
    for t in range(4):
        branch = branch + matmul(S.act[t], S.full[OUT][t])
    normal_two, inverse_two = norm_parts(S.keep[...] + branch)
    result = normal_two * vector(6) + vector(7)
    S.out_low[...] = result.astype(BF)
    finishing = [local(OUTPUT, S.out_low, output)]
    loads[TEACHER].wait()
    diff = jnp.where(own_live, result - S.teacher[...].astype(F32), 0.0)
    count = vector(12)
    upstream = diff * ((ROWS * CTX * GROUP) / count)
    S.sg[...] = jnp.zeros((16, D), F32)

    def note(row, value):
        S.sg[row : row + 1, :] = jnp.sum(value.astype(F32), axis=0, keepdims=True)

    note(12, diff * diff)
    S.sg[13:14, :] = count * (1.0 / (CTX * GROUP))
    note(6, upstream * normal_two)
    note(7, upstream)

    d_second = norm_back(upstream * vector(6), normal_two, inverse_two)
    branch_grad = d_second.astype(BF)
    S.bg[...] = branch_grad
    for name in (K, V, Q):
        pump_x(name)
    to_group((BRANCH_GRAD_ALL,), lambda to: S.bg, S.bg_all)
    S.bg_all[w] = branch_grad
    note(5, branch_grad)
    d_settled = d_second
    for t in range(4):
        d_act = right_product(branch_grad, S.full[OUT][t])
        inner = S.inner[t]
        squared = inner * inner
        bend = jnp.tanh(GELU_C * (inner + 0.044715 * squared * inner))
        slope = 0.5 * (1.0 + bend) + 0.5 * inner * (1.0 - bend * bend) * (
            GELU_C * (1.0 + 3 * 0.044715 * squared)
        )
        inner_grad = (d_act * slope).astype(BF)
        S.ig_half[t // 2, :, D * (t % 2) : D * (t % 2 + 1)] = inner_grad
        note(8 + t, inner_grad)
        w_part = S.full[IN][:, :, D * t : D * (t + 1)].reshape(D, D)
        d_settled = d_settled + right_product(inner_grad, w_part)
    for name in (K, V, Q):
        pump_second(name)
    to_group((INNER_GRAD_ALL,), lambda to: S.ig_half.at[to % 2], S.ig_all)
    S.ig_all[w] = S.ig_half[core]
    normal_one = S.first[...]
    note(3, d_settled * normal_one)
    note(4, d_settled)
    d_first = norm_back(d_settled * vector(3), normal_one, inverse_one)
    S.keep[...] = d_first
    attn_grad = d_first.astype(BF)
    note(2, attn_grad)
    context_grad = right_product(attn_grad, square(O)).T.astype(BF)
    for i in range(4):
        S.cg_send[i] = context_grad[HW * i : HW * (i + 1), :]
    for j in (1, 2, 3):
        to = bit_xor(a, j)
        remote((CONTEXT_GRAD, j), S.cg_send.at[to], S.cg.at[a], bit_xor(c, 2 * j), w)
    S.cg[a] = S.cg_send[a]
    for i in range(2):
        S.ag_half[i] = attn_grad[:, 384 * i : 384 * (i + 1)]
    to_group((ATTN_GRAD_ALL,), lambda to: S.ag_half.at[to % 2], S.ag_all)
    S.ag_all[w] = S.ag_half[core]

    def reduce_send(name, stage):
        mask = HALVING[name][stage]
        source = S.part[name] if stage == 0 else S.sum[name][stage - 1]
        there = source.at[1 - bit(c, mask)]
        remote((REDUCE, name, stage), there, S.got[name][stage], bit_xor(c, mask), w)

    def slot(name):
        return [bit(c, mask) for mask in HALVING[name]]

    def reduce_add(name, stage):
        source = S.part[name] if stage == 0 else S.sum[name][stage - 1]
        got = S.got[name][stage]
        arrived((REDUCE, name, stage), got)
        total = source[bit(c, HALVING[name][stage])].astype(F32) + got[...].astype(F32)
        if stage == 2:
            i, j, k = slot(name)
            S.done[name][i, j, k] = total.astype(BF)
        else:
            rows, cols = PART_SHAPES[name]
            S.sum[name][stage][...] = total.astype(BF).reshape(2, rows >> (stage + 2), cols)

    def spread_send(name, stage):
        i, j, k = slot(name)
        part = S.done[name].at[i, j, k] if stage == 2 else S.done[name].at[i, j]
        remote((SPREAD, name, stage), part, part, bit_xor(c, HALVING[name][stage]), w)

    def spread_wait(name, stage):
        i, j, k = slot(name)
        part = S.done[name].at[i, j, 1 - k] if stage == 2 else S.done[name].at[i, 1 - j]
        arrived((SPREAD, name, stage), part)

    def give(name):
        mask = HALVING[name][0]
        half = bit(c, mask)
        done, out = S.done[name].at[half], grad_out[name]
        if name == OUT:
            remote((GIVE, name), done, out.at[half], bit_xor(c, mask), w)
            finishing.append(local((GIVE, name), done, out.at[half]))
            return
        remote((GIVE, name), done, out.at[core], bit_xor(c, mask), 2 * x + half, core, 2)

        @pl.when(core == half)
        def keep_own():
            local((OWN, name), done, out.at[core])

        @pl.when(core != half)
        def give_core():
            remote((OWN, name), done, out.at[core], c, bit_xor(w, 1))
            started.pop()

    def settle(name):
        half = bit(c, HALVING[name][0])
        done, out = S.done[name].at[half], grad_out[name]
        if name == OUT:
            arrived((GIVE, name), out.at[1 - half])
            return

        @pl.when(core == half)
        def from_chip():
            pltpu.make_async_copy(
                done, out.at[core], local_sems.at[locals_.take((OWN, name))]
            ).wait()
            arrived((OWN, name), out.at[1 - core])

        @pl.when(core != half)
        def from_partner():
            arrived((GIVE, name), out.at[0], 0)
            arrived((GIVE, name), out.at[1], 1)
            sent = numbers.take((OWN, name))
            pltpu.make_async_copy(done, done, send_sems.at[sent]).wait()

    from_group((ACTIVATED_ALL,), S.act_all)
    from_group((BRANCH_GRAD_ALL,), S.bg_all)
    S.part[OUT][...] = (
        tn(S.act_all[...].reshape(GROUP * ROWS, D), S.bg_all[...].reshape(GROUP * ROWS, D))
        .astype(BF)
        .reshape(2, D // 2, D)
    )
    reduce_send(OUT, 0)

    for j in (1, 2, 3):
        arrived((CONTEXT_GRAD, j), S.cg.at[bit_xor(a, j)])
    for h in range(HEADS):
        grad = wide(S.cg, h).astype(F32)
        row_total = S.total[h, 0:1, :]
        S.wg[h] = (grad / row_total).astype(BF)
        S.total[h, 1:2, :] = -jnp.sum(grad * S.mix[h], axis=0, keepdims=True) / (
            row_total * row_total
        )
    S.mix[...] = jnp.zeros(S.mix.shape, F32)

    @pl.loop(0, CTX)
    def attend_back(block):
        for h in range(HEADS):
            key_rows = slice(HD * h, HD * (h + 1))
            value_rows = slice(HW + HD * h, HW + HD * (h + 1))
            weights = S.weights[block, h]
            grad = S.wg[h]
            weight_grad = tn(head(S.vt, block, h), grad) + S.total[h, 1:2, :]
            score_grad = (weights * weight_grad).astype(BF)
            S.mix[h] += matmul(head(S.kt, block, h), score_grad)
            S.dkv_send[block, key_rows, :] = (
                right_product(wide_queries(h), score_grad) * score_scale
            ).astype(BF)
            S.dkv_send[block, value_rows, :] = right_product(grad, weights.astype(BF)).astype(BF)

    for j in range(1, CTX):
        to = bit_xor(c, j)
        remote((KEY_VALUE_GRAD, j), S.dkv_send.at[to], S.dkv.at[c], to, w)
    S.dkv[c] = S.dkv_send[c]
    for h in range(HEADS):
        query_t = (S.mix[h] * score_scale).astype(BF)
        for i in range(4):
            S.dq_send[i, HD * h : HD * (h + 1), :] = query_t[:, ROWS * i : ROWS * (i + 1)]
    for j in (1, 2, 3):
        to = bit_xor(a, j)
        remote((QUERY_GRAD, j), S.dq_send.at[to], S.dq.at[a], bit_xor(c, 2 * j), w)
    S.dq[a] = S.dq_send[a]

    def lanes(ref, pair):
        return jnp.concatenate([ref[2 * i + pair] for i in range(4)], axis=1)

    own_grads = jnp.concatenate(
        [
            lanes(S.dkv_send, b),
            jnp.concatenate([S.dq_send[i] for i in range(4)], axis=1),
            jnp.zeros((HEAD_COLS - 3 * HW, 4 * ROWS), BF),
        ],
        axis=0,
    )
    other = right_product(lanes(S.xt, 1 - b), lanes(S.dkv_send, 1 - b))
    heads = right_product(lanes(S.xt, b), own_grads)
    heads = jnp.concatenate([heads[:, : 2 * HW] + other, heads[:, 2 * HW :]], axis=1).astype(BF)
    S.heads[...] = heads.reshape(2, 2, HW, HEAD_COLS)
    for i in range(2):
        remote((HEADS_CORE, i), S.heads.at[i, 1 - core], S.heads_core.at[i], c, bit_xor(w, 1))

    from_group((SETTLED_ALL,), S.set_all)
    from_group((INNER_GRAD_ALL,), S.ig_all)
    S.part[IN][...] = (
        tn(S.set_all[...].reshape(GROUP * ROWS, 384), S.ig_all[...].reshape(GROUP * ROWS, 1536))
        .astype(BF)
        .reshape(2, HW, 1536)
    )
    reduce_send(IN, 0)
    for i in range(2):
        arrived((HEADS_CORE, i), S.heads_core.at[i])
        S.heads_sum[i] = (S.heads[i, core].astype(F32) + S.heads_core[i].astype(F32)).astype(BF)
    remote((HEADS_X,), S.heads_sum.at[1 - x], S.heads_x, c, bit_xor(w, 2))
    reduce_add(OUT, 0)
    reduce_send(OUT, 1)
    from_group((CONTEXT_ALL,), S.ctx_all)
    from_group((ATTN_GRAD_ALL,), S.ag_all)
    context_all = jnp.concatenate(
        [S.ctx_all[i].reshape(384, ROWS) for i in range(GROUP)], axis=1
    )
    S.part[O][...] = (
        matmul(context_all, S.ag_all[...].reshape(GROUP * ROWS, 384)).astype(BF).reshape(2, HW, 384)
    )
    reduce_send(O, 0)
    arrived((HEADS_X,), S.heads_x)
    S.heads_row[...] = (
        (S.heads_sum[x].astype(F32) + S.heads_x[...].astype(F32))
        .astype(BF)
        .reshape(2, HW // 2, HEAD_COLS)
    )
    remote((HEADS_Y,), S.heads_row.at[1 - b], S.heads_y, bit_xor(c, 1), w)
    reduce_add(OUT, 1)
    reduce_send(OUT, 2)
    reduce_add(IN, 0)
    reduce_send(IN, 1)
    reduce_add(OUT, 2)
    spread_send(OUT, 2)
    arrived((HEADS_Y,), S.heads_y)
    S.heads_done[a] = (S.heads_row[b].astype(F32) + S.heads_y[...].astype(F32)).astype(BF)
    for j in (1, 2, 3):
        remote((HEADS_LINE, j), S.heads_done.at[a], S.heads_done.at[a], bit_xor(c, 2 * j), w)

    for name in (K, V, Q):
        weight_ready(name)
    for j in range(1, CTX):
        arrived((KEY_VALUE_GRAD, j), S.dkv.at[bit_xor(c, j)])
    for j in (1, 2, 3):
        arrived((QUERY_GRAD, j), S.dq.at[bit_xor(a, j)])

    def summed(first):
        parts = []
        for i in range(4):
            rows = slice(first, first + HW)
            both = S.dkv[2 * i, rows, :].astype(F32) + S.dkv[2 * i + 1, rows, :].astype(F32)
            parts.append(both)
        return jnp.concatenate(parts, axis=0).T.astype(BF)

    grads = {V: summed(HW), K: summed(0), Q: S.dq[...].reshape(D, ROWS).T}
    note(1, grads[V])
    note(0, grads[Q])
    for j in (1, 2, 3):
        remote((VECTORS_W, j), S.sg, S.sg_w.at[w], c, bit_xor(w, j))
    S.sg_w[w] = S.sg[...]
    input_grad = S.keep[...]
    for name in (Q, K, V):
        input_grad = input_grad + right_product(grads[name], square(name))
    S.first[...] = input_grad
    finishing.append(local(INPUT_GRAD, S.first, input_grad_out))

    reduce_add(IN, 1)
    reduce_send(IN, 2)
    spread_wait(OUT, 2)
    spread_send(OUT, 1)
    reduce_add(O, 0)
    reduce_send(O, 1)
    reduce_add(IN, 2)
    spread_send(IN, 2)
    for j in (1, 2, 3):
        arrived((VECTORS_W, j), S.sg_w.at[bit_xor(w, j)])
    S.sg_z[a] = (S.sg_w[0] + S.sg_w[1]) + (S.sg_w[2] + S.sg_w[3])
    for j in (1, 2, 3):
        remote((VECTORS_Z, j), S.sg_z.at[a], S.sg_z.at[a], bit_xor(c, 2 * j), w)
    reduce_add(O, 1)
    reduce_send(O, 2)
    spread_wait(OUT, 1)
    give(OUT)
    spread_wait(IN, 2)
    spread_send(IN, 1)
    for j in (1, 2, 3):
        arrived((HEADS_LINE, j), S.heads_done.at[bit_xor(a, j)])
    remote((HEADS_PAIR,), S.heads_done, heads_out.at[b], bit_xor(c, 1), w)
    finishing.append(local((HEADS_PAIR,), S.heads_done, heads_out.at[b]))
    reduce_add(O, 2)
    spread_send(O, 2)
    for j in (1, 2, 3):
        arrived((VECTORS_Z, j), S.sg_z.at[bit_xor(a, j)])
    S.sg_y[b] = (S.sg_z[0] + S.sg_z[1]) + (S.sg_z[2] + S.sg_z[3])
    remote(VECTORS_Y, S.sg_y.at[b], S.sg_y.at[b], bit_xor(c, 1), w)
    spread_wait(IN, 1)
    give(IN)
    spread_wait(O, 2)
    spread_send(O, 1)
    arrived(VECTORS_Y, S.sg_y.at[1 - b])
    everything = S.sg_y[0] + S.sg_y[1]
    S.sg_rows[...] = everything
    for i in range(4):
        S.smalls[i] = everything[:, HW * i : HW * (i + 1)]
    finishing.append(local(VECTORS_Y, S.smalls, smalls_out))
    finishing.append(local(VECTORS_Z, S.sg_rows, rows_out))
    spread_wait(O, 1)
    give(O)
    arrived((HEADS_PAIR,), heads_out.at[1 - b])
    for name in (OUT, IN, O):
        settle(name)
    for copy in finishing:
        copy.wait()
    for copy in started:
        copy.wait_send()


def finish_kernel(*refs):
    g_o, g_in, g_out, heads, smalls, rows, output, input_grad = refs[:8]
    r_q, r_k, r_v, r_o, r_in, r_out = refs[8:14]
    vectors, inner_bias, loss, r_output, r_input = refs[14:22], refs[22], refs[23], refs[24], refs[25]
    step = pl.program_id(0)
    for source, result in ((g_o, r_o), (g_in, r_in)):
        width = source.shape[-1]
        rest = result.shape[0]
        for i in range(2):
            result[:, width * i : width * (i + 1)] = (
                source[i].reshape(rest, width).astype(F32)
            )
    r_out[...] = g_out[...].reshape(D // 2, D).astype(F32)
    for i, result in ((0, r_k), (1, r_v), (2, r_q)):
        result[...] = jnp.concatenate(
            [heads[0, j, :, HW * i : HW * (i + 1)].astype(F32) for j in range(4)], axis=1
        )
    r_output[0] = output[...]
    r_input[0] = input_grad[...]

    @pl.when(step == 0)
    def once():
        w = lax.axis_index("wsh")
        for i in range(8):
            vectors[i][...] = smalls[w, i, :]
        inner_bias[...] = rows[8 + w, :]
        error = jnp.sum(rows[12:13, :])
        count = jnp.max(rows[13:14, :])
        loss[0] = error / (count * D)


def fused_body(tokens, teacher, doc_lengths, valid_len, *weights):
    (
        q_weight,
        q_bias,
        k_weight,
        v_weight,
        v_bias,
        o_weight,
        o_bias,
        ln1_gain,
        ln1_bias,
        in_weight,
        in_bias,
        out_weight,
        out_bias,
        ln2_gain,
        ln2_bias,
    ) = weights
    hbm = pl.BlockSpec(memory_space=pl.ANY)
    smem = pl.BlockSpec(memory_space=pltpu.SMEM)
    vmem = pl.BlockSpec(memory_space=pltpu.VMEM)
    low = lambda *shape: jax.ShapeDtypeStruct(shape, BF)
    full = lambda *shape: jax.ShapeDtypeStruct(shape, F32)
    output, input_grad, g_o, g_in, g_out, heads, smalls, rows = pl.pallas_call(
        fused_kernel,
        out_shape=(
            low(ROWS, D),
            full(ROWS, D),
            low(2, 2, 2, 48, 384),
            low(2, 2, 2, 48, 1536),
            low(2, 2, 2, 96, D),
            low(2, 4, HW // 2, HEAD_COLS),
            full(GROUP, 16, HW),
            full(16, D),
        ),
        in_specs=[hbm] * 8 + [smem] * 2 + [vmem] * 9,
        out_specs=[hbm] * 8,
        scratch_shapes=scratch_shapes()[0]
        + [
            pltpu.SemaphoreType.DMA((REMOTE_SEMS,)),
            pltpu.SemaphoreType.DMA((REMOTE_SEMS,)),
            pltpu.SemaphoreType.DMA((LOCAL_SEMS,)),
        ],
        compiler_params=pltpu.CompilerParams(
            collective_id=0, has_side_effects=True, vmem_limit_bytes=67043328
        ),
        name="layer",
    )(
        tokens,
        teacher,
        q_weight,
        k_weight,
        v_weight,
        o_weight,
        in_weight,
        out_weight,
        doc_lengths,
        valid_len,
        q_bias,
        v_bias,
        o_bias,
        ln1_gain,
        ln1_bias,
        out_bias,
        ln2_gain,
        ln2_bias,
        in_bias,
    )

    steps = 2
    square_out = pl.BlockSpec((HW // steps, D), lambda i: (i, 0))
    whole = lambda *shape: pl.BlockSpec(shape, lambda i: (0,) * len(shape))
    by_row = pl.BlockSpec((ROWS // steps, D), lambda i: (i, 0))
    results = pl.pallas_call(
        finish_kernel,
        grid=(steps,),
        out_shape=(full(HW, D),) * 4
        + (full(HW, FF), full(D, D))
        + (full(HW),) * 8
        + (full(D), full(1), low(1, ROWS, D), full(1, ROWS, D)),
        in_specs=[
            pl.BlockSpec((2, 1, 2, 48, 384), lambda i: (0, i, 0, 0, 0)),
            pl.BlockSpec((2, 1, 2, 48, 1536), lambda i: (0, i, 0, 0, 0)),
            pl.BlockSpec((1, 2, 2, 96, D), lambda i: (i, 0, 0, 0, 0)),
            pl.BlockSpec((1, 4, HW // 2, HEAD_COLS), lambda i: (i, 0, 0, 0)),
            whole(GROUP, 16, HW),
            whole(16, D),
            by_row,
            by_row,
        ],
        out_specs=[square_out] * 4
        + [
            pl.BlockSpec((HW // steps, FF), lambda i: (i, 0)),
            pl.BlockSpec((D // steps, D), lambda i: (i, 0)),
        ]
        + [whole(HW)] * 8
        + [
            whole(D),
            pl.BlockSpec(memory_space=pltpu.SMEM),
            pl.BlockSpec((1, ROWS // steps, D), lambda i: (0, i, 0)),
            pl.BlockSpec((1, ROWS // steps, D), lambda i: (0, i, 0)),
        ],
        compiler_params=pltpu.CompilerParams(dimension_semantics=("arbitrary",)),
        name="finish",
    )(g_o, g_in, g_out, heads, smalls, rows, output, input_grad)
    r_q, r_k, r_v, r_o, r_in, r_out = results[:6]
    vectors, inner_bias, loss, r_output, r_input = results[6:14], *results[14:]
    return (
        r_output,
        loss.reshape(()),
        r_input,
        r_q,
        vectors[0],
        r_k,
        r_v,
        vectors[1],
        r_o,
        vectors[2],
        vectors[3],
        vectors[4],
        r_in,
        inner_bias,
        r_out,
        vectors[5],
        vectors[6],
        vectors[7],
    )


def solution(mesh):
    in_specs = (
        P("wsh", "ctx", None),
        P("wsh", "ctx", None),
        P("wsh", None),
        P("wsh"),
        P("wsh", None),
        P("wsh"),
        P("wsh", None),
        P("wsh", None),
        P("wsh"),
        P("wsh", None),
        P("wsh"),
        P("wsh"),
        P("wsh"),
        P("wsh", None),
        P("wsh"),
        P("wsh", None),
        P("wsh"),
        P("wsh"),
        P("wsh"),
    )
    out_specs = (
        P("wsh", "ctx", None),
        P(),
        P("wsh", "ctx", None),
        P("wsh", None),
        P("wsh"),
        P("wsh", None),
        P("wsh", None),
        P("wsh"),
        P("wsh", None),
        P("wsh"),
        P("wsh"),
        P("wsh"),
        P("wsh", None),
        P("wsh"),
        P("wsh", None),
        P("wsh"),
        P("wsh"),
        P("wsh"),
    )
    program = fused_body if fused_fits(mesh) else body
    return jax.shard_map(program, mesh=mesh, in_specs=in_specs, out_specs=out_specs, check_vma=False)
```

```python
import math
import types

import jax
import jax.numpy as jnp
from jax import lax
from jax.experimental import pallas as pl
from jax.experimental.pallas import tpu as pltpu
from jax.sharding import PartitionSpec as P

D = 768
H = 12
HD = 64


EPSILON = 1e-06
MASKED = -1e30


def shifted(block, axis, distance):
    devices = range(lax.axis_size(axis))
    route = [((i - distance) % len(devices), i) for i in devices]
    return lax.ppermute(block, axis, route)


def layer_norm(value, gain, shift):
    mean = jnp.mean(value, axis=-1, keepdims=True)
    centered = value - mean
    spread = jnp.mean(centered * centered, axis=-1, keepdims=True)
    return centered * lax.rsqrt(spread + EPSILON) * gain + shift


def activate(value):
    return jax.nn.gelu(value, approximate=True)


def matmul(left, right):
    return jnp.dot(left, right, preferred_element_type=jnp.float32)


def left_product(left, right):
    return lax.dot_general(
        left, right, (((0,), (0,)), ((), ())), preferred_element_type=jnp.float32
    )


def right_product(left, right):
    return lax.dot_general(
        left, right, (((1,), (1,)), ((), ())), preferred_element_type=jnp.float32
    )


def document_of(positions, starts):
    return jnp.sum((starts[None, :] <= positions[:, None]).astype(jnp.int32), axis=1) - 1


def permitted(own_doc, own_live, other_doc, other_live):
    return (own_doc[:, None] == other_doc[None, :]) & (own_live[:, None] == other_live[None, :])


def block_weights(queries, key_block, allowed, score_scale):
    scores = (
        jnp.einsum("qhd,khd->hqk", queries, key_block, preferred_element_type=jnp.float32)
        * score_scale
    )
    return jnp.exp(jnp.where(allowed[None], scores, MASKED))


def forward_visit(sums_state, queries, key_block, value_block, allowed, score_scale):
    row_total, weighted = sums_state
    weights = block_weights(queries, key_block, allowed, score_scale)
    row_total = row_total + jnp.sum(weights, axis=-1)
    weighted = weighted + jnp.einsum(
        "hqk,khd->qhd",
        weights.astype(jnp.bfloat16),
        value_block,
        preferred_element_type=jnp.float32,
    )
    return (row_total, weighted)


def backward_visit(
    queries, key_block, value_block, allowed, score_scale, weighted_grad, total_grad
):
    weights = block_weights(queries, key_block, allowed, score_scale)
    value_part = jnp.einsum(
        "hqk,qhd->khd",
        weights.astype(jnp.bfloat16),
        weighted_grad,
        preferred_element_type=jnp.float32,
    )
    weight_grad = (
        jnp.einsum("qhd,khd->hqk", weighted_grad, value_block, preferred_element_type=jnp.float32)
        + total_grad[:, :, None]
    )
    score_grad = (weights * weight_grad).astype(jnp.bfloat16)
    query_part = (
        jnp.einsum("hqk,khd->qhd", score_grad, key_block, preferred_element_type=jnp.float32)
        * score_scale
    )
    key_part = (
        jnp.einsum("hqk,qhd->khd", score_grad, queries, preferred_element_type=jnp.float32)
        * score_scale
    )
    return (query_part, key_part, value_part)


def body(
    tokens,
    teacher,
    doc_lengths,
    valid_len,
    q_weight,
    q_bias,
    k_weight,
    v_weight,
    v_bias,
    o_weight,
    o_bias,
    ln1_gain,
    ln1_bias,
    in_weight,
    in_bias,
    out_weight,
    out_bias,
    ln2_gain,
    ln2_bias,
):
    gathered = (
        lax.all_gather(q_weight, "wsh", axis=0, tiled=True),
        lax.all_gather(q_bias, "wsh", axis=0, tiled=True),
        lax.all_gather(k_weight, "wsh", axis=0, tiled=True),
        lax.all_gather(v_weight, "wsh", axis=0, tiled=True),
        lax.all_gather(v_bias, "wsh", axis=0, tiled=True),
        lax.all_gather(o_weight, "wsh", axis=0, tiled=True),
        lax.all_gather(o_bias, "wsh", axis=0, tiled=True),
        lax.all_gather(ln1_gain, "wsh", axis=0, tiled=True),
        lax.all_gather(ln1_bias, "wsh", axis=0, tiled=True),
        lax.all_gather(in_weight, "wsh", axis=0, tiled=True),
        lax.all_gather(in_bias, "wsh", axis=0, tiled=True),
        lax.all_gather(out_weight, "wsh", axis=0, tiled=True),
        lax.all_gather(out_bias, "wsh", axis=0, tiled=True),
        lax.all_gather(ln2_gain, "wsh", axis=0, tiled=True),
        lax.all_gather(ln2_bias, "wsh", axis=0, tiled=True),
    )
    (
        w_query,
        b_query,
        w_key,
        w_value,
        b_value,
        w_out,
        b_out,
        gain_one,
        shift_one,
        w_inner,
        b_inner,
        w_back,
        b_back,
        gain_two,
        shift_two,
    ) = gathered
    gain_first = gain_one.astype(jnp.float32)
    shift_first = shift_one.astype(jnp.float32)
    gain_second = gain_two.astype(jnp.float32)
    shift_second = shift_two.astype(jnp.float32)
    inputs = tokens[0]
    row_count = inputs.shape[0]
    cycle_size = lax.axis_size("ctx")
    stream_count = lax.axis_size("wsh")
    position = lax.axis_index("ctx")
    score_scale = 1.0 / math.sqrt(HD)
    offsets = jnp.arange(row_count, dtype=jnp.int32)
    lengths = doc_lengths[0]
    starts = jnp.cumsum(lengths) - lengths
    limit = valid_len[0]

    def key_mask(block_index):
        where_rows = jnp.mod(block_index, cycle_size) * row_count + offsets
        return (document_of(where_rows, starts), where_rows < limit)

    own_doc, own_live = key_mask(position)
    input_float = inputs.astype(jnp.float32)
    queries = (
        (matmul(inputs, w_query) + b_query.astype(jnp.float32))
        .astype(jnp.bfloat16)
        .reshape(row_count, H, HD)
    )
    key_rows = matmul(inputs, w_key).astype(jnp.bfloat16).reshape(row_count, H, HD)
    value_rows = (
        (matmul(inputs, w_value) + b_value.astype(jnp.float32))
        .astype(jnp.bfloat16)
        .reshape(row_count, H, HD)
    )

    def visit_forward(sums_state, key_block, value_block, block_index):
        other_doc, other_live = key_mask(block_index)
        allowed = permitted(own_doc, own_live, other_doc, other_live)
        return forward_visit(sums_state, queries, key_block, value_block, allowed, score_scale)

    empty_state = (
        jnp.zeros((H, row_count), jnp.float32),
        jnp.zeros((row_count, H, HD), jnp.float32),
    )
    first_state = visit_forward(empty_state, key_rows, value_rows, position)

    def advance(step_index, loop_state):
        key_block, value_block, running = loop_state
        key_block, value_block = shifted((key_block, value_block), "ctx", 1)
        running = visit_forward(running, key_block, value_block, position - step_index)
        return (key_block, value_block, running)

    row_total, weighted = lax.fori_loop(
        1, cycle_size, advance, (key_rows, value_rows, first_state)
    )[2]
    normed = weighted / jnp.transpose(row_total)[:, :, None]
    context = normed.astype(jnp.bfloat16).reshape(row_count, D)
    attn = matmul(context, w_out) + b_out.astype(jnp.float32)
    first_sum = input_float + attn
    settled = layer_norm(first_sum, gain_first, shift_first)
    settled_low = settled.astype(jnp.bfloat16)
    inner = matmul(settled_low, w_inner) + b_inner.astype(jnp.float32)
    activated = activate(inner).astype(jnp.bfloat16)
    branch = matmul(activated, w_back) + b_back.astype(jnp.float32)
    second_sum = settled + branch
    result = layer_norm(second_sum, gain_second, shift_second)
    target = teacher[0].astype(jnp.float32)
    diff = jnp.where(own_live[:, None], result - target, 0.0)
    error_sum, live_count = lax.psum(
        (jnp.sum(diff * diff), jnp.sum(own_live.astype(jnp.float32))), ("ctx", "wsh")
    )
    loss = error_sum / (live_count * D)
    upstream = diff * (row_count * cycle_size * stream_count / live_count)
    unused_second, second_back = jax.vjp(layer_norm, second_sum, gain_second, shift_second)
    d_second, gain_two_grad, shift_two_grad = second_back(upstream)
    branch_grad = d_second.astype(jnp.bfloat16)
    back_weight_grad = left_product(activated, branch_grad)
    back_bias_grad = jnp.sum(branch_grad, axis=0, dtype=jnp.float32)
    d_activated = right_product(branch_grad, w_back)
    unused_inner, gelu_back = jax.vjp(activate, inner)
    inner_grad = gelu_back(d_activated)[0].astype(jnp.bfloat16)
    inner_weight_grad = left_product(settled_low, inner_grad)
    inner_bias_grad = jnp.sum(inner_grad, axis=0, dtype=jnp.float32)
    d_settled = d_second + right_product(inner_grad, w_inner)
    unused_first, first_back = jax.vjp(layer_norm, first_sum, gain_first, shift_first)
    d_first, gain_one_grad, shift_one_grad = first_back(d_settled)
    attn_grad = d_first.astype(jnp.bfloat16)
    out_weight_grad_local = left_product(context, attn_grad)
    out_bias_grad_local = jnp.sum(attn_grad, axis=0, dtype=jnp.float32)
    context_low = lax.optimization_barrier(right_product(attn_grad, w_out).astype(jnp.bfloat16))
    context_grad = context_low.astype(jnp.float32).reshape(row_count, H, HD)
    weighted_grad = (context_grad / jnp.transpose(row_total)[:, :, None]).astype(jnp.bfloat16)
    total_grad = -jnp.transpose(jnp.sum(context_grad * weighted, axis=-1)) / (row_total * row_total)

    def visit_backward(key_block, value_block, block_index):
        other_doc, other_live = key_mask(block_index)
        allowed = permitted(own_doc, own_live, other_doc, other_live)
        return backward_visit(
            queries, key_block, value_block, allowed, score_scale, weighted_grad, total_grad
        )

    query_sum, key_sum, value_sum = visit_backward(key_rows, value_rows, position)

    def advance_back(step_index, loop_state):
        key_block, value_block, query_acc, key_acc, value_acc = loop_state
        key_block, value_block = shifted((key_block, value_block), "ctx", 1)
        key_acc, value_acc = (
            shifted(key_acc.astype(jnp.bfloat16), "ctx", 1).astype(key_acc.dtype),
            shifted(value_acc.astype(jnp.bfloat16), "ctx", 1).astype(value_acc.dtype),
        )
        query_part, key_part, value_part = visit_backward(
            key_block, value_block, position - step_index
        )
        return (
            key_block,
            value_block,
            query_acc + query_part,
            key_acc + key_part,
            value_acc + value_part,
        )

    loop_state = lax.fori_loop(
        1, cycle_size, advance_back, (key_rows, value_rows, query_sum, key_sum, value_sum)
    )
    query_total = loop_state[2]
    key_total, value_total = (
        shifted(loop_state[3].astype(jnp.bfloat16), "ctx", 1).astype(jnp.float32),
        shifted(loop_state[4].astype(jnp.bfloat16), "ctx", 1).astype(jnp.float32),
    )
    query_grad = query_total.astype(jnp.bfloat16).reshape(row_count, D)
    key_grad = key_total.astype(jnp.bfloat16).reshape(row_count, D)
    value_grad = value_total.astype(jnp.bfloat16).reshape(row_count, D)
    query_weight_grad = left_product(inputs, query_grad)
    query_bias_grad = jnp.sum(query_grad, axis=0, dtype=jnp.float32)
    key_weight_grad = left_product(inputs, key_grad)
    value_weight_grad = left_product(inputs, value_grad)
    value_bias_grad = jnp.sum(value_grad, axis=0, dtype=jnp.float32)
    input_grad = (
        d_first
        + right_product(query_grad, w_query)
        + right_product(key_grad, w_key)
        + right_product(value_grad, w_value)
    )
    reduced = (
        lax.psum_scatter(
            query_weight_grad.astype(jnp.bfloat16), "wsh", scatter_dimension=0, tiled=True
        ).astype(jnp.float32),
        lax.psum_scatter(
            query_bias_grad.astype(jnp.bfloat16), "wsh", scatter_dimension=0, tiled=True
        ).astype(jnp.float32),
        lax.psum_scatter(
            key_weight_grad.astype(jnp.bfloat16), "wsh", scatter_dimension=0, tiled=True
        ).astype(jnp.float32),
        lax.psum_scatter(
            value_weight_grad.astype(jnp.bfloat16), "wsh", scatter_dimension=0, tiled=True
        ).astype(jnp.float32),
        lax.psum_scatter(
            value_bias_grad.astype(jnp.bfloat16), "wsh", scatter_dimension=0, tiled=True
        ).astype(jnp.float32),
        lax.psum_scatter(
            out_weight_grad_local.astype(jnp.bfloat16), "wsh", scatter_dimension=0, tiled=True
        ).astype(jnp.float32),
        lax.psum_scatter(
            out_bias_grad_local.astype(jnp.bfloat16), "wsh", scatter_dimension=0, tiled=True
        ).astype(jnp.float32),
        lax.psum_scatter(
            gain_one_grad.astype(jnp.bfloat16), "wsh", scatter_dimension=0, tiled=True
        ).astype(jnp.float32),
        lax.psum_scatter(
            shift_one_grad.astype(jnp.bfloat16), "wsh", scatter_dimension=0, tiled=True
        ).astype(jnp.float32),
        lax.psum_scatter(
            inner_weight_grad.astype(jnp.bfloat16), "wsh", scatter_dimension=0, tiled=True
        ).astype(jnp.float32),
        lax.psum_scatter(
            inner_bias_grad.astype(jnp.bfloat16), "wsh", scatter_dimension=0, tiled=True
        ).astype(jnp.float32),
        lax.psum_scatter(
            back_weight_grad.astype(jnp.bfloat16), "wsh", scatter_dimension=0, tiled=True
        ).astype(jnp.float32),
        lax.psum_scatter(
            back_bias_grad.astype(jnp.bfloat16), "wsh", scatter_dimension=0, tiled=True
        ).astype(jnp.float32),
        lax.psum_scatter(
            gain_two_grad.astype(jnp.bfloat16), "wsh", scatter_dimension=0, tiled=True
        ).astype(jnp.float32),
        lax.psum_scatter(
            shift_two_grad.astype(jnp.bfloat16), "wsh", scatter_dimension=0, tiled=True
        ).astype(jnp.float32),
    )
    summed = lax.psum(
        (
            reduced[0],
            reduced[1],
            reduced[2],
            reduced[3],
            reduced[4],
            reduced[5],
            reduced[6],
            reduced[7],
            reduced[8],
            reduced[9],
            reduced[10],
            reduced[11],
            reduced[12],
            reduced[13],
            reduced[14],
        ),
        "ctx",
    )
    return (
        result.astype(jnp.bfloat16)[None],
        loss,
        input_grad[None],
        summed[0],
        summed[1],
        summed[2],
        summed[3],
        summed[4],
        summed[5],
        summed[6],
        summed[7],
        summed[8],
        summed[9],
        summed[10],
        summed[11],
        summed[12],
        summed[13],
        summed[14],
    )


BF = jnp.bfloat16
F32 = jnp.float32
FF = 3072
ROWS = 128
HEADS = 3
HW = HEADS * HD
GROUP = 4
CTX = 8
MESH = pl.DeviceIdType.MESH

Q, K, V, O, IN, OUT, PART_Q, PART_K, PART_V = range(9)
SLICE = 256
WEIGHT_SHAPES = [(192, 768)] * 4 + [(192, 3072), (768, 768)] + [(192, SLICE)] * 3
SECOND_WAY = {O: 1, IN: 1, OUT: 2, PART_Q: 1, PART_K: 1, PART_V: 1}
LOT_O, LOT_IN, LOT_OUT = (0,), (1, 2), (3, 4, 5, 6)
LOTS = [(96, 384)] + [(4, 48, 384)] * 2 + [(48, D)] * 4
PIECES = {IN: (1, 4), OUT: (4, 1)}
HEAD_COLS = 640

(
    SMALL,
    WEIGHT_X,
    WEIGHT_SECOND,
    WEIGHT_CORE,
    WEIGHT_CORE_X,
    WEIGHT_CORE_SECOND,
    X_LINE,
    X_EDGE,
    KEY_VALUE,
    CONTEXT,
    CONTEXT_GRAD,
    KEY_VALUE_GRAD,
    INPUT_PARTS,
    SETTLED_ALL,
    CONTEXT_ALL,
    ATTN_GRAD_ALL,
    BRANCH_GRAD_ALL,
    REDUCE,
    SPREAD,
    GIVE,
    OWN,
    GROUP_X,
    HEADS_CORE,
    HEADS_X,
    HEADS_Y,
    HEADS_LINE,
    HEADS_PAIR,
    VECTORS_W,
    VECTORS_Z,
    VECTORS_Y,
    TOKENS,
    TEACHER,
    OUTPUT,
    INPUT_GRAD,
    LOAD,
) = range(35)


def fused_fits(mesh):
    return mesh.shape["ctx"] == CTX and mesh.shape["wsh"] == GROUP


def tn(left, right):
    return lax.dot_general(
        left, right, (((0,), (0,)), ((), ())), preferred_element_type=jnp.float32
    )


def norm_parts(value):
    mean = jnp.mean(value, axis=-1, keepdims=True)
    centered = value - mean
    spread = jnp.mean(centered * centered, axis=-1, keepdims=True)
    inverse = lax.rsqrt(spread + EPSILON)
    return centered * inverse, inverse


def norm_back(upstream_gained, normal, inverse):
    return (
        upstream_gained
        - jnp.mean(upstream_gained, axis=-1, keepdims=True)
        - normal * jnp.mean(upstream_gained * normal, axis=-1, keepdims=True)
    ) * inverse


GELU_C = math.sqrt(2.0 / math.pi)


class Numbers:
    def __init__(self):
        self.count = 0
        self.table = {}

    def take(self, key, size=1):
        if key not in self.table:
            self.table[key] = self.count
            self.count += size
        return self.table[key]


def scratch_table():
    s = types.SimpleNamespace()
    s.full = {k: pltpu.VMEM((GROUP, *WEIGHT_SHAPES[k]), BF) for k in SECOND_WAY}
    s.turned = pltpu.VMEM((SLICE, D), BF)
    s.head_weight = pltpu.VMEM((3 * HW, D), BF)
    s.tall_bias = pltpu.VMEM((SLICE, ROWS), F32)
    s.head_bias = pltpu.VMEM((3 * HW, ROWS), F32)
    s.x = pltpu.VMEM((ROWS, D), BF)
    s.xt = pltpu.VMEM((CTX, D, ROWS), BF)
    s.teacher = pltpu.VMEM((ROWS, D), BF)
    s.small = pltpu.VMEM((GROUP, 16, D), BF)
    s.vectors = pltpu.VMEM((16, D), F32)
    s.kv = pltpu.VMEM((CTX, 2 * HW, ROWS), BF)
    s.q = pltpu.VMEM((4, HW, ROWS), BF)
    s.weights = pltpu.VMEM((CTX, HEADS, ROWS, 4 * ROWS), F32)
    s.mix = pltpu.VMEM((HEADS, HD, 4 * ROWS), F32)
    s.total = pltpu.VMEM((HEADS, 8, 4 * ROWS), F32)
    s.ctx_send = pltpu.VMEM((4, HW, ROWS), BF)
    s.ctx = pltpu.VMEM((4, HW, ROWS), BF)
    s.inner = pltpu.VMEM((4, ROWS, D), F32)
    s.act = pltpu.VMEM((4, ROWS, D), BF)
    s.first = pltpu.VMEM((ROWS, D), F32)
    s.keep = pltpu.VMEM((ROWS, D), F32)
    s.set_low = pltpu.VMEM((ROWS, D), BF)
    s.ag_half = pltpu.VMEM((2, ROWS, 384), BF)
    s.bg = pltpu.VMEM((ROWS, D), BF)
    s.set_all = pltpu.VMEM((GROUP, ROWS, D), BF)
    s.ctx_all = pltpu.VMEM((GROUP, 2, HW, ROWS), BF)
    s.ag_all = pltpu.VMEM((GROUP, ROWS, 384), BF)
    s.inner_all = pltpu.VMEM((GROUP * ROWS, D), F32)
    s.act_all = pltpu.VMEM((GROUP * ROWS, D), BF)
    s.bg_all = pltpu.VMEM((GROUP, ROWS, D), BF)
    s.cg_send = pltpu.VMEM((4, HW, ROWS), BF)
    s.cg = pltpu.VMEM((4, HW, ROWS), BF)
    s.wg = pltpu.VMEM((HEADS, HD, 4 * ROWS), BF)
    s.dkv = pltpu.VMEM((2, 4, 2 * HW, ROWS), BF)
    s.dkv_pair = pltpu.VMEM((4, 2 * HW, ROWS), BF)
    s.grads = pltpu.VMEM((HEAD_COLS, 4 * ROWS), BF)
    s.dx_send = pltpu.VMEM((4, ROWS, D), BF)
    s.dx = pltpu.VMEM((4, ROWS, D), BF)
    s.column = pltpu.VMEM((D, ROWS), F32)
    s.heads = pltpu.VMEM((2, 2, HW, HEAD_COLS), BF)
    s.heads_core = pltpu.VMEM((2, HW, HEAD_COLS), BF)
    s.heads_sum = pltpu.VMEM((2, HW, HEAD_COLS), BF)
    s.heads_x = pltpu.VMEM((HW, HEAD_COLS), BF)
    s.heads_row = pltpu.VMEM((2, HW // 2, HEAD_COLS), BF)
    s.heads_y = pltpu.VMEM((HW // 2, HEAD_COLS), BF)
    s.heads_done = pltpu.VMEM((4, HW // 2, HEAD_COLS), BF)
    s.part = [pltpu.VMEM((2, 2, *shape), BF) for shape in LOTS]
    s.got = [
        [pltpu.VMEM((2, *shape), BF), pltpu.VMEM((2, *shape), BF), pltpu.VMEM(shape, BF)]
        for shape in LOTS
    ]
    s.sum = [[pltpu.VMEM((2, *shape), BF), pltpu.VMEM((2, *shape), BF)] for shape in LOTS]
    s.own = {lot: pltpu.VMEM(LOTS[lot], BF) for lot in LOT_IN}
    s.done = [pltpu.VMEM((2, 2, *shape), BF) for shape in LOTS]
    s.smalls = pltpu.VMEM((GROUP, 16, HW), F32)
    s.sg = pltpu.VMEM((16, D), F32)
    s.sg_rows = pltpu.VMEM((16, D), F32)
    s.sg_w = pltpu.VMEM((GROUP, 16, D), F32)
    s.sg_z = pltpu.VMEM((4, 16, D), F32)
    s.sg_y = pltpu.VMEM((2, 16, D), F32)
    s.out_low = pltpu.VMEM((ROWS, D), BF)
    return vars(s)


LOCAL_SEMS = 32
REMOTE_SEMS = 240


def is_memory(item):
    return not isinstance(item, (dict, list))


def scratch_shapes():
    return jax.tree.flatten(scratch_table(), is_leaf=is_memory)


def fused_kernel(*refs):
    (tokens, teacher), shards = refs[:2], refs[2:8]
    lengths, valid = refs[8:10]
    biases = refs[10:19]
    output, input_grad_out = refs[19:21]
    grad_o, *grad_in, grad_out = refs[21:25]
    heads_out, smalls_out, rows_out = refs[25:28]
    flat, shape = scratch_shapes()
    S = types.SimpleNamespace(**jax.tree.unflatten(shape, refs[28 : 28 + len(flat)]))
    send_sems, recv_sems, local_sems = refs[28 + len(flat) :]

    c = lax.axis_index("ctx")
    w = lax.axis_index("wsh")
    a, b = c // 2, c % 2
    x, core = w // 2, w % 2

    numbers = Numbers()
    locals_ = Numbers()
    started = []

    def bit_xor(value, j):
        out = value
        bit = 1
        while bit <= j:
            if j & bit:
                has = (value // bit) % 2
                out = out + bit * (1 - 2 * has)
            bit *= 2
        return out

    at_end = a * (3 - a) == 0
    roles, sent_by_role = [None], []

    def only(end):
        def run(action):
            roles.append(end)
            pl.when(at_end if end else jnp.logical_not(at_end))(action)
            roles.pop()

        return run

    def remote(key, src, dst, c_bits, w_bits, offset=0, size=1, to=None, like=None):
        number = numbers.take(key, size) + offset
        c_to, w_to = bit_xor(c, c_bits), bit_xor(w, w_bits) if to is None else to
        copy = pltpu.make_async_remote_copy(
            src_ref=src,
            dst_ref=dst,
            send_sem=send_sems.at[number],
            recv_sem=recv_sems.at[number],
            device_id={"ctx": c_to, "wsh": w_to},
            device_id_type=MESH,
        )
        copy.start()
        if roles[-1] is None:
            started.append(copy)
        else:
            sent_by_role.append((roles[-1], like, number))

    def arrived(key, landing, offset=0):
        number = numbers.take(key) + offset
        pltpu.make_async_copy(landing, landing, recv_sems.at[number]).wait()

    def local(key, src, dst):
        copy = pltpu.make_async_copy(src, dst, local_sems.at[locals_.take(key)])
        copy.start()
        return copy

    peers = [(c, bit_xor(w, j)) for j in (1, 2, 3)]
    peers += [(bit_xor(c, j), w) for j in range(1, CTX)]
    peers += [(bit_xor(c, 1), bit_xor(w, 1))]

    def bit(value, mask):
        return (value // mask) % 2

    first_col = pl.multiple_of((3 * a) // 2 * 128, 128)
    first_row = pl.multiple_of(a % 2 * 64, 64)

    def shard(name):
        if name < PART_Q:
            return shards[name]
        return shards[name - PART_Q].at[:, pl.ds(first_col, SLICE)]

    loads = {TOKENS: local(TOKENS, tokens.at[0], S.x)}
    for name in (PART_K, PART_V, PART_Q, O, IN, OUT):
        loads[name] = local((LOAD, name), shard(name), S.full[name].at[w])
    loads[TEACHER] = local(TEACHER, teacher.at[0], S.teacher)

    barrier = pltpu.get_barrier_semaphore()
    for c_to, w_to in peers:
        pl.semaphore_signal(
            barrier, inc=1, device_id={"ctx": c_to, "wsh": w_to}, device_id_type=MESH
        )
    loads[TOKENS].wait()
    x_low = S.x[...]
    S.xt[c] = x_low.T
    bias_rows = [row[...].astype(F32).reshape(1, HW) for row in biases[:8]]
    tall = jnp.concatenate(bias_rows, axis=0)
    valid_high = (valid[0] // 64).astype(F32)
    valid_low = (valid[0] % 64).astype(F32)
    wide_rows = [biases[8][...].astype(F32).reshape(1, D)]
    wide_rows += [jnp.full((1, D), 64.0, F32) * valid_high, jnp.full((1, D), 1.0, F32) * valid_low]
    wide_rows += [jnp.zeros((5, D), F32)]
    S.small[w, :, 0:HW] = jnp.concatenate(
        [tall, jnp.concatenate(wide_rows, axis=0)[:, 0:HW]], axis=0
    ).astype(BF)
    S.small[w, 8:16, HW:D] = jnp.concatenate(wide_rows, axis=0)[:, HW:D].astype(BF)

    pl.semaphore_wait(barrier, len(peers))

    def mine(name):
        return bit(c, SECOND_WAY[name])

    def pieces(name):
        tall, across = PIECES.get(name, (1, 1))
        return range(tall * across)

    def piece(name, which, number):
        rows, cols = WEIGHT_SHAPES[name]
        tall, across = PIECES.get(name, (1, 1))
        high, broad = rows // 2 // tall, cols // across
        row = which * (rows // 2) + number // across * high
        return pl.ds(pl.multiple_of(row, 16), high), slice(
            number % across * broad, (number % across + 1) * broad
        )

    def send_core(name):
        remote((WEIGHT_CORE, name), shard(name), S.full[name].at[w], 0, 1)

    def send_x(name):
        for i in pieces(name):
            rows, cols = piece(name, mine(name), i)
            if name < PART_Q:
                source = shards[name].at[rows, cols]
            else:
                source = shards[name - PART_Q].at[rows, pl.ds(first_col, SLICE)]
            remote((WEIGHT_X, name, i), source, S.full[name].at[w, rows, cols], 0, 2)

    for name in (PART_K, PART_V, PART_Q):
        send_x(name)
        send_core(name)
    for j in (1, 2, 3):
        remote((SMALL, j), S.small.at[w], S.small.at[w], 0, j)
    remote((X_LINE, 1), S.xt.at[c], S.xt.at[c], 2, 0)

    @only(False)
    def x_to_middle():
        remote((X_LINE, 3), S.xt.at[c], S.xt.at[c], 6, 0, like=lambda: S.xt.at[0])

    for name in (O, IN, OUT):
        send_x(name)
        send_core(name)

    def pump_x(name, number=0):
        slot = S.full[name].at[bit_xor(w, 2), *piece(name, mine(name), number)]
        arrived((WEIGHT_X, name, number), slot)
        remote((WEIGHT_SECOND, name, number), slot, slot, SECOND_WAY[name], 0)
        remote((WEIGHT_CORE_X, name, number), slot, slot, 0, 1)

    def pump_second(name, number=0):
        slot = S.full[name].at[bit_xor(w, 2), *piece(name, 1 - mine(name), number)]
        arrived((WEIGHT_SECOND, name, number), slot)
        remote((WEIGHT_CORE_SECOND, name, number), slot, slot, 0, 1)

    def weight_ready(name, numbers_=(0,), first=True):
        full = S.full[name]
        if first:
            loads[name].wait()
            arrived((WEIGHT_CORE, name), full.at[bit_xor(w, 1)])
        for i in numbers_:
            near = full.at[bit_xor(w, 3), *piece(name, mine(name), i)]
            far = full.at[bit_xor(w, 3), *piece(name, 1 - mine(name), i)]
            arrived((WEIGHT_CORE_X, name, i), near)
            arrived((WEIGHT_CORE_SECOND, name, i), far)

    def square(name):
        return S.full[name][...].reshape(D, D)

    starts, running = [], 0
    for i in range(lengths.shape[1]):
        starts.append(running)
        running = running + lengths[0, i]
    limit = valid[0]

    def code_of(position):
        code = jnp.zeros(position.shape, jnp.int32)
        for start in starts:
            code = code + (start <= position).astype(jnp.int32)
        return 2 * code + (position < limit).astype(jnp.int32)

    lane = lax.broadcasted_iota(jnp.int32, (1, 4 * ROWS), 1)
    query_code = code_of((2 * (lane // ROWS) + b) * ROWS + lane % ROWS)

    def key_code(block):
        return code_of(block * ROWS + lax.broadcasted_iota(jnp.int32, (ROWS, 1), 0))

    own_live = c * ROWS + lax.broadcasted_iota(jnp.int32, (ROWS, 1), 0) < limit

    def block_on(j, pair):
        return 2 * bit_xor(a, j) + pair

    def pass_x(key, j, onward, bits):
        block = S.xt.at[block_on(j, b)]
        arrived((key, j), block)
        remote(onward, block, block, bits, 0, like=lambda: S.xt.at[0])

    pump_x(PART_K)
    pump_x(PART_V)
    pump_x(PART_Q)
    for j in (1, 2, 3):
        arrived((SMALL, j), S.small.at[bit_xor(w, j)])
    S.vectors[0:8, :] = jnp.concatenate(
        [S.small[i, 0:8, 0:HW].astype(F32) for i in range(GROUP)], axis=1
    )
    small = [S.small[i, 8:16, :].astype(F32) for i in range(GROUP)]
    S.vectors[8:16, :] = jnp.concatenate(
        [part[0:1] for part in small]
        + [sum(part[1:2] + part[2:3] for part in small), jnp.zeros((3, D), F32)],
        axis=0,
    )

    def vector(row):
        return S.vectors[row : row + 1, :]

    arrived((X_LINE, 1), S.xt.at[block_on(1, b)])

    @only(False)
    def pass_near_end():
        block = S.xt.at[block_on(1, b)]
        remote((X_LINE, 2), block, block, 6, 0, like=lambda: S.xt.at[0])
        pass_x(X_LINE, 3, (X_EDGE, 2), 2)

    pump_second(PART_K)
    pump_second(PART_V)
    pump_second(PART_Q)
    for i, (name, bias) in enumerate(((PART_K, None), (PART_V, 1), (PART_Q, 0))):
        rows = slice(HW * i, HW * (i + 1))
        weight_ready(name)
        S.turned[...] = S.full[name][...].reshape(D, SLICE).T
        S.head_weight[rows, :] = S.turned[pl.ds(first_row, HW), :]
        if bias is None:
            S.head_bias[rows, :] = jnp.zeros((HW, ROWS), F32)
        else:
            row = S.vectors[bias : bias + 1, pl.ds(first_col, SLICE)]
            S.tall_bias[...] = jnp.broadcast_to(row, (ROWS, SLICE)).T
            S.head_bias[rows, :] = S.tall_bias[pl.ds(first_row, HW), :]

    def project(j):
        block = block_on(j, b)
        out = matmul(S.head_weight[...], S.xt[block]) + S.head_bias[...]
        S.kv[block] = out[0 : 2 * HW].astype(BF)
        S.q[block // 2] = out[2 * HW :].astype(BF)
        remote((KEY_VALUE, j), S.kv.at[block], S.kv.at[block], 1, 0)

    project(0)
    project(1)
    pump_x(O)
    pump_x(IN, 0)

    @only(False)
    def pass_far_end():
        pass_x(X_LINE, 2, (X_EDGE, 3), 2)

    @only(True)
    def from_middle():
        arrived((X_EDGE, 2), S.xt.at[block_on(2, b)])

    project(2)
    pump_x(IN, 1)

    @only(True)
    def from_far_end():
        arrived((X_EDGE, 3), S.xt.at[block_on(3, b)])

    project(3)
    pump_x(IN, 2)

    def to_group(key, source_of, everywhere):
        for j in (1, 2, 3):
            to = bit_xor(w, j)
            remote((*key, j), source_of(to), everywhere.at[w], 0, j)

    def from_group(key, everywhere):
        for j in (1, 2, 3):
            arrived((*key, j), everywhere.at[bit_xor(w, j)])

    def to_near(key, source, everywhere):
        for j in (1, 2):
            remote((key, j), source, everywhere.at[w], 0, j)

    def pass_to_core(key, everywhere):
        slot = everywhere.at[bit_xor(w, 2)]
        arrived((key, 2), slot)
        remote((key, 3), slot, slot, 0, 1)

    def from_near(key, everywhere):
        for j in (1, 3):
            arrived((key, j), everywhere.at[bit_xor(w, j)])

    score_scale = 1.0 / math.sqrt(HD)

    def wide(ref, h):
        return jnp.concatenate([ref[i, HD * h : HD * (h + 1), :] for i in range(4)], axis=1)

    S.mix[...] = jnp.zeros(S.mix.shape, F32)
    S.total[...] = jnp.zeros(S.total.shape, F32)

    def attend_block(block):
        allowed = key_code(block) == query_code
        for h in range(HEADS):
            scores = tn(S.kv[block, HD * h : HD * (h + 1), :], wide(S.q, h)) * score_scale
            weights = jnp.exp(jnp.where(allowed, scores, MASKED))
            S.weights[block, h] = weights
            S.total[h, 0:1, :] += jnp.sum(weights, axis=0, keepdims=True)
            value_t = S.kv[block, HW + HD * h : HW + HD * (h + 1), :]
            S.mix[h] += matmul(value_t, weights.astype(BF))

    @pl.loop(0, 4)
    def attend_line(i):
        attend_block(2 * i + b)

    pump_second(O)
    pump_x(IN, 3)
    pump_second(IN, 0)
    pump_x(OUT, 0)
    for j in range(4):
        arrived((KEY_VALUE, j), S.kv.at[block_on(j, 1 - b)])
        attend_block(block_on(j, 1 - b))
        if j == 0:
            pump_second(IN, 1)
        if j == 2:
            pump_x(OUT, 1)

    for h in range(HEADS):
        context_t = (S.mix[h] / S.total[h, 0:1, :]).astype(BF)
        for i in range(4):
            S.ctx_send[i, HD * h : HD * (h + 1), :] = context_t[:, ROWS * i : ROWS * (i + 1)]
    for j in (1, 2, 3):
        to = bit_xor(a, j)
        remote((CONTEXT, j), S.ctx_send.at[to], S.ctx.at[a], 2 * j, 0)
    S.ctx[a] = S.ctx_send[a]
    weight_ready(O)
    pump_second(IN, 2)
    pump_x(OUT, 2)
    pump_second(OUT, 0)
    for j in (1, 2, 3):
        arrived((CONTEXT, j), S.ctx.at[bit_xor(a, j)])

    to_group((CONTEXT_ALL,), lambda to: S.ctx.at[pl.ds(2 * (to // 2), 2)], S.ctx_all)
    S.ctx_all[w] = S.ctx[pl.ds(2 * x, 2)]
    attn = tn(S.ctx[...].reshape(D, ROWS), square(O)) + vector(2)
    first_sum = x_low.astype(F32) + attn
    normal_one, inverse_one = norm_parts(first_sum)
    settled = normal_one * vector(3) + vector(4)
    settled_low = settled.astype(BF)
    S.first[...] = normal_one
    S.keep[...] = settled
    S.set_low[...] = settled_low
    to_near(SETTLED_ALL, S.set_low, S.set_all)
    S.set_all[w] = settled_low
    pump_second(IN, 3)
    pump_x(OUT, 3)
    pump_second(OUT, 1)

    def gelu(inner):
        return 0.5 * inner * (1.0 + jnp.tanh(GELU_C * (inner + 0.044715 * inner * inner * inner)))

    def gelu_slope(inner):
        squared = inner * inner
        bend = jnp.tanh(GELU_C * (inner + 0.044715 * squared * inner))
        return 0.5 * (1.0 + bend) + 0.5 * inner * (1.0 - bend * bend) * (
            GELU_C * (1.0 + 3 * 0.044715 * squared)
        )

    for t in range(4):
        weight_ready(IN, (t,), t == 0)
        w_part = S.full[IN][:, :, D * t : D * (t + 1)].reshape(D, D)
        inner = matmul(settled_low, w_part) + vector(8 + t)
        S.inner[t] = inner
        S.act[t] = gelu(inner).astype(BF)
        if t == 1:
            pump_second(OUT, 2)
    pump_second(OUT, 3)
    pass_to_core(SETTLED_ALL, S.set_all)
    weight_ready(OUT, range(4))
    branch = vector(5)
    for t in range(4):
        branch = branch + matmul(S.act[t], S.full[OUT][t])
    normal_two, inverse_two = norm_parts(S.keep[...] + branch)
    result = normal_two * vector(6) + vector(7)
    S.out_low[...] = result.astype(BF)
    finishing = [local(OUTPUT, S.out_low, output)]
    loads[TEACHER].wait()
    diff = jnp.where(own_live, result - S.teacher[...].astype(F32), 0.0)
    count = vector(12)
    upstream = diff * ((ROWS * CTX * GROUP) / count)
    S.sg[...] = jnp.zeros((16, D), F32)

    def note(row, value):
        S.sg[row : row + 1, :] = jnp.sum(value.astype(F32), axis=0, keepdims=True)

    note(12, diff * diff)
    S.sg[13:14, :] = count * (1.0 / (CTX * GROUP))
    note(6, upstream * normal_two)
    note(7, upstream)

    d_second = norm_back(upstream * vector(6), normal_two, inverse_two)
    branch_grad = d_second.astype(BF)
    S.bg[...] = branch_grad
    to_near(BRANCH_GRAD_ALL, S.bg, S.bg_all)
    S.bg_all[w] = branch_grad
    note(5, branch_grad)
    d_settled = d_second
    for t in range(4):
        d_act = right_product(branch_grad, S.full[OUT][t])
        inner = S.inner[t]
        inner_grad = (d_act * gelu_slope(inner)).astype(BF)
        note(8 + t, inner_grad)
        w_part = S.full[IN][:, :, D * t : D * (t + 1)].reshape(D, D)
        d_settled = d_settled + right_product(inner_grad, w_part)
    pass_to_core(BRANCH_GRAD_ALL, S.bg_all)
    normal_one = S.first[...]
    note(3, d_settled * normal_one)
    note(4, d_settled)
    d_first = norm_back(d_settled * vector(3), normal_one, inverse_one)
    S.keep[...] = d_first
    attn_grad = d_first.astype(BF)
    note(2, attn_grad)
    context_grad = right_product(attn_grad, square(O)).T.astype(BF)
    for i in range(4):
        S.cg_send[i] = context_grad[HW * i : HW * (i + 1), :]
    for j in (1, 2, 3):
        to = bit_xor(a, j)
        remote((CONTEXT_GRAD, j), S.cg_send.at[to], S.cg.at[a], 2 * j, 0)
    S.cg[a] = S.cg_send[a]
    for i in range(2):
        S.ag_half[i] = attn_grad[:, 384 * i : 384 * (i + 1)]
    to_group((ATTN_GRAD_ALL,), lambda to: S.ag_half.at[to % 2], S.ag_all)
    S.ag_all[w] = S.ag_half[core]

    half = a // 2

    def reduce_pair(lot):
        remote((REDUCE, lot, 0), S.part[lot].at[1 - b], S.got[lot][0], 1, 0)

    def reduce_end(lot):
        got = S.got[lot][0]
        arrived((REDUCE, lot, 0), got)
        total = S.part[lot][b].astype(F32) + got[...].astype(F32)
        S.sum[lot][0][...] = total.astype(BF)

        @only(True)
        def to_middle():
            target = S.got[lot][1]
            remote((REDUCE, lot, 1), S.sum[lot][0], target, 2, 0, like=lambda: target)

    def reduce_middle(lot):
        @only(False)
        def swap_halves():
            got = S.got[lot][1]
            arrived((REDUCE, lot, 1), got)
            total = S.sum[lot][0][...].astype(F32) + got[...].astype(F32)
            S.sum[lot][1][...] = total.astype(BF)
            there, target = S.sum[lot][1].at[1 - half], S.got[lot][2]
            remote((REDUCE, lot, 2), there, target, 6, 0, like=lambda: target)

    def reduce_last(lot):
        @only(False)
        def own_half():
            got = S.got[lot][2]
            arrived((REDUCE, lot, 2), got)
            total = (S.sum[lot][1][half].astype(F32) + got[...].astype(F32)).astype(BF)
            if lot in LOT_IN:
                own, done = S.own[lot], S.done[lot]
                own[...] = total
                done[b, half, w] = own[w]
                for q in (1, 2, 3):
                    slot = done.at[b, half, w]
                    to = bit_xor(w, q)
                    remote((GROUP_X, lot, q), own.at[to], slot, 0, q, like=lambda: own.at[0])
            else:
                S.done[lot][b, half] = total
                spread_middle(lot)

    def spread_middle(lot):
        part = S.done[lot].at[b, half]
        remote((SPREAD, lot, 0), part, part, 6, 0, like=lambda: S.done[lot].at[0, 0])

    def spread_group(lot):
        @only(False)
        def gathered():
            for q in (1, 2, 3):
                arrived((GROUP_X, lot, q), S.done[lot].at[b, half, bit_xor(w, q)])
            spread_middle(lot)

    def spread_end(lot):
        @only(False)
        def to_end():
            arrived((SPREAD, lot, 0), S.done[lot].at[b, 1 - half])
            done = S.done[lot].at[b]
            remote((SPREAD, lot, 1), done, done, 2, 0, like=lambda: S.done[lot].at[0])

    def result_of(lot):
        return grad_in[lot - LOT_IN[0]] if lot in LOT_IN else grad_out.at[lot - LOT_OUT[0]]

    def give(lot):
        @only(True)
        def from_middle_device():
            arrived((SPREAD, lot, 1), S.done[lot].at[b])

        done = S.done[lot].at[b]
        if lot not in LOT_O:
            out = result_of(lot).at[b]
            remote((GIVE, lot), done, out, 1, 0)
            finishing.append(local((GIVE, lot), done, out))
            return
        remote((GIVE, lot), done, grad_o.at[core], 1, 0, core, 2, 2 * x + b)

        @pl.when(core == b)
        def keep_own():
            local((OWN, lot), done, grad_o.at[core])

        @pl.when(core != b)
        def give_core():
            remote((OWN, lot), done, grad_o.at[core], 0, 1)
            started.pop()

    def settle(lot):
        if lot not in LOT_O:
            arrived((GIVE, lot), result_of(lot).at[1 - b])
            return
        done = S.done[lot].at[b]

        @pl.when(core == b)
        def from_chip():
            pltpu.make_async_copy(
                done, grad_o.at[core], local_sems.at[locals_.take((OWN, lot))]
            ).wait()
            arrived((OWN, lot), grad_o.at[1 - core])

        @pl.when(core != b)
        def from_partner():
            arrived((GIVE, lot), grad_o.at[0], 0)
            arrived((GIVE, lot), grad_o.at[1], 1)
            sent = numbers.take((OWN, lot))
            pltpu.make_async_copy(done, done, send_sems.at[sent]).wait()

    def lanes(parts):
        return jnp.concatenate(parts, axis=1)

    def inner_again():
        from_near(SETTLED_ALL, S.set_all)
        settled_all = S.set_all[...].reshape(GROUP * ROWS, D)
        hidden = pl.ds(pl.multiple_of(D * w, D), D)
        S.inner_all[...] = (
            matmul(settled_all, S.full[IN][:, :, hidden].reshape(D, D))
            + S.vectors[pl.ds(8 + w, 1), :]
        )
        S.act_all[...] = gelu(S.inner_all[...]).astype(BF)

    def out_part():
        from_near(BRANCH_GRAD_ALL, S.bg_all)
        grad = tn(S.act_all[...], S.bg_all[...].reshape(GROUP * ROWS, D)).astype(BF)
        for i, lot in enumerate(LOT_OUT):
            S.part[lot][...] = grad[HW * i : HW * (i + 1)].reshape(2, 2, 48, D)
            reduce_pair(lot)

    def in_part():
        branch_grad_all = S.bg_all[...].reshape(GROUP * ROWS, D)
        inner_grad_all = (
            right_product(branch_grad_all, S.full[OUT][w]) * gelu_slope(S.inner_all[...])
        ).astype(BF)
        grad = tn(S.set_all[...].reshape(GROUP * ROWS, D), inner_grad_all).astype(BF)
        for i, lot in enumerate(LOT_IN):
            for j in range(2):
                side = grad[:, 384 * j : 384 * (j + 1)].reshape(4, 2, 2, 48, 384)
                for k in range(2):
                    S.part[lot][j, k] = side[:, k, i]
            reduce_pair(lot)

    def attention_back():
        for j in (1, 2, 3):
            arrived((CONTEXT_GRAD, j), S.cg.at[bit_xor(a, j)])
        for h in range(HEADS):
            grad = wide(S.cg, h).astype(F32)
            row_total = S.total[h, 0:1, :]
            S.wg[h] = (grad / row_total).astype(BF)
            S.total[h, 1:2, :] = -jnp.sum(grad * S.mix[h], axis=0, keepdims=True) / (
                row_total * row_total
            )
        S.mix[...] = jnp.zeros(S.mix.shape, F32)

        def attend_back(pair, i):
            block = 2 * i + pair
            for h in range(HEADS):
                key_rows = slice(HD * h, HD * (h + 1))
                value_rows = slice(HW + HD * h, HW + HD * (h + 1))
                weights = S.weights[block, h]
                grad = S.wg[h]
                weight_grad = tn(S.kv[block, value_rows, :], grad) + S.total[h, 1:2, :]
                score_grad = (weights * weight_grad).astype(BF)
                S.mix[h] += matmul(S.kv[block, key_rows, :], score_grad)
                S.dkv[pair, i, key_rows, :] = (
                    right_product(wide(S.q, h), score_grad) * score_scale
                ).astype(BF)
                value_grad = right_product(grad, weights.astype(BF))
                S.dkv[pair, i, value_rows, :] = value_grad.astype(BF)

        @pl.loop(0, CTX)
        def every_block(block):
            attend_back(block % 2, block // 2)

        remote((KEY_VALUE_GRAD,), S.dkv.at[1 - b], S.dkv_pair, 1, 0)
        for h in range(HEADS):
            rows = slice(2 * HW + HD * h, 2 * HW + HD * (h + 1))
            S.grads[rows, :] = (S.mix[h] * score_scale).astype(BF)
        S.grads[3 * HW :, :] = jnp.zeros((HEAD_COLS - 3 * HW, 4 * ROWS), BF)

    def o_part():
        from_group((CONTEXT_ALL,), S.ctx_all)
        from_group((ATTN_GRAD_ALL,), S.ag_all)
        context_all = lanes([S.ctx_all[i].reshape(384, ROWS) for i in range(GROUP)])
        grad = matmul(context_all, S.ag_all[...].reshape(GROUP * ROWS, 384))
        S.part[LOT_O[0]][...] = grad.astype(BF).reshape(2, 2, 96, 384)
        reduce_pair(LOT_O[0])

    def heads_part():
        arrived((KEY_VALUE_GRAD,), S.dkv_pair)
        for i in range(4):
            S.grads[0 : 2 * HW, ROWS * i : ROWS * (i + 1)] = (
                S.dkv[b, i].astype(F32) + S.dkv_pair[i].astype(F32)
            ).astype(BF)
        own_inputs = lanes([S.xt[2 * i + b] for i in range(4)])
        heads = right_product(own_inputs, S.grads[...]).astype(BF)
        S.heads[...] = heads.reshape(2, 2, HW, HEAD_COLS)
        for i in range(2):
            remote((HEADS_CORE, i), S.heads.at[i, 1 - core], S.heads_core.at[i], 0, 1)

    def input_parts():
        parts = tn(S.grads[0 : 3 * HW, :], S.head_weight[...])
        S.dx_send[...] = parts.astype(BF).reshape(4, ROWS, D)
        for j in (1, 2, 3):
            to = bit_xor(a, j)
            remote((INPUT_PARTS, j), S.dx_send.at[to], S.dx.at[a], 2 * j, 0)
        S.dx[a] = S.dx_send[a]

    def vectors_group():
        S.column[...] = jnp.zeros((D, ROWS), F32)
        heads_rows = pl.ds(pl.multiple_of(HW * a, HW), HW)
        for row, first in ((1, HW), (0, 2 * HW)):
            sums = jnp.sum(S.grads[first : first + HW, :].astype(F32), axis=1, keepdims=True)
            S.column[heads_rows, :] = jnp.broadcast_to(sums, (HW, ROWS))
            S.sg[row : row + 1, :] = S.column[...].T[0:1, :]
        for j in (1, 2, 3):
            remote((VECTORS_W, j), S.sg, S.sg_w.at[w], 0, j)
        S.sg_w[w] = S.sg[...]

    def vectors_line():
        for j in (1, 2, 3):
            arrived((VECTORS_W, j), S.sg_w.at[bit_xor(w, j)])
        S.sg_z[a] = (S.sg_w[0] + S.sg_w[1]) + (S.sg_w[2] + S.sg_w[3])
        for j in (1, 2, 3):
            remote((VECTORS_Z, j), S.sg_z.at[a], S.sg_z.at[a], 2 * j, 0)

    def vectors_pair():
        for j in (1, 2, 3):
            arrived((VECTORS_Z, j), S.sg_z.at[bit_xor(a, j)])
        S.sg_y[b] = (S.sg_z[0] + S.sg_z[1]) + (S.sg_z[2] + S.sg_z[3])
        remote(VECTORS_Y, S.sg_y.at[b], S.sg_y.at[b], 1, 0)

    def vectors_done():
        arrived(VECTORS_Y, S.sg_y.at[1 - b])
        everything = S.sg_y[0] + S.sg_y[1]
        S.sg_rows[...] = everything
        for i in range(4):
            S.smalls[i] = everything[:, HW * i : HW * (i + 1)]
        finishing.append(local(VECTORS_Y, S.smalls, smalls_out))
        finishing.append(local(VECTORS_Z, S.sg_rows, rows_out))

    def heads_x():
        for i in range(2):
            arrived((HEADS_CORE, i), S.heads_core.at[i])
        for i in range(2):
            S.heads_sum[i] = (S.heads[i, core].astype(F32) + S.heads_core[i].astype(F32)).astype(BF)
        remote((HEADS_X,), S.heads_sum.at[1 - x], S.heads_x, 0, 2)

    def heads_y():
        arrived((HEADS_X,), S.heads_x)
        S.heads_row[...] = (
            (S.heads_sum[x].astype(F32) + S.heads_x[...].astype(F32))
            .astype(BF)
            .reshape(2, HW // 2, HEAD_COLS)
        )
        remote((HEADS_Y,), S.heads_row.at[1 - b], S.heads_y, 1, 0)

    def heads_line():
        arrived((HEADS_Y,), S.heads_y)
        S.heads_done[a] = (S.heads_row[b].astype(F32) + S.heads_y[...].astype(F32)).astype(BF)
        for j in (1, 2, 3):
            remote((HEADS_LINE, j), S.heads_done.at[a], S.heads_done.at[a], 2 * j, 0)

    def heads_pair():
        for j in (1, 2, 3):
            arrived((HEADS_LINE, j), S.heads_done.at[bit_xor(a, j)])
        remote((HEADS_PAIR,), S.heads_done, heads_out.at[b], 1, 0)
        finishing.append(local((HEADS_PAIR,), S.heads_done, heads_out.at[b]))

    def input_done():
        for j in (1, 2, 3):
            arrived((INPUT_PARTS, j), S.dx.at[bit_xor(a, j)])
        total = S.keep[...]
        for i in range(4):
            total = total + S.dx[i].astype(F32)
        S.first[...] = total
        finishing.append(local(INPUT_GRAD, S.first, input_grad_out))

    for step, *lot in (
        (inner_again,),
        (out_part,),
        (reduce_end, 3),
        (reduce_middle, 3),
        (in_part,),
        (reduce_end, 4),
        (reduce_end, 5),
        (reduce_middle, 4),
        (reduce_end, 6),
        (reduce_end, 1),
        (reduce_middle, 6),
        (reduce_last, 4),
        (attention_back,),
        (reduce_last, 6),
        (reduce_end, 2),
        (reduce_middle, 5),
        (reduce_last, 3),
        (o_part,),
        (reduce_middle, 1),
        (spread_end, 4),
        (reduce_last, 5),
        (spread_end, 3),
        (spread_end, 6),
        (reduce_middle, 2),
        (reduce_last, 1),
        (heads_part,),
        (give, 3),
        (vectors_group,),
        (spread_group, 1),
        (reduce_end, 0),
        (give, 6),
        (spread_end, 5),
        (reduce_last, 2),
        (heads_x,),
        (vectors_line,),
        (spread_end, 1),
        (spread_group, 2),
        (reduce_middle, 0),
        (give, 5),
        (heads_y,),
        (give, 4),
        (spread_end, 2),
        (reduce_last, 0),
        (vectors_pair,),
        (heads_line,),
        (give, 1),
        (input_parts,),
        (vectors_done,),
        (spread_end, 0),
        (give, 2),
        (heads_pair,),
        (give, 0),
        (input_done,),

    ):
        step(*lot)

    arrived((HEADS_PAIR,), heads_out.at[1 - b])
    for lot in range(len(LOTS)):
        settle(lot)
    for copy in finishing:
        copy.wait()
    for copy in started:
        copy.wait_send()
    for end, like, number in sent_by_role:

        @only(end)
        def sent():
            source = like()
            pltpu.make_async_copy(source, source, send_sems.at[number]).wait()


def finish_kernel(*refs):
    g_o, g_in0, g_in1, g_out, heads, smalls, rows, output, input_grad = refs[:9]
    r_q, r_k, r_v, r_o, r_in, r_out = refs[9:15]
    vectors, inner_bias, loss, r_output, r_input = refs[15:23], *refs[23:]
    step = pl.program_id(0)
    for i in range(2):
        r_o[:, 384 * i : 384 * (i + 1)] = g_o[i].reshape(HW // 2, 384).astype(F32)
        for j in range(4):
            first = D * j + 384 * i
            for k, source in enumerate((g_in0, g_in1)):
                r_in[48 * k : 48 * (k + 1), first : first + 384] = source[i, 0, j].astype(F32)
    r_out[...] = g_out[...].reshape(D // 2, D).astype(F32)
    for i, result in ((0, r_k), (1, r_v), (2, r_q)):
        result[...] = jnp.concatenate(
            [heads[0, j, :, HW * i : HW * (i + 1)].astype(F32) for j in range(4)], axis=1
        )
    r_output[0] = output[...]
    r_input[0] = input_grad[...]

    @pl.when(step == 0)
    def once():
        w = lax.axis_index("wsh")
        for i in range(8):
            vectors[i][...] = smalls[w, i, :]
        inner_bias[...] = rows[8 + w, :]
        error = jnp.sum(rows[12:13, :])
        count = jnp.max(rows[13:14, :])
        loss[0] = error / (count * D)


def fused_body(tokens, teacher, doc_lengths, valid_len, *weights):
    (
        q_weight,
        q_bias,
        k_weight,
        v_weight,
        v_bias,
        o_weight,
        o_bias,
        ln1_gain,
        ln1_bias,
        in_weight,
        in_bias,
        out_weight,
        out_bias,
        ln2_gain,
        ln2_bias,
    ) = weights
    hbm = pl.BlockSpec(memory_space=pl.ANY)
    smem = pl.BlockSpec(memory_space=pltpu.SMEM)
    vmem = pl.BlockSpec(memory_space=pltpu.VMEM)
    low = lambda *shape: jax.ShapeDtypeStruct(shape, BF)
    full = lambda *shape: jax.ShapeDtypeStruct(shape, F32)
    output, input_grad, g_o, g_in0, g_in1, g_out, heads, smalls, rows = pl.pallas_call(
        fused_kernel,
        out_shape=(
            low(ROWS, D),
            full(ROWS, D),
            low(2, 2, 96, 384),
            low(2, 2, 4, 48, 384),
            low(2, 2, 4, 48, 384),
            low(4, 2, 2, 48, D),
            low(2, 4, HW // 2, HEAD_COLS),
            full(GROUP, 16, HW),
            full(16, D),
        ),
        in_specs=[hbm] * 8 + [smem] * 2 + [vmem] * 9,
        out_specs=[hbm] * 9,
        scratch_shapes=scratch_shapes()[0]
        + [
            pltpu.SemaphoreType.DMA((REMOTE_SEMS,)),
            pltpu.SemaphoreType.DMA((REMOTE_SEMS,)),
            pltpu.SemaphoreType.DMA((LOCAL_SEMS,)),
        ],
        compiler_params=pltpu.CompilerParams(
            collective_id=0, has_side_effects=True, vmem_limit_bytes=67043328
        ),
        name="layer",
    )(
        tokens,
        teacher,
        q_weight,
        k_weight,
        v_weight,
        o_weight,
        in_weight,
        out_weight,
        doc_lengths,
        valid_len,
        q_bias,
        v_bias,
        o_bias,
        ln1_gain,
        ln1_bias,
        out_bias,
        ln2_gain,
        ln2_bias,
        in_bias,
    )

    steps = 2
    square_out = pl.BlockSpec((HW // steps, D), lambda i: (i, 0))
    whole = lambda *shape: pl.BlockSpec(shape, lambda i: (0,) * len(shape))
    by_row = pl.BlockSpec((ROWS // steps, D), lambda i: (i, 0))
    results = pl.pallas_call(
        finish_kernel,
        grid=(steps,),
        out_shape=(full(HW, D),) * 4
        + (full(HW, FF), full(D, D))
        + (full(HW),) * 8
        + (full(D), full(1), low(1, ROWS, D), full(1, ROWS, D)),
        in_specs=[
            pl.BlockSpec((2, 1, 96, 384), lambda i: (0, i, 0, 0)),
            pl.BlockSpec((2, 1, 4, 48, 384), lambda i: (0, i, 0, 0, 0)),
            pl.BlockSpec((2, 1, 4, 48, 384), lambda i: (0, i, 0, 0, 0)),
            pl.BlockSpec((2, 2, 2, 48, D), lambda i: (i, 0, 0, 0, 0)),
            pl.BlockSpec((1, 4, HW // 2, HEAD_COLS), lambda i: (i, 0, 0, 0)),
            whole(GROUP, 16, HW),
            whole(16, D),
            by_row,
            by_row,
        ],
        out_specs=[square_out] * 4
        + [
            pl.BlockSpec((HW // steps, FF), lambda i: (i, 0)),
            pl.BlockSpec((D // steps, D), lambda i: (i, 0)),
        ]
        + [whole(HW)] * 8
        + [
            whole(D),
            pl.BlockSpec(memory_space=pltpu.SMEM),
            pl.BlockSpec((1, ROWS // steps, D), lambda i: (0, i, 0)),
            pl.BlockSpec((1, ROWS // steps, D), lambda i: (0, i, 0)),
        ],
        compiler_params=pltpu.CompilerParams(dimension_semantics=("arbitrary",)),
        name="finish",
    )(g_o, g_in0, g_in1, g_out, heads, smalls, rows, output, input_grad)
    r_q, r_k, r_v, r_o, r_in, r_out = results[:6]
    vectors, inner_bias, loss, r_output, r_input = results[6:14], *results[14:]
    return (
        r_output,
        loss.reshape(()),
        r_input,
        r_q,
        vectors[0],
        r_k,
        r_v,
        vectors[1],
        r_o,
        vectors[2],
        vectors[3],
        vectors[4],
        r_in,
        inner_bias,
        r_out,
        vectors[5],
        vectors[6],
        vectors[7],
    )


def solution(mesh):
    in_specs = (
        P("wsh", "ctx", None),
        P("wsh", "ctx", None),
        P("wsh", None),
        P("wsh"),
        P("wsh", None),
        P("wsh"),
        P("wsh", None),
        P("wsh", None),
        P("wsh"),
        P("wsh", None),
        P("wsh"),
        P("wsh"),
        P("wsh"),
        P("wsh", None),
        P("wsh"),
        P("wsh", None),
        P("wsh"),
        P("wsh"),
        P("wsh"),
    )
    out_specs = (
        P("wsh", "ctx", None),
        P(),
        P("wsh", "ctx", None),
        P("wsh", None),
        P("wsh"),
        P("wsh", None),
        P("wsh", None),
        P("wsh"),
        P("wsh", None),
        P("wsh"),
        P("wsh"),
        P("wsh"),
        P("wsh", None),
        P("wsh"),
        P("wsh", None),
        P("wsh"),
        P("wsh"),
        P("wsh"),
    )
    program = fused_body if fused_fits(mesh) else body
    return jax.shard_map(program, mesh=mesh, in_specs=in_specs, out_specs=out_specs, check_vma=False)
```

```python
import math
import types

import jax
import jax.numpy as jnp
from jax import lax
from jax.experimental import pallas as pl
from jax.experimental.pallas import tpu as pltpu
from jax.sharding import PartitionSpec as P

D = 768
H = 12
HD = 64


EPSILON = 1e-06
MASKED = -1e30


def shifted(block, axis, distance):
    devices = range(lax.axis_size(axis))
    route = [((i - distance) % len(devices), i) for i in devices]
    return lax.ppermute(block, axis, route)


def layer_norm(value, gain, shift):
    mean = jnp.mean(value, axis=-1, keepdims=True)
    centered = value - mean
    spread = jnp.mean(centered * centered, axis=-1, keepdims=True)
    return centered * lax.rsqrt(spread + EPSILON) * gain + shift


def activate(value):
    return jax.nn.gelu(value, approximate=True)


def matmul(left, right):
    return jnp.dot(left, right, preferred_element_type=jnp.float32)


def left_product(left, right):
    return lax.dot_general(
        left, right, (((0,), (0,)), ((), ())), preferred_element_type=jnp.float32
    )


def right_product(left, right):
    return lax.dot_general(
        left, right, (((1,), (1,)), ((), ())), preferred_element_type=jnp.float32
    )


def document_of(positions, starts):
    return jnp.sum((starts[None, :] <= positions[:, None]).astype(jnp.int32), axis=1) - 1


def permitted(own_doc, own_live, other_doc, other_live):
    return (own_doc[:, None] == other_doc[None, :]) & (own_live[:, None] == other_live[None, :])


def block_weights(queries, key_block, allowed, score_scale):
    scores = (
        jnp.einsum("qhd,khd->hqk", queries, key_block, preferred_element_type=jnp.float32)
        * score_scale
    )
    return jnp.exp(jnp.where(allowed[None], scores, MASKED))


def forward_visit(sums_state, queries, key_block, value_block, allowed, score_scale):
    row_total, weighted = sums_state
    weights = block_weights(queries, key_block, allowed, score_scale)
    row_total = row_total + jnp.sum(weights, axis=-1)
    weighted = weighted + jnp.einsum(
        "hqk,khd->qhd",
        weights.astype(jnp.bfloat16),
        value_block,
        preferred_element_type=jnp.float32,
    )
    return (row_total, weighted)


def backward_visit(
    queries, key_block, value_block, allowed, score_scale, weighted_grad, total_grad
):
    weights = block_weights(queries, key_block, allowed, score_scale)
    value_part = jnp.einsum(
        "hqk,qhd->khd",
        weights.astype(jnp.bfloat16),
        weighted_grad,
        preferred_element_type=jnp.float32,
    )
    weight_grad = (
        jnp.einsum("qhd,khd->hqk", weighted_grad, value_block, preferred_element_type=jnp.float32)
        + total_grad[:, :, None]
    )
    score_grad = (weights * weight_grad).astype(jnp.bfloat16)
    query_part = (
        jnp.einsum("hqk,khd->qhd", score_grad, key_block, preferred_element_type=jnp.float32)
        * score_scale
    )
    key_part = (
        jnp.einsum("hqk,qhd->khd", score_grad, queries, preferred_element_type=jnp.float32)
        * score_scale
    )
    return (query_part, key_part, value_part)


def body(
    tokens,
    teacher,
    doc_lengths,
    valid_len,
    q_weight,
    q_bias,
    k_weight,
    v_weight,
    v_bias,
    o_weight,
    o_bias,
    ln1_gain,
    ln1_bias,
    in_weight,
    in_bias,
    out_weight,
    out_bias,
    ln2_gain,
    ln2_bias,
):
    gathered = (
        lax.all_gather(q_weight, "wsh", axis=0, tiled=True),
        lax.all_gather(q_bias, "wsh", axis=0, tiled=True),
        lax.all_gather(k_weight, "wsh", axis=0, tiled=True),
        lax.all_gather(v_weight, "wsh", axis=0, tiled=True),
        lax.all_gather(v_bias, "wsh", axis=0, tiled=True),
        lax.all_gather(o_weight, "wsh", axis=0, tiled=True),
        lax.all_gather(o_bias, "wsh", axis=0, tiled=True),
        lax.all_gather(ln1_gain, "wsh", axis=0, tiled=True),
        lax.all_gather(ln1_bias, "wsh", axis=0, tiled=True),
        lax.all_gather(in_weight, "wsh", axis=0, tiled=True),
        lax.all_gather(in_bias, "wsh", axis=0, tiled=True),
        lax.all_gather(out_weight, "wsh", axis=0, tiled=True),
        lax.all_gather(out_bias, "wsh", axis=0, tiled=True),
        lax.all_gather(ln2_gain, "wsh", axis=0, tiled=True),
        lax.all_gather(ln2_bias, "wsh", axis=0, tiled=True),
    )
    (
        w_query,
        b_query,
        w_key,
        w_value,
        b_value,
        w_out,
        b_out,
        gain_one,
        shift_one,
        w_inner,
        b_inner,
        w_back,
        b_back,
        gain_two,
        shift_two,
    ) = gathered
    gain_first = gain_one.astype(jnp.float32)
    shift_first = shift_one.astype(jnp.float32)
    gain_second = gain_two.astype(jnp.float32)
    shift_second = shift_two.astype(jnp.float32)
    inputs = tokens[0]
    row_count = inputs.shape[0]
    cycle_size = lax.axis_size("ctx")
    stream_count = lax.axis_size("wsh")
    position = lax.axis_index("ctx")
    score_scale = 1.0 / math.sqrt(HD)
    offsets = jnp.arange(row_count, dtype=jnp.int32)
    lengths = doc_lengths[0]
    starts = jnp.cumsum(lengths) - lengths
    limit = valid_len[0]

    def key_mask(block_index):
        where_rows = jnp.mod(block_index, cycle_size) * row_count + offsets
        return (document_of(where_rows, starts), where_rows < limit)

    own_doc, own_live = key_mask(position)
    input_float = inputs.astype(jnp.float32)
    queries = (
        (matmul(inputs, w_query) + b_query.astype(jnp.float32))
        .astype(jnp.bfloat16)
        .reshape(row_count, H, HD)
    )
    key_rows = matmul(inputs, w_key).astype(jnp.bfloat16).reshape(row_count, H, HD)
    value_rows = (
        (matmul(inputs, w_value) + b_value.astype(jnp.float32))
        .astype(jnp.bfloat16)
        .reshape(row_count, H, HD)
    )

    def visit_forward(sums_state, key_block, value_block, block_index):
        other_doc, other_live = key_mask(block_index)
        allowed = permitted(own_doc, own_live, other_doc, other_live)
        return forward_visit(sums_state, queries, key_block, value_block, allowed, score_scale)

    empty_state = (
        jnp.zeros((H, row_count), jnp.float32),
        jnp.zeros((row_count, H, HD), jnp.float32),
    )
    first_state = visit_forward(empty_state, key_rows, value_rows, position)

    def advance(step_index, loop_state):
        key_block, value_block, running = loop_state
        key_block, value_block = shifted((key_block, value_block), "ctx", 1)
        running = visit_forward(running, key_block, value_block, position - step_index)
        return (key_block, value_block, running)

    row_total, weighted = lax.fori_loop(
        1, cycle_size, advance, (key_rows, value_rows, first_state)
    )[2]
    normed = weighted / jnp.transpose(row_total)[:, :, None]
    context = normed.astype(jnp.bfloat16).reshape(row_count, D)
    attn = matmul(context, w_out) + b_out.astype(jnp.float32)
    first_sum = input_float + attn
    settled = layer_norm(first_sum, gain_first, shift_first)
    settled_low = settled.astype(jnp.bfloat16)
    inner = matmul(settled_low, w_inner) + b_inner.astype(jnp.float32)
    activated = activate(inner).astype(jnp.bfloat16)
    branch = matmul(activated, w_back) + b_back.astype(jnp.float32)
    second_sum = settled + branch
    result = layer_norm(second_sum, gain_second, shift_second)
    target = teacher[0].astype(jnp.float32)
    diff = jnp.where(own_live[:, None], result - target, 0.0)
    error_sum, live_count = lax.psum(
        (jnp.sum(diff * diff), jnp.sum(own_live.astype(jnp.float32))), ("ctx", "wsh")
    )
    loss = error_sum / (live_count * D)
    upstream = diff * (row_count * cycle_size * stream_count / live_count)
    unused_second, second_back = jax.vjp(layer_norm, second_sum, gain_second, shift_second)
    d_second, gain_two_grad, shift_two_grad = second_back(upstream)
    branch_grad = d_second.astype(jnp.bfloat16)
    back_weight_grad = left_product(activated, branch_grad)
    back_bias_grad = jnp.sum(branch_grad, axis=0, dtype=jnp.float32)
    d_activated = right_product(branch_grad, w_back)
    unused_inner, gelu_back = jax.vjp(activate, inner)
    inner_grad = gelu_back(d_activated)[0].astype(jnp.bfloat16)
    inner_weight_grad = left_product(settled_low, inner_grad)
    inner_bias_grad = jnp.sum(inner_grad, axis=0, dtype=jnp.float32)
    d_settled = d_second + right_product(inner_grad, w_inner)
    unused_first, first_back = jax.vjp(layer_norm, first_sum, gain_first, shift_first)
    d_first, gain_one_grad, shift_one_grad = first_back(d_settled)
    attn_grad = d_first.astype(jnp.bfloat16)
    out_weight_grad_local = left_product(context, attn_grad)
    out_bias_grad_local = jnp.sum(attn_grad, axis=0, dtype=jnp.float32)
    context_low = lax.optimization_barrier(right_product(attn_grad, w_out).astype(jnp.bfloat16))
    context_grad = context_low.astype(jnp.float32).reshape(row_count, H, HD)
    weighted_grad = (context_grad / jnp.transpose(row_total)[:, :, None]).astype(jnp.bfloat16)
    total_grad = -jnp.transpose(jnp.sum(context_grad * weighted, axis=-1)) / (row_total * row_total)

    def visit_backward(key_block, value_block, block_index):
        other_doc, other_live = key_mask(block_index)
        allowed = permitted(own_doc, own_live, other_doc, other_live)
        return backward_visit(
            queries, key_block, value_block, allowed, score_scale, weighted_grad, total_grad
        )

    query_sum, key_sum, value_sum = visit_backward(key_rows, value_rows, position)

    def advance_back(step_index, loop_state):
        key_block, value_block, query_acc, key_acc, value_acc = loop_state
        key_block, value_block = shifted((key_block, value_block), "ctx", 1)
        key_acc, value_acc = (
            shifted(key_acc.astype(jnp.bfloat16), "ctx", 1).astype(key_acc.dtype),
            shifted(value_acc.astype(jnp.bfloat16), "ctx", 1).astype(value_acc.dtype),
        )
        query_part, key_part, value_part = visit_backward(
            key_block, value_block, position - step_index
        )
        return (
            key_block,
            value_block,
            query_acc + query_part,
            key_acc + key_part,
            value_acc + value_part,
        )

    loop_state = lax.fori_loop(
        1, cycle_size, advance_back, (key_rows, value_rows, query_sum, key_sum, value_sum)
    )
    query_total = loop_state[2]
    key_total, value_total = (
        shifted(loop_state[3].astype(jnp.bfloat16), "ctx", 1).astype(jnp.float32),
        shifted(loop_state[4].astype(jnp.bfloat16), "ctx", 1).astype(jnp.float32),
    )
    query_grad = query_total.astype(jnp.bfloat16).reshape(row_count, D)
    key_grad = key_total.astype(jnp.bfloat16).reshape(row_count, D)
    value_grad = value_total.astype(jnp.bfloat16).reshape(row_count, D)
    query_weight_grad = left_product(inputs, query_grad)
    query_bias_grad = jnp.sum(query_grad, axis=0, dtype=jnp.float32)
    key_weight_grad = left_product(inputs, key_grad)
    value_weight_grad = left_product(inputs, value_grad)
    value_bias_grad = jnp.sum(value_grad, axis=0, dtype=jnp.float32)
    input_grad = (
        d_first
        + right_product(query_grad, w_query)
        + right_product(key_grad, w_key)
        + right_product(value_grad, w_value)
    )
    reduced = (
        lax.psum_scatter(
            query_weight_grad.astype(jnp.bfloat16), "wsh", scatter_dimension=0, tiled=True
        ).astype(jnp.float32),
        lax.psum_scatter(
            query_bias_grad.astype(jnp.bfloat16), "wsh", scatter_dimension=0, tiled=True
        ).astype(jnp.float32),
        lax.psum_scatter(
            key_weight_grad.astype(jnp.bfloat16), "wsh", scatter_dimension=0, tiled=True
        ).astype(jnp.float32),
        lax.psum_scatter(
            value_weight_grad.astype(jnp.bfloat16), "wsh", scatter_dimension=0, tiled=True
        ).astype(jnp.float32),
        lax.psum_scatter(
            value_bias_grad.astype(jnp.bfloat16), "wsh", scatter_dimension=0, tiled=True
        ).astype(jnp.float32),
        lax.psum_scatter(
            out_weight_grad_local.astype(jnp.bfloat16), "wsh", scatter_dimension=0, tiled=True
        ).astype(jnp.float32),
        lax.psum_scatter(
            out_bias_grad_local.astype(jnp.bfloat16), "wsh", scatter_dimension=0, tiled=True
        ).astype(jnp.float32),
        lax.psum_scatter(
            gain_one_grad.astype(jnp.bfloat16), "wsh", scatter_dimension=0, tiled=True
        ).astype(jnp.float32),
        lax.psum_scatter(
            shift_one_grad.astype(jnp.bfloat16), "wsh", scatter_dimension=0, tiled=True
        ).astype(jnp.float32),
        lax.psum_scatter(
            inner_weight_grad.astype(jnp.bfloat16), "wsh", scatter_dimension=0, tiled=True
        ).astype(jnp.float32),
        lax.psum_scatter(
            inner_bias_grad.astype(jnp.bfloat16), "wsh", scatter_dimension=0, tiled=True
        ).astype(jnp.float32),
        lax.psum_scatter(
            back_weight_grad.astype(jnp.bfloat16), "wsh", scatter_dimension=0, tiled=True
        ).astype(jnp.float32),
        lax.psum_scatter(
            back_bias_grad.astype(jnp.bfloat16), "wsh", scatter_dimension=0, tiled=True
        ).astype(jnp.float32),
        lax.psum_scatter(
            gain_two_grad.astype(jnp.bfloat16), "wsh", scatter_dimension=0, tiled=True
        ).astype(jnp.float32),
        lax.psum_scatter(
            shift_two_grad.astype(jnp.bfloat16), "wsh", scatter_dimension=0, tiled=True
        ).astype(jnp.float32),
    )
    summed = lax.psum(
        (
            reduced[0],
            reduced[1],
            reduced[2],
            reduced[3],
            reduced[4],
            reduced[5],
            reduced[6],
            reduced[7],
            reduced[8],
            reduced[9],
            reduced[10],
            reduced[11],
            reduced[12],
            reduced[13],
            reduced[14],
        ),
        "ctx",
    )
    return (
        result.astype(jnp.bfloat16)[None],
        loss,
        input_grad[None],
        summed[0],
        summed[1],
        summed[2],
        summed[3],
        summed[4],
        summed[5],
        summed[6],
        summed[7],
        summed[8],
        summed[9],
        summed[10],
        summed[11],
        summed[12],
        summed[13],
        summed[14],
    )


BF = jnp.bfloat16
F32 = jnp.float32
FF = 3072
ROWS = 128
HEADS = 3
HW = HEADS * HD
GROUP = 4
CTX = 8
MESH = pl.DeviceIdType.MESH

Q, K, V, O, IN, OUT, PART_Q, PART_K, PART_V = range(9)
SLICE = 256
WEIGHT_SHAPES = [(192, 768)] * 4 + [(192, 3072), (768, 768)] + [(192, SLICE)] * 3
SECOND_WAY = {O: 1, IN: 1, OUT: 2, PART_Q: 1, PART_K: 1, PART_V: 1}
LOT_O, LOT_IN, LOT_OUT = (0,), (1, 2), (3, 4, 5, 6)
LOT_PAIR = LOT_O + LOT_IN + LOT_OUT[:3]
LOTS = [(96, 384)] + [(4, 48, 384)] * 2 + [(48, D)] * 4
PIECES = {IN: (1, 4), OUT: (4, 1)}
HEAD_COLS = 640

(
    SMALL,
    WEIGHT_X,
    WEIGHT_SECOND,
    WEIGHT_CORE,
    WEIGHT_CORE_X,
    WEIGHT_CORE_SECOND,
    X_LINE,
    X_EDGE,
    KEY_VALUE,
    CONTEXT,
    CONTEXT_GRAD,
    KEY_VALUE_GRAD,
    INPUT_PARTS,
    SETTLED_ALL,
    CONTEXT_ALL,
    ATTN_GRAD_ALL,
    BRANCH_GRAD_ALL,
    REDUCE,
    SPREAD,
    GIVE,
    OWN,
    GROUP_X,
    HEADS_CORE,
    HEADS_X,
    HEADS_Y,
    HEADS_LINE,
    HEADS_EDGE,
    HEADS_PAIR,
    VECTORS_W,
    VECTORS_Z,
    VECTORS_Y,
    VECTORS_CORE,
    TOKENS,
    TEACHER,
    OUTPUT,
    INPUT_GRAD,
    LOAD,
) = range(37)


def fused_fits(mesh):
    return mesh.shape["ctx"] == CTX and mesh.shape["wsh"] == GROUP


def tn(left, right):
    return lax.dot_general(
        left, right, (((0,), (0,)), ((), ())), preferred_element_type=jnp.float32
    )


def norm_parts(value):
    mean = jnp.mean(value, axis=-1, keepdims=True)
    centered = value - mean
    spread = jnp.mean(centered * centered, axis=-1, keepdims=True)
    inverse = lax.rsqrt(spread + EPSILON)
    return centered * inverse, inverse


def norm_back(upstream_gained, normal, inverse):
    return (
        upstream_gained
        - jnp.mean(upstream_gained, axis=-1, keepdims=True)
        - normal * jnp.mean(upstream_gained * normal, axis=-1, keepdims=True)
    ) * inverse


GELU_C = math.sqrt(2.0 / math.pi)


class Numbers:
    def __init__(self):
        self.count = 0
        self.table = {}

    def take(self, key, size=1):
        if key not in self.table:
            self.table[key] = self.count
            self.count += size
        return self.table[key]


def scratch_table():
    s = types.SimpleNamespace()
    s.full = {k: pltpu.VMEM((GROUP, *WEIGHT_SHAPES[k]), BF) for k in SECOND_WAY}
    s.turned = pltpu.VMEM((SLICE, D), BF)
    s.head_weight = pltpu.VMEM((3 * HW, D), BF)
    s.tall_bias = pltpu.VMEM((SLICE, ROWS), F32)
    s.head_bias = pltpu.VMEM((3 * HW, ROWS), F32)
    s.x = pltpu.VMEM((ROWS, D), BF)
    s.xt = pltpu.VMEM((CTX, D, ROWS), BF)
    s.teacher = pltpu.VMEM((ROWS, D), BF)
    s.small = pltpu.VMEM((GROUP, 16, D), BF)
    s.vectors = pltpu.VMEM((16, D), F32)
    s.kv = pltpu.VMEM((CTX, 2 * HW, ROWS), BF)
    s.q = pltpu.VMEM((4, HW, ROWS), BF)
    s.weights = pltpu.VMEM((CTX, HEADS, ROWS, 4 * ROWS), F32)
    s.mix = pltpu.VMEM((HEADS, HD, 4 * ROWS), F32)
    s.total = pltpu.VMEM((HEADS, 8, 4 * ROWS), F32)
    s.ctx_send = pltpu.VMEM((4, HW, ROWS), BF)
    s.ctx = pltpu.VMEM((4, HW, ROWS), BF)
    s.inner = pltpu.VMEM((4, ROWS, D), F32)
    s.act = pltpu.VMEM((4, ROWS, D), BF)
    s.first = pltpu.VMEM((ROWS, D), F32)
    s.keep = pltpu.VMEM((ROWS, D), F32)
    s.inverse = pltpu.VMEM((ROWS, 128), F32)
    s.set_low = pltpu.VMEM((ROWS, D), BF)
    s.ag_half = pltpu.VMEM((2, ROWS, 384), BF)
    s.bg = pltpu.VMEM((ROWS, D), BF)
    s.set_all = pltpu.VMEM((GROUP, ROWS, D), BF)
    s.ctx_all = pltpu.VMEM((GROUP, 2, HW, ROWS), BF)
    s.ag_all = pltpu.VMEM((GROUP, ROWS, 384), BF)
    s.inner_all = pltpu.VMEM((GROUP * ROWS, D), F32)
    s.act_all = pltpu.VMEM((GROUP * ROWS, D), BF)
    s.bg_all = pltpu.VMEM((GROUP, ROWS, D), BF)
    s.cg_send = pltpu.VMEM((4, HW, ROWS), BF)
    s.cg = pltpu.VMEM((4, HW, ROWS), BF)
    s.wg = pltpu.VMEM((HEADS, HD, 4 * ROWS), BF)
    s.dkv = pltpu.VMEM((2, 4, 2 * HW, ROWS), BF)
    s.dkv_pair = pltpu.VMEM((4, 2 * HW, ROWS), BF)
    s.grads = pltpu.VMEM((HEAD_COLS, 4 * ROWS), BF)
    s.dx_send = pltpu.VMEM((4, ROWS, D), BF)
    s.dx_end = pltpu.VMEM((3, ROWS, D), BF)
    s.dx_middle = pltpu.VMEM((2, ROWS, D), BF)
    s.dx_got = pltpu.VMEM((2, ROWS, D), BF)
    s.dx_back = pltpu.VMEM((ROWS, D), BF)
    s.dx_last = pltpu.VMEM((ROWS, D), BF)
    s.column = pltpu.VMEM((D, ROWS), F32)
    s.heads = pltpu.VMEM((2, 2, HW, HEAD_COLS), BF)
    s.heads_core = pltpu.VMEM((2, HW, HEAD_COLS), BF)
    s.heads_sum = pltpu.VMEM((2, HW, HEAD_COLS), BF)
    s.heads_x = pltpu.VMEM((HW, HEAD_COLS), BF)
    s.heads_row = pltpu.VMEM((2, HW // 2, HEAD_COLS), BF)
    s.heads_y = pltpu.VMEM((HW // 2, HEAD_COLS), BF)
    s.heads_done = pltpu.VMEM((4, HW // 2, HEAD_COLS), BF)
    s.part = [pltpu.VMEM((2, 2, *shape), BF) for shape in LOTS]
    def lots(*dims):
        return [
            pltpu.VMEM((*dims[1 if k in LOT_PAIR else 0], *shape), BF) for k, shape in enumerate(LOTS)
        ]

    steps = [((2, 2), (2,)), ((2,), (2,)), ((), ())]
    s.got = [list(lot) for lot in zip(*(lots(*step) for step in steps))]
    s.sum = [list(lot) for lot in zip(*(lots(*step) for step in steps[:2]))]
    s.own = {k: pltpu.VMEM(LOTS[k], BF) for k in LOT_IN}
    s.done = [pltpu.VMEM((2, 2, *shape), BF) for shape in LOTS]
    s.smalls = pltpu.VMEM((GROUP, 16, HW), F32)
    s.sg = pltpu.VMEM((16, D), F32)
    s.sg_all = pltpu.VMEM((16, D), F32)
    s.sg_rows = pltpu.VMEM((2, 8, D), F32)
    s.sg_w = pltpu.VMEM((GROUP, 16, D), F32)
    s.sg_z = pltpu.VMEM((4, 8, D), F32)
    s.sg_y = pltpu.VMEM((2, 8, D), F32)
    s.out_low = pltpu.VMEM((ROWS, D), BF)
    return vars(s)


LOCAL_SEMS = 32
REMOTE_SEMS = 240


def is_memory(item):
    return not isinstance(item, (dict, list))


def scratch_shapes():
    return jax.tree.flatten(scratch_table(), is_leaf=is_memory)


def fused_kernel(*refs):
    (tokens, teacher), shards = refs[:2], refs[2:8]
    lengths, valid = refs[8:10]
    biases = refs[10:19]
    output, input_grad_out = refs[19:21]
    grad_o, *grad_in, grad_out = refs[21:25]
    heads_out, smalls_out, rows_out = refs[25:28]
    flat, shape = scratch_shapes()
    S = types.SimpleNamespace(**jax.tree.unflatten(shape, refs[28 : 28 + len(flat)]))
    send_sems, recv_sems, local_sems = refs[28 + len(flat) :]

    c = lax.axis_index("ctx")
    w = lax.axis_index("wsh")
    a, b = c // 2, c % 2
    x, core = w // 2, w % 2

    numbers = Numbers()
    locals_ = Numbers()
    started = []

    def bit_xor(value, j):
        out = value
        bit = 1
        while bit <= j:
            if j & bit:
                has = (value // bit) % 2
                out = out + bit * (1 - 2 * has)
            bit *= 2
        return out

    at_end = a * (3 - a) == 0
    roles, sent_by_role = [None], []

    def only(end):
        def run(action):
            roles.append(end)
            pl.when(at_end if end else jnp.logical_not(at_end))(action)
            roles.pop()

        return run

    def remote(key, src, dst, c_bits, w_bits, offset=0, size=1, to=None, like=None):
        number = numbers.take(key, size) + offset
        c_to, w_to = bit_xor(c, c_bits), bit_xor(w, w_bits) if to is None else to
        copy = pltpu.make_async_remote_copy(
            src_ref=src,
            dst_ref=dst,
            send_sem=send_sems.at[number],
            recv_sem=recv_sems.at[number],
            device_id={"ctx": c_to, "wsh": w_to},
            device_id_type=MESH,
        )
        copy.start()
        if roles[-1] is None:
            started.append(copy)
        else:
            sent_by_role.append((roles[-1], like, number))

    def arrived(key, landing, offset=0):
        number = numbers.take(key) + offset
        pltpu.make_async_copy(landing, landing, recv_sems.at[number]).wait()

    def local(key, src, dst):
        copy = pltpu.make_async_copy(src, dst, local_sems.at[locals_.take(key)])
        copy.start()
        return copy

    peers = [(c, bit_xor(w, j)) for j in (1, 2, 3)]
    peers += [(bit_xor(c, j), w) for j in range(1, CTX)]
    peers += [(bit_xor(c, 1), bit_xor(w, 1))]

    def bit(value, mask):
        return (value // mask) % 2

    first_col = pl.multiple_of((3 * a) // 2 * 128, 128)
    first_row = pl.multiple_of(a % 2 * 64, 64)

    def shard(name):
        if name < PART_Q:
            return shards[name]
        return shards[name - PART_Q].at[:, pl.ds(first_col, SLICE)]

    loads = {TOKENS: local(TOKENS, tokens.at[0], S.x)}
    for name in (PART_K, PART_V, PART_Q, O, IN, OUT):
        loads[name] = local((LOAD, name), shard(name), S.full[name].at[w])
    loads[TEACHER] = local(TEACHER, teacher.at[0], S.teacher)

    barrier = pltpu.get_barrier_semaphore()
    for c_to, w_to in peers:
        pl.semaphore_signal(
            barrier, inc=1, device_id={"ctx": c_to, "wsh": w_to}, device_id_type=MESH
        )
    loads[TOKENS].wait()
    x_low = S.x[...]
    S.xt[c] = x_low.T
    bias_rows = [row[...].astype(F32).reshape(1, HW) for row in biases[:8]]
    tall = jnp.concatenate(bias_rows, axis=0)
    valid_high = (valid[0] // 64).astype(F32)
    valid_low = (valid[0] % 64).astype(F32)
    wide_rows = [biases[8][...].astype(F32).reshape(1, D)]
    wide_rows += [jnp.full((1, D), 64.0, F32) * valid_high, jnp.full((1, D), 1.0, F32) * valid_low]
    wide_rows += [jnp.zeros((5, D), F32)]
    S.small[w, :, 0:HW] = jnp.concatenate(
        [tall, jnp.concatenate(wide_rows, axis=0)[:, 0:HW]], axis=0
    ).astype(BF)
    S.small[w, 8:16, HW:D] = jnp.concatenate(wide_rows, axis=0)[:, HW:D].astype(BF)

    pl.semaphore_wait(barrier, len(peers))

    def mine(name):
        return bit(c, SECOND_WAY[name])

    def pieces(name):
        tall, across = PIECES.get(name, (1, 1))
        return range(tall * across)

    def piece(name, which, number):
        rows, cols = WEIGHT_SHAPES[name]
        tall, across = PIECES.get(name, (1, 1))
        high, broad = rows // 2 // tall, cols // across
        row = which * (rows // 2) + number // across * high
        return pl.ds(pl.multiple_of(row, 16), high), slice(
            number % across * broad, (number % across + 1) * broad
        )

    def send_core(name):
        remote((WEIGHT_CORE, name), shard(name), S.full[name].at[w], 0, 1)

    def send_x(name):
        for i in pieces(name):
            rows, cols = piece(name, mine(name), i)
            if name < PART_Q:
                source = shards[name].at[rows, cols]
            else:
                source = shards[name - PART_Q].at[rows, pl.ds(first_col, SLICE)]
            remote((WEIGHT_X, name, i), source, S.full[name].at[w, rows, cols], 0, 2)

    for name in (PART_K, PART_V, PART_Q):
        send_x(name)
        send_core(name)
    for j in (1, 2, 3):
        remote((SMALL, j), S.small.at[w], S.small.at[w], 0, j)
    remote((X_LINE, 1), S.xt.at[c], S.xt.at[c], 2, 0)

    @only(False)
    def x_to_middle():
        remote((X_LINE, 3), S.xt.at[c], S.xt.at[c], 6, 0, like=lambda: S.xt.at[0])

    for name in (O, IN, OUT):
        send_x(name)
        send_core(name)

    def pump_x(name, number=0):
        slot = S.full[name].at[bit_xor(w, 2), *piece(name, mine(name), number)]
        arrived((WEIGHT_X, name, number), slot)
        remote((WEIGHT_SECOND, name, number), slot, slot, SECOND_WAY[name], 0)
        remote((WEIGHT_CORE_X, name, number), slot, slot, 0, 1)

    def pump_second(name, number=0):
        slot = S.full[name].at[bit_xor(w, 2), *piece(name, 1 - mine(name), number)]
        arrived((WEIGHT_SECOND, name, number), slot)
        remote((WEIGHT_CORE_SECOND, name, number), slot, slot, 0, 1)

    def weight_ready(name, numbers_=(0,), first=True):
        full = S.full[name]
        if first:
            loads[name].wait()
            arrived((WEIGHT_CORE, name), full.at[bit_xor(w, 1)])
        for i in numbers_:
            near = full.at[bit_xor(w, 3), *piece(name, mine(name), i)]
            far = full.at[bit_xor(w, 3), *piece(name, 1 - mine(name), i)]
            arrived((WEIGHT_CORE_X, name, i), near)
            arrived((WEIGHT_CORE_SECOND, name, i), far)

    def square(name):
        return S.full[name][...].reshape(D, D)

    starts, running = [], 0
    for i in range(lengths.shape[1]):
        starts.append(running)
        running = running + lengths[0, i]
    limit = valid[0]

    def code_of(position):
        code = jnp.zeros(position.shape, jnp.int32)
        for start in starts:
            code = code + (start <= position).astype(jnp.int32)
        return 2 * code + (position < limit).astype(jnp.int32)

    lane = lax.broadcasted_iota(jnp.int32, (1, 4 * ROWS), 1)
    query_code = code_of((2 * (lane // ROWS) + b) * ROWS + lane % ROWS)

    def key_code(block):
        return code_of(block * ROWS + lax.broadcasted_iota(jnp.int32, (ROWS, 1), 0))

    own_live = c * ROWS + lax.broadcasted_iota(jnp.int32, (ROWS, 1), 0) < limit

    def block_on(j, pair):
        return 2 * bit_xor(a, j) + pair

    def pass_x(key, j, onward, bits):
        block = S.xt.at[block_on(j, b)]
        arrived((key, j), block)
        remote(onward, block, block, bits, 0, like=lambda: S.xt.at[0])

    def vector(row):
        return S.vectors[row : row + 1, :]

    def to_group(key, source_of, everywhere):
        for j in (1, 2, 3):
            to = bit_xor(w, j)
            remote((*key, j), source_of(to), everywhere.at[w], 0, j)

    def from_group(key, everywhere):
        for j in (1, 2, 3):
            arrived((*key, j), everywhere.at[bit_xor(w, j)])

    def to_near(key, source, everywhere):
        for j in (1, 2):
            remote((key, j), source, everywhere.at[w], 0, j)

    def pass_to_core(key, everywhere):
        slot = everywhere.at[bit_xor(w, 2)]
        arrived((key, 2), slot)
        remote((key, 3), slot, slot, 0, 1)

    def from_near(key, everywhere):
        for j in (1, 3):
            arrived((key, j), everywhere.at[bit_xor(w, j)])

    def lanes(parts):
        return jnp.concatenate(parts, axis=1)

    finishing = []

    def small_vectors():
        for j in (1, 2, 3):
            arrived((SMALL, j), S.small.at[bit_xor(w, j)])
        S.vectors[0:8, :] = jnp.concatenate(
            [S.small[i, 0:8, 0:HW].astype(F32) for i in range(GROUP)], axis=1
        )
        small = [S.small[i, 8:16, :].astype(F32) for i in range(GROUP)]
        S.vectors[8:16, :] = jnp.concatenate(
            [part[0:1] for part in small]
            + [sum(part[1:2] + part[2:3] for part in small), jnp.zeros((3, D), F32)],
            axis=0,
        )

    def pass_near_end():
        arrived((X_LINE, 1), S.xt.at[block_on(1, b)])

        @only(False)
        def to_other_middle():
            block = S.xt.at[block_on(1, b)]
            remote((X_LINE, 2), block, block, 6, 0, like=lambda: S.xt.at[0])

    def pass_middle():
        @only(False)
        def to_near_end():
            pass_x(X_LINE, 3, (X_EDGE, 2), 2)

    def pass_far_end():
        @only(False)
        def to_near_end():
            pass_x(X_LINE, 2, (X_EDGE, 3), 2)

    def head_weights():
        for name in (PART_K, PART_V, PART_Q):
            weight_ready(name)
        for i, (name, bias) in enumerate(((PART_K, None), (PART_V, 1), (PART_Q, 0))):
            rows = slice(HW * i, HW * (i + 1))
            S.turned[...] = S.full[name][...].reshape(D, SLICE).T
            S.head_weight[rows, :] = S.turned[pl.ds(first_row, HW), :]
            if bias is None:
                S.head_bias[rows, :] = jnp.zeros((HW, ROWS), F32)
            else:
                row = S.vectors[bias : bias + 1, pl.ds(first_col, SLICE)]
                S.tall_bias[...] = jnp.broadcast_to(row, (ROWS, SLICE)).T
                S.head_bias[rows, :] = S.tall_bias[pl.ds(first_row, HW), :]

    def project(j):
        if j > 1:

            @only(True)
            def from_middle():
                arrived((X_EDGE, j), S.xt.at[block_on(j, b)])

        block = block_on(j, b)
        out = matmul(S.head_weight[...], S.xt[block]) + S.head_bias[...]
        S.kv[block] = out[0 : 2 * HW].astype(BF)
        S.q[block // 2] = out[2 * HW :].astype(BF)
        remote((KEY_VALUE, j), S.kv.at[block], S.kv.at[block], 1, 0)

    score_scale = 1.0 / math.sqrt(HD)

    def wide(ref, h):
        return lanes([ref[i, HD * h : HD * (h + 1), :] for i in range(4)])

    def attend_block(block):
        allowed = key_code(block) == query_code
        for h in range(HEADS):
            scores = tn(S.kv[block, HD * h : HD * (h + 1), :], wide(S.q, h)) * score_scale
            weights = jnp.exp(jnp.where(allowed, scores, MASKED))
            S.weights[block, h] = weights
            S.total[h, 0:1, :] += jnp.sum(weights, axis=0, keepdims=True)
            value_t = S.kv[block, HW + HD * h : HW + HD * (h + 1), :]
            S.mix[h] += matmul(value_t, weights.astype(BF))

    def attend_line():
        S.mix[...] = jnp.zeros(S.mix.shape, F32)
        S.total[...] = jnp.zeros(S.total.shape, F32)

        @pl.loop(0, 4)
        def every_block(i):
            attend_block(2 * i + b)

    def attend_pair(j):
        arrived((KEY_VALUE, j), S.kv.at[block_on(j, 1 - b)])
        attend_block(block_on(j, 1 - b))

    def send_context():
        for h in range(HEADS):
            context_t = (S.mix[h] / S.total[h, 0:1, :]).astype(BF)
            for i in range(4):
                S.ctx_send[i, HD * h : HD * (h + 1), :] = context_t[:, ROWS * i : ROWS * (i + 1)]
        for j in (1, 2, 3):
            to = bit_xor(a, j)
            remote((CONTEXT, j), S.ctx_send.at[to], S.ctx.at[a], 2 * j, 0)
        S.ctx[a] = S.ctx_send[a]

    def first_norm():
        weight_ready(O)
        for j in (1, 2, 3):
            arrived((CONTEXT, j), S.ctx.at[bit_xor(a, j)])
        attn = tn(S.ctx[...].reshape(D, ROWS), square(O)) + vector(2)
        normal_one, inverse_one = norm_parts(S.x[...].astype(F32) + attn)
        settled = normal_one * vector(3) + vector(4)
        S.first[...] = normal_one
        S.inverse[...] = jnp.broadcast_to(inverse_one, (ROWS, 128))
        S.keep[...] = settled
        S.set_low[...] = settled.astype(BF)
        to_near(SETTLED_ALL, S.set_low, S.set_all)
        S.set_all[w] = S.set_low[...]
        to_group((CONTEXT_ALL,), lambda to: S.ctx.at[pl.ds(2 * (to // 2), 2)], S.ctx_all)
        S.ctx_all[w] = S.ctx[pl.ds(2 * x, 2)]

    def pass_settled():
        pass_to_core(SETTLED_ALL, S.set_all)

    def gelu(inner):
        return 0.5 * inner * (1.0 + jnp.tanh(GELU_C * (inner + 0.044715 * inner * inner * inner)))

    def gelu_slope(inner):
        squared = inner * inner
        bend = jnp.tanh(GELU_C * (inner + 0.044715 * squared * inner))
        return 0.5 * (1.0 + bend) + 0.5 * inner * (1.0 - bend * bend) * (
            GELU_C * (1.0 + 3 * 0.044715 * squared)
        )

    def feed_in(t):
        weight_ready(IN, (t,), t == 0)
        w_part = S.full[IN][:, :, D * t : D * (t + 1)].reshape(D, D)
        inner = matmul(S.set_low[...], w_part) + vector(8 + t)
        S.inner[t] = inner
        S.act[t] = gelu(inner).astype(BF)

    def note(row, value):
        S.sg[row : row + 1, :] = jnp.sum(value.astype(F32), axis=0, keepdims=True)

    def result_and_loss():
        weight_ready(OUT, range(4))
        branch = vector(5)
        for t in range(4):
            branch = branch + matmul(S.act[t], S.full[OUT][t])
        normal_two, inverse_two = norm_parts(S.keep[...] + branch)
        result = normal_two * vector(6) + vector(7)
        S.out_low[...] = result.astype(BF)
        finishing.append(local(OUTPUT, S.out_low, output))
        loads[TEACHER].wait()
        diff = jnp.where(own_live, result - S.teacher[...].astype(F32), 0.0)
        count = vector(12)
        upstream = diff * ((ROWS * CTX * GROUP) / count)
        d_second = norm_back(upstream * vector(6), normal_two, inverse_two)
        S.bg[...] = d_second.astype(BF)
        to_near(BRANCH_GRAD_ALL, S.bg, S.bg_all)
        S.bg_all[w] = S.bg[...]
        S.keep[...] = d_second
        S.sg[...] = jnp.zeros((16, D), F32)
        note(12, diff * diff)
        S.sg[13:14, :] = count * (1.0 / (CTX * GROUP))
        note(6, upstream * normal_two)
        note(7, upstream)
        note(5, S.bg[...])

    def feed_back():
        d_settled = S.keep[...]
        for t in range(4):
            d_act = right_product(S.bg[...], S.full[OUT][t])
            inner_grad = (d_act * gelu_slope(S.inner[t])).astype(BF)
            note(8 + t, inner_grad)
            w_part = S.full[IN][:, :, D * t : D * (t + 1)].reshape(D, D)
            d_settled = d_settled + right_product(inner_grad, w_part)
        S.keep[...] = d_settled

    def pass_branch_grad():
        pass_to_core(BRANCH_GRAD_ALL, S.bg_all)

    def first_norm_back():
        d_settled, normal_one = S.keep[...], S.first[...]
        d_first = norm_back(d_settled * vector(3), normal_one, S.inverse[:, 0:1])
        attn_grad = d_first.astype(BF)
        context_grad = right_product(attn_grad, square(O)).T.astype(BF)
        for i in range(4):
            S.cg_send[i] = context_grad[HW * i : HW * (i + 1), :]
        for j in (1, 2, 3):
            to = bit_xor(a, j)
            remote((CONTEXT_GRAD, j), S.cg_send.at[to], S.cg.at[a], 2 * j, 0)
        S.cg[a] = S.cg_send[a]
        for i in range(2):
            S.ag_half[i] = attn_grad[:, 384 * i : 384 * (i + 1)]
        to_group((ATTN_GRAD_ALL,), lambda to: S.ag_half.at[to % 2], S.ag_all)
        S.ag_all[w] = S.ag_half[core]
        note(3, d_settled * normal_one)
        note(4, d_settled)
        note(2, attn_grad)
        S.keep[...] = d_first

    half = a // 2

    def y_end(lot):
        got, total = S.got[lot], S.sum[lot]
        arrived((REDUCE, lot, 0), got[0])
        total[0][...] = (S.part[lot][b].astype(F32) + got[0][...].astype(F32)).astype(BF)

        @only(True)
        def to_middle():
            remote((REDUCE, lot, 1), total[0], got[1], 2, 0, like=lambda: got[1])

    def y_middle(lot):
        @only(False)
        def swap_halves():
            got, total = S.got[lot], S.sum[lot]
            arrived((REDUCE, lot, 1), got[1])
            total[1][...] = (total[0][...].astype(F32) + got[1][...].astype(F32)).astype(BF)
            there = total[1].at[1 - half]
            remote((REDUCE, lot, 2), there, got[2], 6, 0, like=lambda: got[2])

    def y_spread_middle(lot):
        part = S.done[lot].at[b, half]
        remote((SPREAD, lot, 0), part, part, 6, 0, like=lambda: S.done[lot].at[0, 0])

    def y_last(lot):
        @only(False)
        def own_half():
            got = S.got[lot][2]
            arrived((REDUCE, lot, 2), got)
            total = (S.sum[lot][1][half].astype(F32) + got[...].astype(F32)).astype(BF)
            if lot in LOT_IN:
                own, done = S.own[lot], S.done[lot]
                own[...] = total
                done[b, half, w] = own[w]
                for q in (1, 2, 3):
                    slot = done.at[b, half, w]
                    to = bit_xor(w, q)
                    remote((GROUP_X, lot, q), own.at[to], slot, 0, q, like=lambda: own.at[0])
            else:
                S.done[lot][b, half] = total
                y_spread_middle(lot)

    def y_group(lot):
        @only(False)
        def gathered():
            for q in (1, 2, 3):
                arrived((GROUP_X, lot, q), S.done[lot].at[b, half, bit_xor(w, q)])
            y_spread_middle(lot)

    def y_spread_end(lot):
        @only(False)
        def to_end():
            done = S.done[lot].at[b]
            arrived((SPREAD, lot, 0), S.done[lot].at[b, 1 - half])
            remote((SPREAD, lot, 1), done, done, 2, 0, like=lambda: S.done[lot].at[0])

    def result_of(lot):
        return grad_in[lot - LOT_IN[0]] if lot in LOT_IN else grad_out.at[lot - LOT_OUT[0]]

    def y_give(lot):
        done = S.done[lot].at[b]

        @only(True)
        def from_middle_device():
            arrived((SPREAD, lot, 1), done)

        if lot not in LOT_O:
            out = result_of(lot).at[b]
            remote((GIVE, lot), done, out, 1, 0)
            finishing.append(local((GIVE, lot), done, out))
            return
        remote((GIVE, 0), done, grad_o.at[core], 1, 0, core, 2, 2 * x + b)

        @pl.when(core == b)
        def keep_own():
            local((OWN, 0), done, grad_o.at[core])

        @pl.when(core != b)
        def give_core():
            remote((OWN, 0), done, grad_o.at[core], 0, 1)
            started.pop()

    def settle():
        for lot in LOT_PAIR[1:]:
            arrived((GIVE, lot), result_of(lot).at[1 - b])
        done = S.done[0].at[b]

        @pl.when(core == b)
        def from_chip():
            pltpu.make_async_copy(
                done, grad_o.at[core], local_sems.at[locals_.take((OWN, 0))]
            ).wait()
            arrived((OWN, 0), grad_o.at[1 - core])

        @pl.when(core != b)
        def from_partner():
            arrived((GIVE, 0), grad_o.at[0], 0)
            arrived((GIVE, 0), grad_o.at[1], 1)
            sent = numbers.take((OWN, 0))
            pltpu.make_async_copy(done, done, send_sems.at[sent]).wait()

    def reduce_start(lot):
        @only(True)
        def to_middle():
            target = S.got[lot][0]
            remote((REDUCE, lot, 0), S.part[lot], target, 2, 0, like=lambda: target)

    def reduce_middle(lot):
        @only(False)
        def swap_halves():
            got = S.got[lot][0]
            arrived((REDUCE, lot, 0), got)
            total = S.part[lot][...].astype(F32) + got[...].astype(F32)
            S.sum[lot][0][...] = total.astype(BF)
            there, target = S.sum[lot][0].at[1 - half], S.got[lot][1]
            remote((REDUCE, lot, 1), there, target, 6, 0, like=lambda: target)

    def reduce_pair(lot):
        @only(False)
        def swap_quarters():
            got = S.got[lot][1]
            arrived((REDUCE, lot, 1), got)
            total = S.sum[lot][0][half].astype(F32) + got[...].astype(F32)
            S.sum[lot][1][...] = total.astype(BF)
            there, target = S.sum[lot][1].at[1 - b], S.got[lot][2]
            remote((REDUCE, lot, 2), there, target, 1, 0, like=lambda: target)

    def reduce_last(lot):
        @only(False)
        def own_quarter():
            got = S.got[lot][2]
            arrived((REDUCE, lot, 2), got)
            total = (S.sum[lot][1][b].astype(F32) + got[...].astype(F32)).astype(BF)
            S.done[lot][half, b] = total
            part = S.done[lot].at[half, b]
            remote((SPREAD, lot, 0), part, part, 1, 0, like=lambda: S.done[lot].at[0, 0])

    def spread_middle(lot):
        @only(False)
        def swap_back():
            arrived((SPREAD, lot, 0), S.done[lot].at[half, 1 - b])
            part = S.done[lot].at[half]
            remote((SPREAD, lot, 1), part, part, 6, 0, like=lambda: S.done[lot].at[0])

    def spread_end(lot):
        @only(False)
        def to_end():
            done = S.done[lot]
            arrived((SPREAD, lot, 1), done.at[1 - half])
            part = done.at[:, b]
            remote((SPREAD, lot, 2), part, part, 2, 0, like=lambda: done.at[:, 0])

    def spread_ends(lot):
        @only(True)
        def swap_at_ends():
            done = S.done[lot]
            part = done.at[:, b]
            arrived((SPREAD, lot, 2), part)
            remote((SPREAD, lot, 3), part, part, 1, 0, like=lambda: done.at[:, 0])

    def finish_lot(lot):
        @only(True)
        def from_pair():
            arrived((SPREAD, lot, 3), S.done[lot].at[:, 1 - b])

        finishing.append(local((GIVE, lot), S.done[lot], grad_out.at[lot - LOT_OUT[0]]))

    def inner_again():
        from_near(SETTLED_ALL, S.set_all)
        settled_all = S.set_all[...].reshape(GROUP * ROWS, D)
        hidden = pl.ds(pl.multiple_of(D * w, D), D)
        S.inner_all[...] = (
            matmul(settled_all, S.full[IN][:, :, hidden].reshape(D, D))
            + S.vectors[pl.ds(8 + w, 1), :]
        )
        S.act_all[...] = gelu(S.inner_all[...]).astype(BF)

    def out_part():
        from_near(BRANCH_GRAD_ALL, S.bg_all)
        grad = tn(S.act_all[...], S.bg_all[...].reshape(GROUP * ROWS, D)).astype(BF)
        for i, lot in enumerate(LOT_OUT):
            S.part[lot][...] = grad[HW * i : HW * (i + 1)].reshape(2, 2, 48, D)
            if lot in LOT_PAIR:
                remote((REDUCE, lot, 0), S.part[lot].at[1 - b], S.got[lot][0], 1, 0)
            else:
                reduce_start(lot)

    def in_part():
        branch_grad_all = S.bg_all[...].reshape(GROUP * ROWS, D)
        inner_grad_all = (
            right_product(branch_grad_all, S.full[OUT][w]) * gelu_slope(S.inner_all[...])
        ).astype(BF)
        grad = tn(S.set_all[...].reshape(GROUP * ROWS, D), inner_grad_all).astype(BF)
        for i, lot in enumerate(LOT_IN):
            for j in range(2):
                side = grad[:, 384 * j : 384 * (j + 1)].reshape(4, 2, 2, 48, 384)
                for k in range(2):
                    S.part[lot][j, k] = side[:, k, i]
            remote((REDUCE, lot, 0), S.part[lot].at[1 - b], S.got[lot][0], 1, 0)

    def attention_back():
        for j in (1, 2, 3):
            arrived((CONTEXT_GRAD, j), S.cg.at[bit_xor(a, j)])
        for h in range(HEADS):
            grad = wide(S.cg, h).astype(F32)
            row_total = S.total[h, 0:1, :]
            S.wg[h] = (grad / row_total).astype(BF)
            S.total[h, 1:2, :] = -jnp.sum(grad * S.mix[h], axis=0, keepdims=True) / (
                row_total * row_total
            )
        S.mix[...] = jnp.zeros(S.mix.shape, F32)

        def attend_back(pair, i):
            block = 2 * i + pair
            for h in range(HEADS):
                key_rows = slice(HD * h, HD * (h + 1))
                value_rows = slice(HW + HD * h, HW + HD * (h + 1))
                weights = S.weights[block, h]
                grad = S.wg[h]
                weight_grad = tn(S.kv[block, value_rows, :], grad) + S.total[h, 1:2, :]
                score_grad = (weights * weight_grad).astype(BF)
                S.mix[h] += matmul(S.kv[block, key_rows, :], score_grad)
                S.dkv[pair, i, key_rows, :] = (
                    right_product(wide(S.q, h), score_grad) * score_scale
                ).astype(BF)
                value_grad = right_product(grad, weights.astype(BF))
                S.dkv[pair, i, value_rows, :] = value_grad.astype(BF)

        @pl.loop(0, CTX)
        def every_block(block):
            attend_back(block % 2, block // 2)

        remote((KEY_VALUE_GRAD,), S.dkv.at[1 - b], S.dkv_pair, 1, 0)
        for h in range(HEADS):
            rows = slice(2 * HW + HD * h, 2 * HW + HD * (h + 1))
            S.grads[rows, :] = (S.mix[h] * score_scale).astype(BF)
        S.grads[3 * HW :, :] = jnp.zeros((HEAD_COLS - 3 * HW, 4 * ROWS), BF)

    def o_part():
        from_group((CONTEXT_ALL,), S.ctx_all)
        from_group((ATTN_GRAD_ALL,), S.ag_all)
        context_all = lanes([S.ctx_all[i].reshape(384, ROWS) for i in range(GROUP)])
        grad = matmul(context_all, S.ag_all[...].reshape(GROUP * ROWS, 384))
        S.part[0][...] = grad.astype(BF).reshape(2, 2, 96, 384)
        remote((REDUCE, 0, 0), S.part[0].at[1 - b], S.got[0][0], 1, 0)

    def heads_part():
        arrived((KEY_VALUE_GRAD,), S.dkv_pair)
        for i in range(4):
            S.grads[0 : 2 * HW, ROWS * i : ROWS * (i + 1)] = (
                S.dkv[b, i].astype(F32) + S.dkv_pair[i].astype(F32)
            ).astype(BF)
        own_inputs = lanes([S.xt[2 * i + b] for i in range(4)])
        heads = right_product(own_inputs, S.grads[...]).astype(BF)
        S.heads[...] = heads.reshape(2, 2, HW, HEAD_COLS)
        for i in range(2):
            remote((HEADS_CORE, i), S.heads.at[i, 1 - core], S.heads_core.at[i], 0, 1)

    def input_parts():
        parts = tn(S.grads[0 : 3 * HW, :], S.head_weight[...])
        S.dx_send[...] = parts.astype(BF).reshape(4, ROWS, D)

        @only(True)
        def to_middle():
            for j in (1, 2, 3):
                source, target = S.dx_send.at[bit_xor(a, j)], S.dx_end.at[j - 1]
                remote((INPUT_PARTS, j), source, target, 2, 0, like=lambda: S.dx_end.at[0])

    def input_middle():
        @only(False)
        def to_other_middle():
            for j in (1, 2, 3):
                arrived((INPUT_PARTS, j), S.dx_end.at[j - 1])
            for i, j in enumerate((3, 2)):
                both = S.dx_send[bit_xor(a, j)].astype(F32) + S.dx_end[i + 1].astype(F32)
                S.dx_middle[i] = both.astype(BF)
            remote((INPUT_PARTS, 4), S.dx_middle, S.dx_got, 6, 0, like=lambda: S.dx_middle)

    def input_end():
        @only(False)
        def to_near_end():
            arrived((INPUT_PARTS, 4), S.dx_got)
            both = S.dx_send[bit_xor(a, 1)].astype(F32) + S.dx_got[1].astype(F32)
            S.dx_back[...] = both.astype(BF)
            remote((INPUT_PARTS, 5), S.dx_back, S.dx_last, 2, 0, like=lambda: S.dx_back)

    def vectors_group():
        S.column[...] = jnp.zeros((D, ROWS), F32)
        heads_rows = pl.ds(pl.multiple_of(HW * a, HW), HW)
        for row, first in ((1, HW), (0, 2 * HW)):
            sums = jnp.sum(S.grads[first : first + HW, :].astype(F32), axis=1, keepdims=True)
            S.column[heads_rows, :] = jnp.broadcast_to(sums, (HW, ROWS))
            S.sg[row : row + 1, :] = S.column[...].T[0:1, :]
        for j in (1, 2, 3):
            remote((VECTORS_W, j), S.sg, S.sg_w.at[w], 0, j)
        S.sg_w[w] = S.sg[...]

    own_rows = pl.ds(pl.multiple_of(8 * core, 8), 8)

    def vectors_line():
        for j in (1, 2, 3):
            arrived((VECTORS_W, j), S.sg_w.at[bit_xor(w, j)])
        S.sg_all[...] = (S.sg_w[0] + S.sg_w[1]) + (S.sg_w[2] + S.sg_w[3])
        S.sg_z[a] = S.sg_all[own_rows, :]
        for j in (1, 2, 3):
            remote((VECTORS_Z, j), S.sg_z.at[a], S.sg_z.at[a], 2 * j, 0)

    def vectors_pair():
        for j in (1, 2, 3):
            arrived((VECTORS_Z, j), S.sg_z.at[bit_xor(a, j)])
        S.sg_y[b] = (S.sg_z[0] + S.sg_z[1]) + (S.sg_z[2] + S.sg_z[3])
        remote((VECTORS_Y,), S.sg_y.at[b], S.sg_y.at[b], 1, 0)

    def vectors_core():
        arrived((VECTORS_Y,), S.sg_y.at[1 - b])
        S.sg_rows[core] = S.sg_y[0] + S.sg_y[1]
        remote((VECTORS_CORE,), S.sg_rows.at[core], S.sg_rows.at[core], 0, 1)

    def vectors_done():
        arrived((VECTORS_CORE,), S.sg_rows.at[1 - core])
        everything = S.sg_rows[...].reshape(16, D)
        for i in range(4):
            S.smalls[i] = everything[:, HW * i : HW * (i + 1)]
        finishing.append(local((VECTORS_Y,), S.smalls, smalls_out))
        finishing.append(local((VECTORS_Z,), S.sg_rows, rows_out))

    def heads_x():
        for i in range(2):
            arrived((HEADS_CORE, i), S.heads_core.at[i])
        for i in range(2):
            S.heads_sum[i] = (S.heads[i, core].astype(F32) + S.heads_core[i].astype(F32)).astype(BF)
        remote((HEADS_X,), S.heads_sum.at[1 - x], S.heads_x, 0, 2)

    def heads_y():
        arrived((HEADS_X,), S.heads_x)
        S.heads_row[...] = (
            (S.heads_sum[x].astype(F32) + S.heads_x[...].astype(F32))
            .astype(BF)
            .reshape(2, HW // 2, HEAD_COLS)
        )
        remote((HEADS_Y,), S.heads_row.at[1 - b], S.heads_y, 1, 0)

    def heads_line():
        arrived((HEADS_Y,), S.heads_y)
        S.heads_done[a] = (S.heads_row[b].astype(F32) + S.heads_y[...].astype(F32)).astype(BF)
        own = S.heads_done.at[a]
        remote((HEADS_LINE, 1), own, own, 2, 0)

        @only(False)
        def to_other_middle():
            remote((HEADS_LINE, 3), own, own, 6, 0, like=lambda: S.heads_done.at[0])

    def pass_heads(key, j, onward, bits):
        part = S.heads_done.at[bit_xor(a, j)]
        if key is not None:
            arrived((key, j), part)
        remote(onward, part, part, bits, 0, like=lambda: S.heads_done.at[0])

    def heads_near_end():
        arrived((HEADS_LINE, 1), S.heads_done.at[bit_xor(a, 1)])

        @only(False)
        def to_other_middle():
            pass_heads(None, 1, (HEADS_LINE, 2), 6)

    def heads_middle():
        @only(False)
        def to_near_end():
            pass_heads(HEADS_LINE, 3, (HEADS_EDGE, 2), 2)

    def heads_far_end():
        @only(False)
        def to_near_end():
            pass_heads(HEADS_LINE, 2, (HEADS_EDGE, 3), 2)

    def heads_pair():
        @only(True)
        def from_middle():
            for j in (2, 3):
                arrived((HEADS_EDGE, j), S.heads_done.at[bit_xor(a, j)])

        remote((HEADS_PAIR,), S.heads_done, heads_out.at[b], 1, 0)
        finishing.append(local((HEADS_PAIR,), S.heads_done, heads_out.at[b]))

    def input_done():
        S.first[...] = S.keep[...] + S.dx_send[a].astype(F32)

        @only(True)
        def at_end():
            arrived((INPUT_PARTS, 5), S.dx_last)
            S.first[...] += S.dx_last[...].astype(F32)

        @only(False)
        def in_middle():
            S.first[...] += S.dx_end[0].astype(F32) + S.dx_got[0].astype(F32)

        finishing.append(local(INPUT_GRAD, S.first, input_grad_out))

    for step, *lot in (
        (pump_x, PART_K),
        (pump_x, PART_V),
        (pump_x, PART_Q),
        (pass_near_end,),
        (pump_second, PART_K),
        (small_vectors,),
        (pump_second, PART_V),
        (pump_second, PART_Q),
        (pass_middle,),
        (head_weights,),
        (project, 1),
        (project, 0),
        (pass_far_end,),
        (project, 2),
        (project, 3),
        (pump_x, O),
        (pump_x, IN, 0),
        (attend_line,),
        (attend_pair, 1),
        (attend_pair, 2),
        (attend_pair, 3),
        (attend_pair, 0),
        (send_context,),
        (pump_x, IN, 1),
        (pump_x, OUT, 0),
        (pump_second, IN, 0),
        (pump_second, O),
        (pump_second, IN, 1),
        (pump_x, OUT, 1),
        (pump_x, IN, 2),
        (pump_x, OUT, 2),
        (first_norm,),
        (pump_x, IN, 3),
        (feed_in, 0),
        (pump_x, OUT, 3),
        (pump_second, IN, 2),
        (pump_second, OUT, 0),
        (feed_in, 1),
        (pump_second, OUT, 2),
        (pass_settled,),
        (pump_second, OUT, 1),
        (pump_second, IN, 3),
        (feed_in, 2),
        (pump_second, OUT, 3),
        (feed_in, 3),
        (result_and_loss,),
        (feed_back,),
        (inner_again,),
        (pass_branch_grad,),
        (first_norm_back,),
        (out_part,),
        (y_end, 3),
        (attention_back,),
        (y_end, 4),
        (o_part,),
        (reduce_middle, 6),
        (y_middle, 4),
        (y_end, 5),
        (in_part,),
        (y_last, 4),
        (y_middle, 3),
        (y_middle, 5),
        (heads_part,),
        (vectors_group,),
        (y_end, 0),
        (y_last, 5),
        (y_last, 3),
        (y_middle, 0),
        (y_spread_end, 4),
        (heads_x,),
        (vectors_line,),
        (y_spread_end, 5),
        (y_last, 0),
        (y_end, 1),
        (heads_y,),
        (y_spread_end, 3),
        (reduce_pair, 6),
        (y_give, 4),
        (y_middle, 1),
        (y_spread_end, 0),
        (heads_line,),
        (reduce_last, 6),
        (y_give, 5),
        (y_end, 2),
        (y_give, 0),
        (y_give, 3),
        (y_last, 1),
        (heads_near_end,),
        (input_parts,),
        (heads_middle,),
        (y_group, 1),
        (heads_far_end,),
        (y_middle, 2),
        (vectors_pair,),
        (y_spread_end, 1),
        (spread_middle, 6),
        (heads_pair,),
        (y_last, 2),
        (spread_end, 6),
        (y_give, 1),
        (y_group, 2),
        (vectors_core,),
        (y_spread_end, 2),
        (spread_ends, 6),
        (y_give, 2),
        (input_middle,),
        (input_end,),
        (input_done,),
        (vectors_done,),
        (finish_lot, 6),
    ):
        step(*lot)

    arrived((HEADS_PAIR,), heads_out.at[1 - b])
    settle()
    for copy in finishing:
        copy.wait()
    for copy in started:
        copy.wait_send()
    for end, like, number in sent_by_role:

        @only(end)
        def sent():
            source = like()
            pltpu.make_async_copy(source, source, send_sems.at[number]).wait()


def finish_kernel(*refs):
    g_o, g_in0, g_in1, g_out, heads, smalls, rows, output, input_grad = refs[:9]
    r_q, r_k, r_v, r_o, r_in, r_out = refs[9:15]
    vectors, inner_bias, loss, r_output, r_input = refs[15:23], *refs[23:]
    step = pl.program_id(0)
    for i in range(2):
        r_o[:, 384 * i : 384 * (i + 1)] = g_o[i].reshape(HW // 2, 384).astype(F32)
        for j in range(4):
            first = D * j + 384 * i
            for k, source in enumerate((g_in0, g_in1)):
                r_in[48 * k : 48 * (k + 1), first : first + 384] = source[i, 0, j].astype(F32)
    r_out[...] = g_out[...].reshape(D // 2, D).astype(F32)
    for i, result in ((0, r_k), (1, r_v), (2, r_q)):
        result[...] = jnp.concatenate(
            [heads[0, j, :, HW * i : HW * (i + 1)].astype(F32) for j in range(4)], axis=1
        )
    r_output[0] = output[...]
    r_input[0] = input_grad[...]

    @pl.when(step == 0)
    def once():
        w = lax.axis_index("wsh")
        for i in range(8):
            vectors[i][...] = smalls[w, i, :]
        inner_bias[...] = rows[1, w, :]
        error = jnp.sum(rows[1, 4:5, :])
        count = jnp.max(rows[1, 5:6, :])
        loss[0] = error / (count * D)


def fused_body(tokens, teacher, doc_lengths, valid_len, *weights):
    (
        q_weight,
        q_bias,
        k_weight,
        v_weight,
        v_bias,
        o_weight,
        o_bias,
        ln1_gain,
        ln1_bias,
        in_weight,
        in_bias,
        out_weight,
        out_bias,
        ln2_gain,
        ln2_bias,
    ) = weights
    hbm = pl.BlockSpec(memory_space=pl.ANY)
    smem = pl.BlockSpec(memory_space=pltpu.SMEM)
    vmem = pl.BlockSpec(memory_space=pltpu.VMEM)
    low = lambda *shape: jax.ShapeDtypeStruct(shape, BF)
    full = lambda *shape: jax.ShapeDtypeStruct(shape, F32)
    output, input_grad, g_o, g_in0, g_in1, g_out, heads, smalls, rows = pl.pallas_call(
        fused_kernel,
        out_shape=(
            low(ROWS, D),
            full(ROWS, D),
            low(2, 2, 96, 384),
            low(2, 2, 4, 48, 384),
            low(2, 2, 4, 48, 384),
            low(4, 2, 2, 48, D),
            low(2, 4, HW // 2, HEAD_COLS),
            full(GROUP, 16, HW),
            full(2, 8, D),
        ),
        in_specs=[hbm] * 8 + [smem] * 2 + [vmem] * 9,
        out_specs=[hbm] * 9,
        scratch_shapes=scratch_shapes()[0]
        + [
            pltpu.SemaphoreType.DMA((REMOTE_SEMS,)),
            pltpu.SemaphoreType.DMA((REMOTE_SEMS,)),
            pltpu.SemaphoreType.DMA((LOCAL_SEMS,)),
        ],
        compiler_params=pltpu.CompilerParams(
            collective_id=0, has_side_effects=True, vmem_limit_bytes=67043328
        ),
        name="layer",
    )(
        tokens,
        teacher,
        q_weight,
        k_weight,
        v_weight,
        o_weight,
        in_weight,
        out_weight,
        doc_lengths,
        valid_len,
        q_bias,
        v_bias,
        o_bias,
        ln1_gain,
        ln1_bias,
        out_bias,
        ln2_gain,
        ln2_bias,
        in_bias,
    )

    steps = 2
    square_out = pl.BlockSpec((HW // steps, D), lambda i: (i, 0))
    whole = lambda *shape: pl.BlockSpec(shape, lambda i: (0,) * len(shape))
    by_row = pl.BlockSpec((ROWS // steps, D), lambda i: (i, 0))
    results = pl.pallas_call(
        finish_kernel,
        grid=(steps,),
        out_shape=(full(HW, D),) * 4
        + (full(HW, FF), full(D, D))
        + (full(HW),) * 8
        + (full(D), full(1), low(1, ROWS, D), full(1, ROWS, D)),
        in_specs=[
            pl.BlockSpec((2, 1, 96, 384), lambda i: (0, i, 0, 0)),
            pl.BlockSpec((2, 1, 4, 48, 384), lambda i: (0, i, 0, 0, 0)),
            pl.BlockSpec((2, 1, 4, 48, 384), lambda i: (0, i, 0, 0, 0)),
            pl.BlockSpec((2, 2, 2, 48, D), lambda i: (i, 0, 0, 0, 0)),
            pl.BlockSpec((1, 4, HW // 2, HEAD_COLS), lambda i: (i, 0, 0, 0)),
            whole(GROUP, 16, HW),
            whole(2, 8, D),
            by_row,
            by_row,
        ],
        out_specs=[square_out] * 4
        + [
            pl.BlockSpec((HW // steps, FF), lambda i: (i, 0)),
            pl.BlockSpec((D // steps, D), lambda i: (i, 0)),
        ]
        + [whole(HW)] * 8
        + [
            whole(D),
            pl.BlockSpec(memory_space=pltpu.SMEM),
            pl.BlockSpec((1, ROWS // steps, D), lambda i: (0, i, 0)),
            pl.BlockSpec((1, ROWS // steps, D), lambda i: (0, i, 0)),
        ],
        compiler_params=pltpu.CompilerParams(dimension_semantics=("arbitrary",)),
        name="finish",
    )(g_o, g_in0, g_in1, g_out, heads, smalls, rows, output, input_grad)
    r_q, r_k, r_v, r_o, r_in, r_out = results[:6]
    vectors, inner_bias, loss, r_output, r_input = results[6:14], *results[14:]
    return (
        r_output,
        loss.reshape(()),
        r_input,
        r_q,
        vectors[0],
        r_k,
        r_v,
        vectors[1],
        r_o,
        vectors[2],
        vectors[3],
        vectors[4],
        r_in,
        inner_bias,
        r_out,
        vectors[5],
        vectors[6],
        vectors[7],
    )


def solution(mesh):
    in_specs = (
        P("wsh", "ctx", None),
        P("wsh", "ctx", None),
        P("wsh", None),
        P("wsh"),
        P("wsh", None),
        P("wsh"),
        P("wsh", None),
        P("wsh", None),
        P("wsh"),
        P("wsh", None),
        P("wsh"),
        P("wsh"),
        P("wsh"),
        P("wsh", None),
        P("wsh"),
        P("wsh", None),
        P("wsh"),
        P("wsh"),
        P("wsh"),
    )
    out_specs = (
        P("wsh", "ctx", None),
        P(),
        P("wsh", "ctx", None),
        P("wsh", None),
        P("wsh"),
        P("wsh", None),
        P("wsh", None),
        P("wsh"),
        P("wsh", None),
        P("wsh"),
        P("wsh"),
        P("wsh"),
        P("wsh", None),
        P("wsh"),
        P("wsh", None),
        P("wsh"),
        P("wsh"),
        P("wsh"),
    )
    program = fused_body if fused_fits(mesh) else body
    return jax.shard_map(program, mesh=mesh, in_specs=in_specs, out_specs=out_specs, check_vma=False)
```

```python
import math
import types

import jax
import jax.numpy as jnp
from jax import lax
from jax.experimental import pallas as pl
from jax.experimental.pallas import tpu as pltpu
from jax.sharding import PartitionSpec as P

D = 768
H = 12
HD = 64


EPSILON = 1e-06
MASKED = -1e30


def shifted(block, axis, distance):
    devices = range(lax.axis_size(axis))
    route = [((i - distance) % len(devices), i) for i in devices]
    return lax.ppermute(block, axis, route)


def layer_norm(value, gain, shift):
    mean = jnp.mean(value, axis=-1, keepdims=True)
    centered = value - mean
    spread = jnp.mean(centered * centered, axis=-1, keepdims=True)
    return centered * lax.rsqrt(spread + EPSILON) * gain + shift


def activate(value):
    return jax.nn.gelu(value, approximate=True)


def matmul(left, right):
    return jnp.dot(left, right, preferred_element_type=jnp.float32)


def left_product(left, right):
    return lax.dot_general(
        left, right, (((0,), (0,)), ((), ())), preferred_element_type=jnp.float32
    )


def right_product(left, right):
    return lax.dot_general(
        left, right, (((1,), (1,)), ((), ())), preferred_element_type=jnp.float32
    )


def document_of(positions, starts):
    return jnp.sum((starts[None, :] <= positions[:, None]).astype(jnp.int32), axis=1) - 1


def permitted(own_doc, own_live, other_doc, other_live):
    return (own_doc[:, None] == other_doc[None, :]) & (own_live[:, None] == other_live[None, :])


def block_weights(queries, key_block, allowed, score_scale):
    scores = (
        jnp.einsum("qhd,khd->hqk", queries, key_block, preferred_element_type=jnp.float32)
        * score_scale
    )
    return jnp.exp(jnp.where(allowed[None], scores, MASKED))


def forward_visit(sums_state, queries, key_block, value_block, allowed, score_scale):
    row_total, weighted = sums_state
    weights = block_weights(queries, key_block, allowed, score_scale)
    row_total = row_total + jnp.sum(weights, axis=-1)
    weighted = weighted + jnp.einsum(
        "hqk,khd->qhd",
        weights.astype(jnp.bfloat16),
        value_block,
        preferred_element_type=jnp.float32,
    )
    return (row_total, weighted)


def backward_visit(
    queries, key_block, value_block, allowed, score_scale, weighted_grad, total_grad
):
    weights = block_weights(queries, key_block, allowed, score_scale)
    value_part = jnp.einsum(
        "hqk,qhd->khd",
        weights.astype(jnp.bfloat16),
        weighted_grad,
        preferred_element_type=jnp.float32,
    )
    weight_grad = (
        jnp.einsum("qhd,khd->hqk", weighted_grad, value_block, preferred_element_type=jnp.float32)
        + total_grad[:, :, None]
    )
    score_grad = (weights * weight_grad).astype(jnp.bfloat16)
    query_part = (
        jnp.einsum("hqk,khd->qhd", score_grad, key_block, preferred_element_type=jnp.float32)
        * score_scale
    )
    key_part = (
        jnp.einsum("hqk,qhd->khd", score_grad, queries, preferred_element_type=jnp.float32)
        * score_scale
    )
    return (query_part, key_part, value_part)


def body(
    tokens,
    teacher,
    doc_lengths,
    valid_len,
    q_weight,
    q_bias,
    k_weight,
    v_weight,
    v_bias,
    o_weight,
    o_bias,
    ln1_gain,
    ln1_bias,
    in_weight,
    in_bias,
    out_weight,
    out_bias,
    ln2_gain,
    ln2_bias,
):
    gathered = (
        lax.all_gather(q_weight, "wsh", axis=0, tiled=True),
        lax.all_gather(q_bias, "wsh", axis=0, tiled=True),
        lax.all_gather(k_weight, "wsh", axis=0, tiled=True),
        lax.all_gather(v_weight, "wsh", axis=0, tiled=True),
        lax.all_gather(v_bias, "wsh", axis=0, tiled=True),
        lax.all_gather(o_weight, "wsh", axis=0, tiled=True),
        lax.all_gather(o_bias, "wsh", axis=0, tiled=True),
        lax.all_gather(ln1_gain, "wsh", axis=0, tiled=True),
        lax.all_gather(ln1_bias, "wsh", axis=0, tiled=True),
        lax.all_gather(in_weight, "wsh", axis=0, tiled=True),
        lax.all_gather(in_bias, "wsh", axis=0, tiled=True),
        lax.all_gather(out_weight, "wsh", axis=0, tiled=True),
        lax.all_gather(out_bias, "wsh", axis=0, tiled=True),
        lax.all_gather(ln2_gain, "wsh", axis=0, tiled=True),
        lax.all_gather(ln2_bias, "wsh", axis=0, tiled=True),
    )
    (
        w_query,
        b_query,
        w_key,
        w_value,
        b_value,
        w_out,
        b_out,
        gain_one,
        shift_one,
        w_inner,
        b_inner,
        w_back,
        b_back,
        gain_two,
        shift_two,
    ) = gathered
    gain_first = gain_one.astype(jnp.float32)
    shift_first = shift_one.astype(jnp.float32)
    gain_second = gain_two.astype(jnp.float32)
    shift_second = shift_two.astype(jnp.float32)
    inputs = tokens[0]
    row_count = inputs.shape[0]
    cycle_size = lax.axis_size("ctx")
    stream_count = lax.axis_size("wsh")
    position = lax.axis_index("ctx")
    score_scale = 1.0 / math.sqrt(HD)
    offsets = jnp.arange(row_count, dtype=jnp.int32)
    lengths = doc_lengths[0]
    starts = jnp.cumsum(lengths) - lengths
    limit = valid_len[0]

    def key_mask(block_index):
        where_rows = jnp.mod(block_index, cycle_size) * row_count + offsets
        return (document_of(where_rows, starts), where_rows < limit)

    own_doc, own_live = key_mask(position)
    input_float = inputs.astype(jnp.float32)
    queries = (
        (matmul(inputs, w_query) + b_query.astype(jnp.float32))
        .astype(jnp.bfloat16)
        .reshape(row_count, H, HD)
    )
    key_rows = matmul(inputs, w_key).astype(jnp.bfloat16).reshape(row_count, H, HD)
    value_rows = (
        (matmul(inputs, w_value) + b_value.astype(jnp.float32))
        .astype(jnp.bfloat16)
        .reshape(row_count, H, HD)
    )

    def visit_forward(sums_state, key_block, value_block, block_index):
        other_doc, other_live = key_mask(block_index)
        allowed = permitted(own_doc, own_live, other_doc, other_live)
        return forward_visit(sums_state, queries, key_block, value_block, allowed, score_scale)

    empty_state = (
        jnp.zeros((H, row_count), jnp.float32),
        jnp.zeros((row_count, H, HD), jnp.float32),
    )
    first_state = visit_forward(empty_state, key_rows, value_rows, position)

    def advance(step_index, loop_state):
        key_block, value_block, running = loop_state
        key_block, value_block = shifted((key_block, value_block), "ctx", 1)
        running = visit_forward(running, key_block, value_block, position - step_index)
        return (key_block, value_block, running)

    row_total, weighted = lax.fori_loop(
        1, cycle_size, advance, (key_rows, value_rows, first_state)
    )[2]
    normed = weighted / jnp.transpose(row_total)[:, :, None]
    context = normed.astype(jnp.bfloat16).reshape(row_count, D)
    attn = matmul(context, w_out) + b_out.astype(jnp.float32)
    first_sum = input_float + attn
    settled = layer_norm(first_sum, gain_first, shift_first)
    settled_low = settled.astype(jnp.bfloat16)
    inner = matmul(settled_low, w_inner) + b_inner.astype(jnp.float32)
    activated = activate(inner).astype(jnp.bfloat16)
    branch = matmul(activated, w_back) + b_back.astype(jnp.float32)
    second_sum = settled + branch
    result = layer_norm(second_sum, gain_second, shift_second)
    target = teacher[0].astype(jnp.float32)
    diff = jnp.where(own_live[:, None], result - target, 0.0)
    error_sum, live_count = lax.psum(
        (jnp.sum(diff * diff), jnp.sum(own_live.astype(jnp.float32))), ("ctx", "wsh")
    )
    loss = error_sum / (live_count * D)
    upstream = diff * (row_count * cycle_size * stream_count / live_count)
    unused_second, second_back = jax.vjp(layer_norm, second_sum, gain_second, shift_second)
    d_second, gain_two_grad, shift_two_grad = second_back(upstream)
    branch_grad = d_second.astype(jnp.bfloat16)
    back_weight_grad = left_product(activated, branch_grad)
    back_bias_grad = jnp.sum(branch_grad, axis=0, dtype=jnp.float32)
    d_activated = right_product(branch_grad, w_back)
    unused_inner, gelu_back = jax.vjp(activate, inner)
    inner_grad = gelu_back(d_activated)[0].astype(jnp.bfloat16)
    inner_weight_grad = left_product(settled_low, inner_grad)
    inner_bias_grad = jnp.sum(inner_grad, axis=0, dtype=jnp.float32)
    d_settled = d_second + right_product(inner_grad, w_inner)
    unused_first, first_back = jax.vjp(layer_norm, first_sum, gain_first, shift_first)
    d_first, gain_one_grad, shift_one_grad = first_back(d_settled)
    attn_grad = d_first.astype(jnp.bfloat16)
    out_weight_grad_local = left_product(context, attn_grad)
    out_bias_grad_local = jnp.sum(attn_grad, axis=0, dtype=jnp.float32)
    context_low = lax.optimization_barrier(right_product(attn_grad, w_out).astype(jnp.bfloat16))
    context_grad = context_low.astype(jnp.float32).reshape(row_count, H, HD)
    weighted_grad = (context_grad / jnp.transpose(row_total)[:, :, None]).astype(jnp.bfloat16)
    total_grad = -jnp.transpose(jnp.sum(context_grad * weighted, axis=-1)) / (row_total * row_total)

    def visit_backward(key_block, value_block, block_index):
        other_doc, other_live = key_mask(block_index)
        allowed = permitted(own_doc, own_live, other_doc, other_live)
        return backward_visit(
            queries, key_block, value_block, allowed, score_scale, weighted_grad, total_grad
        )

    query_sum, key_sum, value_sum = visit_backward(key_rows, value_rows, position)

    def advance_back(step_index, loop_state):
        key_block, value_block, query_acc, key_acc, value_acc = loop_state
        key_block, value_block = shifted((key_block, value_block), "ctx", 1)
        key_acc, value_acc = (
            shifted(key_acc.astype(jnp.bfloat16), "ctx", 1).astype(key_acc.dtype),
            shifted(value_acc.astype(jnp.bfloat16), "ctx", 1).astype(value_acc.dtype),
        )
        query_part, key_part, value_part = visit_backward(
            key_block, value_block, position - step_index
        )
        return (
            key_block,
            value_block,
            query_acc + query_part,
            key_acc + key_part,
            value_acc + value_part,
        )

    loop_state = lax.fori_loop(
        1, cycle_size, advance_back, (key_rows, value_rows, query_sum, key_sum, value_sum)
    )
    query_total = loop_state[2]
    key_total, value_total = (
        shifted(loop_state[3].astype(jnp.bfloat16), "ctx", 1).astype(jnp.float32),
        shifted(loop_state[4].astype(jnp.bfloat16), "ctx", 1).astype(jnp.float32),
    )
    query_grad = query_total.astype(jnp.bfloat16).reshape(row_count, D)
    key_grad = key_total.astype(jnp.bfloat16).reshape(row_count, D)
    value_grad = value_total.astype(jnp.bfloat16).reshape(row_count, D)
    query_weight_grad = left_product(inputs, query_grad)
    query_bias_grad = jnp.sum(query_grad, axis=0, dtype=jnp.float32)
    key_weight_grad = left_product(inputs, key_grad)
    value_weight_grad = left_product(inputs, value_grad)
    value_bias_grad = jnp.sum(value_grad, axis=0, dtype=jnp.float32)
    input_grad = (
        d_first
        + right_product(query_grad, w_query)
        + right_product(key_grad, w_key)
        + right_product(value_grad, w_value)
    )
    reduced = (
        lax.psum_scatter(
            query_weight_grad.astype(jnp.bfloat16), "wsh", scatter_dimension=0, tiled=True
        ).astype(jnp.float32),
        lax.psum_scatter(
            query_bias_grad.astype(jnp.bfloat16), "wsh", scatter_dimension=0, tiled=True
        ).astype(jnp.float32),
        lax.psum_scatter(
            key_weight_grad.astype(jnp.bfloat16), "wsh", scatter_dimension=0, tiled=True
        ).astype(jnp.float32),
        lax.psum_scatter(
            value_weight_grad.astype(jnp.bfloat16), "wsh", scatter_dimension=0, tiled=True
        ).astype(jnp.float32),
        lax.psum_scatter(
            value_bias_grad.astype(jnp.bfloat16), "wsh", scatter_dimension=0, tiled=True
        ).astype(jnp.float32),
        lax.psum_scatter(
            out_weight_grad_local.astype(jnp.bfloat16), "wsh", scatter_dimension=0, tiled=True
        ).astype(jnp.float32),
        lax.psum_scatter(
            out_bias_grad_local.astype(jnp.bfloat16), "wsh", scatter_dimension=0, tiled=True
        ).astype(jnp.float32),
        lax.psum_scatter(
            gain_one_grad.astype(jnp.bfloat16), "wsh", scatter_dimension=0, tiled=True
        ).astype(jnp.float32),
        lax.psum_scatter(
            shift_one_grad.astype(jnp.bfloat16), "wsh", scatter_dimension=0, tiled=True
        ).astype(jnp.float32),
        lax.psum_scatter(
            inner_weight_grad.astype(jnp.bfloat16), "wsh", scatter_dimension=0, tiled=True
        ).astype(jnp.float32),
        lax.psum_scatter(
            inner_bias_grad.astype(jnp.bfloat16), "wsh", scatter_dimension=0, tiled=True
        ).astype(jnp.float32),
        lax.psum_scatter(
            back_weight_grad.astype(jnp.bfloat16), "wsh", scatter_dimension=0, tiled=True
        ).astype(jnp.float32),
        lax.psum_scatter(
            back_bias_grad.astype(jnp.bfloat16), "wsh", scatter_dimension=0, tiled=True
        ).astype(jnp.float32),
        lax.psum_scatter(
            gain_two_grad.astype(jnp.bfloat16), "wsh", scatter_dimension=0, tiled=True
        ).astype(jnp.float32),
        lax.psum_scatter(
            shift_two_grad.astype(jnp.bfloat16), "wsh", scatter_dimension=0, tiled=True
        ).astype(jnp.float32),
    )
    summed = lax.psum(
        (
            reduced[0],
            reduced[1],
            reduced[2],
            reduced[3],
            reduced[4],
            reduced[5],
            reduced[6],
            reduced[7],
            reduced[8],
            reduced[9],
            reduced[10],
            reduced[11],
            reduced[12],
            reduced[13],
            reduced[14],
        ),
        "ctx",
    )
    return (
        result.astype(jnp.bfloat16)[None],
        loss,
        input_grad[None],
        summed[0],
        summed[1],
        summed[2],
        summed[3],
        summed[4],
        summed[5],
        summed[6],
        summed[7],
        summed[8],
        summed[9],
        summed[10],
        summed[11],
        summed[12],
        summed[13],
        summed[14],
    )


BF = jnp.bfloat16
F32 = jnp.float32
FF = 3072
ROWS = 128
HEADS = 3
HW = HEADS * HD
GROUP = 4
CTX = 8
MESH = pl.DeviceIdType.MESH

Q, K, V, O, IN, OUT, PART_Q, PART_K, PART_V = range(9)
SLICE = 256
WEIGHT_SHAPES = [(192, 768)] * 4 + [(192, 3072), (768, 768)] + [(192, SLICE)] * 3
SECOND_WAY = {O: 1, IN: 2, OUT: 1, PART_Q: 1, PART_K: 1, PART_V: 1}
LOT_O, LOT_IN, LOT_OUT = (0,), (1, 2), (3, 4, 5, 6)
LOT_PAIR = LOT_O + LOT_IN + LOT_OUT[:2]
LOTS = [(96, 384)] + [(4, 48, 384)] * 2 + [(48, D)] * 4
PIECES = {IN: (1, 4), OUT: (4, 1)}
HEAD_COLS = 640

(
    SMALL,
    WEIGHT_X,
    WEIGHT_SECOND,
    WEIGHT_CORE,
    WEIGHT_CORE_X,
    WEIGHT_CORE_SECOND,
    X_LINE,
    X_EDGE,
    KEY_VALUE,
    CONTEXT,
    CONTEXT_GRAD,
    KEY_VALUE_GRAD,
    INPUT_PARTS,
    SETTLED_ALL,
    CONTEXT_ALL,
    ATTN_GRAD_ALL,
    BRANCH_GRAD_ALL,
    REDUCE,
    SPREAD,
    GIVE,
    OWN,
    GROUP_X,
    HEADS_CORE,
    HEADS_X,
    HEADS_Y,
    HEADS_LINE,
    HEADS_EDGE,
    HEADS_PAIR,
    VECTORS_W,
    VECTORS_Z,
    VECTORS_Y,
    VECTORS_CORE,
    TOKENS,
    TEACHER,
    OUTPUT,
    INPUT_GRAD,
    LOAD,
) = range(37)


def fused_fits(mesh):
    return mesh.shape["ctx"] == CTX and mesh.shape["wsh"] == GROUP


def tn(left, right):
    return lax.dot_general(
        left, right, (((0,), (0,)), ((), ())), preferred_element_type=jnp.float32
    )


def norm_parts(value):
    mean = jnp.mean(value, axis=-1, keepdims=True)
    centered = value - mean
    spread = jnp.mean(centered * centered, axis=-1, keepdims=True)
    inverse = lax.rsqrt(spread + EPSILON)
    return centered * inverse, inverse


def norm_back(upstream_gained, normal, inverse):
    return (
        upstream_gained
        - jnp.mean(upstream_gained, axis=-1, keepdims=True)
        - normal * jnp.mean(upstream_gained * normal, axis=-1, keepdims=True)
    ) * inverse


GELU_C = math.sqrt(2.0 / math.pi)


class Numbers:
    def __init__(self):
        self.count = 0
        self.table = {}

    def take(self, key, size=1):
        if key not in self.table:
            self.table[key] = self.count
            self.count += size
        return self.table[key]


def scratch_table():
    s = types.SimpleNamespace()
    s.full = {k: pltpu.VMEM((GROUP, *WEIGHT_SHAPES[k]), BF) for k in SECOND_WAY}
    s.turned = pltpu.VMEM((SLICE, D), BF)
    s.head_weight = pltpu.VMEM((3 * HW, D), BF)
    s.tall_bias = pltpu.VMEM((SLICE, ROWS), F32)
    s.head_bias = pltpu.VMEM((3 * HW, ROWS), F32)
    s.x = pltpu.VMEM((ROWS, D), BF)
    s.xt = pltpu.VMEM((CTX, D, ROWS), BF)
    s.teacher = pltpu.VMEM((ROWS, D), BF)
    s.small = pltpu.VMEM((GROUP, 16, D), BF)
    s.vectors = pltpu.VMEM((16, D), F32)
    s.kv = pltpu.VMEM((CTX, 2 * HW, ROWS), BF)
    s.q = pltpu.VMEM((4, HW, ROWS), BF)
    s.weights = pltpu.VMEM((CTX, HEADS, ROWS, 4 * ROWS), F32)
    s.mix = pltpu.VMEM((HEADS, HD, 4 * ROWS), F32)
    s.total = pltpu.VMEM((HEADS, 8, 4 * ROWS), F32)
    s.ctx_send = pltpu.VMEM((4, HW, ROWS), BF)
    s.ctx = pltpu.VMEM((4, HW, ROWS), BF)
    s.inner = pltpu.VMEM((4, ROWS, D), F32)
    s.act = pltpu.VMEM((4, ROWS, D), BF)
    s.first = pltpu.VMEM((ROWS, D), F32)
    s.keep = pltpu.VMEM((ROWS, D), F32)
    s.inverse = pltpu.VMEM((ROWS, 128), F32)
    s.set_low = pltpu.VMEM((ROWS, D), BF)
    s.ag_half = pltpu.VMEM((2, ROWS, 384), BF)
    s.bg = pltpu.VMEM((ROWS, D), BF)
    s.set_all = pltpu.VMEM((GROUP, ROWS, D), BF)
    s.ctx_all = pltpu.VMEM((GROUP, 2, HW, ROWS), BF)
    s.ag_all = pltpu.VMEM((GROUP, ROWS, 384), BF)
    s.inner_all = pltpu.VMEM((GROUP * ROWS, D), F32)
    s.act_all = pltpu.VMEM((GROUP * ROWS, D), BF)
    s.bg_all = pltpu.VMEM((GROUP, ROWS, D), BF)
    s.cg_send = pltpu.VMEM((4, HW, ROWS), BF)
    s.cg = pltpu.VMEM((4, HW, ROWS), BF)
    s.wg = pltpu.VMEM((HEADS, HD, 4 * ROWS), BF)
    s.dkv = pltpu.VMEM((2, 4, 2 * HW, ROWS), BF)
    s.dkv_pair = pltpu.VMEM((4, 2 * HW, ROWS), BF)
    s.grads = pltpu.VMEM((HEAD_COLS, 4 * ROWS), BF)
    s.dx_send = pltpu.VMEM((4, ROWS, D), BF)
    s.dx_end = pltpu.VMEM((3, ROWS, D), BF)
    s.dx_middle = pltpu.VMEM((2, ROWS, D), BF)
    s.dx_got = pltpu.VMEM((2, ROWS, D), BF)
    s.dx_back = pltpu.VMEM((ROWS, D), BF)
    s.dx_last = pltpu.VMEM((ROWS, D), BF)
    s.column = pltpu.VMEM((D, ROWS), F32)
    s.heads = pltpu.VMEM((2, 2, HW, HEAD_COLS), BF)
    s.heads_core = pltpu.VMEM((2, HW, HEAD_COLS), BF)
    s.heads_sum = pltpu.VMEM((2, HW, HEAD_COLS), BF)
    s.heads_x = pltpu.VMEM((HW, HEAD_COLS), BF)
    s.heads_row = pltpu.VMEM((2, HW // 2, HEAD_COLS), BF)
    s.heads_y = pltpu.VMEM((HW // 2, HEAD_COLS), BF)
    s.heads_done = pltpu.VMEM((4, HW // 2, HEAD_COLS), BF)
    s.part = [pltpu.VMEM((2, 2, *shape), BF) for shape in LOTS]
    def lots(*dims):
        return [
            pltpu.VMEM((*dims[1 if k in LOT_PAIR else 0], *shape), BF) for k, shape in enumerate(LOTS)
        ]

    steps = [((2, 2), (2,)), ((2,), (2,)), ((), ())]
    s.got = [list(lot) for lot in zip(*(lots(*step) for step in steps))]
    s.sum = [list(lot) for lot in zip(*(lots(*step) for step in steps[:2]))]
    s.own = {k: pltpu.VMEM(LOTS[k], BF) for k in LOT_IN}
    s.done = [pltpu.VMEM((2, 2, *shape), BF) for shape in LOTS]
    s.smalls = pltpu.VMEM((GROUP, 16, HW), F32)
    s.sg = pltpu.VMEM((16, D), F32)
    s.sg_all = pltpu.VMEM((16, D), F32)
    s.sg_rows = pltpu.VMEM((2, 8, D), F32)
    s.sg_w = pltpu.VMEM((GROUP, 16, D), F32)
    s.sg_z = pltpu.VMEM((4, 8, D), F32)
    s.sg_y = pltpu.VMEM((2, 8, D), F32)
    s.out_low = pltpu.VMEM((ROWS, D), BF)
    return vars(s)


LOCAL_SEMS = 32
REMOTE_SEMS = 240


def is_memory(item):
    return not isinstance(item, (dict, list))


def scratch_shapes():
    return jax.tree.flatten(scratch_table(), is_leaf=is_memory)


def fused_kernel(*refs):
    (tokens, teacher), shards = refs[:2], refs[2:8]
    lengths, valid = refs[8:10]
    biases = refs[10:19]
    output, input_grad_out = refs[19:21]
    grad_o, *grad_in, grad_out = refs[21:25]
    heads_out, smalls_out, rows_out = refs[25:28]
    flat, shape = scratch_shapes()
    S = types.SimpleNamespace(**jax.tree.unflatten(shape, refs[28 : 28 + len(flat)]))
    send_sems, recv_sems, local_sems = refs[28 + len(flat) :]

    c = lax.axis_index("ctx")
    w = lax.axis_index("wsh")
    a, b = c // 2, c % 2
    x, core = w // 2, w % 2

    numbers = Numbers()
    locals_ = Numbers()
    started = []

    def bit_xor(value, j):
        out = value
        bit = 1
        while bit <= j:
            if j & bit:
                has = (value // bit) % 2
                out = out + bit * (1 - 2 * has)
            bit *= 2
        return out

    at_end = a * (3 - a) == 0
    roles, sent_by_role = [None], []

    def only(end):
        def run(action):
            roles.append(end)
            pl.when(at_end if end else jnp.logical_not(at_end))(action)
            roles.pop()

        return run

    def remote(key, src, dst, c_bits, w_bits, offset=0, size=1, to=None, like=None):
        number = numbers.take(key, size) + offset
        c_to, w_to = bit_xor(c, c_bits), bit_xor(w, w_bits) if to is None else to
        copy = pltpu.make_async_remote_copy(
            src_ref=src,
            dst_ref=dst,
            send_sem=send_sems.at[number],
            recv_sem=recv_sems.at[number],
            device_id={"ctx": c_to, "wsh": w_to},
            device_id_type=MESH,
        )
        copy.start()
        if roles[-1] is None:
            started.append(copy)
        else:
            sent_by_role.append((roles[-1], like, number))

    def arrived(key, landing, offset=0):
        number = numbers.take(key) + offset
        pltpu.make_async_copy(landing, landing, recv_sems.at[number]).wait()

    def local(key, src, dst):
        copy = pltpu.make_async_copy(src, dst, local_sems.at[locals_.take(key)])
        copy.start()
        return copy

    peers = [(c, bit_xor(w, j)) for j in (1, 2, 3)]
    peers += [(bit_xor(c, j), w) for j in range(1, CTX)]
    peers += [(bit_xor(c, 1), bit_xor(w, 1))]

    def bit(value, mask):
        return (value // mask) % 2

    first_col = pl.multiple_of((3 * a) // 2 * 128, 128)
    first_row = pl.multiple_of(a % 2 * 64, 64)

    def shard(name):
        if name < PART_Q:
            return shards[name]
        return shards[name - PART_Q].at[:, pl.ds(first_col, SLICE)]

    loads = {TOKENS: local(TOKENS, tokens.at[0], S.x)}
    for name in (PART_K, PART_V, PART_Q, O, IN, OUT):
        loads[name] = local((LOAD, name), shard(name), S.full[name].at[w])
    loads[TEACHER] = local(TEACHER, teacher.at[0], S.teacher)

    barrier = pltpu.get_barrier_semaphore()
    for c_to, w_to in peers:
        pl.semaphore_signal(
            barrier, inc=1, device_id={"ctx": c_to, "wsh": w_to}, device_id_type=MESH
        )
    loads[TOKENS].wait()
    x_low = S.x[...]
    S.xt[c] = x_low.T
    bias_rows = [row[...].astype(F32).reshape(1, HW) for row in biases[:8]]
    tall = jnp.concatenate(bias_rows, axis=0)
    valid_high = (valid[0] // 64).astype(F32)
    valid_low = (valid[0] % 64).astype(F32)
    wide_rows = [biases[8][...].astype(F32).reshape(1, D)]
    wide_rows += [jnp.full((1, D), 64.0, F32) * valid_high, jnp.full((1, D), 1.0, F32) * valid_low]
    wide_rows += [jnp.zeros((5, D), F32)]
    S.small[w, :, 0:HW] = jnp.concatenate(
        [tall, jnp.concatenate(wide_rows, axis=0)[:, 0:HW]], axis=0
    ).astype(BF)
    S.small[w, 8:16, HW:D] = jnp.concatenate(wide_rows, axis=0)[:, HW:D].astype(BF)

    pl.semaphore_wait(barrier, len(peers))

    def mine(name):
        return bit(c, SECOND_WAY[name])

    def pieces(name):
        tall, across = PIECES.get(name, (1, 1))
        return range(tall * across)

    def piece(name, which, number):
        rows, cols = WEIGHT_SHAPES[name]
        tall, across = PIECES.get(name, (1, 1))
        high, broad = rows // 2 // tall, cols // across
        row = which * (rows // 2) + number // across * high
        return pl.ds(pl.multiple_of(row, 16), high), slice(
            number % across * broad, (number % across + 1) * broad
        )

    def send_core(name):
        remote((WEIGHT_CORE, name), shard(name), S.full[name].at[w], 0, 1)

    def send_x(name):
        for i in pieces(name):
            rows, cols = piece(name, mine(name), i)
            if name < PART_Q:
                source = shards[name].at[rows, cols]
            else:
                source = shards[name - PART_Q].at[rows, pl.ds(first_col, SLICE)]
            remote((WEIGHT_X, name, i), source, S.full[name].at[w, rows, cols], 0, 2)

    for name in (PART_K, PART_V, PART_Q):
        send_x(name)
        send_core(name)
    for j in (1, 2, 3):
        remote((SMALL, j), S.small.at[w], S.small.at[w], 0, j)
    remote((X_LINE, 1), S.xt.at[c], S.xt.at[c], 2, 0)

    @only(False)
    def x_to_middle():
        remote((X_LINE, 3), S.xt.at[c], S.xt.at[c], 6, 0, like=lambda: S.xt.at[0])

    for name in (O, IN, OUT):
        send_x(name)
        send_core(name)

    def pump_x(name, number=0):
        slot = S.full[name].at[bit_xor(w, 2), *piece(name, mine(name), number)]
        arrived((WEIGHT_X, name, number), slot)
        remote((WEIGHT_SECOND, name, number), slot, slot, SECOND_WAY[name], 0)
        remote((WEIGHT_CORE_X, name, number), slot, slot, 0, 1)

    def pump_second(name, number=0):
        slot = S.full[name].at[bit_xor(w, 2), *piece(name, 1 - mine(name), number)]
        arrived((WEIGHT_SECOND, name, number), slot)
        remote((WEIGHT_CORE_SECOND, name, number), slot, slot, 0, 1)

    def weight_ready(name, numbers_=(0,), first=True):
        full = S.full[name]
        if first:
            loads[name].wait()
            arrived((WEIGHT_CORE, name), full.at[bit_xor(w, 1)])
        for i in numbers_:
            near = full.at[bit_xor(w, 3), *piece(name, mine(name), i)]
            far = full.at[bit_xor(w, 3), *piece(name, 1 - mine(name), i)]
            arrived((WEIGHT_CORE_X, name, i), near)
            arrived((WEIGHT_CORE_SECOND, name, i), far)

    def square(name):
        return S.full[name][...].reshape(D, D)

    starts, running = [], 0
    for i in range(lengths.shape[1]):
        starts.append(running)
        running = running + lengths[0, i]
    limit = valid[0]

    def code_of(position):
        code = jnp.zeros(position.shape, jnp.int32)
        for start in starts:
            code = code + (start <= position).astype(jnp.int32)
        return 2 * code + (position < limit).astype(jnp.int32)

    lane = lax.broadcasted_iota(jnp.int32, (1, 4 * ROWS), 1)
    query_code = code_of((2 * (lane // ROWS) + b) * ROWS + lane % ROWS)

    def key_code(block):
        return code_of(block * ROWS + lax.broadcasted_iota(jnp.int32, (ROWS, 1), 0))

    own_live = c * ROWS + lax.broadcasted_iota(jnp.int32, (ROWS, 1), 0) < limit

    def block_on(j, pair):
        return 2 * bit_xor(a, j) + pair

    def pass_x(key, j, onward, bits):
        block = S.xt.at[block_on(j, b)]
        arrived((key, j), block)
        remote(onward, block, block, bits, 0, like=lambda: S.xt.at[0])

    def vector(row):
        return S.vectors[row : row + 1, :]

    def to_group(key, source_of, everywhere):
        for j in (1, 2, 3):
            to = bit_xor(w, j)
            remote((*key, j), source_of(to), everywhere.at[w], 0, j)

    def from_group(key, everywhere):
        for j in (1, 2, 3):
            arrived((*key, j), everywhere.at[bit_xor(w, j)])

    def to_near(key, source, everywhere):
        for j in (1, 2):
            remote((key, j), source, everywhere.at[w], 0, j)

    def pass_to_core(key, everywhere):
        slot = everywhere.at[bit_xor(w, 2)]
        arrived((key, 2), slot)
        remote((key, 3), slot, slot, 0, 1)

    def from_near(key, everywhere):
        for j in (1, 3):
            arrived((key, j), everywhere.at[bit_xor(w, j)])

    def lanes(parts):
        return jnp.concatenate(parts, axis=1)

    finishing = []

    def small_vectors():
        for j in (1, 2, 3):
            arrived((SMALL, j), S.small.at[bit_xor(w, j)])
        S.vectors[0:8, :] = jnp.concatenate(
            [S.small[i, 0:8, 0:HW].astype(F32) for i in range(GROUP)], axis=1
        )
        small = [S.small[i, 8:16, :].astype(F32) for i in range(GROUP)]
        S.vectors[8:16, :] = jnp.concatenate(
            [part[0:1] for part in small]
            + [sum(part[1:2] + part[2:3] for part in small), jnp.zeros((3, D), F32)],
            axis=0,
        )

    def pass_near_end():
        arrived((X_LINE, 1), S.xt.at[block_on(1, b)])

        @only(False)
        def to_other_middle():
            block = S.xt.at[block_on(1, b)]
            remote((X_LINE, 2), block, block, 6, 0, like=lambda: S.xt.at[0])

    def pass_middle():
        @only(False)
        def to_near_end():
            pass_x(X_LINE, 3, (X_EDGE, 2), 2)

    def pass_far_end():
        @only(False)
        def to_near_end():
            pass_x(X_LINE, 2, (X_EDGE, 3), 2)

    def head_weights():
        for name in (PART_K, PART_V, PART_Q):
            weight_ready(name)
        for i, (name, bias) in enumerate(((PART_K, None), (PART_V, 1), (PART_Q, 0))):
            rows = slice(HW * i, HW * (i + 1))
            S.turned[...] = S.full[name][...].reshape(D, SLICE).T
            S.head_weight[rows, :] = S.turned[pl.ds(first_row, HW), :]
            if bias is None:
                S.head_bias[rows, :] = jnp.zeros((HW, ROWS), F32)
            else:
                row = S.vectors[bias : bias + 1, pl.ds(first_col, SLICE)]
                S.tall_bias[...] = jnp.broadcast_to(row, (ROWS, SLICE)).T
                S.head_bias[rows, :] = S.tall_bias[pl.ds(first_row, HW), :]

    def project(j):
        if j > 1:

            @only(True)
            def from_middle():
                arrived((X_EDGE, j), S.xt.at[block_on(j, b)])

        block = block_on(j, b)
        out = matmul(S.head_weight[...], S.xt[block]) + S.head_bias[...]
        S.kv[block] = out[0 : 2 * HW].astype(BF)
        S.q[block // 2] = out[2 * HW :].astype(BF)
        remote((KEY_VALUE, j), S.kv.at[block], S.kv.at[block], 1, 0)

    score_scale = 1.0 / math.sqrt(HD)

    def wide(ref, h):
        return lanes([ref[i, HD * h : HD * (h + 1), :] for i in range(4)])

    def attend_block(block):
        allowed = key_code(block) == query_code
        for h in range(HEADS):
            scores = tn(S.kv[block, HD * h : HD * (h + 1), :], wide(S.q, h)) * score_scale
            weights = jnp.exp(jnp.where(allowed, scores, MASKED))
            S.weights[block, h] = weights
            S.total[h, 0:1, :] += jnp.sum(weights, axis=0, keepdims=True)
            value_t = S.kv[block, HW + HD * h : HW + HD * (h + 1), :]
            S.mix[h] += matmul(value_t, weights.astype(BF))

    def attend_line():
        S.mix[...] = jnp.zeros(S.mix.shape, F32)
        S.total[...] = jnp.zeros(S.total.shape, F32)

        @pl.loop(0, 4)
        def every_block(i):
            attend_block(2 * i + b)

    def attend_pair(j):
        arrived((KEY_VALUE, j), S.kv.at[block_on(j, 1 - b)])
        attend_block(block_on(j, 1 - b))

    def send_context():
        for h in range(HEADS):
            context_t = (S.mix[h] / S.total[h, 0:1, :]).astype(BF)
            for i in range(4):
                S.ctx_send[i, HD * h : HD * (h + 1), :] = context_t[:, ROWS * i : ROWS * (i + 1)]
        for j in (1, 2, 3):
            to = bit_xor(a, j)
            remote((CONTEXT, j), S.ctx_send.at[to], S.ctx.at[a], 2 * j, 0)
        S.ctx[a] = S.ctx_send[a]

    def first_norm():
        weight_ready(O)
        for j in (1, 2, 3):
            arrived((CONTEXT, j), S.ctx.at[bit_xor(a, j)])
        attn = tn(S.ctx[...].reshape(D, ROWS), square(O)) + vector(2)
        normal_one, inverse_one = norm_parts(S.x[...].astype(F32) + attn)
        settled = normal_one * vector(3) + vector(4)
        S.first[...] = normal_one
        S.inverse[...] = jnp.broadcast_to(inverse_one, (ROWS, 128))
        S.keep[...] = settled
        S.set_low[...] = settled.astype(BF)
        to_near(SETTLED_ALL, S.set_low, S.set_all)
        S.set_all[w] = S.set_low[...]
        to_group((CONTEXT_ALL,), lambda to: S.ctx.at[pl.ds(2 * (to // 2), 2)], S.ctx_all)
        S.ctx_all[w] = S.ctx[pl.ds(2 * x, 2)]

    def pass_settled():
        pass_to_core(SETTLED_ALL, S.set_all)

    def gelu(inner):
        return 0.5 * inner * (1.0 + jnp.tanh(GELU_C * (inner + 0.044715 * inner * inner * inner)))

    def gelu_slope(inner):
        squared = inner * inner
        bend = jnp.tanh(GELU_C * (inner + 0.044715 * squared * inner))
        return 0.5 * (1.0 + bend) + 0.5 * inner * (1.0 - bend * bend) * (
            GELU_C * (1.0 + 3 * 0.044715 * squared)
        )

    def feed_in(t):
        weight_ready(IN, (t,), t == 0)
        w_part = S.full[IN][:, :, D * t : D * (t + 1)].reshape(D, D)
        inner = matmul(S.set_low[...], w_part) + vector(8 + t)
        S.inner[t] = inner
        S.act[t] = gelu(inner).astype(BF)

    def note(row, value):
        S.sg[row : row + 1, :] = jnp.sum(value.astype(F32), axis=0, keepdims=True)

    def result_and_loss():
        weight_ready(OUT, range(4))
        branch = vector(5)
        for t in range(4):
            branch = branch + matmul(S.act[t], S.full[OUT][t])
        normal_two, inverse_two = norm_parts(S.keep[...] + branch)
        result = normal_two * vector(6) + vector(7)
        S.out_low[...] = result.astype(BF)
        finishing.append(local(OUTPUT, S.out_low, output))
        loads[TEACHER].wait()
        diff = jnp.where(own_live, result - S.teacher[...].astype(F32), 0.0)
        count = vector(12)
        upstream = diff * ((ROWS * CTX * GROUP) / count)
        d_second = norm_back(upstream * vector(6), normal_two, inverse_two)
        S.bg[...] = d_second.astype(BF)
        to_near(BRANCH_GRAD_ALL, S.bg, S.bg_all)
        S.bg_all[w] = S.bg[...]
        S.keep[...] = d_second
        S.sg[...] = jnp.zeros((16, D), F32)
        note(12, diff * diff)
        S.sg[13:14, :] = count * (1.0 / (CTX * GROUP))
        note(6, upstream * normal_two)
        note(7, upstream)
        note(5, S.bg[...])

    def feed_back():
        d_settled = S.keep[...]
        for t in range(4):
            d_act = right_product(S.bg[...], S.full[OUT][t])
            inner_grad = (d_act * gelu_slope(S.inner[t])).astype(BF)
            note(8 + t, inner_grad)
            w_part = S.full[IN][:, :, D * t : D * (t + 1)].reshape(D, D)
            d_settled = d_settled + right_product(inner_grad, w_part)
        S.keep[...] = d_settled

    def pass_branch_grad():
        pass_to_core(BRANCH_GRAD_ALL, S.bg_all)

    def first_norm_back():
        d_settled, normal_one = S.keep[...], S.first[...]
        d_first = norm_back(d_settled * vector(3), normal_one, S.inverse[:, 0:1])
        attn_grad = d_first.astype(BF)
        context_grad = right_product(attn_grad, square(O)).T.astype(BF)
        for i in range(4):
            S.cg_send[i] = context_grad[HW * i : HW * (i + 1), :]
        for j in (1, 2, 3):
            to = bit_xor(a, j)
            remote((CONTEXT_GRAD, j), S.cg_send.at[to], S.cg.at[a], 2 * j, 0)
        S.cg[a] = S.cg_send[a]
        for i in range(2):
            S.ag_half[i] = attn_grad[:, 384 * i : 384 * (i + 1)]
        to_group((ATTN_GRAD_ALL,), lambda to: S.ag_half.at[to % 2], S.ag_all)
        S.ag_all[w] = S.ag_half[core]
        note(3, d_settled * normal_one)
        note(4, d_settled)
        note(2, attn_grad)
        S.keep[...] = d_first

    half = a // 2

    def y_end(lot):
        got, total = S.got[lot], S.sum[lot]
        arrived((REDUCE, lot, 0), got[0])
        total[0][...] = (S.part[lot][b].astype(F32) + got[0][...].astype(F32)).astype(BF)

        @only(True)
        def to_middle():
            remote((REDUCE, lot, 1), total[0], got[1], 2, 0, like=lambda: got[1])

    def y_middle(lot):
        @only(False)
        def swap_halves():
            got, total = S.got[lot], S.sum[lot]
            arrived((REDUCE, lot, 1), got[1])
            total[1][...] = (total[0][...].astype(F32) + got[1][...].astype(F32)).astype(BF)
            there = total[1].at[1 - half]
            remote((REDUCE, lot, 2), there, got[2], 6, 0, like=lambda: got[2])

    def y_spread_middle(lot):
        part = S.done[lot].at[b, half]
        remote((SPREAD, lot, 0), part, part, 6, 0, like=lambda: S.done[lot].at[0, 0])

    def y_last(lot):
        @only(False)
        def own_half():
            got = S.got[lot][2]
            arrived((REDUCE, lot, 2), got)
            total = (S.sum[lot][1][half].astype(F32) + got[...].astype(F32)).astype(BF)
            if lot in LOT_IN:
                own, done = S.own[lot], S.done[lot]
                own[...] = total
                done[b, half, w] = own[w]
                for q in (1, 2, 3):
                    slot = done.at[b, half, w]
                    to = bit_xor(w, q)
                    remote((GROUP_X, lot, q), own.at[to], slot, 0, q, like=lambda: own.at[0])
            else:
                S.done[lot][b, half] = total
                y_spread_middle(lot)

    def y_group(lot):
        @only(False)
        def gathered():
            for q in (1, 2, 3):
                arrived((GROUP_X, lot, q), S.done[lot].at[b, half, bit_xor(w, q)])
            y_spread_middle(lot)

    def y_spread_end(lot):
        @only(False)
        def to_end():
            done = S.done[lot].at[b]
            arrived((SPREAD, lot, 0), S.done[lot].at[b, 1 - half])
            remote((SPREAD, lot, 1), done, done, 2, 0, like=lambda: S.done[lot].at[0])

    def result_of(lot):
        return grad_in[lot - LOT_IN[0]] if lot in LOT_IN else grad_out.at[lot - LOT_OUT[0]]

    def y_give(lot):
        done = S.done[lot].at[b]

        @only(True)
        def from_middle_device():
            arrived((SPREAD, lot, 1), done)

        if lot not in LOT_O:
            out = result_of(lot).at[b]
            remote((GIVE, lot), done, out, 1, 0)
            finishing.append(local((GIVE, lot), done, out))
            return
        remote((GIVE, 0), done, grad_o.at[core], 1, 0, core, 2, 2 * x + b)

        @pl.when(core == b)
        def keep_own():
            local((OWN, 0), done, grad_o.at[core])

        @pl.when(core != b)
        def give_core():
            remote((OWN, 0), done, grad_o.at[core], 0, 1)
            started.pop()

    def settle():
        for lot in LOT_PAIR[1:]:
            arrived((GIVE, lot), result_of(lot).at[1 - b])
        done = S.done[0].at[b]

        @pl.when(core == b)
        def from_chip():
            pltpu.make_async_copy(
                done, grad_o.at[core], local_sems.at[locals_.take((OWN, 0))]
            ).wait()
            arrived((OWN, 0), grad_o.at[1 - core])

        @pl.when(core != b)
        def from_partner():
            arrived((GIVE, 0), grad_o.at[0], 0)
            arrived((GIVE, 0), grad_o.at[1], 1)
            sent = numbers.take((OWN, 0))
            pltpu.make_async_copy(done, done, send_sems.at[sent]).wait()

    def reduce_start(lot):
        @only(True)
        def to_middle():
            target = S.got[lot][0]
            remote((REDUCE, lot, 0), S.part[lot], target, 2, 0, like=lambda: target)

    def reduce_middle(lot):
        @only(False)
        def swap_halves():
            got = S.got[lot][0]
            arrived((REDUCE, lot, 0), got)
            total = S.part[lot][...].astype(F32) + got[...].astype(F32)
            S.sum[lot][0][...] = total.astype(BF)
            there, target = S.sum[lot][0].at[1 - half], S.got[lot][1]
            remote((REDUCE, lot, 1), there, target, 6, 0, like=lambda: target)

    def reduce_pair(lot):
        @only(False)
        def swap_quarters():
            got = S.got[lot][1]
            arrived((REDUCE, lot, 1), got)
            total = S.sum[lot][0][half].astype(F32) + got[...].astype(F32)
            S.sum[lot][1][...] = total.astype(BF)
            there, target = S.sum[lot][1].at[1 - b], S.got[lot][2]
            remote((REDUCE, lot, 2), there, target, 1, 0, like=lambda: target)

    def reduce_last(lot):
        @only(False)
        def own_quarter():
            got = S.got[lot][2]
            arrived((REDUCE, lot, 2), got)
            total = (S.sum[lot][1][b].astype(F32) + got[...].astype(F32)).astype(BF)
            S.done[lot][half, b] = total
            part = S.done[lot].at[half, b]
            remote((SPREAD, lot, 0), part, part, 1, 0, like=lambda: S.done[lot].at[0, 0])

    def spread_middle(lot):
        @only(False)
        def swap_back():
            arrived((SPREAD, lot, 0), S.done[lot].at[half, 1 - b])
            part = S.done[lot].at[half]
            remote((SPREAD, lot, 1), part, part, 6, 0, like=lambda: S.done[lot].at[0])

    def spread_end(lot):
        @only(False)
        def to_end():
            done = S.done[lot]
            arrived((SPREAD, lot, 1), done.at[1 - half])
            part = done.at[:, b]
            remote((SPREAD, lot, 2), part, part, 2, 0, like=lambda: done.at[:, 0])

    def spread_ends(lot):
        @only(True)
        def swap_at_ends():
            done = S.done[lot]
            part = done.at[:, b]
            arrived((SPREAD, lot, 2), part)
            remote((SPREAD, lot, 3), part, part, 1, 0, like=lambda: done.at[:, 0])

    def finish_lot(lot):
        @only(True)
        def from_pair():
            arrived((SPREAD, lot, 3), S.done[lot].at[:, 1 - b])

        finishing.append(local((GIVE, lot), S.done[lot], grad_out.at[lot - LOT_OUT[0]]))

    def inner_again():
        from_near(SETTLED_ALL, S.set_all)
        settled_all = S.set_all[...].reshape(GROUP * ROWS, D)
        hidden = pl.ds(pl.multiple_of(D * w, D), D)
        S.inner_all[...] = (
            matmul(settled_all, S.full[IN][:, :, hidden].reshape(D, D))
            + S.vectors[pl.ds(8 + w, 1), :]
        )
        S.act_all[...] = gelu(S.inner_all[...]).astype(BF)

    def out_part():
        from_near(BRANCH_GRAD_ALL, S.bg_all)
        grad = tn(S.act_all[...], S.bg_all[...].reshape(GROUP * ROWS, D)).astype(BF)
        for i, lot in enumerate(LOT_OUT):
            S.part[lot][...] = grad[HW * i : HW * (i + 1)].reshape(2, 2, 48, D)
            if lot in LOT_PAIR:
                remote((REDUCE, lot, 0), S.part[lot].at[1 - b], S.got[lot][0], 1, 0)
            else:
                reduce_start(lot)

    def in_part():
        branch_grad_all = S.bg_all[...].reshape(GROUP * ROWS, D)
        inner_grad_all = (
            right_product(branch_grad_all, S.full[OUT][w]) * gelu_slope(S.inner_all[...])
        ).astype(BF)
        grad = tn(S.set_all[...].reshape(GROUP * ROWS, D), inner_grad_all).astype(BF)
        for i, lot in enumerate(LOT_IN):
            for j in range(2):
                side = grad[:, 384 * j : 384 * (j + 1)].reshape(4, 2, 2, 48, 384)
                for k in range(2):
                    S.part[lot][j, k] = side[:, k, i]
            remote((REDUCE, lot, 0), S.part[lot].at[1 - b], S.got[lot][0], 1, 0)

    def attention_back():
        for j in (1, 2, 3):
            arrived((CONTEXT_GRAD, j), S.cg.at[bit_xor(a, j)])
        for h in range(HEADS):
            grad = wide(S.cg, h).astype(F32)
            row_total = S.total[h, 0:1, :]
            S.wg[h] = (grad / row_total).astype(BF)
            S.total[h, 1:2, :] = -jnp.sum(grad * S.mix[h], axis=0, keepdims=True) / (
                row_total * row_total
            )
        S.mix[...] = jnp.zeros(S.mix.shape, F32)

        def attend_back(pair, i):
            block = 2 * i + pair
            for h in range(HEADS):
                key_rows = slice(HD * h, HD * (h + 1))
                value_rows = slice(HW + HD * h, HW + HD * (h + 1))
                weights = S.weights[block, h]
                grad = S.wg[h]
                weight_grad = tn(S.kv[block, value_rows, :], grad) + S.total[h, 1:2, :]
                score_grad = (weights * weight_grad).astype(BF)
                S.mix[h] += matmul(S.kv[block, key_rows, :], score_grad)
                S.dkv[pair, i, key_rows, :] = (
                    right_product(wide(S.q, h), score_grad) * score_scale
                ).astype(BF)
                value_grad = right_product(grad, weights.astype(BF))
                S.dkv[pair, i, value_rows, :] = value_grad.astype(BF)

        @pl.loop(0, CTX)
        def every_block(block):
            attend_back(block % 2, block // 2)

        remote((KEY_VALUE_GRAD,), S.dkv.at[1 - b], S.dkv_pair, 1, 0)
        for h in range(HEADS):
            rows = slice(2 * HW + HD * h, 2 * HW + HD * (h + 1))
            S.grads[rows, :] = (S.mix[h] * score_scale).astype(BF)
        S.grads[3 * HW :, :] = jnp.zeros((HEAD_COLS - 3 * HW, 4 * ROWS), BF)

    def o_part():
        from_group((CONTEXT_ALL,), S.ctx_all)
        from_group((ATTN_GRAD_ALL,), S.ag_all)
        context_all = lanes([S.ctx_all[i].reshape(384, ROWS) for i in range(GROUP)])
        grad = matmul(context_all, S.ag_all[...].reshape(GROUP * ROWS, 384))
        S.part[0][...] = grad.astype(BF).reshape(2, 2, 96, 384)
        remote((REDUCE, 0, 0), S.part[0].at[1 - b], S.got[0][0], 1, 0)

    def heads_part():
        arrived((KEY_VALUE_GRAD,), S.dkv_pair)
        for i in range(4):
            S.grads[0 : 2 * HW, ROWS * i : ROWS * (i + 1)] = (
                S.dkv[b, i].astype(F32) + S.dkv_pair[i].astype(F32)
            ).astype(BF)
        own_inputs = lanes([S.xt[2 * i + b] for i in range(4)])
        heads = right_product(own_inputs, S.grads[...]).astype(BF)
        S.heads[...] = heads.reshape(2, 2, HW, HEAD_COLS)
        for i in range(2):
            remote((HEADS_CORE, i), S.heads.at[i, 1 - core], S.heads_core.at[i], 0, 1)

    def input_parts():
        parts = tn(S.grads[0 : 3 * HW, :], S.head_weight[...])
        S.dx_send[...] = parts.astype(BF).reshape(4, ROWS, D)

        @only(True)
        def to_middle():
            for j in (1, 2, 3):
                source, target = S.dx_send.at[bit_xor(a, j)], S.dx_end.at[j - 1]
                remote((INPUT_PARTS, j), source, target, 2, 0, like=lambda: S.dx_end.at[0])

    def input_middle():
        @only(False)
        def to_other_middle():
            for j in (1, 2, 3):
                arrived((INPUT_PARTS, j), S.dx_end.at[j - 1])
            for i, j in enumerate((3, 2)):
                both = S.dx_send[bit_xor(a, j)].astype(F32) + S.dx_end[i + 1].astype(F32)
                S.dx_middle[i] = both.astype(BF)
            remote((INPUT_PARTS, 4), S.dx_middle, S.dx_got, 6, 0, like=lambda: S.dx_middle)

    def input_end():
        @only(False)
        def to_near_end():
            arrived((INPUT_PARTS, 4), S.dx_got)
            both = S.dx_send[bit_xor(a, 1)].astype(F32) + S.dx_got[1].astype(F32)
            S.dx_back[...] = both.astype(BF)
            remote((INPUT_PARTS, 5), S.dx_back, S.dx_last, 2, 0, like=lambda: S.dx_back)

    def vectors_group():
        S.column[...] = jnp.zeros((D, ROWS), F32)
        heads_rows = pl.ds(pl.multiple_of(HW * a, HW), HW)
        for row, first in ((1, HW), (0, 2 * HW)):
            sums = jnp.sum(S.grads[first : first + HW, :].astype(F32), axis=1, keepdims=True)
            S.column[heads_rows, :] = jnp.broadcast_to(sums, (HW, ROWS))
            S.sg[row : row + 1, :] = S.column[...].T[0:1, :]
        for j in (1, 2, 3):
            remote((VECTORS_W, j), S.sg, S.sg_w.at[w], 0, j)
        S.sg_w[w] = S.sg[...]

    own_rows = pl.ds(pl.multiple_of(8 * core, 8), 8)

    def vectors_line():
        for j in (1, 2, 3):
            arrived((VECTORS_W, j), S.sg_w.at[bit_xor(w, j)])
        S.sg_all[...] = (S.sg_w[0] + S.sg_w[1]) + (S.sg_w[2] + S.sg_w[3])
        S.sg_z[0] = S.sg_all[own_rows, :]

        @only(True)
        def to_middle():
            remote((VECTORS_Z, 1), S.sg_z.at[0], S.sg_z.at[1], 2, 0, like=lambda: S.sg_z.at[1])

    def vectors_middle():
        @only(False)
        def to_other_middle():
            arrived((VECTORS_Z, 1), S.sg_z.at[1])
            S.sg_z[2] = S.sg_z[0] + S.sg_z[1]
            remote((VECTORS_Z, 2), S.sg_z.at[2], S.sg_z.at[3], 6, 0, like=lambda: S.sg_z.at[2])

    def vectors_end():
        @only(False)
        def to_end():
            arrived((VECTORS_Z, 2), S.sg_z.at[3])
            S.sg_y[b] = S.sg_z[2] + S.sg_z[3]
            whole = S.sg_y.at[b]
            remote((VECTORS_Z, 3), whole, whole, 2, 0, like=lambda: S.sg_y.at[0])

    def vectors_pair():
        @only(True)
        def from_middle():
            arrived((VECTORS_Z, 3), S.sg_y.at[b])

        remote((VECTORS_Y,), S.sg_y.at[b], S.sg_y.at[b], 1, 0)

    def vectors_core():
        arrived((VECTORS_Y,), S.sg_y.at[1 - b])
        S.sg_rows[core] = S.sg_y[0] + S.sg_y[1]
        remote((VECTORS_CORE,), S.sg_rows.at[core], S.sg_rows.at[core], 0, 1)

    def vectors_done():
        arrived((VECTORS_CORE,), S.sg_rows.at[1 - core])
        everything = S.sg_rows[...].reshape(16, D)
        for i in range(4):
            S.smalls[i] = everything[:, HW * i : HW * (i + 1)]
        finishing.append(local((VECTORS_Y,), S.smalls, smalls_out))
        finishing.append(local((VECTORS_Z,), S.sg_rows, rows_out))

    def heads_x():
        for i in range(2):
            arrived((HEADS_CORE, i), S.heads_core.at[i])
        for i in range(2):
            S.heads_sum[i] = (S.heads[i, core].astype(F32) + S.heads_core[i].astype(F32)).astype(BF)
        remote((HEADS_X,), S.heads_sum.at[1 - x], S.heads_x, 0, 2)

    def heads_y():
        arrived((HEADS_X,), S.heads_x)
        S.heads_row[...] = (
            (S.heads_sum[x].astype(F32) + S.heads_x[...].astype(F32))
            .astype(BF)
            .reshape(2, HW // 2, HEAD_COLS)
        )
        remote((HEADS_Y,), S.heads_row.at[1 - b], S.heads_y, 1, 0)

    def heads_line():
        arrived((HEADS_Y,), S.heads_y)
        S.heads_done[a] = (S.heads_row[b].astype(F32) + S.heads_y[...].astype(F32)).astype(BF)
        own = S.heads_done.at[a]
        remote((HEADS_LINE, 1), own, own, 2, 0)

        @only(False)
        def to_other_middle():
            remote((HEADS_LINE, 3), own, own, 6, 0, like=lambda: S.heads_done.at[0])

    def pass_heads(key, j, onward, bits):
        part = S.heads_done.at[bit_xor(a, j)]
        if key is not None:
            arrived((key, j), part)
        remote(onward, part, part, bits, 0, like=lambda: S.heads_done.at[0])

    def heads_near_end():
        arrived((HEADS_LINE, 1), S.heads_done.at[bit_xor(a, 1)])

        @only(False)
        def to_other_middle():
            pass_heads(None, 1, (HEADS_LINE, 2), 6)

    def heads_middle():
        @only(False)
        def to_near_end():
            pass_heads(HEADS_LINE, 3, (HEADS_EDGE, 2), 2)

    def heads_far_end():
        @only(False)
        def to_near_end():
            pass_heads(HEADS_LINE, 2, (HEADS_EDGE, 3), 2)

    def heads_pair():
        @only(True)
        def from_middle():
            for j in (2, 3):
                arrived((HEADS_EDGE, j), S.heads_done.at[bit_xor(a, j)])

        remote((HEADS_PAIR,), S.heads_done, heads_out.at[b], 1, 0)
        finishing.append(local((HEADS_PAIR,), S.heads_done, heads_out.at[b]))

    def input_done():
        S.first[...] = S.keep[...] + S.dx_send[a].astype(F32)

        @only(True)
        def at_end():
            arrived((INPUT_PARTS, 5), S.dx_last)
            S.first[...] += S.dx_last[...].astype(F32)

        @only(False)
        def in_middle():
            S.first[...] += S.dx_end[0].astype(F32) + S.dx_got[0].astype(F32)

        finishing.append(local(INPUT_GRAD, S.first, input_grad_out))

    marked = []

    def mark():
        marked.extend(started)
        started.clear()

    def retire():
        for copy in marked:
            copy.wait_send()
        marked.clear()

    for step, *lot in (
        (pass_near_end,),
        (pump_x, PART_K),
        (pass_middle,),
        (pump_x, PART_Q),
        (pump_x, PART_V),
        (pump_second, PART_Q),
        (pump_x, O),
        (small_vectors,),
        (pass_far_end,),
        (pump_second, PART_V),
        (pump_second, PART_K),
        (head_weights,),
        (project, 0),
        (project, 2),
        (project, 1),
        (pump_x, IN, 0),
        (pump_x, IN, 1),
        (project, 3),
        (pump_second, O),
        (attend_line,),
        (attend_pair, 0),
        (pump_x, IN, 3),
        (attend_pair, 1),
        (attend_pair, 2),
        (pump_x, OUT, 0),
        (pump_second, IN, 1),
        (attend_pair, 3),
        (send_context,),
        (pump_x, IN, 2),
        (pump_x, OUT, 1),
        (pump_second, IN, 0),
        (pump_x, OUT, 2),
        (pump_second, OUT, 1),
        (pump_second, IN, 3),
        (pump_x, OUT, 3),
        (first_norm,),
        (feed_in, 0),
        (pump_second, OUT, 0),
        (feed_in, 1),
        (pump_second, OUT, 2),
        (pump_second, IN, 2),
        (feed_in, 2),
        (pump_second, OUT, 3),
        (feed_in, 3),
        (result_and_loss,),
        (pass_settled,),
        (feed_back,),
        (first_norm_back,),
        (mark,),
        (inner_again,),
        (pass_branch_grad,),
        (out_part,),
        (attention_back,),
        (reduce_middle, 5),
        (reduce_pair, 5),
        (y_end, 3),
        (o_part,),
        (reduce_middle, 6),
        (y_middle, 3),
        (reduce_last, 5),
        (in_part,),
        (y_last, 3),
        (y_end, 4),
        (heads_part,),
        (y_middle, 4),
        (y_end, 0),
        (vectors_group,),
        (spread_middle, 5),
        (y_spread_end, 3),
        (heads_x,),
        (y_last, 4),
        (y_middle, 0),
        (vectors_line,),
        (vectors_middle,),
        (spread_end, 5),
        (y_spread_end, 4),
        (y_end, 1),
        (y_last, 0),
        (heads_y,),
        (y_middle, 1),
        (reduce_pair, 6),
        (spread_ends, 5),
        (retire,),
        (vectors_end,),
        (y_spread_end, 0),
        (heads_line,),
        (y_end, 2),
        (reduce_last, 6),
        (y_give, 3),
        (y_give, 4),
        (y_last, 1),
        (vectors_pair,),
        (y_give, 0),
        (heads_near_end,),
        (heads_middle,),
        (y_group, 1),
        (heads_far_end,),
        (y_middle, 2),
        (input_parts,),
        (spread_middle, 6),
        (heads_pair,),
        (y_last, 2),
        (y_spread_end, 1),
        (spread_end, 6),
        (y_give, 1),
        (y_group, 2),
        (spread_ends, 6),
        (input_middle,),
        (y_spread_end, 2),
        (y_give, 2),
        (vectors_core,),
        (finish_lot, 5),
        (input_end,),
        (input_done,),
        (vectors_done,),
        (finish_lot, 6),
    ):
        step(*lot)

    arrived((HEADS_PAIR,), heads_out.at[1 - b])
    settle()
    for copy in finishing:
        copy.wait()
    for copy in started:
        copy.wait_send()
    for end in (True, False):

        @only(end)
        def sent():
            for role, like, number in sent_by_role:
                if role == end:
                    source = like()
                    pltpu.make_async_copy(source, source, send_sems.at[number]).wait()


def finish_kernel(*refs):
    g_o, g_in0, g_in1, g_out, heads, output, input_grad, smalls, rows = refs[:9]
    r_q, r_k, r_v, r_o, r_in, r_out, r_output, r_input = refs[9:17]
    vectors, inner_bias, loss = refs[17:25], refs[25], refs[26]
    low_o, low_in0, low_in1, low_out, low_heads, low_output, full_input = refs[27:34]
    f_q, f_k, f_v, f_o, f_in, f_out, load_sems, store_sems = refs[34:]

    def load(number, source, target):
        copy = pltpu.make_async_copy(source, target, load_sems.at[number])
        copy.start()
        return copy

    stores = []

    def store(source, target):
        copy = pltpu.make_async_copy(source, target, store_sems.at[len(stores)])
        copy.start()
        stores.append(copy)

    out_loads = [load(i, g_out.at[i], low_out.at[i]) for i in range(4)]
    in_loads = [load(4, g_in0, low_in0), load(5, g_in1, low_in1)]
    heads_load = load(6, heads, low_heads)
    o_load = load(7, g_o, low_o)
    output_load = load(8, output, low_output)
    input_load = load(9, input_grad, full_input)

    for i in range(4):
        out_loads[i].wait()
        rows_here = pl.ds(HW * i, HW)
        f_out[rows_here, :] = low_out[i].reshape(HW, D).astype(F32)
        store(f_out.at[rows_here], r_out.at[rows_here])
    for copy in in_loads:
        copy.wait()
    for z in range(2):
        for k, source in enumerate((low_in0, low_in1)):
            first_row = 96 * z + 48 * k
            for y in range(2):
                for j in range(4):
                    first = D * j + 384 * y
                    f_in[first_row : first_row + 48, first : first + 384] = source[y, z, j].astype(F32)
        store(f_in.at[pl.ds(96 * z, 96)], r_in.at[pl.ds(96 * z, 96)])
    heads_load.wait()
    for i, (made, result) in enumerate(((f_k, r_k), (f_v, r_v), (f_q, r_q))):
        for z in range(2):
            made[96 * z : 96 * (z + 1), :] = jnp.concatenate(
                [low_heads[z, j, :, HW * i : HW * (i + 1)].astype(F32) for j in range(4)], axis=1
            )
        store(made, result)
    o_load.wait()
    for z in range(2):
        for i in range(2):
            f_o[96 * z : 96 * (z + 1), 384 * i : 384 * (i + 1)] = low_o[i, z].astype(F32)
    store(f_o, r_o)
    output_load.wait()
    store(low_output, r_output.at[0])
    input_load.wait()
    store(full_input, r_input.at[0])

    w = lax.axis_index("wsh")
    for i in range(8):
        vectors[i][...] = smalls[w, i, :]
    inner_bias[...] = rows[1, w, :]
    error = jnp.sum(rows[1, 4:5, :])
    count = jnp.max(rows[1, 5:6, :])
    loss[0] = error / (count * D)
    for copy in stores:
        copy.wait()


def fused_body(tokens, teacher, doc_lengths, valid_len, *weights):
    (
        q_weight,
        q_bias,
        k_weight,
        v_weight,
        v_bias,
        o_weight,
        o_bias,
        ln1_gain,
        ln1_bias,
        in_weight,
        in_bias,
        out_weight,
        out_bias,
        ln2_gain,
        ln2_bias,
    ) = weights
    hbm = pl.BlockSpec(memory_space=pl.ANY)
    smem = pl.BlockSpec(memory_space=pltpu.SMEM)
    vmem = pl.BlockSpec(memory_space=pltpu.VMEM)
    low = lambda *shape: jax.ShapeDtypeStruct(shape, BF)
    full = lambda *shape: jax.ShapeDtypeStruct(shape, F32)
    output, input_grad, g_o, g_in0, g_in1, g_out, heads, smalls, rows = pl.pallas_call(
        fused_kernel,
        out_shape=(
            low(ROWS, D),
            full(ROWS, D),
            low(2, 2, 96, 384),
            low(2, 2, 4, 48, 384),
            low(2, 2, 4, 48, 384),
            low(4, 2, 2, 48, D),
            low(2, 4, HW // 2, HEAD_COLS),
            full(GROUP, 16, HW),
            full(2, 8, D),
        ),
        in_specs=[hbm] * 8 + [smem] * 2 + [vmem] * 9,
        out_specs=[hbm] * 9,
        scratch_shapes=scratch_shapes()[0]
        + [
            pltpu.SemaphoreType.DMA((REMOTE_SEMS,)),
            pltpu.SemaphoreType.DMA((REMOTE_SEMS,)),
            pltpu.SemaphoreType.DMA((LOCAL_SEMS,)),
        ],
        compiler_params=pltpu.CompilerParams(
            collective_id=0, has_side_effects=True, vmem_limit_bytes=67043328
        ),
        name="layer",
    )(
        tokens,
        teacher,
        q_weight,
        k_weight,
        v_weight,
        o_weight,
        in_weight,
        out_weight,
        doc_lengths,
        valid_len,
        q_bias,
        v_bias,
        o_bias,
        ln1_gain,
        ln1_bias,
        out_bias,
        ln2_gain,
        ln2_bias,
        in_bias,
    )

    square_low = pltpu.VMEM((2, 2, 96, 384), BF)
    side_low = pltpu.VMEM((2, 2, 4, 48, 384), BF)
    results = pl.pallas_call(
        finish_kernel,
        out_shape=(full(HW, D),) * 4
        + (full(HW, FF), full(D, D), low(1, ROWS, D), full(1, ROWS, D))
        + (full(HW),) * 8
        + (full(D), full(1)),
        in_specs=[hbm] * 7 + [vmem] * 2,
        out_specs=[hbm] * 8 + [vmem] * 9 + [smem],
        scratch_shapes=[
            square_low,
            side_low,
            side_low,
            pltpu.VMEM((4, 2, 2, 48, D), BF),
            pltpu.VMEM((2, 4, HW // 2, HEAD_COLS), BF),
            pltpu.VMEM((ROWS, D), BF),
            pltpu.VMEM((ROWS, D), F32),
        ]
        + [pltpu.VMEM((HW, D), F32)] * 4
        + [
            pltpu.VMEM((HW, FF), F32),
            pltpu.VMEM((D, D), F32),
            pltpu.SemaphoreType.DMA((10,)),
            pltpu.SemaphoreType.DMA((12,)),
        ],
        name="finish",
    )(g_o, g_in0, g_in1, g_out, heads, output, input_grad, smalls, rows)
    r_output, r_input = results[6:8]
    vectors, inner_bias, loss = results[8:16], *results[16:]
    r_q, r_k, r_v, r_o, r_in, r_out = results[:6]
    return (
        r_output,
        loss.reshape(()),
        r_input,
        r_q,
        vectors[0],
        r_k,
        r_v,
        vectors[1],
        r_o,
        vectors[2],
        vectors[3],
        vectors[4],
        r_in,
        inner_bias,
        r_out,
        vectors[5],
        vectors[6],
        vectors[7],
    )


def solution(mesh):
    in_specs = (
        P("wsh", "ctx", None),
        P("wsh", "ctx", None),
        P("wsh", None),
        P("wsh"),
        P("wsh", None),
        P("wsh"),
        P("wsh", None),
        P("wsh", None),
        P("wsh"),
        P("wsh", None),
        P("wsh"),
        P("wsh"),
        P("wsh"),
        P("wsh", None),
        P("wsh"),
        P("wsh", None),
        P("wsh"),
        P("wsh"),
        P("wsh"),
    )
    out_specs = (
        P("wsh", "ctx", None),
        P(),
        P("wsh", "ctx", None),
        P("wsh", None),
        P("wsh"),
        P("wsh", None),
        P("wsh", None),
        P("wsh"),
        P("wsh", None),
        P("wsh"),
        P("wsh"),
        P("wsh"),
        P("wsh", None),
        P("wsh"),
        P("wsh", None),
        P("wsh"),
        P("wsh"),
        P("wsh"),
    )
    program = fused_body if fused_fits(mesh) else body
    return jax.shard_map(program, mesh=mesh, in_specs=in_specs, out_specs=out_specs, check_vma=False)
```

```python
import math
import types

import jax
import jax.numpy as jnp
from jax import lax
from jax.experimental import pallas as pl
from jax.experimental.pallas import tpu as pltpu
from jax.sharding import PartitionSpec as P

D = 768
H = 12
HD = 64


EPSILON = 1e-06
MASKED = -1e30


def shifted(block, axis, distance):
    devices = range(lax.axis_size(axis))
    route = [((i - distance) % len(devices), i) for i in devices]
    return lax.ppermute(block, axis, route)


def layer_norm(value, gain, shift):
    mean = jnp.mean(value, axis=-1, keepdims=True)
    centered = value - mean
    spread = jnp.mean(centered * centered, axis=-1, keepdims=True)
    return centered * lax.rsqrt(spread + EPSILON) * gain + shift


def activate(value):
    return jax.nn.gelu(value, approximate=True)


def matmul(left, right):
    return jnp.dot(left, right, preferred_element_type=jnp.float32)


def left_product(left, right):
    return lax.dot_general(
        left, right, (((0,), (0,)), ((), ())), preferred_element_type=jnp.float32
    )


def right_product(left, right):
    return lax.dot_general(
        left, right, (((1,), (1,)), ((), ())), preferred_element_type=jnp.float32
    )


def document_of(positions, starts):
    return jnp.sum((starts[None, :] <= positions[:, None]).astype(jnp.int32), axis=1) - 1


def permitted(own_doc, own_live, other_doc, other_live):
    return (own_doc[:, None] == other_doc[None, :]) & (own_live[:, None] == other_live[None, :])


def block_weights(queries, key_block, allowed, score_scale):
    scores = (
        jnp.einsum("qhd,khd->hqk", queries, key_block, preferred_element_type=jnp.float32)
        * score_scale
    )
    return jnp.exp(jnp.where(allowed[None], scores, MASKED))


def forward_visit(sums_state, queries, key_block, value_block, allowed, score_scale):
    row_total, weighted = sums_state
    weights = block_weights(queries, key_block, allowed, score_scale)
    row_total = row_total + jnp.sum(weights, axis=-1)
    weighted = weighted + jnp.einsum(
        "hqk,khd->qhd",
        weights.astype(jnp.bfloat16),
        value_block,
        preferred_element_type=jnp.float32,
    )
    return (row_total, weighted)


def backward_visit(
    queries, key_block, value_block, allowed, score_scale, weighted_grad, total_grad
):
    weights = block_weights(queries, key_block, allowed, score_scale)
    value_part = jnp.einsum(
        "hqk,qhd->khd",
        weights.astype(jnp.bfloat16),
        weighted_grad,
        preferred_element_type=jnp.float32,
    )
    weight_grad = (
        jnp.einsum("qhd,khd->hqk", weighted_grad, value_block, preferred_element_type=jnp.float32)
        + total_grad[:, :, None]
    )
    score_grad = (weights * weight_grad).astype(jnp.bfloat16)
    query_part = (
        jnp.einsum("hqk,khd->qhd", score_grad, key_block, preferred_element_type=jnp.float32)
        * score_scale
    )
    key_part = (
        jnp.einsum("hqk,qhd->khd", score_grad, queries, preferred_element_type=jnp.float32)
        * score_scale
    )
    return (query_part, key_part, value_part)


def body(
    tokens,
    teacher,
    doc_lengths,
    valid_len,
    q_weight,
    q_bias,
    k_weight,
    v_weight,
    v_bias,
    o_weight,
    o_bias,
    ln1_gain,
    ln1_bias,
    in_weight,
    in_bias,
    out_weight,
    out_bias,
    ln2_gain,
    ln2_bias,
):
    gathered = (
        lax.all_gather(q_weight, "wsh", axis=0, tiled=True),
        lax.all_gather(q_bias, "wsh", axis=0, tiled=True),
        lax.all_gather(k_weight, "wsh", axis=0, tiled=True),
        lax.all_gather(v_weight, "wsh", axis=0, tiled=True),
        lax.all_gather(v_bias, "wsh", axis=0, tiled=True),
        lax.all_gather(o_weight, "wsh", axis=0, tiled=True),
        lax.all_gather(o_bias, "wsh", axis=0, tiled=True),
        lax.all_gather(ln1_gain, "wsh", axis=0, tiled=True),
        lax.all_gather(ln1_bias, "wsh", axis=0, tiled=True),
        lax.all_gather(in_weight, "wsh", axis=0, tiled=True),
        lax.all_gather(in_bias, "wsh", axis=0, tiled=True),
        lax.all_gather(out_weight, "wsh", axis=0, tiled=True),
        lax.all_gather(out_bias, "wsh", axis=0, tiled=True),
        lax.all_gather(ln2_gain, "wsh", axis=0, tiled=True),
        lax.all_gather(ln2_bias, "wsh", axis=0, tiled=True),
    )
    (
        w_query,
        b_query,
        w_key,
        w_value,
        b_value,
        w_out,
        b_out,
        gain_one,
        shift_one,
        w_inner,
        b_inner,
        w_back,
        b_back,
        gain_two,
        shift_two,
    ) = gathered
    gain_first = gain_one.astype(jnp.float32)
    shift_first = shift_one.astype(jnp.float32)
    gain_second = gain_two.astype(jnp.float32)
    shift_second = shift_two.astype(jnp.float32)
    inputs = tokens[0]
    row_count = inputs.shape[0]
    cycle_size = lax.axis_size("ctx")
    stream_count = lax.axis_size("wsh")
    position = lax.axis_index("ctx")
    score_scale = 1.0 / math.sqrt(HD)
    offsets = jnp.arange(row_count, dtype=jnp.int32)
    lengths = doc_lengths[0]
    starts = jnp.cumsum(lengths) - lengths
    limit = valid_len[0]

    def key_mask(block_index):
        where_rows = jnp.mod(block_index, cycle_size) * row_count + offsets
        return (document_of(where_rows, starts), where_rows < limit)

    own_doc, own_live = key_mask(position)
    input_float = inputs.astype(jnp.float32)
    queries = (
        (matmul(inputs, w_query) + b_query.astype(jnp.float32))
        .astype(jnp.bfloat16)
        .reshape(row_count, H, HD)
    )
    key_rows = matmul(inputs, w_key).astype(jnp.bfloat16).reshape(row_count, H, HD)
    value_rows = (
        (matmul(inputs, w_value) + b_value.astype(jnp.float32))
        .astype(jnp.bfloat16)
        .reshape(row_count, H, HD)
    )

    def visit_forward(sums_state, key_block, value_block, block_index):
        other_doc, other_live = key_mask(block_index)
        allowed = permitted(own_doc, own_live, other_doc, other_live)
        return forward_visit(sums_state, queries, key_block, value_block, allowed, score_scale)

    empty_state = (
        jnp.zeros((H, row_count), jnp.float32),
        jnp.zeros((row_count, H, HD), jnp.float32),
    )
    first_state = visit_forward(empty_state, key_rows, value_rows, position)

    def advance(step_index, loop_state):
        key_block, value_block, running = loop_state
        key_block, value_block = shifted((key_block, value_block), "ctx", 1)
        running = visit_forward(running, key_block, value_block, position - step_index)
        return (key_block, value_block, running)

    row_total, weighted = lax.fori_loop(
        1, cycle_size, advance, (key_rows, value_rows, first_state)
    )[2]
    normed = weighted / jnp.transpose(row_total)[:, :, None]
    context = normed.astype(jnp.bfloat16).reshape(row_count, D)
    attn = matmul(context, w_out) + b_out.astype(jnp.float32)
    first_sum = input_float + attn
    settled = layer_norm(first_sum, gain_first, shift_first)
    settled_low = settled.astype(jnp.bfloat16)
    inner = matmul(settled_low, w_inner) + b_inner.astype(jnp.float32)
    activated = activate(inner).astype(jnp.bfloat16)
    branch = matmul(activated, w_back) + b_back.astype(jnp.float32)
    second_sum = settled + branch
    result = layer_norm(second_sum, gain_second, shift_second)
    target = teacher[0].astype(jnp.float32)
    diff = jnp.where(own_live[:, None], result - target, 0.0)
    error_sum, live_count = lax.psum(
        (jnp.sum(diff * diff), jnp.sum(own_live.astype(jnp.float32))), ("ctx", "wsh")
    )
    loss = error_sum / (live_count * D)
    upstream = diff * (row_count * cycle_size * stream_count / live_count)
    unused_second, second_back = jax.vjp(layer_norm, second_sum, gain_second, shift_second)
    d_second, gain_two_grad, shift_two_grad = second_back(upstream)
    branch_grad = d_second.astype(jnp.bfloat16)
    back_weight_grad = left_product(activated, branch_grad)
    back_bias_grad = jnp.sum(branch_grad, axis=0, dtype=jnp.float32)
    d_activated = right_product(branch_grad, w_back)
    unused_inner, gelu_back = jax.vjp(activate, inner)
    inner_grad = gelu_back(d_activated)[0].astype(jnp.bfloat16)
    inner_weight_grad = left_product(settled_low, inner_grad)
    inner_bias_grad = jnp.sum(inner_grad, axis=0, dtype=jnp.float32)
    d_settled = d_second + right_product(inner_grad, w_inner)
    unused_first, first_back = jax.vjp(layer_norm, first_sum, gain_first, shift_first)
    d_first, gain_one_grad, shift_one_grad = first_back(d_settled)
    attn_grad = d_first.astype(jnp.bfloat16)
    out_weight_grad_local = left_product(context, attn_grad)
    out_bias_grad_local = jnp.sum(attn_grad, axis=0, dtype=jnp.float32)
    context_low = lax.optimization_barrier(right_product(attn_grad, w_out).astype(jnp.bfloat16))
    context_grad = context_low.astype(jnp.float32).reshape(row_count, H, HD)
    weighted_grad = (context_grad / jnp.transpose(row_total)[:, :, None]).astype(jnp.bfloat16)
    total_grad = -jnp.transpose(jnp.sum(context_grad * weighted, axis=-1)) / (row_total * row_total)

    def visit_backward(key_block, value_block, block_index):
        other_doc, other_live = key_mask(block_index)
        allowed = permitted(own_doc, own_live, other_doc, other_live)
        return backward_visit(
            queries, key_block, value_block, allowed, score_scale, weighted_grad, total_grad
        )

    query_sum, key_sum, value_sum = visit_backward(key_rows, value_rows, position)

    def advance_back(step_index, loop_state):
        key_block, value_block, query_acc, key_acc, value_acc = loop_state
        key_block, value_block = shifted((key_block, value_block), "ctx", 1)
        key_acc, value_acc = (
            shifted(key_acc.astype(jnp.bfloat16), "ctx", 1).astype(key_acc.dtype),
            shifted(value_acc.astype(jnp.bfloat16), "ctx", 1).astype(value_acc.dtype),
        )
        query_part, key_part, value_part = visit_backward(
            key_block, value_block, position - step_index
        )
        return (
            key_block,
            value_block,
            query_acc + query_part,
            key_acc + key_part,
            value_acc + value_part,
        )

    loop_state = lax.fori_loop(
        1, cycle_size, advance_back, (key_rows, value_rows, query_sum, key_sum, value_sum)
    )
    query_total = loop_state[2]
    key_total, value_total = (
        shifted(loop_state[3].astype(jnp.bfloat16), "ctx", 1).astype(jnp.float32),
        shifted(loop_state[4].astype(jnp.bfloat16), "ctx", 1).astype(jnp.float32),
    )
    query_grad = query_total.astype(jnp.bfloat16).reshape(row_count, D)
    key_grad = key_total.astype(jnp.bfloat16).reshape(row_count, D)
    value_grad = value_total.astype(jnp.bfloat16).reshape(row_count, D)
    query_weight_grad = left_product(inputs, query_grad)
    query_bias_grad = jnp.sum(query_grad, axis=0, dtype=jnp.float32)
    key_weight_grad = left_product(inputs, key_grad)
    value_weight_grad = left_product(inputs, value_grad)
    value_bias_grad = jnp.sum(value_grad, axis=0, dtype=jnp.float32)
    input_grad = (
        d_first
        + right_product(query_grad, w_query)
        + right_product(key_grad, w_key)
        + right_product(value_grad, w_value)
    )
    reduced = (
        lax.psum_scatter(
            query_weight_grad.astype(jnp.bfloat16), "wsh", scatter_dimension=0, tiled=True
        ).astype(jnp.float32),
        lax.psum_scatter(
            query_bias_grad.astype(jnp.bfloat16), "wsh", scatter_dimension=0, tiled=True
        ).astype(jnp.float32),
        lax.psum_scatter(
            key_weight_grad.astype(jnp.bfloat16), "wsh", scatter_dimension=0, tiled=True
        ).astype(jnp.float32),
        lax.psum_scatter(
            value_weight_grad.astype(jnp.bfloat16), "wsh", scatter_dimension=0, tiled=True
        ).astype(jnp.float32),
        lax.psum_scatter(
            value_bias_grad.astype(jnp.bfloat16), "wsh", scatter_dimension=0, tiled=True
        ).astype(jnp.float32),
        lax.psum_scatter(
            out_weight_grad_local.astype(jnp.bfloat16), "wsh", scatter_dimension=0, tiled=True
        ).astype(jnp.float32),
        lax.psum_scatter(
            out_bias_grad_local.astype(jnp.bfloat16), "wsh", scatter_dimension=0, tiled=True
        ).astype(jnp.float32),
        lax.psum_scatter(
            gain_one_grad.astype(jnp.bfloat16), "wsh", scatter_dimension=0, tiled=True
        ).astype(jnp.float32),
        lax.psum_scatter(
            shift_one_grad.astype(jnp.bfloat16), "wsh", scatter_dimension=0, tiled=True
        ).astype(jnp.float32),
        lax.psum_scatter(
            inner_weight_grad.astype(jnp.bfloat16), "wsh", scatter_dimension=0, tiled=True
        ).astype(jnp.float32),
        lax.psum_scatter(
            inner_bias_grad.astype(jnp.bfloat16), "wsh", scatter_dimension=0, tiled=True
        ).astype(jnp.float32),
        lax.psum_scatter(
            back_weight_grad.astype(jnp.bfloat16), "wsh", scatter_dimension=0, tiled=True
        ).astype(jnp.float32),
        lax.psum_scatter(
            back_bias_grad.astype(jnp.bfloat16), "wsh", scatter_dimension=0, tiled=True
        ).astype(jnp.float32),
        lax.psum_scatter(
            gain_two_grad.astype(jnp.bfloat16), "wsh", scatter_dimension=0, tiled=True
        ).astype(jnp.float32),
        lax.psum_scatter(
            shift_two_grad.astype(jnp.bfloat16), "wsh", scatter_dimension=0, tiled=True
        ).astype(jnp.float32),
    )
    summed = lax.psum(
        (
            reduced[0],
            reduced[1],
            reduced[2],
            reduced[3],
            reduced[4],
            reduced[5],
            reduced[6],
            reduced[7],
            reduced[8],
            reduced[9],
            reduced[10],
            reduced[11],
            reduced[12],
            reduced[13],
            reduced[14],
        ),
        "ctx",
    )
    return (
        result.astype(jnp.bfloat16)[None],
        loss,
        input_grad[None],
        summed[0],
        summed[1],
        summed[2],
        summed[3],
        summed[4],
        summed[5],
        summed[6],
        summed[7],
        summed[8],
        summed[9],
        summed[10],
        summed[11],
        summed[12],
        summed[13],
        summed[14],
    )


BF = jnp.bfloat16
F32 = jnp.float32
FF = 3072
ROWS = 128
HEADS = 3
HW = HEADS * HD
GROUP = 4
CTX = 8
MESH = pl.DeviceIdType.MESH

Q, K, V, O, IN, OUT, PART_Q, PART_K, PART_V = range(9)
SLICE = 256
WEIGHT_SHAPES = [(192, 768)] * 4 + [(192, 3072), (768, 768)] + [(192, SLICE)] * 3
SECOND_WAY = {O: 1, IN: 2, OUT: 1, PART_Q: 1, PART_K: 1, PART_V: 1}
LOT_O, LOT_IN, LOT_OUT = (0,), (1, 2), (3, 4, 5, 6)
LOT_PAIR = LOT_O + LOT_IN + LOT_OUT[:2]
LOTS = [(96, 384)] + [(4, 48, 384)] * 2 + [(96, 384)] * 4
PIECES = {IN: (1, 4), OUT: (4, 1)}
HEAD_COLS = 640

(
    SMALL,
    WEIGHT_X,
    WEIGHT_SECOND,
    WEIGHT_CORE,
    WEIGHT_CORE_X,
    WEIGHT_CORE_SECOND,
    X_LINE,
    X_EDGE,
    KEY_VALUE,
    CONTEXT,
    CONTEXT_GRAD,
    KEY_VALUE_GRAD,
    INPUT_PARTS,
    SETTLED_ALL,
    CONTEXT_ALL,
    ATTN_GRAD_ALL,
    BRANCH_GRAD_ALL,
    REDUCE,
    SPREAD,
    GIVE,
    OWN,
    GROUP_X,
    HEADS_CORE,
    HEADS_X,
    HEADS_Y,
    HEADS_LINE,
    HEADS_EDGE,
    HEADS_PAIR,
    VECTORS_W,
    VECTORS_Z,
    VECTORS_Y,
    VECTORS_CORE,
    TOKENS,
    TEACHER,
    OUTPUT,
    INPUT_GRAD,
    LOAD,
) = range(37)


def fused_fits(mesh):
    return mesh.shape["ctx"] == CTX and mesh.shape["wsh"] == GROUP


def tn(left, right):
    return lax.dot_general(
        left, right, (((0,), (0,)), ((), ())), preferred_element_type=jnp.float32
    )


def norm_parts(value):
    mean = jnp.mean(value, axis=-1, keepdims=True)
    centered = value - mean
    spread = jnp.mean(centered * centered, axis=-1, keepdims=True)
    inverse = lax.rsqrt(spread + EPSILON)
    return centered * inverse, inverse


def norm_back(upstream_gained, normal, inverse):
    return (
        upstream_gained
        - jnp.mean(upstream_gained, axis=-1, keepdims=True)
        - normal * jnp.mean(upstream_gained * normal, axis=-1, keepdims=True)
    ) * inverse


GELU_C = math.sqrt(2.0 / math.pi)


class Numbers:
    def __init__(self):
        self.count = 0
        self.table = {}

    def take(self, key, size=1):
        if key not in self.table:
            self.table[key] = self.count
            self.count += size
        return self.table[key]


def scratch_table():
    s = types.SimpleNamespace()
    s.full = {k: pltpu.VMEM((GROUP, *WEIGHT_SHAPES[k]), BF) for k in SECOND_WAY}
    s.turned = pltpu.VMEM((SLICE, D), BF)
    s.head_weight = pltpu.VMEM((3 * HW, D), BF)
    s.tall_bias = pltpu.VMEM((SLICE, ROWS), F32)
    s.head_bias = pltpu.VMEM((3 * HW, ROWS), F32)
    s.x = pltpu.VMEM((ROWS, D), BF)
    s.xt = pltpu.VMEM((CTX, D, ROWS), BF)
    s.teacher = pltpu.VMEM((ROWS, D), BF)
    s.small = pltpu.VMEM((GROUP, 16, D), BF)
    s.vectors = pltpu.VMEM((16, D), F32)
    s.kv = pltpu.VMEM((CTX, 2 * HW, ROWS), BF)
    s.q = pltpu.VMEM((4, HW, ROWS), BF)
    s.weights = pltpu.VMEM((CTX, HEADS, ROWS, 4 * ROWS), F32)
    s.mix = pltpu.VMEM((HEADS, HD, 4 * ROWS), F32)
    s.total = pltpu.VMEM((HEADS, 8, 4 * ROWS), F32)
    s.ctx_send = pltpu.VMEM((4, HW, ROWS), BF)
    s.ctx = pltpu.VMEM((4, HW, ROWS), BF)
    s.inner = pltpu.VMEM((4, ROWS, D), F32)
    s.act = pltpu.VMEM((4, ROWS, D), BF)
    s.first = pltpu.VMEM((ROWS, D), F32)
    s.keep = pltpu.VMEM((ROWS, D), F32)
    s.inverse = pltpu.VMEM((ROWS, 128), F32)
    s.set_low = pltpu.VMEM((ROWS, D), BF)
    s.ag_half = pltpu.VMEM((2, ROWS, 384), BF)
    s.bg = pltpu.VMEM((2, ROWS, 384), BF)
    s.set_all = pltpu.VMEM((GROUP, ROWS, D), BF)
    s.ctx_all = pltpu.VMEM((GROUP, 2, HW, ROWS), BF)
    s.ag_all = pltpu.VMEM((GROUP, ROWS, 384), BF)
    s.inner_all = pltpu.VMEM((GROUP * ROWS, D), F32)
    s.act_all = pltpu.VMEM((GROUP * ROWS, D), BF)
    s.bg_all = pltpu.VMEM((2, GROUP, ROWS, 384), BF)
    s.cg_send = pltpu.VMEM((4, HW, ROWS), BF)
    s.cg = pltpu.VMEM((4, HW, ROWS), BF)
    s.wg = pltpu.VMEM((HEADS, HD, 4 * ROWS), BF)
    s.dkv = pltpu.VMEM((2, 4, 2 * HW, ROWS), BF)
    s.dkv_pair = pltpu.VMEM((4, 2 * HW, ROWS), BF)
    s.grads = pltpu.VMEM((HEAD_COLS, 4 * ROWS), BF)
    s.dx_send = pltpu.VMEM((4, ROWS, D), BF)
    s.dx_end = pltpu.VMEM((3, ROWS, D), BF)
    s.dx_middle = pltpu.VMEM((2, ROWS, D), BF)
    s.dx_got = pltpu.VMEM((2, ROWS, D), BF)
    s.dx_back = pltpu.VMEM((ROWS, D), BF)
    s.dx_last = pltpu.VMEM((ROWS, D), BF)
    s.column = pltpu.VMEM((D, ROWS), F32)
    s.heads = pltpu.VMEM((2, 2, HW, HEAD_COLS), BF)
    s.heads_core = pltpu.VMEM((2, HW, HEAD_COLS), BF)
    s.heads_sum = pltpu.VMEM((2, HW, HEAD_COLS), BF)
    s.heads_x = pltpu.VMEM((HW, HEAD_COLS), BF)
    s.heads_row = pltpu.VMEM((2, HW // 2, HEAD_COLS), BF)
    s.heads_y = pltpu.VMEM((HW // 2, HEAD_COLS), BF)
    s.heads_done = pltpu.VMEM((4, HW // 2, HEAD_COLS), BF)
    s.part = [pltpu.VMEM((2, 2, *shape), BF) for shape in LOTS]
    def lots(*dims):
        return [
            pltpu.VMEM((*dims[1 if k in LOT_PAIR else 0], *shape), BF) for k, shape in enumerate(LOTS)
        ]

    steps = [((2, 2), (2,)), ((2,), (2,)), ((), ())]
    s.got = [list(lot) for lot in zip(*(lots(*step) for step in steps))]
    s.sum = [list(lot) for lot in zip(*(lots(*step) for step in steps[:2]))]
    s.own = {k: pltpu.VMEM(LOTS[k], BF) for k in LOT_IN}
    s.done = [pltpu.VMEM((2, 2, *shape), BF) for shape in LOTS]
    s.smalls = pltpu.VMEM((GROUP, 16, HW), F32)
    s.sg = pltpu.VMEM((16, D), F32)
    s.sg_all = pltpu.VMEM((16, D), F32)
    s.sg_rows = pltpu.VMEM((2, 8, D), F32)
    s.sg_w = pltpu.VMEM((GROUP, 16, D), F32)
    s.sg_z = pltpu.VMEM((4, 8, D), F32)
    s.sg_y = pltpu.VMEM((2, 8, D), F32)
    s.out_low = pltpu.VMEM((ROWS, D), BF)
    return vars(s)


LOCAL_SEMS = 32
REMOTE_SEMS = 240


def is_memory(item):
    return not isinstance(item, (dict, list))


def scratch_shapes():
    return jax.tree.flatten(scratch_table(), is_leaf=is_memory)


def fused_kernel(*refs):
    (tokens, teacher), shards = refs[:2], refs[2:8]
    lengths, valid = refs[8:10]
    biases = refs[10:19]
    output, input_grad_out = refs[19:21]
    grad_o, *grad_in, grad_out = refs[21:25]
    heads_out, smalls_out, rows_out = refs[25:28]
    flat, shape = scratch_shapes()
    S = types.SimpleNamespace(**jax.tree.unflatten(shape, refs[28 : 28 + len(flat)]))
    send_sems, recv_sems, local_sems = refs[28 + len(flat) :]

    c = lax.axis_index("ctx")
    w = lax.axis_index("wsh")
    a, b = c // 2, c % 2
    x, core = w // 2, w % 2

    numbers = Numbers()
    locals_ = Numbers()
    started = []

    def bit_xor(value, j):
        out = value
        bit = 1
        while bit <= j:
            if j & bit:
                has = (value // bit) % 2
                out = out + bit * (1 - 2 * has)
            bit *= 2
        return out

    at_end = a * (3 - a) == 0
    roles, sent_by_role = [None], []

    def only(end):
        def run(action):
            roles.append(end)
            pl.when(at_end if end else jnp.logical_not(at_end))(action)
            roles.pop()

        return run

    def remote(key, src, dst, c_bits, w_bits, offset=0, size=1, to=None, like=None):
        number = numbers.take(key, size) + offset
        c_to, w_to = bit_xor(c, c_bits), bit_xor(w, w_bits) if to is None else to
        copy = pltpu.make_async_remote_copy(
            src_ref=src,
            dst_ref=dst,
            send_sem=send_sems.at[number],
            recv_sem=recv_sems.at[number],
            device_id={"ctx": c_to, "wsh": w_to},
            device_id_type=MESH,
        )
        copy.start()
        if roles[-1] is None:
            started.append(copy)
        else:
            sent_by_role.append((roles[-1], like, number))

    def arrived(key, landing, offset=0):
        number = numbers.take(key) + offset
        pltpu.make_async_copy(landing, landing, recv_sems.at[number]).wait()

    def local(key, src, dst):
        copy = pltpu.make_async_copy(src, dst, local_sems.at[locals_.take(key)])
        copy.start()
        return copy

    peers = [(c, bit_xor(w, j)) for j in (1, 2, 3)]
    peers += [(bit_xor(c, j), w) for j in range(1, CTX)]
    peers += [(bit_xor(c, 1), bit_xor(w, 1))]

    def bit(value, mask):
        return (value // mask) % 2

    first_col = pl.multiple_of((3 * a) // 2 * 128, 128)
    first_row = pl.multiple_of(a % 2 * 64, 64)

    def shard(name):
        if name < PART_Q:
            return shards[name]
        return shards[name - PART_Q].at[:, pl.ds(first_col, SLICE)]

    loads = {TOKENS: local(TOKENS, tokens.at[0], S.x)}
    for name in (PART_K, PART_V, PART_Q, O, IN, OUT):
        loads[name] = local((LOAD, name), shard(name), S.full[name].at[w])
    loads[TEACHER] = local(TEACHER, teacher.at[0], S.teacher)

    barrier = pltpu.get_barrier_semaphore()
    for c_to, w_to in peers:
        pl.semaphore_signal(
            barrier, inc=1, device_id={"ctx": c_to, "wsh": w_to}, device_id_type=MESH
        )
    loads[TOKENS].wait()
    x_low = S.x[...]
    S.xt[c] = x_low.T
    bias_rows = [row[...].astype(F32).reshape(1, HW) for row in biases[:8]]
    tall = jnp.concatenate(bias_rows, axis=0)
    valid_high = (valid[0] // 64).astype(F32)
    valid_low = (valid[0] % 64).astype(F32)
    wide_rows = [biases[8][...].astype(F32).reshape(1, D)]
    wide_rows += [jnp.full((1, D), 64.0, F32) * valid_high, jnp.full((1, D), 1.0, F32) * valid_low]
    wide_rows += [jnp.zeros((5, D), F32)]
    S.small[w, :, 0:HW] = jnp.concatenate(
        [tall, jnp.concatenate(wide_rows, axis=0)[:, 0:HW]], axis=0
    ).astype(BF)
    S.small[w, 8:16, HW:D] = jnp.concatenate(wide_rows, axis=0)[:, HW:D].astype(BF)

    pl.semaphore_wait(barrier, len(peers))

    def mine(name):
        return bit(c, SECOND_WAY[name])

    def pieces(name):
        tall, across = PIECES.get(name, (1, 1))
        return range(tall * across)

    def piece(name, which, number):
        rows, cols = WEIGHT_SHAPES[name]
        tall, across = PIECES.get(name, (1, 1))
        high, broad = rows // 2 // tall, cols // across
        row = which * (rows // 2) + number // across * high
        return pl.ds(pl.multiple_of(row, 16), high), slice(
            number % across * broad, (number % across + 1) * broad
        )

    def send_core(name):
        remote((WEIGHT_CORE, name), shard(name), S.full[name].at[w], 0, 1)

    def send_x(name):
        for i in pieces(name):
            rows, cols = piece(name, mine(name), i)
            if name < PART_Q:
                source = shards[name].at[rows, cols]
            else:
                source = shards[name - PART_Q].at[rows, pl.ds(first_col, SLICE)]
            remote((WEIGHT_X, name, i), source, S.full[name].at[w, rows, cols], 0, 2)

    for name in (PART_K, PART_V, PART_Q):
        send_x(name)
        send_core(name)
    for j in (1, 2, 3):
        remote((SMALL, j), S.small.at[w], S.small.at[w], 0, j)
    remote((X_LINE, 1), S.xt.at[c], S.xt.at[c], 2, 0)

    @only(False)
    def x_to_middle():
        remote((X_LINE, 3), S.xt.at[c], S.xt.at[c], 6, 0, like=lambda: S.xt.at[0])

    for name in (O, IN, OUT):
        send_x(name)
        send_core(name)

    def pump_x(name, number=0):
        slot = S.full[name].at[bit_xor(w, 2), *piece(name, mine(name), number)]
        arrived((WEIGHT_X, name, number), slot)
        remote((WEIGHT_SECOND, name, number), slot, slot, SECOND_WAY[name], 0)
        remote((WEIGHT_CORE_X, name, number), slot, slot, 0, 1)

    def pump_second(name, number=0):
        slot = S.full[name].at[bit_xor(w, 2), *piece(name, 1 - mine(name), number)]
        arrived((WEIGHT_SECOND, name, number), slot)
        remote((WEIGHT_CORE_SECOND, name, number), slot, slot, 0, 1)

    def weight_ready(name, numbers_=(0,), first=True):
        full = S.full[name]
        if first:
            loads[name].wait()
            arrived((WEIGHT_CORE, name), full.at[bit_xor(w, 1)])
        for i in numbers_:
            near = full.at[bit_xor(w, 3), *piece(name, mine(name), i)]
            far = full.at[bit_xor(w, 3), *piece(name, 1 - mine(name), i)]
            arrived((WEIGHT_CORE_X, name, i), near)
            arrived((WEIGHT_CORE_SECOND, name, i), far)

    def square(name):
        return S.full[name][...].reshape(D, D)

    starts, running = [], 0
    for i in range(lengths.shape[1]):
        starts.append(running)
        running = running + lengths[0, i]
    limit = valid[0]

    def code_of(position):
        code = jnp.zeros(position.shape, jnp.int32)
        for start in starts:
            code = code + (start <= position).astype(jnp.int32)
        return 2 * code + (position < limit).astype(jnp.int32)

    lane = lax.broadcasted_iota(jnp.int32, (1, 4 * ROWS), 1)
    query_code = code_of((2 * (lane // ROWS) + b) * ROWS + lane % ROWS)

    def key_code(block):
        return code_of(block * ROWS + lax.broadcasted_iota(jnp.int32, (ROWS, 1), 0))

    own_live = c * ROWS + lax.broadcasted_iota(jnp.int32, (ROWS, 1), 0) < limit

    def block_on(j, pair):
        return 2 * bit_xor(a, j) + pair

    def pass_x(key, j, onward, bits):
        block = S.xt.at[block_on(j, b)]
        arrived((key, j), block)
        remote(onward, block, block, bits, 0, like=lambda: S.xt.at[0])

    def vector(row):
        return S.vectors[row : row + 1, :]

    def to_group(key, source_of, everywhere):
        for j in (1, 2, 3):
            to = bit_xor(w, j)
            remote((*key, j), source_of(to), everywhere.at[w], 0, j)

    def from_group(key, everywhere):
        for j in (1, 2, 3):
            arrived((*key, j), everywhere.at[bit_xor(w, j)])

    def to_near(key, source, everywhere):
        for j in (1, 2):
            remote((*key, j), source, everywhere.at[w], 0, j)

    def pass_to_core(key, everywhere):
        slot = everywhere.at[bit_xor(w, 2)]
        arrived((*key, 2), slot)
        remote((*key, 3), slot, slot, 0, 1)

    def from_near(key, everywhere):
        for j in (1, 3):
            arrived((*key, j), everywhere.at[bit_xor(w, j)])

    def lanes(parts):
        return jnp.concatenate(parts, axis=1)

    finishing = []

    def small_vectors():
        for j in (1, 2, 3):
            arrived((SMALL, j), S.small.at[bit_xor(w, j)])
        S.vectors[0:8, :] = jnp.concatenate(
            [S.small[i, 0:8, 0:HW].astype(F32) for i in range(GROUP)], axis=1
        )
        small = [S.small[i, 8:16, :].astype(F32) for i in range(GROUP)]
        S.vectors[8:16, :] = jnp.concatenate(
            [part[0:1] for part in small]
            + [sum(part[1:2] + part[2:3] for part in small), jnp.zeros((3, D), F32)],
            axis=0,
        )

    def pass_near_end():
        arrived((X_LINE, 1), S.xt.at[block_on(1, b)])

        @only(False)
        def to_other_middle():
            block = S.xt.at[block_on(1, b)]
            remote((X_LINE, 2), block, block, 6, 0, like=lambda: S.xt.at[0])

    def pass_middle():
        @only(False)
        def to_near_end():
            pass_x(X_LINE, 3, (X_EDGE, 2), 2)

    def pass_far_end():
        @only(False)
        def to_near_end():
            pass_x(X_LINE, 2, (X_EDGE, 3), 2)

    def head_weights():
        for name in (PART_K, PART_V, PART_Q):
            weight_ready(name)
        for i, (name, bias) in enumerate(((PART_K, None), (PART_V, 1), (PART_Q, 0))):
            rows = slice(HW * i, HW * (i + 1))
            S.turned[...] = S.full[name][...].reshape(D, SLICE).T
            S.head_weight[rows, :] = S.turned[pl.ds(first_row, HW), :]
            if bias is None:
                S.head_bias[rows, :] = jnp.zeros((HW, ROWS), F32)
            else:
                row = S.vectors[bias : bias + 1, pl.ds(first_col, SLICE)]
                S.tall_bias[...] = jnp.broadcast_to(row, (ROWS, SLICE)).T
                S.head_bias[rows, :] = S.tall_bias[pl.ds(first_row, HW), :]

    def project(j):
        if j > 1:

            @only(True)
            def from_middle():
                arrived((X_EDGE, j), S.xt.at[block_on(j, b)])

        block = block_on(j, b)
        out = matmul(S.head_weight[...], S.xt[block]) + S.head_bias[...]
        S.kv[block] = out[0 : 2 * HW].astype(BF)
        S.q[block // 2] = out[2 * HW :].astype(BF)
        remote((KEY_VALUE, j), S.kv.at[block], S.kv.at[block], 1, 0)

    score_scale = 1.0 / math.sqrt(HD)

    def wide(ref, h):
        return lanes([ref[i, HD * h : HD * (h + 1), :] for i in range(4)])

    def attend_block(block):
        allowed = key_code(block) == query_code
        for h in range(HEADS):
            scores = tn(S.kv[block, HD * h : HD * (h + 1), :], wide(S.q, h)) * score_scale
            weights = jnp.exp(jnp.where(allowed, scores, MASKED))
            S.weights[block, h] = weights
            S.total[h, 0:1, :] += jnp.sum(weights, axis=0, keepdims=True)
            value_t = S.kv[block, HW + HD * h : HW + HD * (h + 1), :]
            S.mix[h] += matmul(value_t, weights.astype(BF))

    def attend_line():
        S.mix[...] = jnp.zeros(S.mix.shape, F32)
        S.total[...] = jnp.zeros(S.total.shape, F32)

        @pl.loop(0, 4)
        def every_block(i):
            attend_block(2 * i + b)

    def attend_pair(j):
        arrived((KEY_VALUE, j), S.kv.at[block_on(j, 1 - b)])
        attend_block(block_on(j, 1 - b))

    def send_context():
        for h in range(HEADS):
            context_t = (S.mix[h] / S.total[h, 0:1, :]).astype(BF)
            for i in range(4):
                S.ctx_send[i, HD * h : HD * (h + 1), :] = context_t[:, ROWS * i : ROWS * (i + 1)]
        for j in (1, 2, 3):
            to = bit_xor(a, j)
            remote((CONTEXT, j), S.ctx_send.at[to], S.ctx.at[a], 2 * j, 0)
        S.ctx[a] = S.ctx_send[a]

    def first_norm():
        weight_ready(O)
        for j in (1, 2, 3):
            arrived((CONTEXT, j), S.ctx.at[bit_xor(a, j)])
        attn = tn(S.ctx[...].reshape(D, ROWS), square(O)) + vector(2)
        normal_one, inverse_one = norm_parts(S.x[...].astype(F32) + attn)
        settled = normal_one * vector(3) + vector(4)
        S.first[...] = normal_one
        S.inverse[...] = jnp.broadcast_to(inverse_one, (ROWS, 128))
        S.keep[...] = settled
        S.set_low[...] = settled.astype(BF)
        to_near((SETTLED_ALL,), S.set_low, S.set_all)
        S.set_all[w] = S.set_low[...]
        to_group((CONTEXT_ALL,), lambda to: S.ctx.at[pl.ds(2 * (to // 2), 2)], S.ctx_all)
        S.ctx_all[w] = S.ctx[pl.ds(2 * x, 2)]

    def pass_settled():
        pass_to_core((SETTLED_ALL,), S.set_all)

    def gelu(inner):
        return 0.5 * inner * (1.0 + jnp.tanh(GELU_C * (inner + 0.044715 * inner * inner * inner)))

    def gelu_slope(inner):
        squared = inner * inner
        bend = jnp.tanh(GELU_C * (inner + 0.044715 * squared * inner))
        return 0.5 * (1.0 + bend) + 0.5 * inner * (1.0 - bend * bend) * (
            GELU_C * (1.0 + 3 * 0.044715 * squared)
        )

    def feed_in(t):
        weight_ready(IN, (t,), t == 0)
        w_part = S.full[IN][:, :, D * t : D * (t + 1)].reshape(D, D)
        inner = matmul(S.set_low[...], w_part) + vector(8 + t)
        S.inner[t] = inner
        S.act[t] = gelu(inner).astype(BF)

    def note(row, value):
        S.sg[row : row + 1, :] = jnp.sum(value.astype(F32), axis=0, keepdims=True)

    def result_and_loss():
        weight_ready(OUT, range(4))
        branch = vector(5)
        for t in range(4):
            branch = branch + matmul(S.act[t], S.full[OUT][t])
        normal_two, inverse_two = norm_parts(S.keep[...] + branch)
        result = normal_two * vector(6) + vector(7)
        S.out_low[...] = result.astype(BF)
        finishing.append(local(OUTPUT, S.out_low, output))
        loads[TEACHER].wait()
        diff = jnp.where(own_live, result - S.teacher[...].astype(F32), 0.0)
        count = vector(12)
        upstream = diff * ((ROWS * CTX * GROUP) / count)
        d_second = norm_back(upstream * vector(6), normal_two, inverse_two)
        for i in range(2):
            S.bg[i] = d_second[:, 384 * i : 384 * (i + 1)].astype(BF)
            to_near((BRANCH_GRAD_ALL, i), S.bg.at[i], S.bg_all.at[i])
        for i in range(2):
            S.bg_all[i, w] = S.bg[i]
        S.keep[...] = d_second
        S.sg[...] = jnp.zeros((16, D), F32)
        note(12, diff * diff)
        S.sg[13:14, :] = count * (1.0 / (CTX * GROUP))
        note(6, upstream * normal_two)
        note(7, upstream)
        note(5, d_second.astype(BF))

    def feed_back():
        d_settled = S.keep[...]
        branch_grad = lanes([S.bg[0], S.bg[1]])
        for t in range(4):
            d_act = right_product(branch_grad, S.full[OUT][t])
            inner_grad = (d_act * gelu_slope(S.inner[t])).astype(BF)
            note(8 + t, inner_grad)
            w_part = S.full[IN][:, :, D * t : D * (t + 1)].reshape(D, D)
            d_settled = d_settled + right_product(inner_grad, w_part)
        S.keep[...] = d_settled

    def pass_branch_grad(i):
        pass_to_core((BRANCH_GRAD_ALL, i), S.bg_all.at[i])

    def first_norm_back():
        d_settled, normal_one = S.keep[...], S.first[...]
        d_first = norm_back(d_settled * vector(3), normal_one, S.inverse[:, 0:1])
        attn_grad = d_first.astype(BF)
        context_grad = right_product(attn_grad, square(O)).T.astype(BF)
        for i in range(4):
            S.cg_send[i] = context_grad[HW * i : HW * (i + 1), :]
        for j in (1, 2, 3):
            to = bit_xor(a, j)
            remote((CONTEXT_GRAD, j), S.cg_send.at[to], S.cg.at[a], 2 * j, 0)
        S.cg[a] = S.cg_send[a]
        for i in range(2):
            S.ag_half[i] = attn_grad[:, 384 * i : 384 * (i + 1)]
        to_group((ATTN_GRAD_ALL,), lambda to: S.ag_half.at[to % 2], S.ag_all)
        S.ag_all[w] = S.ag_half[core]
        note(3, d_settled * normal_one)
        note(4, d_settled)
        note(2, attn_grad)
        S.keep[...] = d_first

    half = a // 2

    def y_end(lot):
        got, total = S.got[lot], S.sum[lot]
        arrived((REDUCE, lot, 0), got[0])
        total[0][...] = (S.part[lot][b].astype(F32) + got[0][...].astype(F32)).astype(BF)

        @only(True)
        def to_middle():
            remote((REDUCE, lot, 1), total[0], got[1], 2, 0, like=lambda: got[1])

    def y_middle(lot):
        @only(False)
        def swap_halves():
            got, total = S.got[lot], S.sum[lot]
            arrived((REDUCE, lot, 1), got[1])
            total[1][...] = (total[0][...].astype(F32) + got[1][...].astype(F32)).astype(BF)
            there = total[1].at[1 - half]
            remote((REDUCE, lot, 2), there, got[2], 6, 0, like=lambda: got[2])

    def y_spread_middle(lot):
        part = S.done[lot].at[b, half]
        remote((SPREAD, lot, 0), part, part, 6, 0, like=lambda: S.done[lot].at[0, 0])

    def y_last(lot):
        @only(False)
        def own_half():
            got = S.got[lot][2]
            arrived((REDUCE, lot, 2), got)
            total = (S.sum[lot][1][half].astype(F32) + got[...].astype(F32)).astype(BF)
            if lot in LOT_IN:
                own, done = S.own[lot], S.done[lot]
                own[...] = total
                done[b, half, w] = own[w]
                for q in (1, 2, 3):
                    slot = done.at[b, half, w]
                    to = bit_xor(w, q)
                    remote((GROUP_X, lot, q), own.at[to], slot, 0, q, like=lambda: own.at[0])
            else:
                S.done[lot][b, half] = total
                y_spread_middle(lot)

    def y_group(lot):
        @only(False)
        def gathered():
            for q in (1, 2, 3):
                arrived((GROUP_X, lot, q), S.done[lot].at[b, half, bit_xor(w, q)])
            y_spread_middle(lot)

    def y_spread_end(lot):
        @only(False)
        def to_end():
            done = S.done[lot].at[b]
            arrived((SPREAD, lot, 0), S.done[lot].at[b, 1 - half])
            remote((SPREAD, lot, 1), done, done, 2, 0, like=lambda: S.done[lot].at[0])

    def result_of(lot):
        return grad_in[lot - LOT_IN[0]] if lot in LOT_IN else grad_out.at[(lot - LOT_OUT[0]) // 2, (lot - LOT_OUT[0]) % 2]

    def y_give(lot):
        done = S.done[lot].at[b]

        @only(True)
        def from_middle_device():
            arrived((SPREAD, lot, 1), done)

        if lot not in LOT_O:
            out = result_of(lot).at[b]
            remote((GIVE, lot), done, out, 1, 0)
            finishing.append(local((GIVE, lot), done, out))
            return
        remote((GIVE, 0), done, grad_o.at[core], 1, 0, core, 2, 2 * x + b)

        @pl.when(core == b)
        def keep_own():
            local((OWN, 0), done, grad_o.at[core])

        @pl.when(core != b)
        def give_core():
            remote((OWN, 0), done, grad_o.at[core], 0, 1)
            started.pop()

    def settle():
        for lot in LOT_PAIR[1:]:
            arrived((GIVE, lot), result_of(lot).at[1 - b])
        done = S.done[0].at[b]

        @pl.when(core == b)
        def from_chip():
            pltpu.make_async_copy(
                done, grad_o.at[core], local_sems.at[locals_.take((OWN, 0))]
            ).wait()
            arrived((OWN, 0), grad_o.at[1 - core])

        @pl.when(core != b)
        def from_partner():
            arrived((GIVE, 0), grad_o.at[0], 0)
            arrived((GIVE, 0), grad_o.at[1], 1)
            sent = numbers.take((OWN, 0))
            pltpu.make_async_copy(done, done, send_sems.at[sent]).wait()

    def reduce_start(lot):
        @only(True)
        def to_middle():
            target = S.got[lot][0]
            remote((REDUCE, lot, 0), S.part[lot], target, 2, 0, like=lambda: target)

    def reduce_middle(lot):
        @only(False)
        def swap_halves():
            got = S.got[lot][0]
            arrived((REDUCE, lot, 0), got)
            total = S.part[lot][...].astype(F32) + got[...].astype(F32)
            S.sum[lot][0][...] = total.astype(BF)
            there, target = S.sum[lot][0].at[1 - half], S.got[lot][1]
            remote((REDUCE, lot, 1), there, target, 6, 0, like=lambda: target)

    def reduce_pair(lot):
        @only(False)
        def swap_quarters():
            got = S.got[lot][1]
            arrived((REDUCE, lot, 1), got)
            total = S.sum[lot][0][half].astype(F32) + got[...].astype(F32)
            S.sum[lot][1][...] = total.astype(BF)
            there, target = S.sum[lot][1].at[1 - b], S.got[lot][2]
            remote((REDUCE, lot, 2), there, target, 1, 0, like=lambda: target)

    def reduce_last(lot):
        @only(False)
        def own_quarter():
            got = S.got[lot][2]
            arrived((REDUCE, lot, 2), got)
            total = (S.sum[lot][1][b].astype(F32) + got[...].astype(F32)).astype(BF)
            S.done[lot][half, b] = total
            part = S.done[lot].at[half, b]
            remote((SPREAD, lot, 0), part, part, 1, 0, like=lambda: S.done[lot].at[0, 0])

    def spread_middle(lot):
        @only(False)
        def swap_back():
            arrived((SPREAD, lot, 0), S.done[lot].at[half, 1 - b])
            part = S.done[lot].at[half]
            remote((SPREAD, lot, 1), part, part, 6, 0, like=lambda: S.done[lot].at[0])

    def spread_end(lot):
        @only(False)
        def to_end():
            done = S.done[lot]
            arrived((SPREAD, lot, 1), done.at[1 - half])
            part = done.at[:, b]
            remote((SPREAD, lot, 2), part, part, 2, 0, like=lambda: done.at[:, 0])

    def spread_ends(lot):
        @only(True)
        def swap_at_ends():
            done = S.done[lot]
            part = done.at[:, b]
            arrived((SPREAD, lot, 2), part)
            remote((SPREAD, lot, 3), part, part, 1, 0, like=lambda: done.at[:, 0])

    def finish_lot(lot):
        @only(True)
        def from_pair():
            arrived((SPREAD, lot, 3), S.done[lot].at[:, 1 - b])

        finishing.append(local((GIVE, lot), S.done[lot], grad_out.at[(lot - LOT_OUT[0]) // 2, (lot - LOT_OUT[0]) % 2]))

    def inner_again():
        from_near((SETTLED_ALL,), S.set_all)
        settled_all = S.set_all[...].reshape(GROUP * ROWS, D)
        hidden = pl.ds(pl.multiple_of(D * w, D), D)
        S.inner_all[...] = (
            matmul(settled_all, S.full[IN][:, :, hidden].reshape(D, D))
            + S.vectors[pl.ds(8 + w, 1), :]
        )
        S.act_all[...] = gelu(S.inner_all[...]).astype(BF)

    def out_part(i):
        from_near((BRANCH_GRAD_ALL, i), S.bg_all.at[i])
        grad = tn(S.act_all[...], S.bg_all[i].reshape(GROUP * ROWS, 384)).astype(BF)
        for k in range(2):
            lot = LOT_OUT[2 * i + k]
            S.part[lot][...] = grad[384 * k : 384 * (k + 1)].reshape(2, 2, 96, 384)
            if lot in LOT_PAIR:
                remote((REDUCE, lot, 0), S.part[lot].at[1 - b], S.got[lot][0], 1, 0)
            else:
                reduce_start(lot)

    def in_part():
        branch_grad_all = lanes([S.bg_all[i].reshape(GROUP * ROWS, 384) for i in range(2)])
        inner_grad_all = (
            right_product(branch_grad_all, S.full[OUT][w]) * gelu_slope(S.inner_all[...])
        ).astype(BF)
        grad = tn(S.set_all[...].reshape(GROUP * ROWS, D), inner_grad_all).astype(BF)
        for i, lot in enumerate(LOT_IN):
            for j in range(2):
                side = grad[:, 384 * j : 384 * (j + 1)].reshape(4, 2, 2, 48, 384)
                for k in range(2):
                    S.part[lot][j, k] = side[:, k, i]
            remote((REDUCE, lot, 0), S.part[lot].at[1 - b], S.got[lot][0], 1, 0)

    def attention_back():
        for j in (1, 2, 3):
            arrived((CONTEXT_GRAD, j), S.cg.at[bit_xor(a, j)])
        for h in range(HEADS):
            grad = wide(S.cg, h).astype(F32)
            row_total = S.total[h, 0:1, :]
            S.wg[h] = (grad / row_total).astype(BF)
            S.total[h, 1:2, :] = -jnp.sum(grad * S.mix[h], axis=0, keepdims=True) / (
                row_total * row_total
            )
        S.mix[...] = jnp.zeros(S.mix.shape, F32)

        def attend_back(pair, i):
            block = 2 * i + pair
            for h in range(HEADS):
                key_rows = slice(HD * h, HD * (h + 1))
                value_rows = slice(HW + HD * h, HW + HD * (h + 1))
                weights = S.weights[block, h]
                grad = S.wg[h]
                weight_grad = tn(S.kv[block, value_rows, :], grad) + S.total[h, 1:2, :]
                score_grad = (weights * weight_grad).astype(BF)
                S.mix[h] += matmul(S.kv[block, key_rows, :], score_grad)
                S.dkv[pair, i, key_rows, :] = (
                    right_product(wide(S.q, h), score_grad) * score_scale
                ).astype(BF)
                value_grad = right_product(grad, weights.astype(BF))
                S.dkv[pair, i, value_rows, :] = value_grad.astype(BF)

        @pl.loop(0, CTX)
        def every_block(block):
            attend_back(block % 2, block // 2)

        remote((KEY_VALUE_GRAD,), S.dkv.at[1 - b], S.dkv_pair, 1, 0)
        for h in range(HEADS):
            rows = slice(2 * HW + HD * h, 2 * HW + HD * (h + 1))
            S.grads[rows, :] = (S.mix[h] * score_scale).astype(BF)
        S.grads[3 * HW :, :] = jnp.zeros((HEAD_COLS - 3 * HW, 4 * ROWS), BF)

    def o_part():
        from_group((CONTEXT_ALL,), S.ctx_all)
        from_group((ATTN_GRAD_ALL,), S.ag_all)
        context_all = lanes([S.ctx_all[i].reshape(384, ROWS) for i in range(GROUP)])
        grad = matmul(context_all, S.ag_all[...].reshape(GROUP * ROWS, 384))
        S.part[0][...] = grad.astype(BF).reshape(2, 2, 96, 384)
        remote((REDUCE, 0, 0), S.part[0].at[1 - b], S.got[0][0], 1, 0)

    def heads_part():
        arrived((KEY_VALUE_GRAD,), S.dkv_pair)
        for i in range(4):
            S.grads[0 : 2 * HW, ROWS * i : ROWS * (i + 1)] = (
                S.dkv[b, i].astype(F32) + S.dkv_pair[i].astype(F32)
            ).astype(BF)
        own_inputs = lanes([S.xt[2 * i + b] for i in range(4)])
        heads = right_product(own_inputs, S.grads[...]).astype(BF)
        S.heads[...] = heads.reshape(2, 2, HW, HEAD_COLS)
        for i in range(2):
            remote((HEADS_CORE, i), S.heads.at[i, 1 - core], S.heads_core.at[i], 0, 1)

    def input_parts():
        parts = tn(S.grads[0 : 3 * HW, :], S.head_weight[...])
        S.dx_send[...] = parts.astype(BF).reshape(4, ROWS, D)

        @only(True)
        def to_middle():
            for j in (1, 2, 3):
                source, target = S.dx_send.at[bit_xor(a, j)], S.dx_end.at[j - 1]
                remote((INPUT_PARTS, j), source, target, 2, 0, like=lambda: S.dx_end.at[0])

    def input_middle():
        @only(False)
        def to_other_middle():
            for j in (1, 2, 3):
                arrived((INPUT_PARTS, j), S.dx_end.at[j - 1])
            for i, j in enumerate((3, 2)):
                both = S.dx_send[bit_xor(a, j)].astype(F32) + S.dx_end[i + 1].astype(F32)
                S.dx_middle[i] = both.astype(BF)
            remote((INPUT_PARTS, 4), S.dx_middle, S.dx_got, 6, 0, like=lambda: S.dx_middle)

    def input_end():
        @only(False)
        def to_near_end():
            arrived((INPUT_PARTS, 4), S.dx_got)
            both = S.dx_send[bit_xor(a, 1)].astype(F32) + S.dx_got[1].astype(F32)
            S.dx_back[...] = both.astype(BF)
            remote((INPUT_PARTS, 5), S.dx_back, S.dx_last, 2, 0, like=lambda: S.dx_back)

    def vectors_group():
        S.column[...] = jnp.zeros((D, ROWS), F32)
        heads_rows = pl.ds(pl.multiple_of(HW * a, HW), HW)
        for row, first in ((1, HW), (0, 2 * HW)):
            sums = jnp.sum(S.grads[first : first + HW, :].astype(F32), axis=1, keepdims=True)
            S.column[heads_rows, :] = jnp.broadcast_to(sums, (HW, ROWS))
            S.sg[row : row + 1, :] = S.column[...].T[0:1, :]
        for j in (1, 2, 3):
            remote((VECTORS_W, j), S.sg, S.sg_w.at[w], 0, j)
        S.sg_w[w] = S.sg[...]

    own_rows = pl.ds(pl.multiple_of(8 * core, 8), 8)

    def vectors_line():
        for j in (1, 2, 3):
            arrived((VECTORS_W, j), S.sg_w.at[bit_xor(w, j)])
        S.sg_all[...] = (S.sg_w[0] + S.sg_w[1]) + (S.sg_w[2] + S.sg_w[3])
        S.sg_z[0] = S.sg_all[own_rows, :]

        @only(True)
        def to_middle():
            remote((VECTORS_Z, 1), S.sg_z.at[0], S.sg_z.at[1], 2, 0, like=lambda: S.sg_z.at[1])

    def vectors_middle():
        @only(False)
        def to_other_middle():
            arrived((VECTORS_Z, 1), S.sg_z.at[1])
            S.sg_z[2] = S.sg_z[0] + S.sg_z[1]
            remote((VECTORS_Z, 2), S.sg_z.at[2], S.sg_z.at[3], 6, 0, like=lambda: S.sg_z.at[2])

    def vectors_end():
        @only(False)
        def to_end():
            arrived((VECTORS_Z, 2), S.sg_z.at[3])
            S.sg_y[b] = S.sg_z[2] + S.sg_z[3]
            whole = S.sg_y.at[b]
            remote((VECTORS_Z, 3), whole, whole, 2, 0, like=lambda: S.sg_y.at[0])

    def vectors_pair():
        @only(True)
        def from_middle():
            arrived((VECTORS_Z, 3), S.sg_y.at[b])

        remote((VECTORS_Y,), S.sg_y.at[b], S.sg_y.at[b], 1, 0)

    def vectors_core():
        arrived((VECTORS_Y,), S.sg_y.at[1 - b])
        S.sg_rows[core] = S.sg_y[0] + S.sg_y[1]
        remote((VECTORS_CORE,), S.sg_rows.at[core], S.sg_rows.at[core], 0, 1)

    def vectors_done():
        arrived((VECTORS_CORE,), S.sg_rows.at[1 - core])
        everything = S.sg_rows[...].reshape(16, D)
        for i in range(4):
            S.smalls[i] = everything[:, HW * i : HW * (i + 1)]
        finishing.append(local((VECTORS_Y,), S.smalls, smalls_out))
        finishing.append(local((VECTORS_Z,), S.sg_rows, rows_out))

    def heads_x():
        for i in range(2):
            arrived((HEADS_CORE, i), S.heads_core.at[i])
        for i in range(2):
            S.heads_sum[i] = (S.heads[i, core].astype(F32) + S.heads_core[i].astype(F32)).astype(BF)
        remote((HEADS_X,), S.heads_sum.at[1 - x], S.heads_x, 0, 2)

    def heads_y():
        arrived((HEADS_X,), S.heads_x)
        S.heads_row[...] = (
            (S.heads_sum[x].astype(F32) + S.heads_x[...].astype(F32))
            .astype(BF)
            .reshape(2, HW // 2, HEAD_COLS)
        )
        remote((HEADS_Y,), S.heads_row.at[1 - b], S.heads_y, 1, 0)

    def heads_line():
        arrived((HEADS_Y,), S.heads_y)
        S.heads_done[a] = (S.heads_row[b].astype(F32) + S.heads_y[...].astype(F32)).astype(BF)
        own = S.heads_done.at[a]
        remote((HEADS_LINE, 1), own, own, 2, 0)

        @only(False)
        def to_other_middle():
            remote((HEADS_LINE, 3), own, own, 6, 0, like=lambda: S.heads_done.at[0])

    def pass_heads(key, j, onward, bits):
        part = S.heads_done.at[bit_xor(a, j)]
        if key is not None:
            arrived((key, j), part)
        remote(onward, part, part, bits, 0, like=lambda: S.heads_done.at[0])

    def heads_near_end():
        arrived((HEADS_LINE, 1), S.heads_done.at[bit_xor(a, 1)])

        @only(False)
        def to_other_middle():
            pass_heads(None, 1, (HEADS_LINE, 2), 6)

    def heads_middle():
        @only(False)
        def to_near_end():
            pass_heads(HEADS_LINE, 3, (HEADS_EDGE, 2), 2)

    def heads_far_end():
        @only(False)
        def to_near_end():
            pass_heads(HEADS_LINE, 2, (HEADS_EDGE, 3), 2)

    def heads_pair():
        @only(True)
        def from_middle():
            for j in (2, 3):
                arrived((HEADS_EDGE, j), S.heads_done.at[bit_xor(a, j)])

        remote((HEADS_PAIR,), S.heads_done, heads_out.at[b], 1, 0)
        finishing.append(local((HEADS_PAIR,), S.heads_done, heads_out.at[b]))

    def input_done():
        S.first[...] = S.keep[...] + S.dx_send[a].astype(F32)

        @only(True)
        def at_end():
            arrived((INPUT_PARTS, 5), S.dx_last)
            S.first[...] += S.dx_last[...].astype(F32)

        @only(False)
        def in_middle():
            S.first[...] += S.dx_end[0].astype(F32) + S.dx_got[0].astype(F32)

        finishing.append(local(INPUT_GRAD, S.first, input_grad_out))

    marked = []

    def mark():
        marked.extend(started)
        started.clear()

    def retire():
        for copy in marked:
            copy.wait_send()
        marked.clear()

    def mark_late():
        mark()

    def retire_late():
        retire()

    for step, *lot in (
        (pass_near_end,),
        (pump_x, PART_K),
        (pass_middle,),
        (pump_x, PART_Q),
        (pump_x, PART_V),
        (pump_second, PART_Q),
        (pump_x, O),
        (small_vectors,),
        (pass_far_end,),
        (pump_second, PART_V),
        (pump_second, PART_K),
        (head_weights,),
        (project, 0),
        (project, 2),
        (project, 1),
        (pump_x, IN, 0),
        (pump_x, IN, 1),
        (project, 3),
        (pump_second, O),
        (attend_line,),
        (attend_pair, 0),
        (pump_x, IN, 3),
        (attend_pair, 1),
        (attend_pair, 2),
        (pump_x, OUT, 0),
        (pump_second, IN, 1),
        (attend_pair, 3),
        (send_context,),
        (pump_x, IN, 2),
        (pump_x, OUT, 1),
        (pump_second, IN, 0),
        (pump_x, OUT, 2),
        (pump_second, OUT, 1),
        (pump_second, IN, 3),
        (pump_x, OUT, 3),
        (first_norm,),
        (feed_in, 0),
        (pump_second, OUT, 0),
        (feed_in, 1),
        (pump_second, OUT, 2),
        (pump_second, IN, 2),
        (feed_in, 2),
        (pump_second, OUT, 3),
        (feed_in, 3),
        (result_and_loss,),
        (pass_settled,),
        (feed_back,),
        (first_norm_back,),
        (mark,),
        (inner_again,),
        (pass_branch_grad, 0),
        (pass_branch_grad, 1),
        (out_part, 0),
        (out_part, 1),
        (attention_back,),
        (reduce_middle, 5),
        (reduce_pair, 5),
        (y_end, 3),
        (o_part,),
        (reduce_middle, 6),
        (y_middle, 3),
        (reduce_last, 5),
        (in_part,),
        (y_last, 3),
        (y_end, 4),
        (heads_part,),
        (y_middle, 4),
        (y_end, 0),
        (vectors_group,),
        (spread_middle, 5),
        (y_spread_end, 3),
        (heads_x,),
        (y_last, 4),
        (y_middle, 0),
        (vectors_line,),
        (vectors_middle,),
        (spread_end, 5),
        (y_spread_end, 4),
        (y_end, 1),
        (y_last, 0),
        (heads_y,),
        (y_middle, 1),
        (reduce_pair, 6),
        (spread_ends, 5),
        (retire,),
        (vectors_end,),
        (y_spread_end, 0),
        (heads_line,),
        (mark_late,),
        (y_end, 2),
        (reduce_last, 6),
        (y_give, 3),
        (y_give, 4),
        (y_last, 1),
        (vectors_pair,),
        (y_give, 0),
        (heads_near_end,),
        (heads_middle,),
        (y_group, 1),
        (heads_far_end,),
        (y_middle, 2),
        (input_parts,),
        (spread_middle, 6),
        (heads_pair,),
        (y_last, 2),
        (y_spread_end, 1),
        (spread_end, 6),
        (y_give, 1),
        (y_group, 2),
        (spread_ends, 6),
        (input_middle,),
        (y_spread_end, 2),
        (y_give, 2),
        (vectors_core,),
        (finish_lot, 5),
        (input_end,),
        (input_done,),
        (retire_late,),
        (vectors_done,),
        (finish_lot, 6),
    ):
        step(*lot)

    arrived((HEADS_PAIR,), heads_out.at[1 - b])
    settle()
    for copy in finishing:
        copy.wait()
    for copy in started:
        copy.wait_send()
    for end in (True, False):

        @only(end)
        def sent():
            for role, like, number in sent_by_role:
                if role == end:
                    source = like()
                    pltpu.make_async_copy(source, source, send_sems.at[number]).wait()


def finish_kernel(*refs):
    g_o, g_in0, g_in1, g_out, heads, smalls, rows, output, input_grad = refs[:9]
    r_q, r_k, r_v, r_o, r_in, r_out = refs[9:15]
    vectors, inner_bias, loss, r_output, r_input = refs[15:23], *refs[23:]
    step = pl.program_id(0)
    for i in range(2):
        r_o[:, 384 * i : 384 * (i + 1)] = g_o[i].reshape(HW // 2, 384).astype(F32)
        for j in range(4):
            first = D * j + 384 * i
            for k, source in enumerate((g_in0, g_in1)):
                r_in[48 * k : 48 * (k + 1), first : first + 384] = source[i, 0, j].astype(F32)
    for i in range(2):
        r_out[:, 384 * i : 384 * (i + 1)] = g_out[i].reshape(D // 2, 384).astype(F32)
    for i, result in ((0, r_k), (1, r_v), (2, r_q)):
        result[...] = jnp.concatenate(
            [heads[0, j, :, HW * i : HW * (i + 1)].astype(F32) for j in range(4)], axis=1
        )
    r_output[0] = output[...]
    r_input[0] = input_grad[...]

    @pl.when(step == 0)
    def once():
        w = lax.axis_index("wsh")
        for i in range(8):
            vectors[i][...] = smalls[w, i, :]
        inner_bias[...] = rows[1, w, :]
        error = jnp.sum(rows[1, 4:5, :])
        count = jnp.max(rows[1, 5:6, :])
        loss[0] = error / (count * D)


def fused_body(tokens, teacher, doc_lengths, valid_len, *weights):
    (
        q_weight,
        q_bias,
        k_weight,
        v_weight,
        v_bias,
        o_weight,
        o_bias,
        ln1_gain,
        ln1_bias,
        in_weight,
        in_bias,
        out_weight,
        out_bias,
        ln2_gain,
        ln2_bias,
    ) = weights
    hbm = pl.BlockSpec(memory_space=pl.ANY)
    smem = pl.BlockSpec(memory_space=pltpu.SMEM)
    vmem = pl.BlockSpec(memory_space=pltpu.VMEM)
    low = lambda *shape: jax.ShapeDtypeStruct(shape, BF)
    full = lambda *shape: jax.ShapeDtypeStruct(shape, F32)
    output, input_grad, g_o, g_in0, g_in1, g_out, heads, smalls, rows = pl.pallas_call(
        fused_kernel,
        out_shape=(
            low(ROWS, D),
            full(ROWS, D),
            low(2, 2, 96, 384),
            low(2, 2, 4, 48, 384),
            low(2, 2, 4, 48, 384),
            low(2, 2, 2, 2, 96, 384),
            low(2, 4, HW // 2, HEAD_COLS),
            full(GROUP, 16, HW),
            full(2, 8, D),
        ),
        in_specs=[hbm] * 8 + [smem] * 2 + [vmem] * 9,
        out_specs=[hbm] * 9,
        scratch_shapes=scratch_shapes()[0]
        + [
            pltpu.SemaphoreType.DMA((REMOTE_SEMS,)),
            pltpu.SemaphoreType.DMA((REMOTE_SEMS,)),
            pltpu.SemaphoreType.DMA((LOCAL_SEMS,)),
        ],
        compiler_params=pltpu.CompilerParams(
            collective_id=0, has_side_effects=True, vmem_limit_bytes=67043328
        ),
        name="layer",
    )(
        tokens,
        teacher,
        q_weight,
        k_weight,
        v_weight,
        o_weight,
        in_weight,
        out_weight,
        doc_lengths,
        valid_len,
        q_bias,
        v_bias,
        o_bias,
        ln1_gain,
        ln1_bias,
        out_bias,
        ln2_gain,
        ln2_bias,
        in_bias,
    )

    steps = 2
    square_out = pl.BlockSpec((HW // steps, D), lambda i: (i, 0))
    whole = lambda *shape: pl.BlockSpec(shape, lambda i: (0,) * len(shape))
    by_row = pl.BlockSpec((ROWS // steps, D), lambda i: (i, 0))
    results = pl.pallas_call(
        finish_kernel,
        grid=(steps,),
        out_shape=(full(HW, D),) * 4
        + (full(HW, FF), full(D, D))
        + (full(HW),) * 8
        + (full(D), full(1), low(1, ROWS, D), full(1, ROWS, D)),
        in_specs=[
            pl.BlockSpec((2, 1, 96, 384), lambda i: (0, i, 0, 0)),
            pl.BlockSpec((2, 1, 4, 48, 384), lambda i: (0, i, 0, 0, 0)),
            pl.BlockSpec((2, 1, 4, 48, 384), lambda i: (0, i, 0, 0, 0)),
            pl.BlockSpec((2, 1, 2, 2, 96, 384), lambda i: (0, i, 0, 0, 0, 0)),
            pl.BlockSpec((1, 4, HW // 2, HEAD_COLS), lambda i: (i, 0, 0, 0)),
            whole(GROUP, 16, HW),
            whole(2, 8, D),
            by_row,
            by_row,
        ],
        out_specs=[square_out] * 4
        + [
            pl.BlockSpec((HW // steps, FF), lambda i: (i, 0)),
            pl.BlockSpec((D // steps, D), lambda i: (i, 0)),
        ]
        + [whole(HW)] * 8
        + [
            whole(D),
            pl.BlockSpec(memory_space=pltpu.SMEM),
            pl.BlockSpec((1, ROWS // steps, D), lambda i: (0, i, 0)),
            pl.BlockSpec((1, ROWS // steps, D), lambda i: (0, i, 0)),
        ],
        compiler_params=pltpu.CompilerParams(dimension_semantics=("arbitrary",)),
        name="finish",
    )(g_o, g_in0, g_in1, g_out, heads, smalls, rows, output, input_grad)
    r_q, r_k, r_v, r_o, r_in, r_out = results[:6]
    vectors, inner_bias, loss, r_output, r_input = results[6:14], *results[14:]
    return (
        r_output,
        loss.reshape(()),
        r_input,
        r_q,
        vectors[0],
        r_k,
        r_v,
        vectors[1],
        r_o,
        vectors[2],
        vectors[3],
        vectors[4],
        r_in,
        inner_bias,
        r_out,
        vectors[5],
        vectors[6],
        vectors[7],
    )


def solution(mesh):
    in_specs = (
        P("wsh", "ctx", None),
        P("wsh", "ctx", None),
        P("wsh", None),
        P("wsh"),
        P("wsh", None),
        P("wsh"),
        P("wsh", None),
        P("wsh", None),
        P("wsh"),
        P("wsh", None),
        P("wsh"),
        P("wsh"),
        P("wsh"),
        P("wsh", None),
        P("wsh"),
        P("wsh", None),
        P("wsh"),
        P("wsh"),
        P("wsh"),
    )
    out_specs = (
        P("wsh", "ctx", None),
        P(),
        P("wsh", "ctx", None),
        P("wsh", None),
        P("wsh"),
        P("wsh", None),
        P("wsh", None),
        P("wsh"),
        P("wsh", None),
        P("wsh"),
        P("wsh"),
        P("wsh"),
        P("wsh", None),
        P("wsh"),
        P("wsh", None),
        P("wsh"),
        P("wsh"),
        P("wsh"),
    )
    program = fused_body if fused_fits(mesh) else body
    return jax.shard_map(program, mesh=mesh, in_specs=in_specs, out_specs=out_specs, check_vma=False)
```

```python
import math
import types

import jax
import jax.numpy as jnp
from jax import lax
from jax.experimental import pallas as pl
from jax.experimental.pallas import tpu as pltpu
from jax.sharding import PartitionSpec as P

D = 768
H = 12
HD = 64


EPSILON = 1e-06
MASKED = -1e30


def shifted(block, axis, distance):
    devices = range(lax.axis_size(axis))
    route = [((i - distance) % len(devices), i) for i in devices]
    return lax.ppermute(block, axis, route)


def layer_norm(value, gain, shift):
    mean = jnp.mean(value, axis=-1, keepdims=True)
    centered = value - mean
    spread = jnp.mean(centered * centered, axis=-1, keepdims=True)
    return centered * lax.rsqrt(spread + EPSILON) * gain + shift


def activate(value):
    return jax.nn.gelu(value, approximate=True)


def matmul(left, right):
    return jnp.dot(left, right, preferred_element_type=jnp.float32)


def left_product(left, right):
    return lax.dot_general(
        left, right, (((0,), (0,)), ((), ())), preferred_element_type=jnp.float32
    )


def right_product(left, right):
    return lax.dot_general(
        left, right, (((1,), (1,)), ((), ())), preferred_element_type=jnp.float32
    )


def document_of(positions, starts):
    return jnp.sum((starts[None, :] <= positions[:, None]).astype(jnp.int32), axis=1) - 1


def permitted(own_doc, own_live, other_doc, other_live):
    return (own_doc[:, None] == other_doc[None, :]) & (own_live[:, None] == other_live[None, :])


def block_weights(queries, key_block, allowed, score_scale):
    scores = (
        jnp.einsum("qhd,khd->hqk", queries, key_block, preferred_element_type=jnp.float32)
        * score_scale
    )
    return jnp.exp(jnp.where(allowed[None], scores, MASKED))


def forward_visit(sums_state, queries, key_block, value_block, allowed, score_scale):
    row_total, weighted = sums_state
    weights = block_weights(queries, key_block, allowed, score_scale)
    row_total = row_total + jnp.sum(weights, axis=-1)
    weighted = weighted + jnp.einsum(
        "hqk,khd->qhd",
        weights.astype(jnp.bfloat16),
        value_block,
        preferred_element_type=jnp.float32,
    )
    return (row_total, weighted)


def backward_visit(
    queries, key_block, value_block, allowed, score_scale, weighted_grad, total_grad
):
    weights = block_weights(queries, key_block, allowed, score_scale)
    value_part = jnp.einsum(
        "hqk,qhd->khd",
        weights.astype(jnp.bfloat16),
        weighted_grad,
        preferred_element_type=jnp.float32,
    )
    weight_grad = (
        jnp.einsum("qhd,khd->hqk", weighted_grad, value_block, preferred_element_type=jnp.float32)
        + total_grad[:, :, None]
    )
    score_grad = (weights * weight_grad).astype(jnp.bfloat16)
    query_part = (
        jnp.einsum("hqk,khd->qhd", score_grad, key_block, preferred_element_type=jnp.float32)
        * score_scale
    )
    key_part = (
        jnp.einsum("hqk,qhd->khd", score_grad, queries, preferred_element_type=jnp.float32)
        * score_scale
    )
    return (query_part, key_part, value_part)


def body(
    tokens,
    teacher,
    doc_lengths,
    valid_len,
    q_weight,
    q_bias,
    k_weight,
    v_weight,
    v_bias,
    o_weight,
    o_bias,
    ln1_gain,
    ln1_bias,
    in_weight,
    in_bias,
    out_weight,
    out_bias,
    ln2_gain,
    ln2_bias,
):
    gathered = (
        lax.all_gather(q_weight, "wsh", axis=0, tiled=True),
        lax.all_gather(q_bias, "wsh", axis=0, tiled=True),
        lax.all_gather(k_weight, "wsh", axis=0, tiled=True),
        lax.all_gather(v_weight, "wsh", axis=0, tiled=True),
        lax.all_gather(v_bias, "wsh", axis=0, tiled=True),
        lax.all_gather(o_weight, "wsh", axis=0, tiled=True),
        lax.all_gather(o_bias, "wsh", axis=0, tiled=True),
        lax.all_gather(ln1_gain, "wsh", axis=0, tiled=True),
        lax.all_gather(ln1_bias, "wsh", axis=0, tiled=True),
        lax.all_gather(in_weight, "wsh", axis=0, tiled=True),
        lax.all_gather(in_bias, "wsh", axis=0, tiled=True),
        lax.all_gather(out_weight, "wsh", axis=0, tiled=True),
        lax.all_gather(out_bias, "wsh", axis=0, tiled=True),
        lax.all_gather(ln2_gain, "wsh", axis=0, tiled=True),
        lax.all_gather(ln2_bias, "wsh", axis=0, tiled=True),
    )
    (
        w_query,
        b_query,
        w_key,
        w_value,
        b_value,
        w_out,
        b_out,
        gain_one,
        shift_one,
        w_inner,
        b_inner,
        w_back,
        b_back,
        gain_two,
        shift_two,
    ) = gathered
    gain_first = gain_one.astype(jnp.float32)
    shift_first = shift_one.astype(jnp.float32)
    gain_second = gain_two.astype(jnp.float32)
    shift_second = shift_two.astype(jnp.float32)
    inputs = tokens[0]
    row_count = inputs.shape[0]
    cycle_size = lax.axis_size("ctx")
    stream_count = lax.axis_size("wsh")
    position = lax.axis_index("ctx")
    score_scale = 1.0 / math.sqrt(HD)
    offsets = jnp.arange(row_count, dtype=jnp.int32)
    lengths = doc_lengths[0]
    starts = jnp.cumsum(lengths) - lengths
    limit = valid_len[0]

    def key_mask(block_index):
        where_rows = jnp.mod(block_index, cycle_size) * row_count + offsets
        return (document_of(where_rows, starts), where_rows < limit)

    own_doc, own_live = key_mask(position)
    input_float = inputs.astype(jnp.float32)
    queries = (
        (matmul(inputs, w_query) + b_query.astype(jnp.float32))
        .astype(jnp.bfloat16)
        .reshape(row_count, H, HD)
    )
    key_rows = matmul(inputs, w_key).astype(jnp.bfloat16).reshape(row_count, H, HD)
    value_rows = (
        (matmul(inputs, w_value) + b_value.astype(jnp.float32))
        .astype(jnp.bfloat16)
        .reshape(row_count, H, HD)
    )

    def visit_forward(sums_state, key_block, value_block, block_index):
        other_doc, other_live = key_mask(block_index)
        allowed = permitted(own_doc, own_live, other_doc, other_live)
        return forward_visit(sums_state, queries, key_block, value_block, allowed, score_scale)

    empty_state = (
        jnp.zeros((H, row_count), jnp.float32),
        jnp.zeros((row_count, H, HD), jnp.float32),
    )
    first_state = visit_forward(empty_state, key_rows, value_rows, position)

    def advance(step_index, loop_state):
        key_block, value_block, running = loop_state
        key_block, value_block = shifted((key_block, value_block), "ctx", 1)
        running = visit_forward(running, key_block, value_block, position - step_index)
        return (key_block, value_block, running)

    row_total, weighted = lax.fori_loop(
        1, cycle_size, advance, (key_rows, value_rows, first_state)
    )[2]
    normed = weighted / jnp.transpose(row_total)[:, :, None]
    context = normed.astype(jnp.bfloat16).reshape(row_count, D)
    attn = matmul(context, w_out) + b_out.astype(jnp.float32)
    first_sum = input_float + attn
    settled = layer_norm(first_sum, gain_first, shift_first)
    settled_low = settled.astype(jnp.bfloat16)
    inner = matmul(settled_low, w_inner) + b_inner.astype(jnp.float32)
    activated = activate(inner).astype(jnp.bfloat16)
    branch = matmul(activated, w_back) + b_back.astype(jnp.float32)
    second_sum = settled + branch
    result = layer_norm(second_sum, gain_second, shift_second)
    target = teacher[0].astype(jnp.float32)
    diff = jnp.where(own_live[:, None], result - target, 0.0)
    error_sum, live_count = lax.psum(
        (jnp.sum(diff * diff), jnp.sum(own_live.astype(jnp.float32))), ("ctx", "wsh")
    )
    loss = error_sum / (live_count * D)
    upstream = diff * (row_count * cycle_size * stream_count / live_count)
    unused_second, second_back = jax.vjp(layer_norm, second_sum, gain_second, shift_second)
    d_second, gain_two_grad, shift_two_grad = second_back(upstream)
    branch_grad = d_second.astype(jnp.bfloat16)
    back_weight_grad = left_product(activated, branch_grad)
    back_bias_grad = jnp.sum(branch_grad, axis=0, dtype=jnp.float32)
    d_activated = right_product(branch_grad, w_back)
    unused_inner, gelu_back = jax.vjp(activate, inner)
    inner_grad = gelu_back(d_activated)[0].astype(jnp.bfloat16)
    inner_weight_grad = left_product(settled_low, inner_grad)
    inner_bias_grad = jnp.sum(inner_grad, axis=0, dtype=jnp.float32)
    d_settled = d_second + right_product(inner_grad, w_inner)
    unused_first, first_back = jax.vjp(layer_norm, first_sum, gain_first, shift_first)
    d_first, gain_one_grad, shift_one_grad = first_back(d_settled)
    attn_grad = d_first.astype(jnp.bfloat16)
    out_weight_grad_local = left_product(context, attn_grad)
    out_bias_grad_local = jnp.sum(attn_grad, axis=0, dtype=jnp.float32)
    context_low = lax.optimization_barrier(right_product(attn_grad, w_out).astype(jnp.bfloat16))
    context_grad = context_low.astype(jnp.float32).reshape(row_count, H, HD)
    weighted_grad = (context_grad / jnp.transpose(row_total)[:, :, None]).astype(jnp.bfloat16)
    total_grad = -jnp.transpose(jnp.sum(context_grad * weighted, axis=-1)) / (row_total * row_total)

    def visit_backward(key_block, value_block, block_index):
        other_doc, other_live = key_mask(block_index)
        allowed = permitted(own_doc, own_live, other_doc, other_live)
        return backward_visit(
            queries, key_block, value_block, allowed, score_scale, weighted_grad, total_grad
        )

    query_sum, key_sum, value_sum = visit_backward(key_rows, value_rows, position)

    def advance_back(step_index, loop_state):
        key_block, value_block, query_acc, key_acc, value_acc = loop_state
        key_block, value_block = shifted((key_block, value_block), "ctx", 1)
        key_acc, value_acc = (
            shifted(key_acc.astype(jnp.bfloat16), "ctx", 1).astype(key_acc.dtype),
            shifted(value_acc.astype(jnp.bfloat16), "ctx", 1).astype(value_acc.dtype),
        )
        query_part, key_part, value_part = visit_backward(
            key_block, value_block, position - step_index
        )
        return (
            key_block,
            value_block,
            query_acc + query_part,
            key_acc + key_part,
            value_acc + value_part,
        )

    loop_state = lax.fori_loop(
        1, cycle_size, advance_back, (key_rows, value_rows, query_sum, key_sum, value_sum)
    )
    query_total = loop_state[2]
    key_total, value_total = (
        shifted(loop_state[3].astype(jnp.bfloat16), "ctx", 1).astype(jnp.float32),
        shifted(loop_state[4].astype(jnp.bfloat16), "ctx", 1).astype(jnp.float32),
    )
    query_grad = query_total.astype(jnp.bfloat16).reshape(row_count, D)
    key_grad = key_total.astype(jnp.bfloat16).reshape(row_count, D)
    value_grad = value_total.astype(jnp.bfloat16).reshape(row_count, D)
    query_weight_grad = left_product(inputs, query_grad)
    query_bias_grad = jnp.sum(query_grad, axis=0, dtype=jnp.float32)
    key_weight_grad = left_product(inputs, key_grad)
    value_weight_grad = left_product(inputs, value_grad)
    value_bias_grad = jnp.sum(value_grad, axis=0, dtype=jnp.float32)
    input_grad = (
        d_first
        + right_product(query_grad, w_query)
        + right_product(key_grad, w_key)
        + right_product(value_grad, w_value)
    )
    reduced = (
        lax.psum_scatter(
            query_weight_grad.astype(jnp.bfloat16), "wsh", scatter_dimension=0, tiled=True
        ).astype(jnp.float32),
        lax.psum_scatter(
            query_bias_grad.astype(jnp.bfloat16), "wsh", scatter_dimension=0, tiled=True
        ).astype(jnp.float32),
        lax.psum_scatter(
            key_weight_grad.astype(jnp.bfloat16), "wsh", scatter_dimension=0, tiled=True
        ).astype(jnp.float32),
        lax.psum_scatter(
            value_weight_grad.astype(jnp.bfloat16), "wsh", scatter_dimension=0, tiled=True
        ).astype(jnp.float32),
        lax.psum_scatter(
            value_bias_grad.astype(jnp.bfloat16), "wsh", scatter_dimension=0, tiled=True
        ).astype(jnp.float32),
        lax.psum_scatter(
            out_weight_grad_local.astype(jnp.bfloat16), "wsh", scatter_dimension=0, tiled=True
        ).astype(jnp.float32),
        lax.psum_scatter(
            out_bias_grad_local.astype(jnp.bfloat16), "wsh", scatter_dimension=0, tiled=True
        ).astype(jnp.float32),
        lax.psum_scatter(
            gain_one_grad.astype(jnp.bfloat16), "wsh", scatter_dimension=0, tiled=True
        ).astype(jnp.float32),
        lax.psum_scatter(
            shift_one_grad.astype(jnp.bfloat16), "wsh", scatter_dimension=0, tiled=True
        ).astype(jnp.float32),
        lax.psum_scatter(
            inner_weight_grad.astype(jnp.bfloat16), "wsh", scatter_dimension=0, tiled=True
        ).astype(jnp.float32),
        lax.psum_scatter(
            inner_bias_grad.astype(jnp.bfloat16), "wsh", scatter_dimension=0, tiled=True
        ).astype(jnp.float32),
        lax.psum_scatter(
            back_weight_grad.astype(jnp.bfloat16), "wsh", scatter_dimension=0, tiled=True
        ).astype(jnp.float32),
        lax.psum_scatter(
            back_bias_grad.astype(jnp.bfloat16), "wsh", scatter_dimension=0, tiled=True
        ).astype(jnp.float32),
        lax.psum_scatter(
            gain_two_grad.astype(jnp.bfloat16), "wsh", scatter_dimension=0, tiled=True
        ).astype(jnp.float32),
        lax.psum_scatter(
            shift_two_grad.astype(jnp.bfloat16), "wsh", scatter_dimension=0, tiled=True
        ).astype(jnp.float32),
    )
    summed = lax.psum(
        (
            reduced[0],
            reduced[1],
            reduced[2],
            reduced[3],
            reduced[4],
            reduced[5],
            reduced[6],
            reduced[7],
            reduced[8],
            reduced[9],
            reduced[10],
            reduced[11],
            reduced[12],
            reduced[13],
            reduced[14],
        ),
        "ctx",
    )
    return (
        result.astype(jnp.bfloat16)[None],
        loss,
        input_grad[None],
        summed[0],
        summed[1],
        summed[2],
        summed[3],
        summed[4],
        summed[5],
        summed[6],
        summed[7],
        summed[8],
        summed[9],
        summed[10],
        summed[11],
        summed[12],
        summed[13],
        summed[14],
    )


BF = jnp.bfloat16
F32 = jnp.float32
FF = 3072
ROWS = 128
HEADS = 3
HW = HEADS * HD
GROUP = 4
CTX = 8
MESH = pl.DeviceIdType.MESH

Q, K, V, O, IN, OUT, PART_Q, PART_K, PART_V = range(9)
SLICE = 256
WEIGHT_SHAPES = [(192, 768)] * 4 + [(192, 3072), (768, 768)] + [(192, SLICE)] * 3
SECOND_WAY = {O: 1, IN: 2, OUT: 1, PART_Q: 1, PART_K: 1, PART_V: 1}
LOT_O, LOT_IN, LOT_OUT = (0,), (1, 2), (3, 4, 5, 6)
LOT_PAIR = LOT_O + LOT_IN + LOT_OUT[:2]
LOTS = [(96, 384)] + [(4, 48, 384)] * 2 + [(96, 384)] * 4
PIECES = {IN: (1, 4), OUT: (4, 1)}
HEAD_COLS = 640

(
    SMALL,
    WEIGHT_X,
    WEIGHT_SECOND,
    WEIGHT_CORE,
    WEIGHT_CORE_X,
    WEIGHT_CORE_SECOND,
    X_LINE,
    X_EDGE,
    KEY_VALUE,
    CONTEXT,
    CONTEXT_GRAD,
    KEY_VALUE_GRAD,
    INPUT_PARTS,
    SETTLED_ALL,
    CONTEXT_ALL,
    ATTN_GRAD_ALL,
    BRANCH_GRAD_ALL,
    REDUCE,
    SPREAD,
    GIVE,
    OWN,
    GROUP_X,
    HEADS_CORE,
    HEADS_X,
    HEADS_Y,
    HEADS_LINE,
    HEADS_EDGE,
    HEADS_PAIR,
    VECTORS_W,
    VECTORS_Z,
    VECTORS_Y,
    VECTORS_CORE,
    TOKENS,
    TEACHER,
    OUTPUT,
    INPUT_GRAD,
    LOAD,
) = range(37)


def fused_fits(mesh):
    return mesh.shape["ctx"] == CTX and mesh.shape["wsh"] == GROUP


def tn(left, right):
    return lax.dot_general(
        left, right, (((0,), (0,)), ((), ())), preferred_element_type=jnp.float32
    )


def norm_parts(value):
    mean = jnp.mean(value, axis=-1, keepdims=True)
    centered = value - mean
    spread = jnp.mean(centered * centered, axis=-1, keepdims=True)
    inverse = lax.rsqrt(spread + EPSILON)
    return centered * inverse, inverse


def norm_back(upstream_gained, normal, inverse):
    return (
        upstream_gained
        - jnp.mean(upstream_gained, axis=-1, keepdims=True)
        - normal * jnp.mean(upstream_gained * normal, axis=-1, keepdims=True)
    ) * inverse


GELU_C = math.sqrt(2.0 / math.pi)


class Numbers:
    def __init__(self):
        self.count = 0
        self.table = {}

    def take(self, key, size=1):
        if key not in self.table:
            self.table[key] = self.count
            self.count += size
        return self.table[key]


def scratch_table():
    s = types.SimpleNamespace()
    s.full = {k: pltpu.VMEM((GROUP, *WEIGHT_SHAPES[k]), BF) for k in SECOND_WAY}
    s.turned = pltpu.VMEM((SLICE, D), BF)
    s.head_weight = pltpu.VMEM((3 * HW, D), BF)
    s.tall_bias = pltpu.VMEM((SLICE, ROWS), F32)
    s.head_bias = pltpu.VMEM((3 * HW, ROWS), F32)
    s.x = pltpu.VMEM((ROWS, D), BF)
    s.xt = pltpu.VMEM((CTX, D, ROWS), BF)
    s.teacher = pltpu.VMEM((ROWS, D), BF)
    s.small = pltpu.VMEM((GROUP, 16, D), BF)
    s.vectors = pltpu.VMEM((16, D), F32)
    s.kv = pltpu.VMEM((CTX, 2 * HW, ROWS), BF)
    s.q = pltpu.VMEM((4, HW, ROWS), BF)
    s.weights = pltpu.VMEM((CTX, HEADS, ROWS, 4 * ROWS), F32)
    s.mix = pltpu.VMEM((HEADS, HD, 4 * ROWS), F32)
    s.total = pltpu.VMEM((HEADS, 8, 4 * ROWS), F32)
    s.ctx_send = pltpu.VMEM((4, HW, ROWS), BF)
    s.ctx = pltpu.VMEM((4, HW, ROWS), BF)
    s.inner = pltpu.VMEM((4, ROWS, D), F32)
    s.act = pltpu.VMEM((4, ROWS, D), BF)
    s.first = pltpu.VMEM((ROWS, D), F32)
    s.keep = pltpu.VMEM((ROWS, D), F32)
    s.inverse = pltpu.VMEM((ROWS, 128), F32)
    s.set_low = pltpu.VMEM((ROWS, D), BF)
    s.ag_half = pltpu.VMEM((2, ROWS, 384), BF)
    s.bg = pltpu.VMEM((2, ROWS, 384), BF)
    s.set_all = pltpu.VMEM((GROUP, ROWS, D), BF)
    s.ctx_all = pltpu.VMEM((GROUP, 2, HW, ROWS), BF)
    s.ag_all = pltpu.VMEM((GROUP, ROWS, 384), BF)
    s.inner_all = pltpu.VMEM((GROUP * ROWS, D), F32)
    s.act_all = pltpu.VMEM((GROUP * ROWS, D), BF)
    s.bg_all = pltpu.VMEM((2, GROUP, ROWS, 384), BF)
    s.cg_send = pltpu.VMEM((4, HW, ROWS), BF)
    s.cg = pltpu.VMEM((4, HW, ROWS), BF)
    s.wg = pltpu.VMEM((HEADS, HD, 4 * ROWS), BF)
    s.dkv = pltpu.VMEM((2, 4, 2 * HW, ROWS), BF)
    s.dkv_pair = pltpu.VMEM((4, 2 * HW, ROWS), BF)
    s.grads = pltpu.VMEM((HEAD_COLS, 4 * ROWS), BF)
    s.dx_send = pltpu.VMEM((4, ROWS, D), BF)
    s.dx_end = pltpu.VMEM((3, ROWS, D), BF)
    s.dx_middle = pltpu.VMEM((2, ROWS, D), BF)
    s.dx_got = pltpu.VMEM((2, ROWS, D), BF)
    s.dx_back = pltpu.VMEM((ROWS, D), BF)
    s.dx_last = pltpu.VMEM((ROWS, D), BF)
    s.column = pltpu.VMEM((D, ROWS), F32)
    s.heads = pltpu.VMEM((2, 2, HW, HEAD_COLS), BF)
    s.heads_core = pltpu.VMEM((2, HW, HEAD_COLS), BF)
    s.heads_sum = pltpu.VMEM((2, HW, HEAD_COLS), BF)
    s.heads_x = pltpu.VMEM((HW, HEAD_COLS), BF)
    s.heads_row = pltpu.VMEM((2, HW // 2, HEAD_COLS), BF)
    s.heads_y = pltpu.VMEM((HW // 2, HEAD_COLS), BF)
    s.heads_done = pltpu.VMEM((4, HW // 2, HEAD_COLS), BF)
    s.part = [pltpu.VMEM((2, 2, *shape), BF) for shape in LOTS]
    def lots(*dims):
        return [
            pltpu.VMEM((*dims[1 if k in LOT_PAIR else 0], *shape), BF) for k, shape in enumerate(LOTS)
        ]

    steps = [((2, 2), (2,)), ((2,), (2,)), ((), ())]
    s.got = [list(lot) for lot in zip(*(lots(*step) for step in steps))]
    s.sum = [list(lot) for lot in zip(*(lots(*step) for step in steps[:2]))]
    s.own = {k: pltpu.VMEM(LOTS[k], BF) for k in LOT_IN}
    s.done = [pltpu.VMEM((2, 2, *shape), BF) for shape in LOTS]
    s.smalls = pltpu.VMEM((GROUP, 16, HW), F32)
    s.sg = pltpu.VMEM((16, D), F32)
    s.sg_all = pltpu.VMEM((16, D), F32)
    s.sg_rows = pltpu.VMEM((2, 8, D), F32)
    s.sg_w = pltpu.VMEM((GROUP, 16, D), F32)
    s.sg_z = pltpu.VMEM((4, 8, D), F32)
    s.sg_y = pltpu.VMEM((2, 8, D), F32)
    s.out_low = pltpu.VMEM((ROWS, D), BF)
    return vars(s)


LOCAL_SEMS = 32
REMOTE_SEMS = 240


def is_memory(item):
    return not isinstance(item, (dict, list))


def scratch_shapes():
    return jax.tree.flatten(scratch_table(), is_leaf=is_memory)


def fused_kernel(*refs):
    (tokens, teacher), shards = refs[:2], refs[2:8]
    lengths, valid = refs[8:10]
    biases = refs[10:19]
    output, input_grad_out = refs[19:21]
    grad_o, *grad_in, grad_out = refs[21:25]
    heads_out, smalls_out, rows_out = refs[25:28]
    flat, shape = scratch_shapes()
    S = types.SimpleNamespace(**jax.tree.unflatten(shape, refs[28 : 28 + len(flat)]))
    send_sems, recv_sems, local_sems = refs[28 + len(flat) :]

    c = lax.axis_index("ctx")
    w = lax.axis_index("wsh")
    a, b = c // 2, c % 2
    x, core = w // 2, w % 2

    numbers = Numbers()
    locals_ = Numbers()
    started = []

    def bit_xor(value, j):
        out = value
        bit = 1
        while bit <= j:
            if j & bit:
                has = (value // bit) % 2
                out = out + bit * (1 - 2 * has)
            bit *= 2
        return out

    at_end = a * (3 - a) == 0
    roles, sent_by_role = [None], []

    def only(end):
        def run(action):
            roles.append(end)
            pl.when(at_end if end else jnp.logical_not(at_end))(action)
            roles.pop()

        return run

    def remote(key, src, dst, c_bits, w_bits, offset=0, size=1, to=None, like=None):
        number = numbers.take(key, size) + offset
        c_to, w_to = bit_xor(c, c_bits), bit_xor(w, w_bits) if to is None else to
        copy = pltpu.make_async_remote_copy(
            src_ref=src,
            dst_ref=dst,
            send_sem=send_sems.at[number],
            recv_sem=recv_sems.at[number],
            device_id={"ctx": c_to, "wsh": w_to},
            device_id_type=MESH,
        )
        copy.start()
        if roles[-1] is None:
            started.append(copy)
        else:
            sent_by_role.append((roles[-1], like, number))

    def arrived(key, landing, offset=0):
        number = numbers.take(key) + offset
        pltpu.make_async_copy(landing, landing, recv_sems.at[number]).wait()

    def local(key, src, dst):
        copy = pltpu.make_async_copy(src, dst, local_sems.at[locals_.take(key)])
        copy.start()
        return copy

    peers = [(c, bit_xor(w, j)) for j in (1, 2, 3)]
    peers += [(bit_xor(c, j), w) for j in range(1, CTX)]
    peers += [(bit_xor(c, 1), bit_xor(w, 1))]

    def bit(value, mask):
        return (value // mask) % 2

    first_col = pl.multiple_of((3 * a) // 2 * 128, 128)
    first_row = pl.multiple_of(a % 2 * 64, 64)

    def shard(name):
        if name < PART_Q:
            return shards[name]
        return shards[name - PART_Q].at[:, pl.ds(first_col, SLICE)]

    loads = {TOKENS: local(TOKENS, tokens.at[0], S.x)}
    for name in (PART_K, PART_V, PART_Q, O, IN, OUT):
        loads[name] = local((LOAD, name), shard(name), S.full[name].at[w])
    loads[TEACHER] = local(TEACHER, teacher.at[0], S.teacher)

    barrier = pltpu.get_barrier_semaphore()
    for c_to, w_to in peers:
        pl.semaphore_signal(
            barrier, inc=1, device_id={"ctx": c_to, "wsh": w_to}, device_id_type=MESH
        )
    pl.semaphore_wait(barrier, len(peers))

    def mine(name):
        return bit(c, SECOND_WAY[name])

    def pieces(name):
        tall, across = PIECES.get(name, (1, 1))
        return range(tall * across)

    def piece(name, which, number):
        rows, cols = WEIGHT_SHAPES[name]
        tall, across = PIECES.get(name, (1, 1))
        high, broad = rows // 2 // tall, cols // across
        row = which * (rows // 2) + number // across * high
        return pl.ds(pl.multiple_of(row, 16), high), slice(
            number % across * broad, (number % across + 1) * broad
        )

    def send_core(name):
        remote((WEIGHT_CORE, name), shard(name), S.full[name].at[w], 0, 1)

    def send_x(name):
        for i in pieces(name):
            rows, cols = piece(name, mine(name), i)
            if name < PART_Q:
                source = shards[name].at[rows, cols]
            else:
                source = shards[name - PART_Q].at[rows, pl.ds(first_col, SLICE)]
            remote((WEIGHT_X, name, i), source, S.full[name].at[w, rows, cols], 0, 2)

    for name in (PART_K, PART_V, PART_Q):
        send_x(name)
        send_core(name)
    loads[TOKENS].wait()
    x_low = S.x[...]
    S.xt[c] = x_low.T
    bias_rows = [row[...].astype(F32).reshape(1, HW) for row in biases[:8]]
    tall = jnp.concatenate(bias_rows, axis=0)
    valid_high = (valid[0] // 64).astype(F32)
    valid_low = (valid[0] % 64).astype(F32)
    wide_rows = [biases[8][...].astype(F32).reshape(1, D)]
    wide_rows += [jnp.full((1, D), 64.0, F32) * valid_high, jnp.full((1, D), 1.0, F32) * valid_low]
    wide_rows += [jnp.zeros((5, D), F32)]
    S.small[w, :, 0:HW] = jnp.concatenate(
        [tall, jnp.concatenate(wide_rows, axis=0)[:, 0:HW]], axis=0
    ).astype(BF)
    S.small[w, 8:16, HW:D] = jnp.concatenate(wide_rows, axis=0)[:, HW:D].astype(BF)

    for j in (1, 2, 3):
        remote((SMALL, j), S.small.at[w], S.small.at[w], 0, j)
    remote((X_LINE, 1), S.xt.at[c], S.xt.at[c], 2, 0)

    @only(False)
    def x_to_middle():
        remote((X_LINE, 3), S.xt.at[c], S.xt.at[c], 6, 0, like=lambda: S.xt.at[0])

    for name in (O, IN, OUT):
        send_x(name)
        send_core(name)

    def pump_x(name, number=0):
        slot = S.full[name].at[bit_xor(w, 2), *piece(name, mine(name), number)]
        arrived((WEIGHT_X, name, number), slot)
        remote((WEIGHT_SECOND, name, number), slot, slot, SECOND_WAY[name], 0)
        remote((WEIGHT_CORE_X, name, number), slot, slot, 0, 1)

    def pump_second(name, number=0):
        slot = S.full[name].at[bit_xor(w, 2), *piece(name, 1 - mine(name), number)]
        arrived((WEIGHT_SECOND, name, number), slot)
        remote((WEIGHT_CORE_SECOND, name, number), slot, slot, 0, 1)

    def weight_ready(name, numbers_=(0,), first=True):
        full = S.full[name]
        if first:
            loads[name].wait()
            arrived((WEIGHT_CORE, name), full.at[bit_xor(w, 1)])
        for i in numbers_:
            near = full.at[bit_xor(w, 3), *piece(name, mine(name), i)]
            far = full.at[bit_xor(w, 3), *piece(name, 1 - mine(name), i)]
            arrived((WEIGHT_CORE_X, name, i), near)
            arrived((WEIGHT_CORE_SECOND, name, i), far)

    def square(name):
        return S.full[name][...].reshape(D, D)

    starts, running = [], 0
    for i in range(lengths.shape[1]):
        starts.append(running)
        running = running + lengths[0, i]
    limit = valid[0]

    def code_of(position):
        code = jnp.zeros(position.shape, jnp.int32)
        for start in starts:
            code = code + (start <= position).astype(jnp.int32)
        return 2 * code + (position < limit).astype(jnp.int32)

    lane = lax.broadcasted_iota(jnp.int32, (1, 4 * ROWS), 1)
    query_code = code_of((2 * (lane // ROWS) + b) * ROWS + lane % ROWS)

    def key_code(block):
        return code_of(block * ROWS + lax.broadcasted_iota(jnp.int32, (ROWS, 1), 0))

    own_live = c * ROWS + lax.broadcasted_iota(jnp.int32, (ROWS, 1), 0) < limit

    def block_on(j, pair):
        return 2 * bit_xor(a, j) + pair

    def pass_x(key, j, onward, bits):
        block = S.xt.at[block_on(j, b)]
        arrived((key, j), block)
        remote(onward, block, block, bits, 0, like=lambda: S.xt.at[0])

    def vector(row):
        return S.vectors[row : row + 1, :]

    def to_group(key, source_of, everywhere):
        for j in (1, 2, 3):
            to = bit_xor(w, j)
            remote((*key, j), source_of(to), everywhere.at[w], 0, j)

    def from_group(key, everywhere):
        for j in (1, 2, 3):
            arrived((*key, j), everywhere.at[bit_xor(w, j)])

    def to_near(key, source, everywhere):
        for j in (1, 2):
            remote((*key, j), source, everywhere.at[w], 0, j)

    def pass_to_core(key, everywhere):
        slot = everywhere.at[bit_xor(w, 2)]
        arrived((*key, 2), slot)
        remote((*key, 3), slot, slot, 0, 1)

    def from_near(key, everywhere):
        for j in (1, 3):
            arrived((*key, j), everywhere.at[bit_xor(w, j)])

    def lanes(parts):
        return jnp.concatenate(parts, axis=1)

    finishing = []

    def small_vectors():
        for j in (1, 2, 3):
            arrived((SMALL, j), S.small.at[bit_xor(w, j)])
        S.vectors[0:8, :] = jnp.concatenate(
            [S.small[i, 0:8, 0:HW].astype(F32) for i in range(GROUP)], axis=1
        )
        small = [S.small[i, 8:16, :].astype(F32) for i in range(GROUP)]
        S.vectors[8:16, :] = jnp.concatenate(
            [part[0:1] for part in small]
            + [sum(part[1:2] + part[2:3] for part in small), jnp.zeros((3, D), F32)],
            axis=0,
        )

    def pass_near_end():
        arrived((X_LINE, 1), S.xt.at[block_on(1, b)])

        @only(False)
        def to_other_middle():
            block = S.xt.at[block_on(1, b)]
            remote((X_LINE, 2), block, block, 6, 0, like=lambda: S.xt.at[0])

    def pass_middle():
        @only(False)
        def to_near_end():
            pass_x(X_LINE, 3, (X_EDGE, 2), 2)

    def pass_far_end():
        @only(False)
        def to_near_end():
            pass_x(X_LINE, 2, (X_EDGE, 3), 2)

    def head_weights():
        for name in (PART_K, PART_V, PART_Q):
            weight_ready(name)
        for i, (name, bias) in enumerate(((PART_K, None), (PART_V, 1), (PART_Q, 0))):
            rows = slice(HW * i, HW * (i + 1))
            S.turned[...] = S.full[name][...].reshape(D, SLICE).T
            S.head_weight[rows, :] = S.turned[pl.ds(first_row, HW), :]
            if bias is None:
                S.head_bias[rows, :] = jnp.zeros((HW, ROWS), F32)
            else:
                row = S.vectors[bias : bias + 1, pl.ds(first_col, SLICE)]
                S.tall_bias[...] = jnp.broadcast_to(row, (ROWS, SLICE)).T
                S.head_bias[rows, :] = S.tall_bias[pl.ds(first_row, HW), :]

    def project(j):
        if j > 1:

            @only(True)
            def from_middle():
                arrived((X_EDGE, j), S.xt.at[block_on(j, b)])

        block = block_on(j, b)
        out = matmul(S.head_weight[...], S.xt[block]) + S.head_bias[...]
        S.kv[block] = out[0 : 2 * HW].astype(BF)
        S.q[block // 2] = out[2 * HW :].astype(BF)
        remote((KEY_VALUE, j), S.kv.at[block], S.kv.at[block], 1, 0)

    score_scale = 1.0 / math.sqrt(HD)

    def wide(ref, h):
        return lanes([ref[i, HD * h : HD * (h + 1), :] for i in range(4)])

    def attend_block(block):
        allowed = key_code(block) == query_code
        for h in range(HEADS):
            scores = tn(S.kv[block, HD * h : HD * (h + 1), :], wide(S.q, h)) * score_scale
            weights = jnp.exp(jnp.where(allowed, scores, MASKED))
            S.weights[block, h] = weights
            S.total[h, 0:1, :] += jnp.sum(weights, axis=0, keepdims=True)
            value_t = S.kv[block, HW + HD * h : HW + HD * (h + 1), :]
            S.mix[h] += matmul(value_t, weights.astype(BF))

    def attend_line():
        S.mix[...] = jnp.zeros(S.mix.shape, F32)
        S.total[...] = jnp.zeros(S.total.shape, F32)

        @pl.loop(0, 4)
        def every_block(i):
            attend_block(2 * i + b)

    def attend_pair(j):
        arrived((KEY_VALUE, j), S.kv.at[block_on(j, 1 - b)])
        attend_block(block_on(j, 1 - b))

    def send_context():
        for h in range(HEADS):
            context_t = (S.mix[h] / S.total[h, 0:1, :]).astype(BF)
            for i in range(4):
                S.ctx_send[i, HD * h : HD * (h + 1), :] = context_t[:, ROWS * i : ROWS * (i + 1)]
        for j in (1, 2, 3):
            to = bit_xor(a, j)
            remote((CONTEXT, j), S.ctx_send.at[to], S.ctx.at[a], 2 * j, 0)
        S.ctx[a] = S.ctx_send[a]

    def first_norm():
        weight_ready(O)
        for j in (1, 2, 3):
            arrived((CONTEXT, j), S.ctx.at[bit_xor(a, j)])
        attn = tn(S.ctx[...].reshape(D, ROWS), square(O)) + vector(2)
        normal_one, inverse_one = norm_parts(S.x[...].astype(F32) + attn)
        settled = normal_one * vector(3) + vector(4)
        S.first[...] = normal_one
        S.inverse[...] = jnp.broadcast_to(inverse_one, (ROWS, 128))
        S.keep[...] = settled
        S.set_low[...] = settled.astype(BF)
        to_near((SETTLED_ALL,), S.set_low, S.set_all)
        S.set_all[w] = S.set_low[...]
        to_group((CONTEXT_ALL,), lambda to: S.ctx.at[pl.ds(2 * (to // 2), 2)], S.ctx_all)
        S.ctx_all[w] = S.ctx[pl.ds(2 * x, 2)]

    def pass_settled():
        pass_to_core((SETTLED_ALL,), S.set_all)

    def gelu(inner):
        return 0.5 * inner * (1.0 + jnp.tanh(GELU_C * (inner + 0.044715 * inner * inner * inner)))

    def gelu_slope(inner):
        squared = inner * inner
        bend = jnp.tanh(GELU_C * (inner + 0.044715 * squared * inner))
        return 0.5 * (1.0 + bend) + 0.5 * inner * (1.0 - bend * bend) * (
            GELU_C * (1.0 + 3 * 0.044715 * squared)
        )

    def feed_in(t):
        weight_ready(IN, (t,), t == 0)
        w_part = S.full[IN][:, :, D * t : D * (t + 1)].reshape(D, D)
        inner = matmul(S.set_low[...], w_part) + vector(8 + t)
        S.inner[t] = inner
        S.act[t] = gelu(inner).astype(BF)

    def note(row, value):
        S.sg[row : row + 1, :] = jnp.sum(value.astype(F32), axis=0, keepdims=True)

    def result_and_loss():
        weight_ready(OUT, range(4))
        branch = vector(5)
        for t in range(4):
            branch = branch + matmul(S.act[t], S.full[OUT][t])
        normal_two, inverse_two = norm_parts(S.keep[...] + branch)
        result = normal_two * vector(6) + vector(7)
        S.out_low[...] = result.astype(BF)
        finishing.append(local(OUTPUT, S.out_low, output))
        loads[TEACHER].wait()
        diff = jnp.where(own_live, result - S.teacher[...].astype(F32), 0.0)
        count = vector(12)
        upstream = diff * ((ROWS * CTX * GROUP) / count)
        d_second = norm_back(upstream * vector(6), normal_two, inverse_two)
        for i in range(2):
            S.bg[i] = d_second[:, 384 * i : 384 * (i + 1)].astype(BF)
            to_near((BRANCH_GRAD_ALL, i), S.bg.at[i], S.bg_all.at[i])
        for i in range(2):
            S.bg_all[i, w] = S.bg[i]
        S.keep[...] = d_second
        S.sg[...] = jnp.zeros((16, D), F32)
        note(12, diff * diff)
        S.sg[13:14, :] = count * (1.0 / (CTX * GROUP))
        note(6, upstream * normal_two)
        note(7, upstream)
        note(5, d_second.astype(BF))

    def feed_back():
        d_settled = S.keep[...]
        branch_grad = lanes([S.bg[0], S.bg[1]])
        for t in range(4):
            d_act = right_product(branch_grad, S.full[OUT][t])
            inner_grad = (d_act * gelu_slope(S.inner[t])).astype(BF)
            note(8 + t, inner_grad)
            w_part = S.full[IN][:, :, D * t : D * (t + 1)].reshape(D, D)
            d_settled = d_settled + right_product(inner_grad, w_part)
        S.keep[...] = d_settled

    def pass_branch_grad(i):
        pass_to_core((BRANCH_GRAD_ALL, i), S.bg_all.at[i])

    def first_norm_back():
        d_settled, normal_one = S.keep[...], S.first[...]
        d_first = norm_back(d_settled * vector(3), normal_one, S.inverse[:, 0:1])
        attn_grad = d_first.astype(BF)
        context_grad = right_product(attn_grad, square(O)).T.astype(BF)
        for i in range(4):
            S.cg_send[i] = context_grad[HW * i : HW * (i + 1), :]
        for j in (1, 2, 3):
            to = bit_xor(a, j)
            remote((CONTEXT_GRAD, j), S.cg_send.at[to], S.cg.at[a], 2 * j, 0)
        S.cg[a] = S.cg_send[a]
        for i in range(2):
            S.ag_half[i] = attn_grad[:, 384 * i : 384 * (i + 1)]
        to_group((ATTN_GRAD_ALL,), lambda to: S.ag_half.at[to % 2], S.ag_all)
        S.ag_all[w] = S.ag_half[core]
        note(3, d_settled * normal_one)
        note(4, d_settled)
        note(2, attn_grad)
        S.keep[...] = d_first

    half = a // 2

    def y_end(lot):
        got, total = S.got[lot], S.sum[lot]
        arrived((REDUCE, lot, 0), got[0])
        total[0][...] = (S.part[lot][b].astype(F32) + got[0][...].astype(F32)).astype(BF)

        @only(True)
        def to_middle():
            remote((REDUCE, lot, 1), total[0], got[1], 2, 0, like=lambda: got[1])

    def y_middle(lot):
        @only(False)
        def swap_halves():
            got, total = S.got[lot], S.sum[lot]
            arrived((REDUCE, lot, 1), got[1])
            total[1][...] = (total[0][...].astype(F32) + got[1][...].astype(F32)).astype(BF)
            there = total[1].at[1 - half]
            remote((REDUCE, lot, 2), there, got[2], 6, 0, like=lambda: got[2])

    def y_spread_middle(lot):
        part = S.done[lot].at[b, half]
        remote((SPREAD, lot, 0), part, part, 6, 0, like=lambda: S.done[lot].at[0, 0])

    def y_last(lot):
        @only(False)
        def own_half():
            got = S.got[lot][2]
            arrived((REDUCE, lot, 2), got)
            total = (S.sum[lot][1][half].astype(F32) + got[...].astype(F32)).astype(BF)
            if lot in LOT_IN:
                own, done = S.own[lot], S.done[lot]
                own[...] = total
                done[b, half, w] = own[w]
                for q in (1, 2, 3):
                    slot = done.at[b, half, w]
                    to = bit_xor(w, q)
                    remote((GROUP_X, lot, q), own.at[to], slot, 0, q, like=lambda: own.at[0])
            else:
                S.done[lot][b, half] = total
                y_spread_middle(lot)

    def y_group(lot):
        @only(False)
        def gathered():
            for q in (1, 2, 3):
                arrived((GROUP_X, lot, q), S.done[lot].at[b, half, bit_xor(w, q)])
            y_spread_middle(lot)

    def y_spread_end(lot):
        @only(False)
        def to_end():
            done = S.done[lot].at[b]
            arrived((SPREAD, lot, 0), S.done[lot].at[b, 1 - half])
            remote((SPREAD, lot, 1), done, done, 2, 0, like=lambda: S.done[lot].at[0])

    def result_of(lot):
        return grad_in[lot - LOT_IN[0]] if lot in LOT_IN else grad_out.at[(lot - LOT_OUT[0]) // 2, (lot - LOT_OUT[0]) % 2]

    def y_give(lot):
        done = S.done[lot].at[b]

        @only(True)
        def from_middle_device():
            arrived((SPREAD, lot, 1), done)

        if lot not in LOT_O:
            out = result_of(lot).at[b]
            remote((GIVE, lot), done, out, 1, 0)
            finishing.append(local((GIVE, lot), done, out))
            return
        remote((GIVE, 0), done, grad_o.at[core], 1, 0, core, 2, 2 * x + b)

        @pl.when(core == b)
        def keep_own():
            local((OWN, 0), done, grad_o.at[core])

        @pl.when(core != b)
        def give_core():
            remote((OWN, 0), done, grad_o.at[core], 0, 1)
            started.pop()

    def settle():
        for lot in LOT_PAIR[1:]:
            arrived((GIVE, lot), result_of(lot).at[1 - b])
        done = S.done[0].at[b]

        @pl.when(core == b)
        def from_chip():
            pltpu.make_async_copy(
                done, grad_o.at[core], local_sems.at[locals_.take((OWN, 0))]
            ).wait()
            arrived((OWN, 0), grad_o.at[1 - core])

        @pl.when(core != b)
        def from_partner():
            arrived((GIVE, 0), grad_o.at[0], 0)
            arrived((GIVE, 0), grad_o.at[1], 1)
            sent = numbers.take((OWN, 0))
            pltpu.make_async_copy(done, done, send_sems.at[sent]).wait()

    def reduce_start(lot):
        @only(True)
        def to_middle():
            target = S.got[lot][0]
            remote((REDUCE, lot, 0), S.part[lot], target, 2, 0, like=lambda: target)

    def reduce_middle(lot):
        @only(False)
        def swap_halves():
            got = S.got[lot][0]
            arrived((REDUCE, lot, 0), got)
            total = S.part[lot][...].astype(F32) + got[...].astype(F32)
            S.sum[lot][0][...] = total.astype(BF)
            there, target = S.sum[lot][0].at[1 - half], S.got[lot][1]
            remote((REDUCE, lot, 1), there, target, 6, 0, like=lambda: target)

    def reduce_pair(lot):
        @only(False)
        def swap_quarters():
            got = S.got[lot][1]
            arrived((REDUCE, lot, 1), got)
            total = S.sum[lot][0][half].astype(F32) + got[...].astype(F32)
            S.sum[lot][1][...] = total.astype(BF)
            there, target = S.sum[lot][1].at[1 - b], S.got[lot][2]
            remote((REDUCE, lot, 2), there, target, 1, 0, like=lambda: target)

    def reduce_last(lot):
        @only(False)
        def own_quarter():
            got = S.got[lot][2]
            arrived((REDUCE, lot, 2), got)
            total = (S.sum[lot][1][b].astype(F32) + got[...].astype(F32)).astype(BF)
            S.done[lot][half, b] = total
            part = S.done[lot].at[half, b]
            remote((SPREAD, lot, 0), part, part, 1, 0, like=lambda: S.done[lot].at[0, 0])

    def spread_middle(lot):
        @only(False)
        def swap_back():
            arrived((SPREAD, lot, 0), S.done[lot].at[half, 1 - b])
            part = S.done[lot].at[half]
            remote((SPREAD, lot, 1), part, part, 6, 0, like=lambda: S.done[lot].at[0])

    def spread_end(lot):
        @only(False)
        def to_end():
            done = S.done[lot]
            arrived((SPREAD, lot, 1), done.at[1 - half])
            part = done.at[:, b]
            remote((SPREAD, lot, 2), part, part, 2, 0, like=lambda: done.at[:, 0])

    def spread_ends(lot):
        @only(True)
        def swap_at_ends():
            done = S.done[lot]
            part = done.at[:, b]
            arrived((SPREAD, lot, 2), part)
            remote((SPREAD, lot, 3), part, part, 1, 0, like=lambda: done.at[:, 0])

    def finish_lot(lot):
        @only(True)
        def from_pair():
            arrived((SPREAD, lot, 3), S.done[lot].at[:, 1 - b])

        finishing.append(local((GIVE, lot), S.done[lot], grad_out.at[(lot - LOT_OUT[0]) // 2, (lot - LOT_OUT[0]) % 2]))

    def inner_again():
        from_near((SETTLED_ALL,), S.set_all)
        settled_all = S.set_all[...].reshape(GROUP * ROWS, D)
        hidden = pl.ds(pl.multiple_of(D * w, D), D)
        S.inner_all[...] = (
            matmul(settled_all, S.full[IN][:, :, hidden].reshape(D, D))
            + S.vectors[pl.ds(8 + w, 1), :]
        )
        S.act_all[...] = gelu(S.inner_all[...]).astype(BF)

    def out_part(i):
        from_near((BRANCH_GRAD_ALL, i), S.bg_all.at[i])
        grad = tn(S.act_all[...], S.bg_all[i].reshape(GROUP * ROWS, 384)).astype(BF)
        for k in range(2):
            lot = LOT_OUT[2 * i + k]
            S.part[lot][...] = grad[384 * k : 384 * (k + 1)].reshape(2, 2, 96, 384)
            if lot in LOT_PAIR:
                remote((REDUCE, lot, 0), S.part[lot].at[1 - b], S.got[lot][0], 1, 0)
            else:
                reduce_start(lot)

    def in_part():
        branch_grad_all = lanes([S.bg_all[i].reshape(GROUP * ROWS, 384) for i in range(2)])
        inner_grad_all = (
            right_product(branch_grad_all, S.full[OUT][w]) * gelu_slope(S.inner_all[...])
        ).astype(BF)
        grad = tn(S.set_all[...].reshape(GROUP * ROWS, D), inner_grad_all).astype(BF)
        for i, lot in enumerate(LOT_IN):
            for j in range(2):
                side = grad[:, 384 * j : 384 * (j + 1)].reshape(4, 2, 2, 48, 384)
                for k in range(2):
                    S.part[lot][j, k] = side[:, k, i]
            remote((REDUCE, lot, 0), S.part[lot].at[1 - b], S.got[lot][0], 1, 0)

    def attention_back():
        for j in (1, 2, 3):
            arrived((CONTEXT_GRAD, j), S.cg.at[bit_xor(a, j)])
        for h in range(HEADS):
            grad = wide(S.cg, h).astype(F32)
            row_total = S.total[h, 0:1, :]
            S.wg[h] = (grad / row_total).astype(BF)
            S.total[h, 1:2, :] = -jnp.sum(grad * S.mix[h], axis=0, keepdims=True) / (
                row_total * row_total
            )
        S.mix[...] = jnp.zeros(S.mix.shape, F32)

        def attend_back(pair, i):
            block = 2 * i + pair
            for h in range(HEADS):
                key_rows = slice(HD * h, HD * (h + 1))
                value_rows = slice(HW + HD * h, HW + HD * (h + 1))
                weights = S.weights[block, h]
                grad = S.wg[h]
                weight_grad = tn(S.kv[block, value_rows, :], grad) + S.total[h, 1:2, :]
                score_grad = (weights * weight_grad).astype(BF)
                S.mix[h] += matmul(S.kv[block, key_rows, :], score_grad)
                S.dkv[pair, i, key_rows, :] = (
                    right_product(wide(S.q, h), score_grad) * score_scale
                ).astype(BF)
                value_grad = right_product(grad, weights.astype(BF))
                S.dkv[pair, i, value_rows, :] = value_grad.astype(BF)

        @pl.loop(0, CTX)
        def every_block(block):
            attend_back(block % 2, block // 2)

        remote((KEY_VALUE_GRAD,), S.dkv.at[1 - b], S.dkv_pair, 1, 0)
        for h in range(HEADS):
            rows = slice(2 * HW + HD * h, 2 * HW + HD * (h + 1))
            S.grads[rows, :] = (S.mix[h] * score_scale).astype(BF)
        S.grads[3 * HW :, :] = jnp.zeros((HEAD_COLS - 3 * HW, 4 * ROWS), BF)

    def o_part():
        from_group((CONTEXT_ALL,), S.ctx_all)
        from_group((ATTN_GRAD_ALL,), S.ag_all)
        context_all = lanes([S.ctx_all[i].reshape(384, ROWS) for i in range(GROUP)])
        grad = matmul(context_all, S.ag_all[...].reshape(GROUP * ROWS, 384))
        S.part[0][...] = grad.astype(BF).reshape(2, 2, 96, 384)
        remote((REDUCE, 0, 0), S.part[0].at[1 - b], S.got[0][0], 1, 0)

    def heads_part():
        arrived((KEY_VALUE_GRAD,), S.dkv_pair)
        for i in range(4):
            S.grads[0 : 2 * HW, ROWS * i : ROWS * (i + 1)] = (
                S.dkv[b, i].astype(F32) + S.dkv_pair[i].astype(F32)
            ).astype(BF)
        own_inputs = lanes([S.xt[2 * i + b] for i in range(4)])
        heads = right_product(own_inputs, S.grads[...]).astype(BF)
        S.heads[...] = heads.reshape(2, 2, HW, HEAD_COLS)
        for i in range(2):
            remote((HEADS_CORE, i), S.heads.at[i, 1 - core], S.heads_core.at[i], 0, 1)

    def input_parts():
        parts = tn(S.grads[0 : 3 * HW, :], S.head_weight[...])
        S.dx_send[...] = parts.astype(BF).reshape(4, ROWS, D)

        @only(True)
        def to_middle():
            for j in (1, 2, 3):
                source, target = S.dx_send.at[bit_xor(a, j)], S.dx_end.at[j - 1]
                remote((INPUT_PARTS, j), source, target, 2, 0, like=lambda: S.dx_end.at[0])

    def input_middle():
        @only(False)
        def to_other_middle():
            for j in (1, 2, 3):
                arrived((INPUT_PARTS, j), S.dx_end.at[j - 1])
            for i, j in enumerate((3, 2)):
                both = S.dx_send[bit_xor(a, j)].astype(F32) + S.dx_end[i + 1].astype(F32)
                S.dx_middle[i] = both.astype(BF)
            remote((INPUT_PARTS, 4), S.dx_middle, S.dx_got, 6, 0, like=lambda: S.dx_middle)

    def input_end():
        @only(False)
        def to_near_end():
            arrived((INPUT_PARTS, 4), S.dx_got)
            both = S.dx_send[bit_xor(a, 1)].astype(F32) + S.dx_got[1].astype(F32)
            S.dx_back[...] = both.astype(BF)
            remote((INPUT_PARTS, 5), S.dx_back, S.dx_last, 2, 0, like=lambda: S.dx_back)

    def vectors_group():
        S.column[...] = jnp.zeros((D, ROWS), F32)
        heads_rows = pl.ds(pl.multiple_of(HW * a, HW), HW)
        for row, first in ((1, HW), (0, 2 * HW)):
            sums = jnp.sum(S.grads[first : first + HW, :].astype(F32), axis=1, keepdims=True)
            S.column[heads_rows, :] = jnp.broadcast_to(sums, (HW, ROWS))
            S.sg[row : row + 1, :] = S.column[...].T[0:1, :]
        for j in (1, 2, 3):
            remote((VECTORS_W, j), S.sg, S.sg_w.at[w], 0, j)
        S.sg_w[w] = S.sg[...]

    own_rows = pl.ds(pl.multiple_of(8 * core, 8), 8)

    def vectors_line():
        for j in (1, 2, 3):
            arrived((VECTORS_W, j), S.sg_w.at[bit_xor(w, j)])
        S.sg_all[...] = (S.sg_w[0] + S.sg_w[1]) + (S.sg_w[2] + S.sg_w[3])
        S.sg_z[0] = S.sg_all[own_rows, :]

        @only(True)
        def to_middle():
            remote((VECTORS_Z, 1), S.sg_z.at[0], S.sg_z.at[1], 2, 0, like=lambda: S.sg_z.at[1])

    def vectors_middle():
        @only(False)
        def to_other_middle():
            arrived((VECTORS_Z, 1), S.sg_z.at[1])
            S.sg_z[2] = S.sg_z[0] + S.sg_z[1]
            remote((VECTORS_Z, 2), S.sg_z.at[2], S.sg_z.at[3], 6, 0, like=lambda: S.sg_z.at[2])

    def vectors_end():
        @only(False)
        def to_end():
            arrived((VECTORS_Z, 2), S.sg_z.at[3])
            S.sg_y[b] = S.sg_z[2] + S.sg_z[3]
            whole = S.sg_y.at[b]
            remote((VECTORS_Z, 3), whole, whole, 2, 0, like=lambda: S.sg_y.at[0])

    def vectors_pair():
        @only(True)
        def from_middle():
            arrived((VECTORS_Z, 3), S.sg_y.at[b])

        remote((VECTORS_Y,), S.sg_y.at[b], S.sg_y.at[b], 1, 0)

    def vectors_core():
        arrived((VECTORS_Y,), S.sg_y.at[1 - b])
        S.sg_rows[core] = S.sg_y[0] + S.sg_y[1]
        remote((VECTORS_CORE,), S.sg_rows.at[core], S.sg_rows.at[core], 0, 1)

    def vectors_done():
        arrived((VECTORS_CORE,), S.sg_rows.at[1 - core])
        everything = S.sg_rows[...].reshape(16, D)
        for i in range(4):
            S.smalls[i] = everything[:, HW * i : HW * (i + 1)]
        finishing.append(local((VECTORS_Y,), S.smalls, smalls_out))
        finishing.append(local((VECTORS_Z,), S.sg_rows, rows_out))

    def heads_x():
        for i in range(2):
            arrived((HEADS_CORE, i), S.heads_core.at[i])
        for i in range(2):
            S.heads_sum[i] = (S.heads[i, core].astype(F32) + S.heads_core[i].astype(F32)).astype(BF)
        remote((HEADS_X,), S.heads_sum.at[1 - x], S.heads_x, 0, 2)

    def heads_y():
        arrived((HEADS_X,), S.heads_x)
        S.heads_row[...] = (
            (S.heads_sum[x].astype(F32) + S.heads_x[...].astype(F32))
            .astype(BF)
            .reshape(2, HW // 2, HEAD_COLS)
        )
        remote((HEADS_Y,), S.heads_row.at[1 - b], S.heads_y, 1, 0)

    def heads_line():
        arrived((HEADS_Y,), S.heads_y)
        S.heads_done[a] = (S.heads_row[b].astype(F32) + S.heads_y[...].astype(F32)).astype(BF)
        own = S.heads_done.at[a]
        remote((HEADS_LINE, 1), own, own, 2, 0)

        @only(False)
        def to_other_middle():
            remote((HEADS_LINE, 3), own, own, 6, 0, like=lambda: S.heads_done.at[0])

    def pass_heads(key, j, onward, bits):
        part = S.heads_done.at[bit_xor(a, j)]
        if key is not None:
            arrived((key, j), part)
        remote(onward, part, part, bits, 0, like=lambda: S.heads_done.at[0])

    def heads_near_end():
        arrived((HEADS_LINE, 1), S.heads_done.at[bit_xor(a, 1)])

        @only(False)
        def to_other_middle():
            pass_heads(None, 1, (HEADS_LINE, 2), 6)

    def heads_middle():
        @only(False)
        def to_near_end():
            pass_heads(HEADS_LINE, 3, (HEADS_EDGE, 2), 2)

    def heads_far_end():
        @only(False)
        def to_near_end():
            pass_heads(HEADS_LINE, 2, (HEADS_EDGE, 3), 2)

    def heads_pair():
        @only(True)
        def from_middle():
            for j in (2, 3):
                arrived((HEADS_EDGE, j), S.heads_done.at[bit_xor(a, j)])

        remote((HEADS_PAIR,), S.heads_done, heads_out.at[b], 1, 0)
        finishing.append(local((HEADS_PAIR,), S.heads_done, heads_out.at[b]))

    def input_done():
        S.first[...] = S.keep[...] + S.dx_send[a].astype(F32)

        @only(True)
        def at_end():
            arrived((INPUT_PARTS, 5), S.dx_last)
            S.first[...] += S.dx_last[...].astype(F32)

        @only(False)
        def in_middle():
            S.first[...] += S.dx_end[0].astype(F32) + S.dx_got[0].astype(F32)

        finishing.append(local(INPUT_GRAD, S.first, input_grad_out))

    marked = []

    def mark():
        marked.extend(started)
        started.clear()

    def retire():
        for copy in marked:
            copy.wait_send()
        marked.clear()

    def mark_late():
        mark()

    def retire_late():
        retire()

    for step, *lot in (
        (pass_near_end,),
        (pump_x, PART_K),
        (pass_middle,),
        (pump_x, PART_Q),
        (pump_x, PART_V),
        (pump_second, PART_Q),
        (pump_x, O),
        (small_vectors,),
        (pass_far_end,),
        (pump_second, PART_V),
        (pump_second, PART_K),
        (head_weights,),
        (project, 0),
        (project, 2),
        (project, 1),
        (pump_x, IN, 0),
        (pump_x, IN, 1),
        (project, 3),
        (pump_second, O),
        (attend_line,),
        (attend_pair, 0),
        (pump_x, IN, 3),
        (attend_pair, 1),
        (attend_pair, 2),
        (pump_x, OUT, 0),
        (pump_second, IN, 1),
        (attend_pair, 3),
        (send_context,),
        (pump_x, IN, 2),
        (pump_x, OUT, 1),
        (pump_second, IN, 0),
        (pump_x, OUT, 2),
        (pump_second, OUT, 1),
        (pump_second, IN, 3),
        (pump_x, OUT, 3),
        (first_norm,),
        (feed_in, 0),
        (pump_second, OUT, 0),
        (feed_in, 1),
        (pump_second, OUT, 2),
        (pump_second, IN, 2),
        (feed_in, 2),
        (pump_second, OUT, 3),
        (feed_in, 3),
        (result_and_loss,),
        (pass_settled,),
        (feed_back,),
        (first_norm_back,),
        (mark,),
        (inner_again,),
        (pass_branch_grad, 0),
        (pass_branch_grad, 1),
        (out_part, 0),
        (out_part, 1),
        (attention_back,),
        (reduce_middle, 5),
        (reduce_pair, 5),
        (y_end, 3),
        (o_part,),
        (reduce_middle, 6),
        (y_middle, 3),
        (reduce_last, 5),
        (in_part,),
        (y_last, 3),
        (y_end, 4),
        (heads_part,),
        (y_middle, 4),
        (y_end, 0),
        (vectors_group,),
        (spread_middle, 5),
        (y_spread_end, 3),
        (heads_x,),
        (y_last, 4),
        (y_middle, 0),
        (vectors_line,),
        (vectors_middle,),
        (spread_end, 5),
        (y_spread_end, 4),
        (y_end, 1),
        (y_last, 0),
        (heads_y,),
        (y_middle, 1),
        (reduce_pair, 6),
        (spread_ends, 5),
        (retire,),
        (vectors_end,),
        (y_spread_end, 0),
        (heads_line,),
        (mark_late,),
        (y_end, 2),
        (reduce_last, 6),
        (y_give, 3),
        (y_give, 4),
        (y_last, 1),
        (vectors_pair,),
        (y_give, 0),
        (heads_near_end,),
        (heads_middle,),
        (y_group, 1),
        (heads_far_end,),
        (y_middle, 2),
        (input_parts,),
        (spread_middle, 6),
        (heads_pair,),
        (y_last, 2),
        (y_spread_end, 1),
        (spread_end, 6),
        (y_give, 1),
        (y_group, 2),
        (spread_ends, 6),
        (input_middle,),
        (y_spread_end, 2),
        (y_give, 2),
        (vectors_core,),
        (finish_lot, 5),
        (input_end,),
        (input_done,),
        (retire_late,),
        (vectors_done,),
        (finish_lot, 6),
    ):
        step(*lot)

    arrived((HEADS_PAIR,), heads_out.at[1 - b])
    settle()
    for copy in finishing:
        copy.wait()
    for copy in started:
        copy.wait_send()
    for end in (True, False):

        @only(end)
        def sent():
            for role, like, number in sent_by_role:
                if role == end:
                    source = like()
                    pltpu.make_async_copy(source, source, send_sems.at[number]).wait()


def finish_kernel(*refs):
    g_o, g_in0, g_in1, g_out, heads, smalls, rows, output, input_grad = refs[:9]
    r_q, r_k, r_v, r_o, r_in, r_out = refs[9:15]
    vectors, inner_bias, loss, r_output, r_input = refs[15:23], *refs[23:]
    step = pl.program_id(0)
    for i in range(2):
        r_o[:, 384 * i : 384 * (i + 1)] = g_o[i].reshape(HW // 2, 384).astype(F32)
        for j in range(4):
            first = D * j + 384 * i
            for k, source in enumerate((g_in0, g_in1)):
                r_in[48 * k : 48 * (k + 1), first : first + 384] = source[i, 0, j].astype(F32)
    for i in range(2):
        r_out[:, 384 * i : 384 * (i + 1)] = g_out[i].reshape(D // 2, 384).astype(F32)
    for i, result in ((0, r_k), (1, r_v), (2, r_q)):
        result[...] = jnp.concatenate(
            [heads[0, j, :, HW * i : HW * (i + 1)].astype(F32) for j in range(4)], axis=1
        )
    r_output[0] = output[...]
    r_input[0] = input_grad[...]

    @pl.when(step == 0)
    def once():
        w = lax.axis_index("wsh")
        for i in range(8):
            vectors[i][...] = smalls[w, i, :]
        inner_bias[...] = rows[1, w, :]
        error = jnp.sum(rows[1, 4:5, :])
        count = jnp.max(rows[1, 5:6, :])
        loss[0] = error / (count * D)


def fused_body(tokens, teacher, doc_lengths, valid_len, *weights):
    (
        q_weight,
        q_bias,
        k_weight,
        v_weight,
        v_bias,
        o_weight,
        o_bias,
        ln1_gain,
        ln1_bias,
        in_weight,
        in_bias,
        out_weight,
        out_bias,
        ln2_gain,
        ln2_bias,
    ) = weights
    hbm = pl.BlockSpec(memory_space=pl.ANY)
    smem = pl.BlockSpec(memory_space=pltpu.SMEM)
    vmem = pl.BlockSpec(memory_space=pltpu.VMEM)
    low = lambda *shape: jax.ShapeDtypeStruct(shape, BF)
    full = lambda *shape: jax.ShapeDtypeStruct(shape, F32)
    output, input_grad, g_o, g_in0, g_in1, g_out, heads, smalls, rows = pl.pallas_call(
        fused_kernel,
        out_shape=(
            low(ROWS, D),
            full(ROWS, D),
            low(2, 2, 96, 384),
            low(2, 2, 4, 48, 384),
            low(2, 2, 4, 48, 384),
            low(2, 2, 2, 2, 96, 384),
            low(2, 4, HW // 2, HEAD_COLS),
            full(GROUP, 16, HW),
            full(2, 8, D),
        ),
        in_specs=[hbm] * 8 + [smem] * 2 + [vmem] * 9,
        out_specs=[hbm] * 9,
        scratch_shapes=scratch_shapes()[0]
        + [
            pltpu.SemaphoreType.DMA((REMOTE_SEMS,)),
            pltpu.SemaphoreType.DMA((REMOTE_SEMS,)),
            pltpu.SemaphoreType.DMA((LOCAL_SEMS,)),
        ],
        compiler_params=pltpu.CompilerParams(
            collective_id=0, has_side_effects=True, vmem_limit_bytes=67043328
        ),
        name="layer",
    )(
        tokens,
        teacher,
        q_weight,
        k_weight,
        v_weight,
        o_weight,
        in_weight,
        out_weight,
        doc_lengths,
        valid_len,
        q_bias,
        v_bias,
        o_bias,
        ln1_gain,
        ln1_bias,
        out_bias,
        ln2_gain,
        ln2_bias,
        in_bias,
    )

    steps = 2
    square_out = pl.BlockSpec((HW // steps, D), lambda i: (i, 0))
    whole = lambda *shape: pl.BlockSpec(shape, lambda i: (0,) * len(shape))
    by_row = pl.BlockSpec((ROWS // steps, D), lambda i: (i, 0))
    results = pl.pallas_call(
        finish_kernel,
        grid=(steps,),
        out_shape=(full(HW, D),) * 4
        + (full(HW, FF), full(D, D))
        + (full(HW),) * 8
        + (full(D), full(1), low(1, ROWS, D), full(1, ROWS, D)),
        in_specs=[
            pl.BlockSpec((2, 1, 96, 384), lambda i: (0, i, 0, 0)),
            pl.BlockSpec((2, 1, 4, 48, 384), lambda i: (0, i, 0, 0, 0)),
            pl.BlockSpec((2, 1, 4, 48, 384), lambda i: (0, i, 0, 0, 0)),
            pl.BlockSpec((2, 1, 2, 2, 96, 384), lambda i: (0, i, 0, 0, 0, 0)),
            pl.BlockSpec((1, 4, HW // 2, HEAD_COLS), lambda i: (i, 0, 0, 0)),
            whole(GROUP, 16, HW),
            whole(2, 8, D),
            by_row,
            by_row,
        ],
        out_specs=[square_out] * 4
        + [
            pl.BlockSpec((HW // steps, FF), lambda i: (i, 0)),
            pl.BlockSpec((D // steps, D), lambda i: (i, 0)),
        ]
        + [whole(HW)] * 8
        + [
            whole(D),
            pl.BlockSpec(memory_space=pltpu.SMEM),
            pl.BlockSpec((1, ROWS // steps, D), lambda i: (0, i, 0)),
            pl.BlockSpec((1, ROWS // steps, D), lambda i: (0, i, 0)),
        ],
        compiler_params=pltpu.CompilerParams(dimension_semantics=("arbitrary",)),
        name="finish",
    )(g_o, g_in0, g_in1, g_out, heads, smalls, rows, output, input_grad)
    r_q, r_k, r_v, r_o, r_in, r_out = results[:6]
    vectors, inner_bias, loss, r_output, r_input = results[6:14], *results[14:]
    return (
        r_output,
        loss.reshape(()),
        r_input,
        r_q,
        vectors[0],
        r_k,
        r_v,
        vectors[1],
        r_o,
        vectors[2],
        vectors[3],
        vectors[4],
        r_in,
        inner_bias,
        r_out,
        vectors[5],
        vectors[6],
        vectors[7],
    )


def solution(mesh):
    in_specs = (
        P("wsh", "ctx", None),
        P("wsh", "ctx", None),
        P("wsh", None),
        P("wsh"),
        P("wsh", None),
        P("wsh"),
        P("wsh", None),
        P("wsh", None),
        P("wsh"),
        P("wsh", None),
        P("wsh"),
        P("wsh"),
        P("wsh"),
        P("wsh", None),
        P("wsh"),
        P("wsh", None),
        P("wsh"),
        P("wsh"),
        P("wsh"),
    )
    out_specs = (
        P("wsh", "ctx", None),
        P(),
        P("wsh", "ctx", None),
        P("wsh", None),
        P("wsh"),
        P("wsh", None),
        P("wsh", None),
        P("wsh"),
        P("wsh", None),
        P("wsh"),
        P("wsh"),
        P("wsh"),
        P("wsh", None),
        P("wsh"),
        P("wsh", None),
        P("wsh"),
        P("wsh"),
        P("wsh"),
    )
    program = fused_body if fused_fits(mesh) else body
    return jax.shard_map(program, mesh=mesh, in_specs=in_specs, out_specs=out_specs, check_vma=False)
```

```python
import math
import types

import jax
import jax.numpy as jnp
from jax import lax
from jax.experimental import pallas as pl
from jax.experimental.pallas import tpu as pltpu
from jax.sharding import PartitionSpec as P

D = 768
H = 12
HD = 64


EPSILON = 1e-06
MASKED = -1e30


def shifted(block, axis, distance):
    devices = range(lax.axis_size(axis))
    route = [((i - distance) % len(devices), i) for i in devices]
    return lax.ppermute(block, axis, route)


def layer_norm(value, gain, shift):
    mean = jnp.mean(value, axis=-1, keepdims=True)
    centered = value - mean
    spread = jnp.mean(centered * centered, axis=-1, keepdims=True)
    return centered * lax.rsqrt(spread + EPSILON) * gain + shift


def activate(value):
    return jax.nn.gelu(value, approximate=True)


def matmul(left, right):
    return jnp.dot(left, right, preferred_element_type=jnp.float32)


def left_product(left, right):
    return lax.dot_general(
        left, right, (((0,), (0,)), ((), ())), preferred_element_type=jnp.float32
    )


def right_product(left, right):
    return lax.dot_general(
        left, right, (((1,), (1,)), ((), ())), preferred_element_type=jnp.float32
    )


def document_of(positions, starts):
    return jnp.sum((starts[None, :] <= positions[:, None]).astype(jnp.int32), axis=1) - 1


def permitted(own_doc, own_live, other_doc, other_live):
    return (own_doc[:, None] == other_doc[None, :]) & (own_live[:, None] == other_live[None, :])


def block_weights(queries, key_block, allowed, score_scale):
    scores = (
        jnp.einsum("qhd,khd->hqk", queries, key_block, preferred_element_type=jnp.float32)
        * score_scale
    )
    return jnp.exp(jnp.where(allowed[None], scores, MASKED))


def forward_visit(sums_state, queries, key_block, value_block, allowed, score_scale):
    row_total, weighted = sums_state
    weights = block_weights(queries, key_block, allowed, score_scale)
    row_total = row_total + jnp.sum(weights, axis=-1)
    weighted = weighted + jnp.einsum(
        "hqk,khd->qhd",
        weights.astype(jnp.bfloat16),
        value_block,
        preferred_element_type=jnp.float32,
    )
    return (row_total, weighted)


def backward_visit(
    queries, key_block, value_block, allowed, score_scale, weighted_grad, total_grad
):
    weights = block_weights(queries, key_block, allowed, score_scale)
    value_part = jnp.einsum(
        "hqk,qhd->khd",
        weights.astype(jnp.bfloat16),
        weighted_grad,
        preferred_element_type=jnp.float32,
    )
    weight_grad = (
        jnp.einsum("qhd,khd->hqk", weighted_grad, value_block, preferred_element_type=jnp.float32)
        + total_grad[:, :, None]
    )
    score_grad = (weights * weight_grad).astype(jnp.bfloat16)
    query_part = (
        jnp.einsum("hqk,khd->qhd", score_grad, key_block, preferred_element_type=jnp.float32)
        * score_scale
    )
    key_part = (
        jnp.einsum("hqk,qhd->khd", score_grad, queries, preferred_element_type=jnp.float32)
        * score_scale
    )
    return (query_part, key_part, value_part)


def body(
    tokens,
    teacher,
    doc_lengths,
    valid_len,
    q_weight,
    q_bias,
    k_weight,
    v_weight,
    v_bias,
    o_weight,
    o_bias,
    ln1_gain,
    ln1_bias,
    in_weight,
    in_bias,
    out_weight,
    out_bias,
    ln2_gain,
    ln2_bias,
):
    gathered = (
        lax.all_gather(q_weight, "wsh", axis=0, tiled=True),
        lax.all_gather(q_bias, "wsh", axis=0, tiled=True),
        lax.all_gather(k_weight, "wsh", axis=0, tiled=True),
        lax.all_gather(v_weight, "wsh", axis=0, tiled=True),
        lax.all_gather(v_bias, "wsh", axis=0, tiled=True),
        lax.all_gather(o_weight, "wsh", axis=0, tiled=True),
        lax.all_gather(o_bias, "wsh", axis=0, tiled=True),
        lax.all_gather(ln1_gain, "wsh", axis=0, tiled=True),
        lax.all_gather(ln1_bias, "wsh", axis=0, tiled=True),
        lax.all_gather(in_weight, "wsh", axis=0, tiled=True),
        lax.all_gather(in_bias, "wsh", axis=0, tiled=True),
        lax.all_gather(out_weight, "wsh", axis=0, tiled=True),
        lax.all_gather(out_bias, "wsh", axis=0, tiled=True),
        lax.all_gather(ln2_gain, "wsh", axis=0, tiled=True),
        lax.all_gather(ln2_bias, "wsh", axis=0, tiled=True),
    )
    (
        w_query,
        b_query,
        w_key,
        w_value,
        b_value,
        w_out,
        b_out,
        gain_one,
        shift_one,
        w_inner,
        b_inner,
        w_back,
        b_back,
        gain_two,
        shift_two,
    ) = gathered
    gain_first = gain_one.astype(jnp.float32)
    shift_first = shift_one.astype(jnp.float32)
    gain_second = gain_two.astype(jnp.float32)
    shift_second = shift_two.astype(jnp.float32)
    inputs = tokens[0]
    row_count = inputs.shape[0]
    cycle_size = lax.axis_size("ctx")
    stream_count = lax.axis_size("wsh")
    position = lax.axis_index("ctx")
    score_scale = 1.0 / math.sqrt(HD)
    offsets = jnp.arange(row_count, dtype=jnp.int32)
    lengths = doc_lengths[0]
    starts = jnp.cumsum(lengths) - lengths
    limit = valid_len[0]

    def key_mask(block_index):
        where_rows = jnp.mod(block_index, cycle_size) * row_count + offsets
        return (document_of(where_rows, starts), where_rows < limit)

    own_doc, own_live = key_mask(position)
    input_float = inputs.astype(jnp.float32)
    queries = (
        (matmul(inputs, w_query) + b_query.astype(jnp.float32))
        .astype(jnp.bfloat16)
        .reshape(row_count, H, HD)
    )
    key_rows = matmul(inputs, w_key).astype(jnp.bfloat16).reshape(row_count, H, HD)
    value_rows = (
        (matmul(inputs, w_value) + b_value.astype(jnp.float32))
        .astype(jnp.bfloat16)
        .reshape(row_count, H, HD)
    )

    def visit_forward(sums_state, key_block, value_block, block_index):
        other_doc, other_live = key_mask(block_index)
        allowed = permitted(own_doc, own_live, other_doc, other_live)
        return forward_visit(sums_state, queries, key_block, value_block, allowed, score_scale)

    empty_state = (
        jnp.zeros((H, row_count), jnp.float32),
        jnp.zeros((row_count, H, HD), jnp.float32),
    )
    first_state = visit_forward(empty_state, key_rows, value_rows, position)

    def advance(step_index, loop_state):
        key_block, value_block, running = loop_state
        key_block, value_block = shifted((key_block, value_block), "ctx", 1)
        running = visit_forward(running, key_block, value_block, position - step_index)
        return (key_block, value_block, running)

    row_total, weighted = lax.fori_loop(
        1, cycle_size, advance, (key_rows, value_rows, first_state)
    )[2]
    normed = weighted / jnp.transpose(row_total)[:, :, None]
    context = normed.astype(jnp.bfloat16).reshape(row_count, D)
    attn = matmul(context, w_out) + b_out.astype(jnp.float32)
    first_sum = input_float + attn
    settled = layer_norm(first_sum, gain_first, shift_first)
    settled_low = settled.astype(jnp.bfloat16)
    inner = matmul(settled_low, w_inner) + b_inner.astype(jnp.float32)
    activated = activate(inner).astype(jnp.bfloat16)
    branch = matmul(activated, w_back) + b_back.astype(jnp.float32)
    second_sum = settled + branch
    result = layer_norm(second_sum, gain_second, shift_second)
    target = teacher[0].astype(jnp.float32)
    diff = jnp.where(own_live[:, None], result - target, 0.0)
    error_sum, live_count = lax.psum(
        (jnp.sum(diff * diff), jnp.sum(own_live.astype(jnp.float32))), ("ctx", "wsh")
    )
    loss = error_sum / (live_count * D)
    upstream = diff * (row_count * cycle_size * stream_count / live_count)
    unused_second, second_back = jax.vjp(layer_norm, second_sum, gain_second, shift_second)
    d_second, gain_two_grad, shift_two_grad = second_back(upstream)
    branch_grad = d_second.astype(jnp.bfloat16)
    back_weight_grad = left_product(activated, branch_grad)
    back_bias_grad = jnp.sum(branch_grad, axis=0, dtype=jnp.float32)
    d_activated = right_product(branch_grad, w_back)
    unused_inner, gelu_back = jax.vjp(activate, inner)
    inner_grad = gelu_back(d_activated)[0].astype(jnp.bfloat16)
    inner_weight_grad = left_product(settled_low, inner_grad)
    inner_bias_grad = jnp.sum(inner_grad, axis=0, dtype=jnp.float32)
    d_settled = d_second + right_product(inner_grad, w_inner)
    unused_first, first_back = jax.vjp(layer_norm, first_sum, gain_first, shift_first)
    d_first, gain_one_grad, shift_one_grad = first_back(d_settled)
    attn_grad = d_first.astype(jnp.bfloat16)
    out_weight_grad_local = left_product(context, attn_grad)
    out_bias_grad_local = jnp.sum(attn_grad, axis=0, dtype=jnp.float32)
    context_low = lax.optimization_barrier(right_product(attn_grad, w_out).astype(jnp.bfloat16))
    context_grad = context_low.astype(jnp.float32).reshape(row_count, H, HD)
    weighted_grad = (context_grad / jnp.transpose(row_total)[:, :, None]).astype(jnp.bfloat16)
    total_grad = -jnp.transpose(jnp.sum(context_grad * weighted, axis=-1)) / (row_total * row_total)

    def visit_backward(key_block, value_block, block_index):
        other_doc, other_live = key_mask(block_index)
        allowed = permitted(own_doc, own_live, other_doc, other_live)
        return backward_visit(
            queries, key_block, value_block, allowed, score_scale, weighted_grad, total_grad
        )

    query_sum, key_sum, value_sum = visit_backward(key_rows, value_rows, position)

    def advance_back(step_index, loop_state):
        key_block, value_block, query_acc, key_acc, value_acc = loop_state
        key_block, value_block = shifted((key_block, value_block), "ctx", 1)
        key_acc, value_acc = (
            shifted(key_acc.astype(jnp.bfloat16), "ctx", 1).astype(key_acc.dtype),
            shifted(value_acc.astype(jnp.bfloat16), "ctx", 1).astype(value_acc.dtype),
        )
        query_part, key_part, value_part = visit_backward(
            key_block, value_block, position - step_index
        )
        return (
            key_block,
            value_block,
            query_acc + query_part,
            key_acc + key_part,
            value_acc + value_part,
        )

    loop_state = lax.fori_loop(
        1, cycle_size, advance_back, (key_rows, value_rows, query_sum, key_sum, value_sum)
    )
    query_total = loop_state[2]
    key_total, value_total = (
        shifted(loop_state[3].astype(jnp.bfloat16), "ctx", 1).astype(jnp.float32),
        shifted(loop_state[4].astype(jnp.bfloat16), "ctx", 1).astype(jnp.float32),
    )
    query_grad = query_total.astype(jnp.bfloat16).reshape(row_count, D)
    key_grad = key_total.astype(jnp.bfloat16).reshape(row_count, D)
    value_grad = value_total.astype(jnp.bfloat16).reshape(row_count, D)
    query_weight_grad = left_product(inputs, query_grad)
    query_bias_grad = jnp.sum(query_grad, axis=0, dtype=jnp.float32)
    key_weight_grad = left_product(inputs, key_grad)
    value_weight_grad = left_product(inputs, value_grad)
    value_bias_grad = jnp.sum(value_grad, axis=0, dtype=jnp.float32)
    input_grad = (
        d_first
        + right_product(query_grad, w_query)
        + right_product(key_grad, w_key)
        + right_product(value_grad, w_value)
    )
    reduced = (
        lax.psum_scatter(
            query_weight_grad.astype(jnp.bfloat16), "wsh", scatter_dimension=0, tiled=True
        ).astype(jnp.float32),
        lax.psum_scatter(
            query_bias_grad.astype(jnp.bfloat16), "wsh", scatter_dimension=0, tiled=True
        ).astype(jnp.float32),
        lax.psum_scatter(
            key_weight_grad.astype(jnp.bfloat16), "wsh", scatter_dimension=0, tiled=True
        ).astype(jnp.float32),
        lax.psum_scatter(
            value_weight_grad.astype(jnp.bfloat16), "wsh", scatter_dimension=0, tiled=True
        ).astype(jnp.float32),
        lax.psum_scatter(
            value_bias_grad.astype(jnp.bfloat16), "wsh", scatter_dimension=0, tiled=True
        ).astype(jnp.float32),
        lax.psum_scatter(
            out_weight_grad_local.astype(jnp.bfloat16), "wsh", scatter_dimension=0, tiled=True
        ).astype(jnp.float32),
        lax.psum_scatter(
            out_bias_grad_local.astype(jnp.bfloat16), "wsh", scatter_dimension=0, tiled=True
        ).astype(jnp.float32),
        lax.psum_scatter(
            gain_one_grad.astype(jnp.bfloat16), "wsh", scatter_dimension=0, tiled=True
        ).astype(jnp.float32),
        lax.psum_scatter(
            shift_one_grad.astype(jnp.bfloat16), "wsh", scatter_dimension=0, tiled=True
        ).astype(jnp.float32),
        lax.psum_scatter(
            inner_weight_grad.astype(jnp.bfloat16), "wsh", scatter_dimension=0, tiled=True
        ).astype(jnp.float32),
        lax.psum_scatter(
            inner_bias_grad.astype(jnp.bfloat16), "wsh", scatter_dimension=0, tiled=True
        ).astype(jnp.float32),
        lax.psum_scatter(
            back_weight_grad.astype(jnp.bfloat16), "wsh", scatter_dimension=0, tiled=True
        ).astype(jnp.float32),
        lax.psum_scatter(
            back_bias_grad.astype(jnp.bfloat16), "wsh", scatter_dimension=0, tiled=True
        ).astype(jnp.float32),
        lax.psum_scatter(
            gain_two_grad.astype(jnp.bfloat16), "wsh", scatter_dimension=0, tiled=True
        ).astype(jnp.float32),
        lax.psum_scatter(
            shift_two_grad.astype(jnp.bfloat16), "wsh", scatter_dimension=0, tiled=True
        ).astype(jnp.float32),
    )
    summed = lax.psum(
        (
            reduced[0],
            reduced[1],
            reduced[2],
            reduced[3],
            reduced[4],
            reduced[5],
            reduced[6],
            reduced[7],
            reduced[8],
            reduced[9],
            reduced[10],
            reduced[11],
            reduced[12],
            reduced[13],
            reduced[14],
        ),
        "ctx",
    )
    return (
        result.astype(jnp.bfloat16)[None],
        loss,
        input_grad[None],
        summed[0],
        summed[1],
        summed[2],
        summed[3],
        summed[4],
        summed[5],
        summed[6],
        summed[7],
        summed[8],
        summed[9],
        summed[10],
        summed[11],
        summed[12],
        summed[13],
        summed[14],
    )


BF = jnp.bfloat16
F32 = jnp.float32
FF = 3072
ROWS = 128
HEADS = 3
HW = HEADS * HD
GROUP = 4
CTX = 8
MESH = pl.DeviceIdType.MESH

Q, K, V, O, IN, OUT, PART_Q, PART_K, PART_V = range(9)
SLICE = 256
WEIGHT_SHAPES = [(192, 768)] * 4 + [(192, 3072), (768, 768)] + [(192, SLICE)] * 3
SECOND_WAY = {O: 1, IN: 2, OUT: 1, PART_Q: 1, PART_K: 1, PART_V: 1}
LOT_O, LOT_IN, LOT_OUT = (0,), (1, 2), (3, 4, 5, 6)
LOT_PAIR = LOT_O + LOT_IN + LOT_OUT[:2]
LOTS = [(96, 384)] + [(4, 48, 384)] * 2 + [(96, 384)] * 4
PIECES = {IN: (1, 4), OUT: (4, 1)}
HEAD_COLS = 640

(
    SMALL,
    WEIGHT_X,
    WEIGHT_SECOND,
    WEIGHT_CORE,
    WEIGHT_CORE_X,
    WEIGHT_CORE_SECOND,
    X_LINE,
    X_EDGE,
    KEY_VALUE,
    CONTEXT,
    CONTEXT_GRAD,
    KEY_VALUE_GRAD,
    INPUT_PARTS,
    SETTLED_ALL,
    CONTEXT_ALL,
    ATTN_GRAD_ALL,
    BRANCH_GRAD_ALL,
    REDUCE,
    SPREAD,
    GIVE,
    OWN,
    GROUP_X,
    HEADS_CORE,
    HEADS_X,
    HEADS_Y,
    HEADS_LINE,
    HEADS_EDGE,
    HEADS_PAIR,
    VECTORS_W,
    VECTORS_Z,
    VECTORS_Y,
    VECTORS_CORE,
    TOKENS,
    TEACHER,
    OUTPUT,
    INPUT_GRAD,
    LOAD,
) = range(37)


def fused_fits(mesh):
    return mesh.shape["ctx"] == CTX and mesh.shape["wsh"] == GROUP


def tn(left, right):
    return lax.dot_general(
        left, right, (((0,), (0,)), ((), ())), preferred_element_type=jnp.float32
    )


def norm_parts(value):
    mean = jnp.mean(value, axis=-1, keepdims=True)
    centered = value - mean
    spread = jnp.mean(centered * centered, axis=-1, keepdims=True)
    inverse = lax.rsqrt(spread + EPSILON)
    return centered * inverse, inverse


def norm_back(upstream_gained, normal, inverse):
    return (
        upstream_gained
        - jnp.mean(upstream_gained, axis=-1, keepdims=True)
        - normal * jnp.mean(upstream_gained * normal, axis=-1, keepdims=True)
    ) * inverse


GELU_C = math.sqrt(2.0 / math.pi)


class Numbers:
    def __init__(self):
        self.count = 0
        self.table = {}

    def take(self, key, size=1):
        if key not in self.table:
            self.table[key] = self.count
            self.count += size
        return self.table[key]


def scratch_table():
    s = types.SimpleNamespace()
    s.full = {k: pltpu.VMEM((GROUP, *WEIGHT_SHAPES[k]), BF) for k in SECOND_WAY}
    s.turned = pltpu.VMEM((SLICE, D), BF)
    s.head_weight = pltpu.VMEM((3 * HW, D), BF)
    s.tall_bias = pltpu.VMEM((SLICE, ROWS), F32)
    s.head_bias = pltpu.VMEM((3 * HW, ROWS), F32)
    s.x = pltpu.VMEM((ROWS, D), BF)
    s.xt = pltpu.VMEM((CTX, D, ROWS), BF)
    s.teacher = pltpu.VMEM((ROWS, D), BF)
    s.small = pltpu.VMEM((GROUP, 16, D), BF)
    s.vectors = pltpu.VMEM((16, D), F32)
    s.kv = pltpu.VMEM((CTX, 2 * HW, ROWS), BF)
    s.q = pltpu.VMEM((4, HW, ROWS), BF)
    s.weights = pltpu.VMEM((CTX, HEADS, ROWS, 4 * ROWS), F32)
    s.mix = pltpu.VMEM((HEADS, HD, 4 * ROWS), F32)
    s.total = pltpu.VMEM((HEADS, 8, 4 * ROWS), F32)
    s.ctx_send = pltpu.VMEM((4, HW, ROWS), BF)
    s.ctx = pltpu.VMEM((4, HW, ROWS), BF)
    s.inner = pltpu.VMEM((4, ROWS, D), F32)
    s.act = pltpu.VMEM((4, ROWS, D), BF)
    s.first = pltpu.VMEM((ROWS, D), F32)
    s.keep = pltpu.VMEM((ROWS, D), F32)
    s.inverse = pltpu.VMEM((ROWS, 128), F32)
    s.set_low = pltpu.VMEM((ROWS, D), BF)
    s.ag_half = pltpu.VMEM((2, ROWS, 384), BF)
    s.bg = pltpu.VMEM((2, ROWS, 384), BF)
    s.set_all = pltpu.VMEM((GROUP, ROWS, D), BF)
    s.ctx_all = pltpu.VMEM((GROUP, 2, HW, ROWS), BF)
    s.ag_all = pltpu.VMEM((GROUP, ROWS, 384), BF)
    s.inner_all = pltpu.VMEM((GROUP * ROWS, D), F32)
    s.act_all = pltpu.VMEM((GROUP * ROWS, D), BF)
    s.bg_all = pltpu.VMEM((2, GROUP, ROWS, 384), BF)
    s.cg_send = pltpu.VMEM((4, HW, ROWS), BF)
    s.cg = pltpu.VMEM((4, HW, ROWS), BF)
    s.wg = pltpu.VMEM((HEADS, HD, 4 * ROWS), BF)
    s.dkv = pltpu.VMEM((2, 4, 2 * HW, ROWS), BF)
    s.dkv_pair = pltpu.VMEM((4, 2 * HW, ROWS), BF)
    s.grads = pltpu.VMEM((HEAD_COLS, 4 * ROWS), BF)
    s.dx_send = pltpu.VMEM((4, ROWS, D), BF)
    s.dx_end = pltpu.VMEM((3, ROWS, D), BF)
    s.dx_middle = pltpu.VMEM((2, ROWS, D), BF)
    s.dx_got = pltpu.VMEM((2, ROWS, D), BF)
    s.dx_back = pltpu.VMEM((ROWS, D), BF)
    s.dx_last = pltpu.VMEM((ROWS, D), BF)
    s.column = pltpu.VMEM((D, ROWS), F32)
    s.heads = pltpu.VMEM((2, 2, HW, HEAD_COLS), BF)
    s.heads_core = pltpu.VMEM((2, HW, HEAD_COLS), BF)
    s.heads_sum = pltpu.VMEM((2, HW, HEAD_COLS), BF)
    s.heads_x = pltpu.VMEM((HW, HEAD_COLS), BF)
    s.heads_row = pltpu.VMEM((2, HW // 2, HEAD_COLS), BF)
    s.heads_y = pltpu.VMEM((HW // 2, HEAD_COLS), BF)
    s.heads_done = pltpu.VMEM((4, HW // 2, HEAD_COLS), BF)
    s.part = [pltpu.VMEM((2, 2, *shape), BF) for shape in LOTS]
    def lots(*dims):
        return [
            pltpu.VMEM((*dims[1 if k in LOT_PAIR else 0], *shape), BF) for k, shape in enumerate(LOTS)
        ]

    steps = [((2, 2), (2,)), ((2,), (2,)), ((), ())]
    s.got = [list(lot) for lot in zip(*(lots(*step) for step in steps))]
    s.sum = [list(lot) for lot in zip(*(lots(*step) for step in steps[:2]))]
    s.own = {k: pltpu.VMEM(LOTS[k], BF) for k in LOT_IN}
    s.done = [pltpu.VMEM((2, 2, *shape), BF) for shape in LOTS]
    s.smalls = pltpu.VMEM((GROUP, 16, HW), F32)
    s.sg = pltpu.VMEM((16, D), F32)
    s.sg_all = pltpu.VMEM((16, D), F32)
    s.sg_rows = pltpu.VMEM((2, 8, D), F32)
    s.sg_w = pltpu.VMEM((GROUP, 16, D), F32)
    s.sg_z = pltpu.VMEM((4, 8, D), F32)
    s.sg_y = pltpu.VMEM((2, 8, D), F32)
    s.out_low = pltpu.VMEM((ROWS, D), BF)
    return vars(s)


LOCAL_SEMS = 32
REMOTE_SEMS = 240


def is_memory(item):
    return not isinstance(item, (dict, list))


def scratch_shapes():
    return jax.tree.flatten(scratch_table(), is_leaf=is_memory)


def fused_kernel(*refs):
    (tokens, teacher), shards = refs[:2], refs[2:8]
    lengths, valid = refs[8:10]
    biases = refs[10:19]
    output, input_grad_out = refs[19:21]
    grad_o, *grad_in, grad_out = refs[21:25]
    heads_out, smalls_out, rows_out = refs[25:28]
    flat, shape = scratch_shapes()
    S = types.SimpleNamespace(**jax.tree.unflatten(shape, refs[28 : 28 + len(flat)]))
    send_sems, recv_sems, local_sems = refs[28 + len(flat) :]

    c = lax.axis_index("ctx")
    w = lax.axis_index("wsh")
    a, b = c // 2, c % 2
    x, core = w // 2, w % 2

    numbers = Numbers()
    locals_ = Numbers()
    started = []

    def bit_xor(value, j):
        out = value
        bit = 1
        while bit <= j:
            if j & bit:
                has = (value // bit) % 2
                out = out + bit * (1 - 2 * has)
            bit *= 2
        return out

    at_end = a * (3 - a) == 0
    roles, sent_by_role = [None], []

    def only(end):
        def run(action):
            roles.append(end)
            pl.when(at_end if end else jnp.logical_not(at_end))(action)
            roles.pop()

        return run

    def remote(key, src, dst, c_bits, w_bits, offset=0, size=1, to=None, like=None):
        number = numbers.take(key, size) + offset
        c_to, w_to = bit_xor(c, c_bits), bit_xor(w, w_bits) if to is None else to
        copy = pltpu.make_async_remote_copy(
            src_ref=src,
            dst_ref=dst,
            send_sem=send_sems.at[number],
            recv_sem=recv_sems.at[number],
            device_id={"ctx": c_to, "wsh": w_to},
            device_id_type=MESH,
        )
        copy.start()
        if roles[-1] is None:
            started.append(copy)
        else:
            sent_by_role.append((roles[-1], like, number))

    def arrived(key, landing, offset=0):
        number = numbers.take(key) + offset
        pltpu.make_async_copy(landing, landing, recv_sems.at[number]).wait()

    def local(key, src, dst):
        copy = pltpu.make_async_copy(src, dst, local_sems.at[locals_.take(key)])
        copy.start()
        return copy

    peers = [(c, bit_xor(w, j)) for j in (1, 2, 3)]
    peers += [(bit_xor(c, j), w) for j in range(1, CTX)]
    peers += [(bit_xor(c, 1), bit_xor(w, 1))]

    def bit(value, mask):
        return (value // mask) % 2

    first_col = pl.multiple_of((3 * a) // 2 * 128, 128)
    first_row = pl.multiple_of(a % 2 * 64, 64)

    def shard(name):
        if name < PART_Q:
            return shards[name]
        return shards[name - PART_Q].at[:, pl.ds(first_col, SLICE)]

    loads = {TOKENS: local(TOKENS, tokens.at[0], S.x)}
    for name in (PART_K, PART_V, PART_Q, O, IN, OUT):
        loads[name] = local((LOAD, name), shard(name), S.full[name].at[w])
    loads[TEACHER] = local(TEACHER, teacher.at[0], S.teacher)

    barrier = pltpu.get_barrier_semaphore()
    for c_to, w_to in peers:
        pl.semaphore_signal(
            barrier, inc=1, device_id={"ctx": c_to, "wsh": w_to}, device_id_type=MESH
        )
    pl.semaphore_wait(barrier, len(peers))

    def mine(name):
        return bit(c, SECOND_WAY[name])

    def pieces(name):
        tall, across = PIECES.get(name, (1, 1))
        return range(tall * across)

    def piece(name, which, number):
        rows, cols = WEIGHT_SHAPES[name]
        tall, across = PIECES.get(name, (1, 1))
        high, broad = rows // 2 // tall, cols // across
        row = which * (rows // 2) + number // across * high
        return pl.ds(pl.multiple_of(row, 16), high), slice(
            number % across * broad, (number % across + 1) * broad
        )

    def send_core(name):
        remote((WEIGHT_CORE, name), shard(name), S.full[name].at[w], 0, 1)

    def send_x(name):
        for i in pieces(name):
            rows, cols = piece(name, mine(name), i)
            if name < PART_Q:
                source = shards[name].at[rows, cols]
            else:
                source = shards[name - PART_Q].at[rows, pl.ds(first_col, SLICE)]
            remote((WEIGHT_X, name, i), source, S.full[name].at[w, rows, cols], 0, 2)

    for name in (PART_K, PART_V, PART_Q):
        send_x(name)
        send_core(name)
    loads[TOKENS].wait()
    x_low = S.x[...]
    S.xt[c] = x_low.T
    remote((X_LINE, 1), S.xt.at[c], S.xt.at[c], 2, 0)

    @only(False)
    def x_to_middle():
        remote((X_LINE, 3), S.xt.at[c], S.xt.at[c], 6, 0, like=lambda: S.xt.at[0])

    bias_rows = [row[...].astype(F32).reshape(1, HW) for row in biases[:8]]
    tall = jnp.concatenate(bias_rows, axis=0)
    valid_high = (valid[0] // 64).astype(F32)
    valid_low = (valid[0] % 64).astype(F32)
    wide_rows = [biases[8][...].astype(F32).reshape(1, D)]
    wide_rows += [jnp.full((1, D), 64.0, F32) * valid_high, jnp.full((1, D), 1.0, F32) * valid_low]
    wide_rows += [jnp.zeros((5, D), F32)]
    S.small[w, :, 0:HW] = jnp.concatenate(
        [tall, jnp.concatenate(wide_rows, axis=0)[:, 0:HW]], axis=0
    ).astype(BF)
    S.small[w, 8:16, HW:D] = jnp.concatenate(wide_rows, axis=0)[:, HW:D].astype(BF)

    for j in (1, 2, 3):
        remote((SMALL, j), S.small.at[w], S.small.at[w], 0, j)
    for name in (O, IN, OUT):
        send_x(name)
        send_core(name)

    def pump_x(name, number=0):
        slot = S.full[name].at[bit_xor(w, 2), *piece(name, mine(name), number)]
        arrived((WEIGHT_X, name, number), slot)
        remote((WEIGHT_SECOND, name, number), slot, slot, SECOND_WAY[name], 0)
        remote((WEIGHT_CORE_X, name, number), slot, slot, 0, 1)

    def pump_second(name, number=0):
        slot = S.full[name].at[bit_xor(w, 2), *piece(name, 1 - mine(name), number)]
        arrived((WEIGHT_SECOND, name, number), slot)
        remote((WEIGHT_CORE_SECOND, name, number), slot, slot, 0, 1)

    def weight_ready(name, numbers_=(0,), first=True):
        full = S.full[name]
        if first:
            loads[name].wait()
            arrived((WEIGHT_CORE, name), full.at[bit_xor(w, 1)])
        for i in numbers_:
            near = full.at[bit_xor(w, 3), *piece(name, mine(name), i)]
            far = full.at[bit_xor(w, 3), *piece(name, 1 - mine(name), i)]
            arrived((WEIGHT_CORE_X, name, i), near)
            arrived((WEIGHT_CORE_SECOND, name, i), far)

    def square(name):
        return S.full[name][...].reshape(D, D)

    starts, running = [], 0
    for i in range(lengths.shape[1]):
        starts.append(running)
        running = running + lengths[0, i]
    limit = valid[0]

    def code_of(position):
        code = jnp.zeros(position.shape, jnp.int32)
        for start in starts:
            code = code + (start <= position).astype(jnp.int32)
        return 2 * code + (position < limit).astype(jnp.int32)

    lane = lax.broadcasted_iota(jnp.int32, (1, 4 * ROWS), 1)
    query_code = code_of((2 * (lane // ROWS) + b) * ROWS + lane % ROWS)

    def key_code(block):
        return code_of(block * ROWS + lax.broadcasted_iota(jnp.int32, (ROWS, 1), 0))

    own_live = c * ROWS + lax.broadcasted_iota(jnp.int32, (ROWS, 1), 0) < limit

    def block_on(j, pair):
        return 2 * bit_xor(a, j) + pair

    def pass_x(key, j, onward, bits):
        block = S.xt.at[block_on(j, b)]
        arrived((key, j), block)
        remote(onward, block, block, bits, 0, like=lambda: S.xt.at[0])

    def vector(row):
        return S.vectors[row : row + 1, :]

    def to_group(key, source_of, everywhere):
        for j in (1, 2, 3):
            to = bit_xor(w, j)
            remote((*key, j), source_of(to), everywhere.at[w], 0, j)

    def from_group(key, everywhere):
        for j in (1, 2, 3):
            arrived((*key, j), everywhere.at[bit_xor(w, j)])

    def to_near(key, source, everywhere):
        for j in (1, 2):
            remote((*key, j), source, everywhere.at[w], 0, j)

    def pass_to_core(key, everywhere):
        slot = everywhere.at[bit_xor(w, 2)]
        arrived((*key, 2), slot)
        remote((*key, 3), slot, slot, 0, 1)

    def from_near(key, everywhere):
        for j in (1, 3):
            arrived((*key, j), everywhere.at[bit_xor(w, j)])

    def lanes(parts):
        return jnp.concatenate(parts, axis=1)

    finishing = []

    def small_vectors():
        for j in (1, 2, 3):
            arrived((SMALL, j), S.small.at[bit_xor(w, j)])
        S.vectors[0:8, :] = jnp.concatenate(
            [S.small[i, 0:8, 0:HW].astype(F32) for i in range(GROUP)], axis=1
        )
        small = [S.small[i, 8:16, :].astype(F32) for i in range(GROUP)]
        S.vectors[8:16, :] = jnp.concatenate(
            [part[0:1] for part in small]
            + [sum(part[1:2] + part[2:3] for part in small), jnp.zeros((3, D), F32)],
            axis=0,
        )

    def pass_near_end():
        arrived((X_LINE, 1), S.xt.at[block_on(1, b)])

        @only(False)
        def to_other_middle():
            block = S.xt.at[block_on(1, b)]
            remote((X_LINE, 2), block, block, 6, 0, like=lambda: S.xt.at[0])

    def pass_middle():
        @only(False)
        def to_near_end():
            pass_x(X_LINE, 3, (X_EDGE, 2), 2)

    def pass_far_end():
        @only(False)
        def to_near_end():
            pass_x(X_LINE, 2, (X_EDGE, 3), 2)

    def head_weights():
        for name in (PART_K, PART_V, PART_Q):
            weight_ready(name)
        for i, (name, bias) in enumerate(((PART_K, None), (PART_V, 1), (PART_Q, 0))):
            rows = slice(HW * i, HW * (i + 1))
            S.turned[...] = S.full[name][...].reshape(D, SLICE).T
            S.head_weight[rows, :] = S.turned[pl.ds(first_row, HW), :]
            if bias is None:
                S.head_bias[rows, :] = jnp.zeros((HW, ROWS), F32)
            else:
                row = S.vectors[bias : bias + 1, pl.ds(first_col, SLICE)]
                S.tall_bias[...] = jnp.broadcast_to(row, (ROWS, SLICE)).T
                S.head_bias[rows, :] = S.tall_bias[pl.ds(first_row, HW), :]

    def project(j):
        if j > 1:

            @only(True)
            def from_middle():
                arrived((X_EDGE, j), S.xt.at[block_on(j, b)])

        block = block_on(j, b)
        out = matmul(S.head_weight[...], S.xt[block]) + S.head_bias[...]
        S.kv[block] = out[0 : 2 * HW].astype(BF)
        S.q[block // 2] = out[2 * HW :].astype(BF)
        remote((KEY_VALUE, j), S.kv.at[block], S.kv.at[block], 1, 0)

    score_scale = 1.0 / math.sqrt(HD)

    def wide(ref, h):
        return lanes([ref[i, HD * h : HD * (h + 1), :] for i in range(4)])

    def attend_block(block):
        allowed = key_code(block) == query_code
        for h in range(HEADS):
            scores = tn(S.kv[block, HD * h : HD * (h + 1), :], wide(S.q, h)) * score_scale
            weights = jnp.exp(jnp.where(allowed, scores, MASKED))
            S.weights[block, h] = weights
            S.total[h, 0:1, :] += jnp.sum(weights, axis=0, keepdims=True)
            value_t = S.kv[block, HW + HD * h : HW + HD * (h + 1), :]
            S.mix[h] += matmul(value_t, weights.astype(BF))

    def attend_line():
        S.mix[...] = jnp.zeros(S.mix.shape, F32)
        S.total[...] = jnp.zeros(S.total.shape, F32)

        @pl.loop(0, 4)
        def every_block(i):
            attend_block(2 * i + b)

    def attend_pair(j):
        arrived((KEY_VALUE, j), S.kv.at[block_on(j, 1 - b)])
        attend_block(block_on(j, 1 - b))

    def send_context():
        for h in range(HEADS):
            context_t = (S.mix[h] / S.total[h, 0:1, :]).astype(BF)
            for i in range(4):
                S.ctx_send[i, HD * h : HD * (h + 1), :] = context_t[:, ROWS * i : ROWS * (i + 1)]
        for j in (1, 2, 3):
            to = bit_xor(a, j)
            remote((CONTEXT, j), S.ctx_send.at[to], S.ctx.at[a], 2 * j, 0)
        S.ctx[a] = S.ctx_send[a]

    def first_norm():
        weight_ready(O)
        for j in (1, 2, 3):
            arrived((CONTEXT, j), S.ctx.at[bit_xor(a, j)])
        attn = tn(S.ctx[...].reshape(D, ROWS), square(O)) + vector(2)
        normal_one, inverse_one = norm_parts(S.x[...].astype(F32) + attn)
        settled = normal_one * vector(3) + vector(4)
        S.first[...] = normal_one
        S.inverse[...] = jnp.broadcast_to(inverse_one, (ROWS, 128))
        S.keep[...] = settled
        S.set_low[...] = settled.astype(BF)
        to_near((SETTLED_ALL,), S.set_low, S.set_all)
        S.set_all[w] = S.set_low[...]
        to_group((CONTEXT_ALL,), lambda to: S.ctx.at[pl.ds(2 * (to // 2), 2)], S.ctx_all)
        S.ctx_all[w] = S.ctx[pl.ds(2 * x, 2)]

    def pass_settled():
        pass_to_core((SETTLED_ALL,), S.set_all)

    def gelu(inner):
        return 0.5 * inner * (1.0 + jnp.tanh(GELU_C * (inner + 0.044715 * inner * inner * inner)))

    def gelu_slope(inner):
        squared = inner * inner
        bend = jnp.tanh(GELU_C * (inner + 0.044715 * squared * inner))
        return 0.5 * (1.0 + bend) + 0.5 * inner * (1.0 - bend * bend) * (
            GELU_C * (1.0 + 3 * 0.044715 * squared)
        )

    def feed_in(t):
        weight_ready(IN, (t,), t == 0)
        w_part = S.full[IN][:, :, D * t : D * (t + 1)].reshape(D, D)
        inner = matmul(S.set_low[...], w_part) + vector(8 + t)
        S.inner[t] = inner
        S.act[t] = gelu(inner).astype(BF)

    def note(row, value):
        S.sg[row : row + 1, :] = jnp.sum(value.astype(F32), axis=0, keepdims=True)

    def result_and_loss():
        weight_ready(OUT, range(4))
        branch = vector(5)
        for t in range(4):
            branch = branch + matmul(S.act[t], S.full[OUT][t])
        normal_two, inverse_two = norm_parts(S.keep[...] + branch)
        result = normal_two * vector(6) + vector(7)
        S.out_low[...] = result.astype(BF)
        finishing.append(local(OUTPUT, S.out_low, output))
        loads[TEACHER].wait()
        diff = jnp.where(own_live, result - S.teacher[...].astype(F32), 0.0)
        count = vector(12)
        upstream = diff * ((ROWS * CTX * GROUP) / count)
        d_second = norm_back(upstream * vector(6), normal_two, inverse_two)
        for i in range(2):
            S.bg[i] = d_second[:, 384 * i : 384 * (i + 1)].astype(BF)
            to_near((BRANCH_GRAD_ALL, i), S.bg.at[i], S.bg_all.at[i])
        for i in range(2):
            S.bg_all[i, w] = S.bg[i]
        S.keep[...] = d_second
        S.sg[...] = jnp.zeros((16, D), F32)
        note(12, diff * diff)
        S.sg[13:14, :] = count * (1.0 / (CTX * GROUP))
        note(6, upstream * normal_two)
        note(7, upstream)
        note(5, d_second.astype(BF))

    def feed_back():
        d_settled = S.keep[...]
        branch_grad = lanes([S.bg[0], S.bg[1]])
        for t in range(4):
            d_act = right_product(branch_grad, S.full[OUT][t])
            inner_grad = (d_act * gelu_slope(S.inner[t])).astype(BF)
            note(8 + t, inner_grad)
            w_part = S.full[IN][:, :, D * t : D * (t + 1)].reshape(D, D)
            d_settled = d_settled + right_product(inner_grad, w_part)
        S.keep[...] = d_settled

    def pass_branch_grad(i):
        pass_to_core((BRANCH_GRAD_ALL, i), S.bg_all.at[i])

    def first_norm_back():
        d_settled, normal_one = S.keep[...], S.first[...]
        d_first = norm_back(d_settled * vector(3), normal_one, S.inverse[:, 0:1])
        attn_grad = d_first.astype(BF)
        context_grad = right_product(attn_grad, square(O)).T.astype(BF)
        for i in range(4):
            S.cg_send[i] = context_grad[HW * i : HW * (i + 1), :]
        for j in (1, 2, 3):
            to = bit_xor(a, j)
            remote((CONTEXT_GRAD, j), S.cg_send.at[to], S.cg.at[a], 2 * j, 0)
        S.cg[a] = S.cg_send[a]
        for i in range(2):
            S.ag_half[i] = attn_grad[:, 384 * i : 384 * (i + 1)]
        to_group((ATTN_GRAD_ALL,), lambda to: S.ag_half.at[to % 2], S.ag_all)
        S.ag_all[w] = S.ag_half[core]
        note(3, d_settled * normal_one)
        note(4, d_settled)
        note(2, attn_grad)
        S.keep[...] = d_first

    half = a // 2

    def y_end(lot):
        got, total = S.got[lot], S.sum[lot]
        arrived((REDUCE, lot, 0), got[0])
        total[0][...] = (S.part[lot][b].astype(F32) + got[0][...].astype(F32)).astype(BF)

        @only(True)
        def to_middle():
            remote((REDUCE, lot, 1), total[0], got[1], 2, 0, like=lambda: got[1])

    def y_middle(lot):
        @only(False)
        def swap_halves():
            got, total = S.got[lot], S.sum[lot]
            arrived((REDUCE, lot, 1), got[1])
            total[1][...] = (total[0][...].astype(F32) + got[1][...].astype(F32)).astype(BF)
            there = total[1].at[1 - half]
            remote((REDUCE, lot, 2), there, got[2], 6, 0, like=lambda: got[2])

    def y_spread_middle(lot):
        part = S.done[lot].at[b, half]
        remote((SPREAD, lot, 0), part, part, 6, 0, like=lambda: S.done[lot].at[0, 0])

    def y_last(lot):
        @only(False)
        def own_half():
            got = S.got[lot][2]
            arrived((REDUCE, lot, 2), got)
            total = (S.sum[lot][1][half].astype(F32) + got[...].astype(F32)).astype(BF)
            if lot in LOT_IN:
                own, done = S.own[lot], S.done[lot]
                own[...] = total
                done[b, half, w] = own[w]
                for q in (1, 2, 3):
                    slot = done.at[b, half, w]
                    to = bit_xor(w, q)
                    remote((GROUP_X, lot, q), own.at[to], slot, 0, q, like=lambda: own.at[0])
            else:
                S.done[lot][b, half] = total
                y_spread_middle(lot)

    def y_group(lot):
        @only(False)
        def gathered():
            for q in (1, 2, 3):
                arrived((GROUP_X, lot, q), S.done[lot].at[b, half, bit_xor(w, q)])
            y_spread_middle(lot)

    def y_spread_end(lot):
        @only(False)
        def to_end():
            done = S.done[lot].at[b]
            arrived((SPREAD, lot, 0), S.done[lot].at[b, 1 - half])
            remote((SPREAD, lot, 1), done, done, 2, 0, like=lambda: S.done[lot].at[0])

    def result_of(lot):
        return grad_in[lot - LOT_IN[0]] if lot in LOT_IN else grad_out.at[(lot - LOT_OUT[0]) // 2, (lot - LOT_OUT[0]) % 2]

    def y_give(lot):
        done = S.done[lot].at[b]

        @only(True)
        def from_middle_device():
            arrived((SPREAD, lot, 1), done)

        if lot not in LOT_O:
            out = result_of(lot).at[b]
            remote((GIVE, lot), done, out, 1, 0)
            finishing.append(local((GIVE, lot), done, out))
            return
        remote((GIVE, 0), done, grad_o.at[core], 1, 0, core, 2, 2 * x + b)

        @pl.when(core == b)
        def keep_own():
            local((OWN, 0), done, grad_o.at[core])

        @pl.when(core != b)
        def give_core():
            remote((OWN, 0), done, grad_o.at[core], 0, 1)
            started.pop()

    def settle():
        for lot in LOT_PAIR[1:]:
            arrived((GIVE, lot), result_of(lot).at[1 - b])
        done = S.done[0].at[b]

        @pl.when(core == b)
        def from_chip():
            pltpu.make_async_copy(
                done, grad_o.at[core], local_sems.at[locals_.take((OWN, 0))]
            ).wait()
            arrived((OWN, 0), grad_o.at[1 - core])

        @pl.when(core != b)
        def from_partner():
            arrived((GIVE, 0), grad_o.at[0], 0)
            arrived((GIVE, 0), grad_o.at[1], 1)
            sent = numbers.take((OWN, 0))
            pltpu.make_async_copy(done, done, send_sems.at[sent]).wait()

    def reduce_start(lot):
        @only(True)
        def to_middle():
            target = S.got[lot][0]
            remote((REDUCE, lot, 0), S.part[lot], target, 2, 0, like=lambda: target)

    def reduce_middle(lot):
        @only(False)
        def swap_halves():
            got = S.got[lot][0]
            arrived((REDUCE, lot, 0), got)
            total = S.part[lot][...].astype(F32) + got[...].astype(F32)
            S.sum[lot][0][...] = total.astype(BF)
            there, target = S.sum[lot][0].at[1 - half], S.got[lot][1]
            remote((REDUCE, lot, 1), there, target, 6, 0, like=lambda: target)

    def reduce_pair(lot):
        @only(False)
        def swap_quarters():
            got = S.got[lot][1]
            arrived((REDUCE, lot, 1), got)
            total = S.sum[lot][0][half].astype(F32) + got[...].astype(F32)
            S.sum[lot][1][...] = total.astype(BF)
            there, target = S.sum[lot][1].at[1 - b], S.got[lot][2]
            remote((REDUCE, lot, 2), there, target, 1, 0, like=lambda: target)

    def reduce_last(lot):
        @only(False)
        def own_quarter():
            got = S.got[lot][2]
            arrived((REDUCE, lot, 2), got)
            total = (S.sum[lot][1][b].astype(F32) + got[...].astype(F32)).astype(BF)
            S.done[lot][half, b] = total
            part = S.done[lot].at[half, b]
            remote((SPREAD, lot, 0), part, part, 1, 0, like=lambda: S.done[lot].at[0, 0])

    def spread_middle(lot):
        @only(False)
        def swap_back():
            arrived((SPREAD, lot, 0), S.done[lot].at[half, 1 - b])
            part = S.done[lot].at[half]
            remote((SPREAD, lot, 1), part, part, 6, 0, like=lambda: S.done[lot].at[0])

    def spread_end(lot):
        @only(False)
        def to_end():
            done = S.done[lot]
            arrived((SPREAD, lot, 1), done.at[1 - half])
            part = done.at[:, b]
            remote((SPREAD, lot, 2), part, part, 2, 0, like=lambda: done.at[:, 0])

    def spread_ends(lot):
        @only(True)
        def swap_at_ends():
            done = S.done[lot]
            part = done.at[:, b]
            arrived((SPREAD, lot, 2), part)
            remote((SPREAD, lot, 3), part, part, 1, 0, like=lambda: done.at[:, 0])

    def finish_lot(lot):
        @only(True)
        def from_pair():
            arrived((SPREAD, lot, 3), S.done[lot].at[:, 1 - b])

        finishing.append(local((GIVE, lot), S.done[lot], grad_out.at[(lot - LOT_OUT[0]) // 2, (lot - LOT_OUT[0]) % 2]))

    def inner_again():
        from_near((SETTLED_ALL,), S.set_all)
        settled_all = S.set_all[...].reshape(GROUP * ROWS, D)
        hidden = pl.ds(pl.multiple_of(D * w, D), D)
        S.inner_all[...] = (
            matmul(settled_all, S.full[IN][:, :, hidden].reshape(D, D))
            + S.vectors[pl.ds(8 + w, 1), :]
        )
        S.act_all[...] = gelu(S.inner_all[...]).astype(BF)

    def out_part(i):
        from_near((BRANCH_GRAD_ALL, i), S.bg_all.at[i])
        grad = tn(S.act_all[...], S.bg_all[i].reshape(GROUP * ROWS, 384)).astype(BF)
        for k in range(2):
            lot = LOT_OUT[2 * i + k]
            S.part[lot][...] = grad[384 * k : 384 * (k + 1)].reshape(2, 2, 96, 384)
            if lot in LOT_PAIR:
                remote((REDUCE, lot, 0), S.part[lot].at[1 - b], S.got[lot][0], 1, 0)
            else:
                reduce_start(lot)

    def in_part():
        branch_grad_all = lanes([S.bg_all[i].reshape(GROUP * ROWS, 384) for i in range(2)])
        inner_grad_all = (
            right_product(branch_grad_all, S.full[OUT][w]) * gelu_slope(S.inner_all[...])
        ).astype(BF)
        grad = tn(S.set_all[...].reshape(GROUP * ROWS, D), inner_grad_all).astype(BF)
        for i, lot in enumerate(LOT_IN):
            for j in range(2):
                side = grad[:, 384 * j : 384 * (j + 1)].reshape(4, 2, 2, 48, 384)
                for k in range(2):
                    S.part[lot][j, k] = side[:, k, i]
            remote((REDUCE, lot, 0), S.part[lot].at[1 - b], S.got[lot][0], 1, 0)

    def attention_back():
        for j in (1, 2, 3):
            arrived((CONTEXT_GRAD, j), S.cg.at[bit_xor(a, j)])
        for h in range(HEADS):
            grad = wide(S.cg, h).astype(F32)
            row_total = S.total[h, 0:1, :]
            S.wg[h] = (grad / row_total).astype(BF)
            S.total[h, 1:2, :] = -jnp.sum(grad * S.mix[h], axis=0, keepdims=True) / (
                row_total * row_total
            )
        S.mix[...] = jnp.zeros(S.mix.shape, F32)

        def attend_back(pair, i):
            block = 2 * i + pair
            for h in range(HEADS):
                key_rows = slice(HD * h, HD * (h + 1))
                value_rows = slice(HW + HD * h, HW + HD * (h + 1))
                weights = S.weights[block, h]
                grad = S.wg[h]
                weight_grad = tn(S.kv[block, value_rows, :], grad) + S.total[h, 1:2, :]
                score_grad = (weights * weight_grad).astype(BF)
                S.mix[h] += matmul(S.kv[block, key_rows, :], score_grad)
                S.dkv[pair, i, key_rows, :] = (
                    right_product(wide(S.q, h), score_grad) * score_scale
                ).astype(BF)
                value_grad = right_product(grad, weights.astype(BF))
                S.dkv[pair, i, value_rows, :] = value_grad.astype(BF)

        @pl.loop(0, CTX)
        def every_block(block):
            attend_back(block % 2, block // 2)

        remote((KEY_VALUE_GRAD,), S.dkv.at[1 - b], S.dkv_pair, 1, 0)
        for h in range(HEADS):
            rows = slice(2 * HW + HD * h, 2 * HW + HD * (h + 1))
            S.grads[rows, :] = (S.mix[h] * score_scale).astype(BF)
        S.grads[3 * HW :, :] = jnp.zeros((HEAD_COLS - 3 * HW, 4 * ROWS), BF)

    def o_part():
        from_group((CONTEXT_ALL,), S.ctx_all)
        from_group((ATTN_GRAD_ALL,), S.ag_all)
        context_all = lanes([S.ctx_all[i].reshape(384, ROWS) for i in range(GROUP)])
        grad = matmul(context_all, S.ag_all[...].reshape(GROUP * ROWS, 384))
        S.part[0][...] = grad.astype(BF).reshape(2, 2, 96, 384)
        remote((REDUCE, 0, 0), S.part[0].at[1 - b], S.got[0][0], 1, 0)

    def heads_part():
        arrived((KEY_VALUE_GRAD,), S.dkv_pair)
        for i in range(4):
            S.grads[0 : 2 * HW, ROWS * i : ROWS * (i + 1)] = (
                S.dkv[b, i].astype(F32) + S.dkv_pair[i].astype(F32)
            ).astype(BF)
        own_inputs = lanes([S.xt[2 * i + b] for i in range(4)])
        heads = right_product(own_inputs, S.grads[...]).astype(BF)
        S.heads[...] = heads.reshape(2, 2, HW, HEAD_COLS)
        for i in range(2):
            remote((HEADS_CORE, i), S.heads.at[i, 1 - core], S.heads_core.at[i], 0, 1)

    def input_parts():
        parts = tn(S.grads[0 : 3 * HW, :], S.head_weight[...])
        S.dx_send[...] = parts.astype(BF).reshape(4, ROWS, D)

        @only(True)
        def to_middle():
            for j in (1, 2, 3):
                source, target = S.dx_send.at[bit_xor(a, j)], S.dx_end.at[j - 1]
                remote((INPUT_PARTS, j), source, target, 2, 0, like=lambda: S.dx_end.at[0])

    def input_middle():
        @only(False)
        def to_other_middle():
            for j in (1, 2, 3):
                arrived((INPUT_PARTS, j), S.dx_end.at[j - 1])
            for i, j in enumerate((3, 2)):
                both = S.dx_send[bit_xor(a, j)].astype(F32) + S.dx_end[i + 1].astype(F32)
                S.dx_middle[i] = both.astype(BF)
            remote((INPUT_PARTS, 4), S.dx_middle, S.dx_got, 6, 0, like=lambda: S.dx_middle)

    def input_end():
        @only(False)
        def to_near_end():
            arrived((INPUT_PARTS, 4), S.dx_got)
            both = S.dx_send[bit_xor(a, 1)].astype(F32) + S.dx_got[1].astype(F32)
            S.dx_back[...] = both.astype(BF)
            remote((INPUT_PARTS, 5), S.dx_back, S.dx_last, 2, 0, like=lambda: S.dx_back)

    def vectors_group():
        S.column[...] = jnp.zeros((D, ROWS), F32)
        heads_rows = pl.ds(pl.multiple_of(HW * a, HW), HW)
        for row, first in ((1, HW), (0, 2 * HW)):
            sums = jnp.sum(S.grads[first : first + HW, :].astype(F32), axis=1, keepdims=True)
            S.column[heads_rows, :] = jnp.broadcast_to(sums, (HW, ROWS))
            S.sg[row : row + 1, :] = S.column[...].T[0:1, :]
        for j in (1, 2, 3):
            remote((VECTORS_W, j), S.sg, S.sg_w.at[w], 0, j)
        S.sg_w[w] = S.sg[...]

    own_rows = pl.ds(pl.multiple_of(8 * core, 8), 8)

    def vectors_line():
        for j in (1, 2, 3):
            arrived((VECTORS_W, j), S.sg_w.at[bit_xor(w, j)])
        S.sg_all[...] = (S.sg_w[0] + S.sg_w[1]) + (S.sg_w[2] + S.sg_w[3])
        S.sg_z[0] = S.sg_all[own_rows, :]

        @only(True)
        def to_middle():
            remote((VECTORS_Z, 1), S.sg_z.at[0], S.sg_z.at[1], 2, 0, like=lambda: S.sg_z.at[1])

    def vectors_middle():
        @only(False)
        def to_other_middle():
            arrived((VECTORS_Z, 1), S.sg_z.at[1])
            S.sg_z[2] = S.sg_z[0] + S.sg_z[1]
            remote((VECTORS_Z, 2), S.sg_z.at[2], S.sg_z.at[3], 6, 0, like=lambda: S.sg_z.at[2])

    def vectors_end():
        @only(False)
        def to_end():
            arrived((VECTORS_Z, 2), S.sg_z.at[3])
            S.sg_y[b] = S.sg_z[2] + S.sg_z[3]
            whole = S.sg_y.at[b]
            remote((VECTORS_Z, 3), whole, whole, 2, 0, like=lambda: S.sg_y.at[0])

    def vectors_pair():
        @only(True)
        def from_middle():
            arrived((VECTORS_Z, 3), S.sg_y.at[b])

        remote((VECTORS_Y,), S.sg_y.at[b], S.sg_y.at[b], 1, 0)

    def vectors_core():
        arrived((VECTORS_Y,), S.sg_y.at[1 - b])
        S.sg_rows[core] = S.sg_y[0] + S.sg_y[1]
        remote((VECTORS_CORE,), S.sg_rows.at[core], S.sg_rows.at[core], 0, 1)

    def vectors_done():
        arrived((VECTORS_CORE,), S.sg_rows.at[1 - core])
        everything = S.sg_rows[...].reshape(16, D)
        for i in range(4):
            S.smalls[i] = everything[:, HW * i : HW * (i + 1)]
        finishing.append(local((VECTORS_Y,), S.smalls, smalls_out))
        finishing.append(local((VECTORS_Z,), S.sg_rows, rows_out))

    def heads_x():
        for i in range(2):
            arrived((HEADS_CORE, i), S.heads_core.at[i])
        for i in range(2):
            S.heads_sum[i] = (S.heads[i, core].astype(F32) + S.heads_core[i].astype(F32)).astype(BF)
        remote((HEADS_X,), S.heads_sum.at[1 - x], S.heads_x, 0, 2)

    def heads_y():
        arrived((HEADS_X,), S.heads_x)
        S.heads_row[...] = (
            (S.heads_sum[x].astype(F32) + S.heads_x[...].astype(F32))
            .astype(BF)
            .reshape(2, HW // 2, HEAD_COLS)
        )
        remote((HEADS_Y,), S.heads_row.at[1 - b], S.heads_y, 1, 0)

    def heads_line():
        arrived((HEADS_Y,), S.heads_y)
        S.heads_done[a] = (S.heads_row[b].astype(F32) + S.heads_y[...].astype(F32)).astype(BF)
        own = S.heads_done.at[a]
        remote((HEADS_LINE, 1), own, own, 2, 0)

        @only(False)
        def to_other_middle():
            remote((HEADS_LINE, 3), own, own, 6, 0, like=lambda: S.heads_done.at[0])

    def pass_heads(key, j, onward, bits):
        part = S.heads_done.at[bit_xor(a, j)]
        if key is not None:
            arrived((key, j), part)
        remote(onward, part, part, bits, 0, like=lambda: S.heads_done.at[0])

    def heads_near_end():
        arrived((HEADS_LINE, 1), S.heads_done.at[bit_xor(a, 1)])

        @only(False)
        def to_other_middle():
            pass_heads(None, 1, (HEADS_LINE, 2), 6)

    def heads_middle():
        @only(False)
        def to_near_end():
            pass_heads(HEADS_LINE, 3, (HEADS_EDGE, 2), 2)

    def heads_far_end():
        @only(False)
        def to_near_end():
            pass_heads(HEADS_LINE, 2, (HEADS_EDGE, 3), 2)

    def heads_pair():
        @only(True)
        def from_middle():
            for j in (2, 3):
                arrived((HEADS_EDGE, j), S.heads_done.at[bit_xor(a, j)])

        remote((HEADS_PAIR,), S.heads_done, heads_out.at[b], 1, 0)
        finishing.append(local((HEADS_PAIR,), S.heads_done, heads_out.at[b]))

    def input_done():
        S.first[...] = S.keep[...] + S.dx_send[a].astype(F32)

        @only(True)
        def at_end():
            arrived((INPUT_PARTS, 5), S.dx_last)
            S.first[...] += S.dx_last[...].astype(F32)

        @only(False)
        def in_middle():
            S.first[...] += S.dx_end[0].astype(F32) + S.dx_got[0].astype(F32)

        finishing.append(local(INPUT_GRAD, S.first, input_grad_out))

    marked = []

    def mark():
        marked.extend(started)
        started.clear()

    def retire():
        for copy in marked:
            copy.wait_send()
        marked.clear()

    def mark_late():
        mark()

    def retire_late():
        retire()

    for step, *lot in (
        (pass_near_end,),
        (pump_x, PART_K),
        (pass_middle,),
        (pump_x, PART_Q),
        (pump_x, PART_V),
        (pump_second, PART_Q),
        (pump_x, O),
        (small_vectors,),
        (pass_far_end,),
        (pump_second, PART_V),
        (pump_second, PART_K),
        (head_weights,),
        (project, 0),
        (project, 2),
        (project, 1),
        (pump_x, IN, 0),
        (pump_x, IN, 1),
        (project, 3),
        (pump_second, O),
        (attend_line,),
        (attend_pair, 0),
        (pump_x, IN, 3),
        (attend_pair, 1),
        (attend_pair, 2),
        (pump_x, OUT, 0),
        (pump_second, IN, 1),
        (attend_pair, 3),
        (send_context,),
        (pump_x, IN, 2),
        (pump_x, OUT, 1),
        (pump_second, IN, 0),
        (pump_x, OUT, 2),
        (pump_second, OUT, 1),
        (pump_second, IN, 3),
        (pump_x, OUT, 3),
        (first_norm,),
        (feed_in, 0),
        (pump_second, OUT, 0),
        (feed_in, 1),
        (pump_second, OUT, 2),
        (pump_second, IN, 2),
        (feed_in, 2),
        (pump_second, OUT, 3),
        (feed_in, 3),
        (result_and_loss,),
        (pass_settled,),
        (feed_back,),
        (first_norm_back,),
        (mark,),
        (inner_again,),
        (pass_branch_grad, 0),
        (pass_branch_grad, 1),
        (out_part, 0),
        (out_part, 1),
        (attention_back,),
        (reduce_middle, 5),
        (reduce_pair, 5),
        (y_end, 3),
        (o_part,),
        (reduce_middle, 6),
        (y_middle, 3),
        (reduce_last, 5),
        (in_part,),
        (y_last, 3),
        (y_end, 4),
        (heads_part,),
        (y_middle, 4),
        (y_end, 0),
        (vectors_group,),
        (spread_middle, 5),
        (y_spread_end, 3),
        (heads_x,),
        (y_last, 4),
        (y_middle, 0),
        (vectors_line,),
        (vectors_middle,),
        (spread_end, 5),
        (y_spread_end, 4),
        (y_end, 1),
        (y_last, 0),
        (heads_y,),
        (y_middle, 1),
        (reduce_pair, 6),
        (spread_ends, 5),
        (retire,),
        (vectors_end,),
        (y_spread_end, 0),
        (heads_line,),
        (mark_late,),
        (y_end, 2),
        (reduce_last, 6),
        (y_give, 3),
        (y_give, 4),
        (y_last, 1),
        (vectors_pair,),
        (y_give, 0),
        (heads_near_end,),
        (heads_middle,),
        (y_group, 1),
        (heads_far_end,),
        (y_middle, 2),
        (input_parts,),
        (spread_middle, 6),
        (heads_pair,),
        (y_last, 2),
        (y_spread_end, 1),
        (spread_end, 6),
        (y_give, 1),
        (y_group, 2),
        (spread_ends, 6),
        (input_middle,),
        (y_spread_end, 2),
        (y_give, 2),
        (vectors_core,),
        (finish_lot, 5),
        (input_end,),
        (input_done,),
        (retire_late,),
        (vectors_done,),
        (finish_lot, 6),
    ):
        step(*lot)

    arrived((HEADS_PAIR,), heads_out.at[1 - b])
    settle()
    for copy in finishing:
        copy.wait()
    for copy in started:
        copy.wait_send()
    for end in (True, False):

        @only(end)
        def sent():
            for role, like, number in sent_by_role:
                if role == end:
                    source = like()
                    pltpu.make_async_copy(source, source, send_sems.at[number]).wait()


def finish_kernel(*refs):
    g_o, g_in0, g_in1, g_out, heads, smalls, rows, output, input_grad = refs[:9]
    r_q, r_k, r_v, r_o, r_in, r_out = refs[9:15]
    vectors, inner_bias, loss, r_output, r_input = refs[15:23], *refs[23:]
    step = pl.program_id(0)
    for i in range(2):
        r_o[:, 384 * i : 384 * (i + 1)] = g_o[i].reshape(HW // 2, 384).astype(F32)
        for j in range(4):
            first = D * j + 384 * i
            for k, source in enumerate((g_in0, g_in1)):
                r_in[48 * k : 48 * (k + 1), first : first + 384] = source[i, 0, j].astype(F32)
    for i in range(2):
        r_out[:, 384 * i : 384 * (i + 1)] = g_out[i].reshape(D // 2, 384).astype(F32)
    for i, result in ((0, r_k), (1, r_v), (2, r_q)):
        result[...] = jnp.concatenate(
            [heads[0, j, :, HW * i : HW * (i + 1)].astype(F32) for j in range(4)], axis=1
        )
    r_output[0] = output[...]
    r_input[0] = input_grad[...]

    @pl.when(step == 0)
    def once():
        w = lax.axis_index("wsh")
        for i in range(8):
            vectors[i][...] = smalls[w, i, :]
        inner_bias[...] = rows[1, w, :]
        error = jnp.sum(rows[1, 4:5, :])
        count = jnp.max(rows[1, 5:6, :])
        loss[0] = error / (count * D)


def fused_body(tokens, teacher, doc_lengths, valid_len, *weights):
    (
        q_weight,
        q_bias,
        k_weight,
        v_weight,
        v_bias,
        o_weight,
        o_bias,
        ln1_gain,
        ln1_bias,
        in_weight,
        in_bias,
        out_weight,
        out_bias,
        ln2_gain,
        ln2_bias,
    ) = weights
    hbm = pl.BlockSpec(memory_space=pl.ANY)
    smem = pl.BlockSpec(memory_space=pltpu.SMEM)
    vmem = pl.BlockSpec(memory_space=pltpu.VMEM)
    low = lambda *shape: jax.ShapeDtypeStruct(shape, BF)
    full = lambda *shape: jax.ShapeDtypeStruct(shape, F32)
    output, input_grad, g_o, g_in0, g_in1, g_out, heads, smalls, rows = pl.pallas_call(
        fused_kernel,
        out_shape=(
            low(ROWS, D),
            full(ROWS, D),
            low(2, 2, 96, 384),
            low(2, 2, 4, 48, 384),
            low(2, 2, 4, 48, 384),
            low(2, 2, 2, 2, 96, 384),
            low(2, 4, HW // 2, HEAD_COLS),
            full(GROUP, 16, HW),
            full(2, 8, D),
        ),
        in_specs=[hbm] * 8 + [smem] * 2 + [vmem] * 9,
        out_specs=[hbm] * 9,
        scratch_shapes=scratch_shapes()[0]
        + [
            pltpu.SemaphoreType.DMA((REMOTE_SEMS,)),
            pltpu.SemaphoreType.DMA((REMOTE_SEMS,)),
            pltpu.SemaphoreType.DMA((LOCAL_SEMS,)),
        ],
        compiler_params=pltpu.CompilerParams(
            collective_id=0, has_side_effects=True, vmem_limit_bytes=67043328
        ),
        name="layer",
    )(
        tokens,
        teacher,
        q_weight,
        k_weight,
        v_weight,
        o_weight,
        in_weight,
        out_weight,
        doc_lengths,
        valid_len,
        q_bias,
        v_bias,
        o_bias,
        ln1_gain,
        ln1_bias,
        out_bias,
        ln2_gain,
        ln2_bias,
        in_bias,
    )

    steps = 2
    square_out = pl.BlockSpec((HW // steps, D), lambda i: (i, 0))
    whole = lambda *shape: pl.BlockSpec(shape, lambda i: (0,) * len(shape))
    by_row = pl.BlockSpec((ROWS // steps, D), lambda i: (i, 0))
    results = pl.pallas_call(
        finish_kernel,
        grid=(steps,),
        out_shape=(full(HW, D),) * 4
        + (full(HW, FF), full(D, D))
        + (full(HW),) * 8
        + (full(D), full(1), low(1, ROWS, D), full(1, ROWS, D)),
        in_specs=[
            pl.BlockSpec((2, 1, 96, 384), lambda i: (0, i, 0, 0)),
            pl.BlockSpec((2, 1, 4, 48, 384), lambda i: (0, i, 0, 0, 0)),
            pl.BlockSpec((2, 1, 4, 48, 384), lambda i: (0, i, 0, 0, 0)),
            pl.BlockSpec((2, 1, 2, 2, 96, 384), lambda i: (0, i, 0, 0, 0, 0)),
            pl.BlockSpec((1, 4, HW // 2, HEAD_COLS), lambda i: (i, 0, 0, 0)),
            whole(GROUP, 16, HW),
            whole(2, 8, D),
            by_row,
            by_row,
        ],
        out_specs=[square_out] * 4
        + [
            pl.BlockSpec((HW // steps, FF), lambda i: (i, 0)),
            pl.BlockSpec((D // steps, D), lambda i: (i, 0)),
        ]
        + [whole(HW)] * 8
        + [
            whole(D),
            pl.BlockSpec(memory_space=pltpu.SMEM),
            pl.BlockSpec((1, ROWS // steps, D), lambda i: (0, i, 0)),
            pl.BlockSpec((1, ROWS // steps, D), lambda i: (0, i, 0)),
        ],
        compiler_params=pltpu.CompilerParams(dimension_semantics=("arbitrary",)),
        name="finish",
    )(g_o, g_in0, g_in1, g_out, heads, smalls, rows, output, input_grad)
    r_q, r_k, r_v, r_o, r_in, r_out = results[:6]
    vectors, inner_bias, loss, r_output, r_input = results[6:14], *results[14:]
    return (
        r_output,
        loss.reshape(()),
        r_input,
        r_q,
        vectors[0],
        r_k,
        r_v,
        vectors[1],
        r_o,
        vectors[2],
        vectors[3],
        vectors[4],
        r_in,
        inner_bias,
        r_out,
        vectors[5],
        vectors[6],
        vectors[7],
    )


def solution(mesh):
    in_specs = (
        P("wsh", "ctx", None),
        P("wsh", "ctx", None),
        P("wsh", None),
        P("wsh"),
        P("wsh", None),
        P("wsh"),
        P("wsh", None),
        P("wsh", None),
        P("wsh"),
        P("wsh", None),
        P("wsh"),
        P("wsh"),
        P("wsh"),
        P("wsh", None),
        P("wsh"),
        P("wsh", None),
        P("wsh"),
        P("wsh"),
        P("wsh"),
    )
    out_specs = (
        P("wsh", "ctx", None),
        P(),
        P("wsh", "ctx", None),
        P("wsh", None),
        P("wsh"),
        P("wsh", None),
        P("wsh", None),
        P("wsh"),
        P("wsh", None),
        P("wsh"),
        P("wsh"),
        P("wsh"),
        P("wsh", None),
        P("wsh"),
        P("wsh", None),
        P("wsh"),
        P("wsh"),
        P("wsh"),
    )
    program = fused_body if fused_fits(mesh) else body
    return jax.shard_map(program, mesh=mesh, in_specs=in_specs, out_specs=out_specs, check_vma=False)
```
